32 devices in a mesh: ctx: 4 (over y, x), exp: 8 (over z, core).
Axes of the slice: x: 2, y: 2, z: 4, core: 2. Of those that a mesh axis runs over, the one named last changes fastest.
Arguments:
- tokens: bfloat16 [12288, 2048], P(('ctx', 'exp')), may hold values from -6 to 6
- cotangent: bfloat16 [12288, 2048], P(('ctx', 'exp')), may hold values from -6 to 6
- routes: int32 [12288, 8], P(('ctx', 'exp')), may hold values from 0 to 15, all different within a row; in each aligned block of 384 rows (0 to 383, 384 to 767, ...) at most 240 rows name the same one
- block_of_slot: int32 [8, 8], P('exp'), may hold values from 0 to 7, as said below
- cont_seg: int32 [8, 512], P('exp'), may hold values from 0 to 1, never falling along the last dimension, each value on 1 to 384 neighbouring positions
- w_query: bfloat16 [2048, 2048], P(('ctx', 'exp')), may hold values from -0.125 to 0.125
- w_key: bfloat16 [2048, 2048], P(('ctx', 'exp')), may hold values from -0.125 to 0.125
- w_value: bfloat16 [2048, 2048], P(('ctx', 'exp')), may hold values from -0.125 to 0.125
- w_out: bfloat16 [2048, 2048], P(('ctx', 'exp')), may hold values from -0.75 to 0.75
- w_router: bfloat16 [2048, 16], P(('ctx', 'exp')), may hold values from -0.0625 to 0.0625
- attn_gain: bfloat16 [2048], P(('ctx', 'exp')), may hold values from 0.099609375 to 1.8984375
- query_gain: bfloat16 [2048], P(('ctx', 'exp')), may hold values from 0.099609375 to 1.8984375
- key_gain: bfloat16 [2048], P(('ctx', 'exp')), may hold values from 0.099609375 to 1.8984375
- ffn_gain: bfloat16 [2048], P(('ctx', 'exp')), may hold values from 0.099609375 to 1.8984375
- w_gate: bfloat16 [16, 2048, 1024], P('exp', 'ctx'), may hold values from -0.125 to 0.125
- w_up: bfloat16 [16, 2048, 1024], P('exp', 'ctx'), may hold values from -0.125 to 0.125
- w_down: bfloat16 [16, 1024, 2048], P('exp', 'ctx'), may hold values from -3 to 3
Outputs:
- activations: bfloat16 [12288, 2048], P(('ctx', 'exp'))
- input_grad: float32 [12288, 2048], P(('ctx', 'exp'))
- query_grad: float32 [2048, 2048], P(('ctx', 'exp'))
- key_grad: float32 [2048, 2048], P(('ctx', 'exp'))
- value_grad: float32 [2048, 2048], P(('ctx', 'exp'))
- out_grad: float32 [2048, 2048], P(('ctx', 'exp'))
- router_grad: float32 [2048, 16], P(('ctx', 'exp'))
- attn_gain_grad: float32 [2048], P(('ctx', 'exp'))
- query_gain_grad: float32 [2048], P(('ctx', 'exp'))
- key_gain_grad: float32 [2048], P(('ctx', 'exp'))
- ffn_gain_grad: float32 [2048], P(('ctx', 'exp'))
- gate_grad: float32 [16, 2048, 1024], P('exp', 'ctx')
- up_grad: float32 [16, 2048, 1024], P('exp', 'ctx')
- down_grad: float32 [16, 1024, 2048], P('exp', 'ctx')
The draws below stay inside these ranges and needn't reach their ends.
Inputs may be any that keep to these rules, and one draw needn't show every extreme that they name: `block_of_slot`: each row is a permutation of the group's 8 blocks, and slots 2c and 2c + 1 hold blocks b and 7 - b for some b. `cont_seg`: numbers never fall along a row; every continuation has 128 to 384 positions. `routes`: A row names 8 different experts; in the rows of one device no expert is named more than 240 times, a bound that some block reaches.
All inputs are finite; a program needn't handle non-finite values.
Results may differ from the reference program's by a relative error of at most 0.019.
Values may be sent and summed in bfloat16 or wider, within the bound.
No kernel may reach another device: no remote copies, remote signals or barrier semaphores. Data moves between devices by JAX's collectives and lax.ppermute only.
A program may use at most 512 MiB of HBM per device.

```python
import math
import jax
import jax.numpy as jnp
import numpy as np
from jax import lax

D = 2048
HEADS = 16
HD = 128
FF = 1024
TOP = 8
PROMPT = 1024
CONT = 2
EXPERTS = 16
CTOK = 512
SEGMOST = 384
GLEN = 1536
GROUPS = 8
TOKENS = 12288
NBLK = 8
BLK = 192
TD = 384
CAP = 240
N_CTX = 4
N_EXP = 8


def draw_block_of_slot(key, part):

    def one_group(group_key):
        key_order, key_flip = jax.random.split(group_key)
        order = jax.random.permutation(key_order, NBLK // 2).astype(jnp.int32)
        flips = jax.random.randint(key_flip, (NBLK // 2,), 0, 2)
        mirror = NBLK - 1 - order
        former = jnp.where(flips == 1, mirror, order)
        latter = jnp.where(flips == 1, order, mirror)
        return jnp.stack([former, latter], axis=1).reshape(NBLK)
    return jax.vmap(one_group)(jax.random.split(key, GROUPS)).astype(jnp.int32)


def levels(own_key, dims, shards, smallest, top_value):
    def one(dim, shards_of):
        steps = jax.random.uniform(jax.random.fold_in(jax.random.fold_in(own_key, 6), dim), (shards_of,), jnp.float32, smallest / len(shards), top_value / len(shards))
        return jnp.repeat(jnp.exp(steps), dims[dim] // shards_of).reshape((-1,) + (1,) * (len(dims) - dim - 1))

    loudness = one(*shards[0])
    for cut in shards[1:]:
        loudness = loudness * one(*cut)
    return loudness


def length_profile(amount, total, limit, slope):
    portions = [(1 << 20) // math.isqrt(standing ** slope) + 1 for standing in range(2, amount + 1)]
    surplus, given = total - limit - (amount - 1), [1] * (amount - 1)
    while surplus > 0:
        free = [i for i in range(amount - 1) if given[i] < limit]
        pool, remaining = sum([portions[i] for i in free]), surplus
        for i in free:
            addition = min(limit - given[i], max(1, remaining * portions[i] // pool), surplus)
            given[i] = given[i] + addition
            surplus = surplus - addition
    return np.array([limit] + given)


def ragged(own_key, amount, total, most, skew):
    if amount == 2:
        one = jax.random.randint(own_key, (), max(1, total - most), min(most, total - 1) + 1)
        return jnp.stack([one, total - one])
    tallies = jnp.asarray(length_profile(amount, total, most, skew), jnp.int32)
    couples = (amount - 1) // 2
    source_of, sink = tallies[1:1 + 2 * couples:2], tallies[2:2 + 2 * couples:2]
    margin = jnp.minimum(source_of - 1, most - sink)
    shifted = jax.random.randint(jax.random.fold_in(own_key, 1), (couples,), 0, 1 << 20) % (margin + 1)
    tallies = tallies.at[1:1 + 2 * couples:2].set(source_of - shifted).at[2:2 + 2 * couples:2].set(sink + shifted)
    return tallies[jax.random.permutation(jax.random.fold_in(own_key, 2), amount)]


def shared_out(rng, own, number, rows, number_of, top, reach, skew):
    order = jax.random.permutation(rng, number_of)
    heavy_load, usual = portions_of(number_of, rows * top, reach, skew, True), portions_of(number_of, rows * top, reach, skew, False)
    places = jnp.arange(number_of)

    def named(sizes, turn):
        used = int((sizes > 0).sum())
        fixed = max(1, used // 4)
        moved = fixed + (places - fixed + turn * (used - fixed)) % max(1, number_of - fixed)
        return jnp.zeros((number_of,), jnp.int32).at[order[jnp.where(places < fixed, places, moved)]].set(jnp.asarray(sizes, jnp.int32))

    sizes = jnp.where(number % 4 == 0, named(heavy_load, number // 4), named(usual, number - number // 4 - 1))
    mixed = jax.random.permutation(jax.random.fold_in(own, 3), number_of)
    donor, receiver = mixed[0:number_of // 2 * 2:2], mixed[1:number_of // 2 * 2:2]
    slack = jnp.minimum(sizes[donor] - 1, reach - sizes[receiver]) // 2
    slack = jnp.where((donor == order[0]) | (receiver == order[0]) | (sizes[receiver] == 0), 0, jnp.maximum(slack, 0))
    moved = jax.random.randint(jax.random.fold_in(own, 4), (number_of // 2,), 0, 1 << 20) % (slack + 1)
    sizes = sizes.at[donor].add(-moved).at[receiver].add(moved)
    members = jnp.searchsorted(jnp.cumsum(sizes), jnp.arange(rows * top), side="right").astype(jnp.int32)
    table = members.reshape(top, rows).T
    table = table[jax.random.permutation(jax.random.fold_in(own, 1), rows)]
    turn = jax.random.randint(jax.random.fold_in(own, 2), (rows, 1), 0, top)
    return jnp.take_along_axis(table, (jnp.arange(top)[None, :] + turn) % top, axis=1)


def portions_of(number_of, total, reach, slope, full):
    portions = [(1 << 20) // math.isqrt(standing ** slope) + 1 for standing in range(1, number_of + 1)]
    largest = reach if full else min(reach, max(-(-total // number_of), total * portions[0] // sum(portions)))
    least = 1 if total - largest >= number_of - 1 else 0
    counts, rest = [largest] + [least] * (number_of - 1), total - largest - least * (number_of - 1)
    while rest > 0:
        candidates = [i for i in range(1, number_of) if counts[i] < largest] or [i for i in range(1, number_of) if counts[i] < reach]
        whole, budget = sum([portions[i] for i in candidates]), rest
        for i in candidates:
            addition = min(reach - counts[i], max(1, budget * portions[i] // whole), rest)
            counts[i] = counts[i] + addition
            rest = rest - addition
    return np.array(counts)


def noise(key, dims, width, limit, cuts=(), kind=jnp.bfloat16):
    factor_of = levels(key, dims, cuts, -0.22, 0.18) if cuts else 1.0
    entries = jax.random.normal(key, dims, jnp.float32) * width * factor_of
    return jnp.minimum(jnp.maximum(entries, -limit), limit).astype(kind)


def setup_inputs(seed: int = 0) -> dict:
    arg_keys = jax.random.split(jax.random.key(seed), 18)
    tokens = noise(arg_keys[0], (TOKENS, D), 1.0, 6.0, ((0, 32),))
    cotangent = noise(arg_keys[1], (TOKENS, D), 1.0, 6.0, ((0, 32),))
    routes_keys = jax.random.split(jax.random.fold_in(arg_keys[2], 1), TOKENS // TD)
    routes_turns = jax.random.permutation(jax.random.fold_in(arg_keys[2], 3), TOKENS // TD)
    routes = jax.vmap(lambda own, number: shared_out(jax.random.fold_in(arg_keys[2], 2), own, number, TD, EXPERTS, TOP, CAP, 1))(routes_keys, routes_turns).reshape((TOKENS, TOP))
    block_of_slot = draw_block_of_slot(jax.random.fold_in(arg_keys[17], 71), 0)
    cont_seg = jax.vmap(lambda own: jnp.searchsorted(jnp.cumsum(ragged(own, CONT, CTOK, SEGMOST, 1)), jnp.arange(CTOK), side="right"))(jax.random.split(arg_keys[4], GROUPS)).reshape((GROUPS, CTOK)).astype(jnp.int32)
    w_query = noise(arg_keys[5], (D, D), D ** -0.5, 0.125, ((0, 32),))
    w_key = noise(arg_keys[6], (D, D), D ** -0.5, 0.125, ((0, 32),))
    w_value = noise(arg_keys[7], (D, D), D ** -0.5, 0.125, ((0, 32),))
    w_out = noise(arg_keys[8], (D, D), (D // 32) ** -0.5, 0.75, ((0, 32),))
    w_router = noise(arg_keys[9], (D, EXPERTS), (4 * D) ** -0.5, 0.0625, ((0, 32),))
    attn_gain = jnp.clip(1.0 + 0.18 * jax.random.normal(arg_keys[10], (D,), jnp.float32), 0.099609375, 1.8984375).astype(jnp.bfloat16)
    query_gain = jnp.clip(1.0 + 0.18 * jax.random.normal(arg_keys[11], (D,), jnp.float32), 0.099609375, 1.8984375).astype(jnp.bfloat16)
    key_gain = jnp.clip(1.0 + 0.18 * jax.random.normal(arg_keys[12], (D,), jnp.float32), 0.099609375, 1.8984375).astype(jnp.bfloat16)
    ffn_gain = jnp.clip(1.0 + 0.18 * jax.random.normal(arg_keys[13], (D,), jnp.float32), 0.099609375, 1.8984375).astype(jnp.bfloat16)
    w_gate = noise(arg_keys[14], (EXPERTS, D, FF), D ** -0.5, 0.125, ((0, 8), (1, 4)))
    w_up = noise(arg_keys[15], (EXPERTS, D, FF), D ** -0.5, 0.125, ((0, 8), (1, 4)))
    w_down = noise(arg_keys[16], (EXPERTS, FF, D), (max(FF // 256, 1)) ** -0.5, 3.0, ((0, 8), (1, 4)))
    return {"tokens": tokens, "cotangent": cotangent, "routes": routes, "block_of_slot": block_of_slot, "cont_seg": cont_seg, "w_query": w_query, "w_key": w_key, "w_value": w_value, "w_out": w_out, "w_router": w_router, "attn_gain": attn_gain, "query_gain": query_gain, "key_gain": key_gain, "ffn_gain": ffn_gain, "w_gate": w_gate, "w_up": w_up, "w_down": w_down}


epsilon = 1e-05
rope_base = 10000.0
highest = lax.Precision.HIGHEST

@jax.custom_vjp
def low(v):
    return lax.optimization_barrier(v.astype(jnp.bfloat16)).astype(jnp.float32)

@jax.custom_vjp
def low_back(v):
    return v

def low_keep(v):
    return (low(v), None)

def low_pass(kept, grad):
    return (grad,)

def back_keep(v):
    return (v, None)

def back_low(kept, grad):
    return (low(grad),)
low.defvjp(low_keep, low_pass)
low_back.defvjp(back_keep, back_low)

def inverse_root(values):
    return lax.rsqrt(lax.optimization_barrier(jnp.mean(values * values, axis=-1, keepdims=True)) + epsilon)

def angles(position):
    half_dim = HD // 2
    inverse = rope_base ** (-2.0 * jnp.arange(half_dim, dtype=jnp.float32) / HD)
    phases = position.astype(jnp.float32)[:, None] * inverse[None, :]
    return (jnp.cos(phases)[:, None, :], jnp.sin(phases)[:, None, :])

def rotate(values, cos_part, sin_part):
    half_dim = HD // 2
    former = values[..., :half_dim]
    latter = values[..., half_dim:]
    return jnp.concatenate([former * cos_part - latter * sin_part, latter * cos_part + former * sin_part], axis=-1)

def token_meta(place, seg_row):
    in_cont = place >= PROMPT
    cont_index = jnp.clip(place - PROMPT, 0, CTOK - 1)
    seg_ids = jnp.where(in_cont, jnp.take(seg_row, cont_index), -1)
    starts = lax.optimization_barrier(jnp.sum((seg_row[None, :] < jnp.arange(CONT, dtype=jnp.int32)[:, None]).astype(jnp.int32), axis=1))
    first_pos = jnp.take(starts, jnp.clip(seg_ids, 0, CONT - 1))
    position = jnp.where(in_cont, PROMPT + cont_index - first_pos, place)
    return (seg_ids, position)

def visible(query_place, query_seg, key_place, key_seg):
    causal = key_place[None, :] <= query_place[:, None]
    shared = (key_seg[None, :] < 0) | (key_seg[None, :] == query_seg[:, None])
    return causal & shared

def grouped(values):
    per_dev = GLEN // N_CTX
    shaped = values.reshape((N_CTX, N_EXP, per_dev) + values.shape[1:])
    return jnp.swapaxes(shaped, 0, 1).reshape((N_EXP, GLEN) + values.shape[1:])

def ungrouped(values):
    per_dev = GLEN // N_CTX
    shaped = values.reshape((N_EXP, N_CTX, per_dev) + values.shape[2:])
    return jnp.swapaxes(shaped, 0, 1).reshape((N_CTX * N_EXP * per_dev,) + values.shape[2:])

def attend_group(items):
    query_rot, key_rot, value_low, place, seg_ids = items
    factor = 1.0 / math.sqrt(HD)
    scores = jnp.einsum('qhd,khd->hqk', query_rot, key_rot, precision=highest) * factor
    scores = low_back(scores)
    allowed = visible(place, seg_ids, place, seg_ids)
    scores = jnp.where(allowed[None], scores, -1e+30)
    weights = jax.nn.softmax(scores, axis=-1)
    return jnp.einsum('hqk,khd->qhd', low(weights), value_low, precision=highest)

def route_table(routes):
    devices = N_CTX * N_EXP
    per_dev = GLEN // N_CTX
    route_count = per_dev * TOP
    flat_routes = routes.reshape(devices, route_count)
    route_hits = (flat_routes[:, :, None] == jnp.arange(EXPERTS, dtype=jnp.int32)[None, None, :]).astype(jnp.int32)
    slot_index = lax.optimization_barrier(jnp.sum((jnp.cumsum(route_hits, axis=1) - route_hits) * route_hits, axis=2))
    dest_row = flat_routes * (devices * CAP) + jnp.arange(devices, dtype=jnp.int32)[:, None] * CAP + slot_index
    route_total = devices * route_count
    slot_table = jnp.full((EXPERTS * devices * CAP,), route_total, jnp.int32)
    slot_table = slot_table.at[dest_row.reshape(-1)].set(jnp.arange(route_total, dtype=jnp.int32))
    return slot_table.reshape(EXPERTS, devices * CAP)

def reference(tokens, cotangent, routes, block_of_slot, cont_seg, w_query, w_key, w_value, w_out, w_router, attn_gain, query_gain, key_gain, ffn_gain, w_gate, w_up, w_down):
    within = jnp.arange(BLK, dtype=jnp.int32)
    group_place = (block_of_slot[:, :, None] * BLK + within[None, None, :]).reshape(N_EXP, GLEN)
    group_seg, group_pos = jax.vmap(token_meta)(group_place, cont_seg)
    cos_part, sin_part = angles(ungrouped(group_pos))
    slot_table = route_table(routes)

    def forward(inputs, query_w, key_w, value_w, out_w, router_w, gain_attn, gain_query, gain_key, gain_ffn, gate_w, up_w, down_w):
        token_total = inputs.shape[0]
        hidden_one = low(inputs * inverse_root(inputs) * gain_attn)
        query_pre = low_back(jnp.dot(hidden_one, query_w, precision=highest))
        key_pre = low_back(jnp.dot(hidden_one, key_w, precision=highest))
        value_pre = low_back(jnp.dot(hidden_one, value_w, precision=highest))
        query_normed = (query_pre * inverse_root(query_pre) * gain_query).reshape(token_total, HEADS, HD)
        key_normed = (key_pre * inverse_root(key_pre) * gain_key).reshape(token_total, HEADS, HD)
        query_rot = low(rotate(query_normed, cos_part, sin_part))
        key_rot = low(rotate(key_normed, cos_part, sin_part))
        value_low = low(value_pre).reshape(token_total, HEADS, HD)
        context = lax.map(jax.checkpoint(attend_group), (grouped(query_rot), grouped(key_rot), grouped(value_low), group_place, group_seg))
        context = low_back(low(ungrouped(context).reshape(token_total, D)))
        middle = inputs + low_back(jnp.dot(context, out_w, precision=highest))
        hidden_two = low(middle * inverse_root(middle) * gain_ffn)
        logits = low_back(jnp.dot(hidden_two, router_w, precision=highest))
        router_prob = jax.nn.softmax(logits, axis=-1)
        gate_share = jnp.take_along_axis(router_prob, routes, axis=1).reshape(-1)
        padded_two = jnp.concatenate([hidden_two, jnp.zeros((1, D), jnp.float32)], axis=0)
        padded_share = jnp.concatenate([gate_share, jnp.zeros((1,), jnp.float32)], axis=0)

        def expert_step(mixture, items):
            rows_of, gate_one, up_one, down_one = items
            token_of = rows_of // TOP
            chosen = padded_two[token_of]
            gate_pre = low_back(jnp.dot(chosen, gate_one, precision=highest))
            up_pre = low_back(jnp.dot(chosen, up_one, precision=highest))
            hidden = low(jax.nn.silu(gate_pre) * up_pre)
            result = low_back(low(jnp.dot(hidden, down_one, precision=highest)))
            return (mixture.at[token_of].add(padded_share[rows_of][:, None] * result), None)
        start_mix = jnp.zeros((token_total + 1, D), jnp.float32)
        mixture, unused = lax.scan(jax.checkpoint(expert_step), start_mix, (slot_table, gate_w, up_w, down_w))
        return middle + mixture[:token_total]
    primals = tuple((array.astype(jnp.float32) for array in (tokens, w_query, w_key, w_value, w_out, w_router, attn_gain, query_gain, key_gain, ffn_gain, w_gate, w_up, w_down)))
    activations, pullback = jax.vjp(forward, *primals)
    gradients = pullback(cotangent.astype(jnp.float32))
    return (activations.astype(jnp.bfloat16), gradients[0], gradients[1], gradients[2], gradients[3], gradients[4], gradients[5], gradients[6], gradients[7], gradients[8], gradients[9], gradients[10], gradients[11], gradients[12])
```

```python
import math

import jax
import jax.numpy as jnp
from jax import lax
from jax.sharding import PartitionSpec as P

D = 2048
HEADS = 16
HD = 128
TOP = 8
PROMPT = 1024
CONT = 2
CTOK = 512

epsilon = 1e-05
rope_base = 10000.0
BF = jnp.bfloat16
F32 = jnp.float32
BOTH = ("ctx", "exp")
X_PAIRS = [(i, i ^ 1) for i in range(4)]
Y_PAIRS = [(i, i ^ 2) for i in range(4)]


def inverse_root(values):
    return lax.rsqrt(jnp.mean(values * values, axis=-1, keepdims=True) + epsilon)


def norm_back(gradient, normed, root_part):
    return root_part * (gradient - normed * jnp.mean(gradient * normed, axis=-1, keepdims=True))


def angles(position):
    half_dim = HD // 2
    inverse = rope_base ** (-2.0 * jnp.arange(half_dim, dtype=F32) / HD)
    phases = position.astype(F32)[:, None] * inverse[None, :]
    return (jnp.cos(phases)[:, None, :], jnp.sin(phases)[:, None, :])


def rotate(values, cos_part, sin_part):
    half_dim = HD // 2
    former = values[..., :half_dim]
    latter = values[..., half_dim:]
    return jnp.concatenate(
        [former * cos_part - latter * sin_part, latter * cos_part + former * sin_part], axis=-1
    )


def rotate_back(gradient, cos_part, sin_part):
    half_dim = HD // 2
    former = gradient[..., :half_dim]
    latter = gradient[..., half_dim:]
    return jnp.concatenate(
        [former * cos_part + latter * sin_part, latter * cos_part - former * sin_part], axis=-1
    )


def send_x(value):
    return lax.ppermute(value, "ctx", X_PAIRS)


def send_y(value):
    return lax.ppermute(value, "ctx", Y_PAIRS)


def after(value, *others):
    return lax.optimization_barrier((value,) + others)[0]


def gather_pieces(value, half):
    from_x = send_x(value)
    from_y = send_y(value)
    far_low = send_y(from_x[:half])
    far_high = send_x(from_y[half:])
    return from_x, from_y, far_low, far_high


def scatter_sum(take, me):
    low = send_x(jnp.stack([take(me ^ 1, 0), take(me ^ 3, 0)]).astype(BF))
    high = send_y(jnp.stack([take(me ^ 2, 1), take(me ^ 3, 1)]).astype(BF))
    low_next = send_y((take(me ^ 2, 0).astype(F32) + low[1].astype(F32)).astype(BF))
    high_next = send_x((take(me ^ 1, 1).astype(F32) + high[1].astype(F32)).astype(BF))
    first = take(me, 0).astype(F32) + low[0].astype(F32) + low_next.astype(F32)
    second = take(me, 1).astype(F32) + high[0].astype(F32) + high_next.astype(F32)
    return first, second


def gather_rows(weight, me):
    if lax.axis_size("ctx") != 4:
        return lax.all_gather(weight, "ctx", axis=1, tiled=True), weight
    count, rows, columns = weight.shape
    from_x, from_y, far_low, far_high = gather_pieces(weight, count // 2)
    whole = jnp.zeros((count, 4 * rows, columns), weight.dtype)
    whole = lax.dynamic_update_slice(whole, weight, (0, me * rows, 0))
    whole = lax.dynamic_update_slice(whole, from_x, (0, (me ^ 1) * rows, 0))
    whole = lax.dynamic_update_slice(whole, from_y, (0, (me ^ 2) * rows, 0))
    whole = lax.dynamic_update_slice(whole, far_low, (0, (me ^ 3) * rows, 0))
    whole = lax.dynamic_update_slice(whole, far_high, (count // 2, (me ^ 3) * rows, 0))
    return whole, far_low


def scatter_rows(gradient, me):
    if lax.axis_size("ctx") != 4:
        return lax.psum_scatter(gradient, "ctx", scatter_dimension=1, tiled=True).astype(F32)
    count, rows, columns = gradient.shape
    rows, half = rows // 4, count // 2

    def take(owner, part):
        return lax.dynamic_slice(gradient, (part * half, owner * rows, 0), (half, rows, columns))

    return jnp.concatenate(scatter_sum(take, me), axis=0)


def pick_blocks(blocks, order):
    return jnp.concatenate(
        [
            lax.dynamic_index_in_dim(blocks, order[i], 0, keepdims=False)
            for i in range(order.shape[0])
        ],
        axis=0,
    )


def gather_group(rows, slot_table, me):
    block = rows.shape[0] // 2
    if lax.axis_size("ctx") != 4:
        blocks = slot_table.shape[0]
        whole = lax.all_gather(rows, "ctx", axis=0, tiled=True).reshape(blocks, block, -1)
        match = slot_table[None, :] == jnp.arange(blocks, dtype=jnp.int32)[:, None]
        order = jnp.sum(jnp.where(match, jnp.arange(blocks, dtype=jnp.int32)[None, :], 0), axis=1)
        return pick_blocks(whole, order), rows
    from_x, from_y, far_low, far_high = gather_pieces(rows, block)
    parts = (
        (rows[:block], me, 0),
        (rows[block:], me, 1),
        (from_x[:block], me ^ 1, 0),
        (from_x[block:], me ^ 1, 1),
        (from_y[:block], me ^ 2, 0),
        (from_y[block:], me ^ 2, 1),
        (far_low, me ^ 3, 0),
        (far_high, me ^ 3, 1),
    )
    whole = jnp.zeros((8 * block, rows.shape[1]), rows.dtype)
    for part, owner, slot in parts:
        start = slot_table[2 * owner + slot] * block
        whole = lax.dynamic_update_slice(whole, part, (start, 0))
    return whole, far_low


def scatter_group(partial, slot_table, me):
    blocks = slot_table.shape[0]
    block = partial.shape[0] // blocks
    if lax.axis_size("ctx") != 4:
        ordered = pick_blocks(partial.reshape(blocks, block, -1), slot_table)
        return lax.psum_scatter(
            ordered.astype(BF), "ctx", scatter_dimension=0, tiled=True
        ).astype(F32)

    def take(owner, part):
        start = slot_table[2 * owner + part] * block
        return lax.dynamic_slice(partial, (start, 0), (block, partial.shape[1]))

    return jnp.concatenate(scatter_sum(take, me), axis=0)


def prefix_count(member):
    rows, columns = member.shape
    width = 128
    blocks = rows // width
    ones = member.astype(BF).reshape(blocks, width, columns)
    lower = (
        jnp.arange(width)[:, None] > jnp.arange(width)[None, :]
    ).astype(BF)
    inner = jnp.einsum("pq,bqc->bpc", lower, ones, preferred_element_type=F32)
    totals = jnp.sum(ones.astype(F32), axis=1)
    before = (jnp.arange(blocks)[:, None] > jnp.arange(blocks)[None, :]).astype(F32)
    outer = jnp.sum(before[:, :, None] * totals[None, :, :], axis=1)
    return (inner + outer[:, None, :]).reshape(rows, columns).astype(jnp.int32)


def local(
    tokens,
    cotangent,
    routes,
    block_of_slot,
    cont_seg,
    w_query,
    w_key,
    w_value,
    w_out,
    w_router,
    attn_gain,
    query_gain,
    key_gain,
    ffn_gain,
    w_gate,
    w_up,
    w_down,
):
    ctx_size = lax.axis_size("ctx")
    exp_size = lax.axis_size("exp")
    me = lax.axis_index("ctx")
    exp_index = lax.axis_index("exp")
    tok_rows = tokens.shape[0]
    part_rows = w_query.shape[0]
    own_width = D // ctx_size
    own_heads = HEADS // ctx_size
    experts = w_router.shape[1]
    own_experts = w_gate.shape[0]
    slot_table = block_of_slot[0]
    seg_row = cont_seg[0]
    group_rows = ctx_size * tok_rows
    factor = 1.0 / math.sqrt(HD)

    tokens_group, tokens_there = gather_group(tokens, slot_table, me)
    small = jnp.concatenate(
        [w_router] + [g[:, None] for g in (attn_gain, query_gain, key_gain, ffn_gain)], axis=1
    )
    small_full = lax.all_gather(small, BOTH, axis=0, tiled=True)
    router_full = small_full[:, :experts]
    gains = small_full[:, experts:].astype(F32)
    gain_attn, gain_ffn = gains[:, 0], gains[:, 3]
    own_gains = lax.dynamic_slice(gains, (me * own_width, 0), (own_width, 4))
    gain_query, gain_key = own_gains[:, 1], own_gains[:, 2]
    by_owner = jnp.stack(
        [w.reshape(part_rows, ctx_size, own_width) for w in (w_query, w_key, w_value)], axis=2
    )
    by_owner = jnp.swapaxes(by_owner, 0, 1).reshape(ctx_size, part_rows, 3 * own_width)
    own_columns = lax.all_to_all(by_owner, "ctx", split_axis=0, concat_axis=0, tiled=True)
    qkv_full = lax.all_gather(own_columns, "exp", axis=1, tiled=True).reshape(D, 3 * own_width)
    out_full = lax.all_gather(w_out, "exp", axis=0, tiled=True)
    routes_all = lax.all_gather(routes, "exp", axis=0, tiled=True)
    upstream_all = lax.all_gather(cotangent, "exp", axis=0, tiled=True)
    gate_full, gate_there = gather_rows(after(w_gate, tokens_there), me)
    up_full, up_there = gather_rows(after(w_up, gate_there), me)

    own_ids = exp_index * own_experts + jnp.arange(own_experts, dtype=jnp.int32)
    member = jnp.any(routes_all[:, :, None] == own_ids[None, None, :], axis=1)
    place_of = prefix_count(member)
    capacity = exp_size * 8 * ((5 * tok_rows * TOP // (4 * experts) + 7) // 8)
    all_rows = exp_size * tok_rows
    row_ids = jnp.arange(capacity, dtype=jnp.int32)
    hit = (place_of.T[:, None, :] == row_ids[None, :, None]) & member.T[:, None, :]
    token_ids = jnp.arange(all_rows, dtype=jnp.int32)
    token_of_row = jnp.sum(jnp.where(hit, token_ids[None, None, :], 0), axis=2)
    counts = jnp.sum(member.astype(jnp.int32), axis=0)
    real_row = row_ids[None, :] < counts[:, None]
    row_of = jnp.where(
        member, place_of + capacity * jnp.arange(own_experts, dtype=jnp.int32)[None, :], 0
    )

    seg_ids = jnp.concatenate([jnp.full((PROMPT,), -1, jnp.int32), seg_row])
    starts = jnp.sum(
        (seg_row[None, :] < jnp.arange(CONT, dtype=jnp.int32)[:, None]).astype(jnp.int32), axis=1
    )
    first_pos = jnp.sum(
        jnp.where(
            seg_row[:, None] == jnp.arange(CONT, dtype=jnp.int32)[None, :], starts[None, :], 0
        ),
        axis=1,
    )
    cont_pos = PROMPT + jnp.arange(CTOK, dtype=jnp.int32) - first_pos
    position = jnp.concatenate([jnp.arange(PROMPT, dtype=jnp.int32), cont_pos])
    place = jnp.arange(group_rows, dtype=jnp.int32)
    allowed = (place[None, :] <= place[:, None]) & (
        (seg_ids[None, :] < 0) | (seg_ids[None, :] == seg_ids[:, None])
    )
    cos_part, sin_part = angles(position)
    group_inputs = tokens_group.astype(F32)
    hidden_one = (group_inputs * inverse_root(group_inputs) * gain_attn).astype(BF)
    projected = jnp.dot(hidden_one, qkv_full, preferred_element_type=F32)
    query_pre = projected[:, :own_width]
    key_pre = projected[:, own_width : 2 * own_width]
    value_low = projected[:, 2 * own_width :].astype(BF).reshape(group_rows, own_heads, HD)
    squares = jnp.stack([jnp.sum(query_pre * query_pre, axis=1), jnp.sum(key_pre * key_pre, axis=1)])
    roots = lax.rsqrt(lax.psum(squares, "ctx") / D + epsilon)
    root_query, root_key = roots[0][:, None], roots[1][:, None]
    normed_query = query_pre * root_query
    normed_key = key_pre * root_key
    query_rot = rotate(
        (normed_query * gain_query).reshape(group_rows, own_heads, HD), cos_part, sin_part
    ).astype(BF)
    key_rot = rotate(
        (normed_key * gain_key).reshape(group_rows, own_heads, HD), cos_part, sin_part
    ).astype(BF)

    def masked_scores():
        raw = jnp.einsum("qhd,khd->hqk", query_rot, key_rot, preferred_element_type=F32) * factor
        return jnp.where(allowed[None], raw, -1e30)

    masked = masked_scores()
    row_max = jnp.max(masked, axis=-1, keepdims=True)
    exponent = jnp.exp(masked - row_max)
    row_total = jnp.sum(exponent, axis=-1, keepdims=True)
    log_total = row_max + jnp.log(row_total)
    context = jnp.einsum(
        "hqk,khd->qhd", (exponent / row_total).astype(BF), value_low, preferred_element_type=F32
    )
    context_low = context.reshape(group_rows, own_width).astype(BF)
    branch_part = jnp.dot(context_low, out_full, preferred_element_type=F32)
    branch = scatter_group(branch_part, slot_table, me)
    down_full, unused = gather_rows(after(w_down, up_there, branch), me)

    inputs = tokens.astype(F32)
    middle = inputs + branch
    root_two = inverse_root(middle)
    normed_two = middle * root_two
    hidden_two = (normed_two * gain_ffn).astype(BF)
    hidden_all = lax.all_gather(hidden_two, "exp", axis=0, tiled=True)
    logits = jnp.dot(hidden_two, router_full, preferred_element_type=F32)
    router_prob = jax.nn.softmax(logits, axis=-1)

    arrived = hidden_all[token_of_row]
    upstream_rows = upstream_all[token_of_row]
    row_logits = jnp.einsum("erd,dx->erx", arrived, router_full, preferred_element_type=F32)
    row_prob = jax.nn.softmax(row_logits, axis=-1)
    own_column = own_ids[:, None, None] == jnp.arange(experts, dtype=jnp.int32)[None, None, :]
    gate_row = jnp.sum(jnp.where(own_column, row_prob, 0.0), axis=-1)
    gate_row = jnp.where(real_row, gate_row, 0.0)[:, :, None]
    gate_pre = jnp.einsum("erd,edf->erf", arrived, gate_full, preferred_element_type=F32)
    up_pre = jnp.einsum("erd,edf->erf", arrived, up_full, preferred_element_type=F32)
    grad_raw = jnp.einsum("erd,efd->erf", upstream_rows, down_full, preferred_element_type=F32)
    sigmoid_gate = jax.nn.sigmoid(gate_pre)
    silu_gate = gate_pre * sigmoid_gate
    hidden = silu_gate * up_pre
    hidden_gated = (hidden * gate_row).astype(BF)
    share_row = jnp.sum(hidden * grad_raw, axis=-1)
    grad_hidden = grad_raw * gate_row
    grad_gate_pre = (
        grad_hidden * up_pre * (sigmoid_gate * (1.0 + gate_pre * (1.0 - sigmoid_gate)))
    ).astype(BF)
    grad_up_pre = (grad_hidden * silu_gate).astype(BF)
    grad_rows = (
        jnp.einsum("erf,edf->erd", grad_gate_pre, gate_full, preferred_element_type=F32)
        + jnp.einsum("erf,edf->erd", grad_up_pre, up_full, preferred_element_type=F32)
    ).astype(BF)

    def combine(rows_given):
        flat = rows_given.reshape(own_experts * capacity, -1)
        total = 0.0
        for own in range(own_experts):
            total = total + jnp.where(member[:, own : own + 1], flat[row_of[:, own]], 0).astype(F32)
        return total

    grad_two = lax.psum_scatter(
        combine(grad_rows).astype(BF), "exp", scatter_dimension=0, tiled=True
    ).astype(F32)
    share_token = jnp.sum(jnp.where(hit, share_row[:, :, None], 0.0), axis=1)
    share_token = jnp.swapaxes(share_token.reshape(own_experts, exp_size, tok_rows), 0, 1)
    share_back = lax.all_to_all(share_token, "exp", split_axis=0, concat_axis=0, tiled=True)
    grad_prob = share_back.reshape(experts, tok_rows).T
    result = jnp.einsum(
        "erf,efd->erd", hidden_gated, down_full, preferred_element_type=F32
    ).astype(BF)
    mixture = lax.psum_scatter(
        combine(result).astype(BF), "exp", scatter_dimension=0, tiled=True
    ).astype(F32)
    output = (middle + mixture).astype(BF)

    def weight_grad(left, right):
        return jnp.einsum("era,erb->eab", left, right, preferred_element_type=F32).astype(BF)

    gate_grad = scatter_rows(weight_grad(arrived, grad_gate_pre), me)
    up_grad = scatter_rows(weight_grad(arrived, grad_up_pre), me)
    down_grad = scatter_rows(weight_grad(hidden_gated, upstream_rows), me)

    grad_logits = (
        router_prob * (grad_prob - jnp.sum(router_prob * grad_prob, axis=-1, keepdims=True))
    ).astype(BF)
    grad_router = jnp.einsum("td,te->de", hidden_two, grad_logits, preferred_element_type=F32)
    grad_two = grad_two + jnp.einsum(
        "te,de->td", grad_logits, router_full, preferred_element_type=F32
    )
    grad_ffn_gain = jnp.sum(grad_two * normed_two, axis=0)
    grad_middle = cotangent.astype(F32) + norm_back(grad_two * gain_ffn, normed_two, root_two)

    branch_grad, unused = gather_group(grad_middle.astype(BF), slot_table, me)
    grad_context = (
        jnp.einsum("te,de->td", branch_grad, out_full, preferred_element_type=F32)
        .astype(BF)
        .reshape(group_rows, own_heads, HD)
    )
    out_grad = jnp.einsum("td,te->de", context_low, branch_grad, preferred_element_type=F32)
    prob_again = jnp.exp(masked_scores() - log_total)
    grad_weights = jnp.einsum("qhd,khd->hqk", grad_context, value_low, preferred_element_type=F32)
    row_delta = jnp.sum(prob_again * grad_weights, axis=-1, keepdims=True)
    grad_scores = (prob_again * (grad_weights - row_delta)).astype(BF)
    grad_query_rot = (
        jnp.einsum("hqk,khd->qhd", grad_scores, key_rot, preferred_element_type=F32) * factor
    )
    grad_key_rot = (
        jnp.einsum("hqk,qhd->khd", grad_scores, query_rot, preferred_element_type=F32) * factor
    )
    grad_value = jnp.einsum(
        "hqk,qhd->khd", prob_again.astype(BF), grad_context, preferred_element_type=F32
    ).reshape(group_rows, own_width)
    grad_query_norm = rotate_back(grad_query_rot, cos_part, sin_part).reshape(group_rows, own_width)
    grad_key_norm = rotate_back(grad_key_rot, cos_part, sin_part).reshape(group_rows, own_width)
    grad_query_gain = jnp.sum(grad_query_norm * normed_query, axis=0)
    grad_key_gain = jnp.sum(grad_key_norm * normed_key, axis=0)
    scaled_query = grad_query_norm * gain_query
    scaled_key = grad_key_norm * gain_key
    means = (
        lax.psum(
            jnp.stack(
                [
                    jnp.sum(scaled_query * normed_query, axis=1),
                    jnp.sum(scaled_key * normed_key, axis=1),
                ]
            ),
            "ctx",
        )
        / D
    )
    grad_projected = jnp.concatenate(
        [
            root_query * (scaled_query - normed_query * means[0][:, None]),
            root_key * (scaled_key - normed_key * means[1][:, None]),
            grad_value,
        ],
        axis=1,
    ).astype(BF)
    grad_one_part = jnp.einsum("te,de->td", grad_projected, qkv_full, preferred_element_type=F32)
    grad_one = scatter_group(grad_one_part, slot_table, me)
    qkv_grad = jnp.einsum("td,te->de", hidden_one, grad_projected, preferred_element_type=F32)
    out_sum = lax.psum_scatter(
        out_grad.astype(BF), "exp", scatter_dimension=0, tiled=True
    ).astype(F32)
    qkv_sum = lax.psum_scatter(
        qkv_grad.astype(BF).reshape(ctx_size, exp_size * part_rows, 3 * own_width),
        "exp",
        scatter_dimension=1,
        tiled=True,
    )
    qkv_own = lax.all_to_all(qkv_sum, "ctx", split_axis=0, concat_axis=0, tiled=True).astype(F32)
    projection_grads = [
        jnp.swapaxes(qkv_own[:, :, i * own_width : (i + 1) * own_width], 0, 1).reshape(part_rows, D)
        for i in range(3)
    ]
    root_one = inverse_root(inputs)
    normed_one = inputs * root_one
    grad_attn_gain = jnp.sum(grad_one * normed_one, axis=0)
    grad_input = grad_middle + norm_back(grad_one * gain_attn, normed_one, root_one)
    head_gains = lax.psum_scatter(
        jnp.stack([grad_query_gain, grad_key_gain], axis=1), "exp", scatter_dimension=0, tiled=True
    )
    whole_sums = lax.psum_scatter(
        jnp.concatenate([grad_router, grad_ffn_gain[:, None], grad_attn_gain[:, None]], axis=1),
        BOTH,
        scatter_dimension=0,
        tiled=True,
    )
    return (
        output,
        grad_input,
        projection_grads[0],
        projection_grads[1],
        projection_grads[2],
        out_sum,
        whole_sums[:, :experts],
        whole_sums[:, experts + 1],
        head_gains[:, 0],
        head_gains[:, 1],
        whole_sums[:, experts],
        gate_grad,
        up_grad,
        down_grad,
    )


def solution(mesh):
    rows = P(BOTH, None)
    weights = P("exp", "ctx", None)
    in_specs = (
        (rows, rows, rows, P("exp", None), P("exp", None))
        + (rows,) * 5
        + (P(BOTH),) * 4
        + (weights,) * 3
    )
    out_specs = (rows,) * 7 + (P(BOTH),) * 4 + (weights,) * 3
    return jax.shard_map(local, mesh=mesh, in_specs=in_specs, out_specs=out_specs, check_vma=False)
```

```python
import functools
import math

import jax
import jax.numpy as jnp
from jax import lax
from jax.experimental import pallas as pl
from jax.experimental.pallas import tpu as pltpu
from jax.sharding import PartitionSpec as P

D = 2048
HEADS = 16
HD = 128
TOP = 8
PROMPT = 1024
CONT = 2
CTOK = 512

epsilon = 1e-05
rope_base = 10000.0
BF = jnp.bfloat16
F32 = jnp.float32
BOTH = ("ctx", "exp")
X_PAIRS = [(i, i ^ 1) for i in range(4)]
Y_PAIRS = [(i, i ^ 2) for i in range(4)]
XY_PAIRS = [(i, i ^ 3) for i in range(4)]
NT = (((1,), (1,)), ((), ()))
TN = (((0,), (0,)), ((), ()))
TILE = 256
WIN = 512
NOWHERE = -(1 << 20)


def inverse_root(values):
    return lax.rsqrt(jnp.mean(values * values, axis=-1, keepdims=True) + epsilon)


def norm_back(gradient, normed, root_part):
    return root_part * (gradient - normed * jnp.mean(gradient * normed, axis=-1, keepdims=True))


def angles(position):
    half_dim = HD // 2
    inverse = rope_base ** (-2.0 * jnp.arange(half_dim, dtype=F32) / HD)
    phases = position.astype(F32)[:, None] * inverse[None, :]
    return (jnp.cos(phases)[:, None, :], jnp.sin(phases)[:, None, :])


def rotate(values, cos_part, sin_part):
    half_dim = HD // 2
    former = values[..., :half_dim]
    latter = values[..., half_dim:]
    return jnp.concatenate(
        [former * cos_part - latter * sin_part, latter * cos_part + former * sin_part], axis=-1
    )


def rotate_back(gradient, cos_part, sin_part):
    half_dim = HD // 2
    former = gradient[..., :half_dim]
    latter = gradient[..., half_dim:]
    return jnp.concatenate(
        [former * cos_part + latter * sin_part, latter * cos_part - former * sin_part], axis=-1
    )


def send_x(value):
    return lax.ppermute(value, "ctx", X_PAIRS)


def send_y(value):
    return lax.ppermute(value, "ctx", Y_PAIRS)


def send_xy(value):
    return lax.ppermute(value, "ctx", XY_PAIRS)


def after(value, *others):
    return lax.optimization_barrier((value,) + others)[0]


def gather_pieces(value, half):
    from_x = send_x(value)
    from_y = send_y(value)
    far_low = send_y(from_x[:half])
    far_high = send_x(from_y[half:])
    return from_x, from_y, far_low, far_high


def scatter_sum(take, me):
    low = send_x(jnp.stack([take(me ^ 1, 0), take(me ^ 3, 0)]).astype(BF))
    high = send_y(jnp.stack([take(me ^ 2, 1), take(me ^ 3, 1)]).astype(BF))
    low_next = send_y((take(me ^ 2, 0).astype(F32) + low[1].astype(F32)).astype(BF))
    high_next = send_x((take(me ^ 1, 1).astype(F32) + high[1].astype(F32)).astype(BF))
    first = take(me, 0).astype(F32) + low[0].astype(F32) + low_next.astype(F32)
    second = take(me, 1).astype(F32) + high[0].astype(F32) + high_next.astype(F32)
    return first, second


def gather_rows(weight, me):
    if lax.axis_size("ctx") != 4:
        return lax.all_gather(weight, "ctx", axis=1, tiled=True)
    count, rows, columns = weight.shape
    whole = jnp.zeros((count, 4 * rows, columns), weight.dtype)
    parts = (weight, send_x(weight), send_y(weight), send_xy(weight))
    for away, part in enumerate(parts):
        whole = lax.dynamic_update_slice(whole, part, (0, (me ^ away) * rows, 0))
    return whole


def scatter_rows(gradient, me):
    if lax.axis_size("ctx") != 4:
        return lax.psum_scatter(gradient, "ctx", scatter_dimension=1, tiled=True).astype(F32)
    count, rows, columns = gradient.shape
    rows = rows // 4

    def take(away):
        return lax.dynamic_slice(gradient, (0, (me ^ away) * rows, 0), (count, rows, columns))

    parts = (take(0), send_x(take(1)), send_y(take(2)), send_xy(take(3)))
    return sum(part.astype(F32) for part in parts)


def exchange(blocks, me):
    if lax.axis_size("ctx") != 4:
        return lax.all_to_all(blocks, "ctx", split_axis=0, concat_axis=0, tiled=True)
    sends = (lambda part: part, send_x, send_y, send_xy)
    whole = jnp.zeros_like(blocks)
    for away, send in enumerate(sends):
        part = send(lax.dynamic_slice_in_dim(blocks, me ^ away, 1, 0))
        whole = lax.dynamic_update_slice_in_dim(whole, part, me ^ away, 0)
    return whole


def sum_over_ctx(value):
    if lax.axis_size("ctx") != 4:
        return lax.psum(value, "ctx")
    return (value + send_x(value)) + (send_y(value) + send_xy(value))


def pick_blocks(blocks, order):
    return jnp.concatenate(
        [
            lax.dynamic_index_in_dim(blocks, order[i], 0, keepdims=False)
            for i in range(order.shape[0])
        ],
        axis=0,
    )


def gather_group(rows, slot_table, me):
    block = rows.shape[0] // 2
    if lax.axis_size("ctx") != 4:
        blocks = slot_table.shape[0]
        whole = lax.all_gather(rows, "ctx", axis=0, tiled=True).reshape(blocks, block, -1)
        match = slot_table[None, :] == jnp.arange(blocks, dtype=jnp.int32)[:, None]
        order = jnp.sum(jnp.where(match, jnp.arange(blocks, dtype=jnp.int32)[None, :], 0), axis=1)
        return pick_blocks(whole, order), rows
    from_x, from_y, far_low, far_high = gather_pieces(rows, block)
    parts = (
        (rows[:block], me, 0),
        (rows[block:], me, 1),
        (from_x[:block], me ^ 1, 0),
        (from_x[block:], me ^ 1, 1),
        (from_y[:block], me ^ 2, 0),
        (from_y[block:], me ^ 2, 1),
        (far_low, me ^ 3, 0),
        (far_high, me ^ 3, 1),
    )
    whole = jnp.zeros((8 * block, rows.shape[1]), rows.dtype)
    for part, owner, slot in parts:
        start = slot_table[2 * owner + slot] * block
        whole = lax.dynamic_update_slice(whole, part, (start, 0))
    return whole, far_low


def scatter_group(partial, slot_table, me):
    blocks = slot_table.shape[0]
    block = partial.shape[0] // blocks
    if lax.axis_size("ctx") != 4:
        ordered = pick_blocks(partial.reshape(blocks, block, -1), slot_table)
        return lax.psum_scatter(
            ordered.astype(BF), "ctx", scatter_dimension=0, tiled=True
        ).astype(F32)

    def take(owner, part):
        start = slot_table[2 * owner + part] * block
        return lax.dynamic_slice(partial, (start, 0), (block, partial.shape[1]))

    return jnp.concatenate(scatter_sum(take, me), axis=0)


def prefix_count(member):
    rows, columns = member.shape
    width = 128
    blocks = rows // width
    ones = member.astype(BF).reshape(blocks, width, columns)
    lower = (
        jnp.arange(width)[:, None] > jnp.arange(width)[None, :]
    ).astype(BF)
    inner = jnp.einsum("pq,bqc->bpc", lower, ones, preferred_element_type=F32)
    totals = jnp.sum(ones.astype(F32), axis=1)
    before = (jnp.arange(blocks)[:, None] > jnp.arange(blocks)[None, :]).astype(F32)
    outer = jnp.sum(before[:, :, None] * totals[None, :, :], axis=1)
    return (inner + outer[:, None, :]).reshape(rows, columns).astype(jnp.int32)


def dot(a,b,dims=(((1,),(0,)),((),()))):
    return lax.dot_general(a,b,dims,preferred_element_type=F32)

def tile_scores(query, key, seg_q, seg_k, first, width, factor):
    scores = dot(query, key, NT) * factor
    rows = query.shape[0]
    q_place = first + lax.broadcasted_iota(jnp.int32, (rows, width), 0)
    k_place = lax.broadcasted_iota(jnp.int32, (rows, width), 1)
    allowed = k_place <= q_place
    if first >= PROMPT:
        allowed = allowed & ((seg_k < 0) | (seg_k == seg_q))
    return jnp.where(allowed, scores, -1e30)

def attend_kernel(tile, tiles, factor, q_ref, k_ref, v_ref, sq_ref, sk_ref, o_ref):
    at = pl.program_id(1)
    for i in range(tiles):
        @pl.when(at == i)
        def _():
            width = (i + 1) * tile
            scores = tile_scores(q_ref[...], k_ref[:width], sq_ref[...], sk_ref[:, :width], i * tile, width, factor)
            weight = jnp.exp(scores - jnp.max(scores, axis=1, keepdims=True))
            total = jnp.sum(weight, axis=1, keepdims=True)
            o_ref[...] = (dot(weight.astype(BF), v_ref[:width]) / total).astype(BF)

def attend(q, k, v, seg, tile=512):
    rows, width = q.shape
    heads, tiles = width // HD, rows // tile
    return pl.pallas_call(
        functools.partial(attend_kernel, tile, tiles, 1.0 / math.sqrt(HD)),
        out_shape=jax.ShapeDtypeStruct((rows, width), BF),
        grid=(heads, tiles),
        in_specs=[
            pl.BlockSpec((tile, HD), lambda h, i: (i, h)),
            pl.BlockSpec((rows, HD), lambda h, i: (0, h)),
            pl.BlockSpec((rows, HD), lambda h, i: (0, h)),
            pl.BlockSpec((tile, 1), lambda h, i: (i, 0)),
            pl.BlockSpec((1, rows), lambda h, i: (0, 0)),
        ],
        out_specs=pl.BlockSpec((tile, HD), lambda h, i: (i, h)),
        compiler_params=pltpu.CompilerParams(vmem_limit_bytes=40 << 20),
        cost_estimate=pl.CostEstimate(flops=2*2*heads*rows*rows*HD*6//10, bytes_accessed=8*rows*width, transcendentals=heads*rows*rows*6//10),
    )(q, k, v, seg[:, None], seg[None, :])

def attend_back_kernel(tile, tiles, factor, q_ref, k_ref, v_ref, d_ref, sq_ref, sk_ref, dq_ref, dk_ref, dv_ref):
    at = pl.program_id(1)
    @pl.when(at == 0)
    def _():
        dk_ref[...] = jnp.zeros_like(dk_ref)
        dv_ref[...] = jnp.zeros_like(dv_ref)
    for i in range(tiles):
        @pl.when(at == i)
        def _():
            width = (i + 1) * tile
            query, grad = q_ref[...], d_ref[...]
            scores = tile_scores(query, k_ref[:width], sq_ref[...], sk_ref[:, :width], i * tile, width, factor)
            weight = jnp.exp(scores - jnp.max(scores, axis=1, keepdims=True))
            weight = weight / jnp.sum(weight, axis=1, keepdims=True)
            grad_weight = dot(grad, v_ref[:width], NT)
            delta = jnp.sum(weight * grad_weight, axis=1, keepdims=True)
            grad_score = (weight * (grad_weight - delta)).astype(BF)
            dq_ref[...] = dot(grad_score, k_ref[:width]) * factor
            dk_ref[:width] += dot(grad_score, query, TN) * factor
            dv_ref[:width] += dot(weight.astype(BF), grad, TN)

def attend_back(q, k, v, d, seg, tile=512):
    rows, width = q.shape
    heads, tiles = width // HD, rows // tile
    own = pl.BlockSpec((tile, HD), lambda h, i: (i, h))
    whole = pl.BlockSpec((rows, HD), lambda h, i: (0, h))
    return pl.pallas_call(
        functools.partial(attend_back_kernel, tile, tiles, 1.0 / math.sqrt(HD)),
        out_shape=[jax.ShapeDtypeStruct((rows, width), F32)] * 3,
        grid=(heads, tiles),
        in_specs=[own, whole, whole, own,
            pl.BlockSpec((tile, 1), lambda h, i: (i, 0)),
            pl.BlockSpec((1, rows), lambda h, i: (0, 0)),
        ],
        out_specs=[own, whole, whole],
        compiler_params=pltpu.CompilerParams(vmem_limit_bytes=40 << 20),
        cost_estimate=pl.CostEstimate(flops=5*2*heads*rows*rows*HD*6//10, bytes_accessed=20*rows*width, transcendentals=heads*rows*rows*6//10),
    )(q, k, v, d, seg[:, None], seg[None, :])


def pick_rows(tok, lo, windows, source_ref, acc_ref, total):
    span = lax.broadcasted_iota(jnp.int32, (TILE, WIN), 1)
    def window(j):
        base = lo + j * WIN
        start = pl.multiple_of(jnp.minimum(base, total - WIN), 128)
        match = (tok - start == span) & (tok >= base)
        return dot(match.astype(F32).astype(BF), source_ref[pl.ds(start, WIN), :])
    acc_ref[...] = window(0)
    @pl.loop(1, windows)
    def _(j):
        acc_ref[...] += window(j)
    return acc_ref[...].astype(BF)

def back_rows_kernel(total, tiles_ref, lo_ref, win_ref, tok_ref, dy_ref, wd_ref, rows_ref, raw_ref, acc_ref):
    e, i = pl.program_id(0), pl.program_id(1)
    at = e * pl.num_programs(1) + i
    @pl.when(i < tiles_ref[e])
    def _():
        rows = pick_rows(tok_ref[...], lo_ref[at], win_ref[at], dy_ref, acc_ref, total)
        rows_ref[...] = rows
        raw_ref[...] = dot(rows, wd_ref[...], NT)
    @pl.when(i >= tiles_ref[e])
    def _():
        rows_ref[...] = jnp.zeros_like(rows_ref)

def back_rows(tiles, lo, win, tok, dy, wd):
    total, width = dy.shape
    experts, ff, _ = wd.shape
    nt = tok.shape[0] // (experts * TILE)
    last = lambda e, i, t: jnp.minimum(i, jnp.maximum(t[e] - 1, 0))
    spec = lambda n: pl.BlockSpec((None, TILE, n), lambda e, i, t, a, b: (e, i, 0))
    return pl.pallas_call(
        functools.partial(back_rows_kernel, total),
        out_shape=[jax.ShapeDtypeStruct((experts, nt * TILE, width), BF), jax.ShapeDtypeStruct((experts, nt * TILE, ff), F32)],
        grid_spec=pltpu.PrefetchScalarGridSpec(
            num_scalar_prefetch=3, grid=(experts, nt),
            in_specs=[
                pl.BlockSpec((TILE, 1), lambda e, i, t, a, b: (e * nt + i, 0)),
                pl.BlockSpec((total, width), lambda e, i, t, a, b: (0, 0), pipeline_mode=pl.Buffered(1)),
                pl.BlockSpec((None, ff, width), lambda e, i, t, a, b: (e, 0, 0)),
            ],
            out_specs=[spec(width), pl.BlockSpec((None, TILE, ff), lambda e, i, t, a, b: (e, last(e, i, t), 0))],
            scratch_shapes=[pltpu.VMEM((TILE, width), F32)],
        ),
        compiler_params=pltpu.CompilerParams(vmem_limit_bytes=56 << 20),
        cost_estimate=pl.CostEstimate(flops=experts*total*(width*ff+WIN*width), bytes_accessed=4*total*width+2*experts*ff*width+4*experts*total*(width+ff)//2, transcendentals=0),
    )(tiles, lo, win, tok, dy, wd)

def expert_kernel(total, own, tiles_ref, lo_ref, win_ref, id_ref, tok_ref, h_ref, wr_ref, wg_ref, wu_ref, raw_ref,
                  rows_ref, hid_ref, da_ref, db_ref, dh_ref, share_ref, acc_ref):
    e, i = pl.program_id(0), pl.program_id(1)
    at = e * pl.num_programs(1) + i
    @pl.when(i < tiles_ref[e])
    def _():
        rows = pick_rows(tok_ref[...], lo_ref[at], win_ref[at], h_ref, acc_ref, total)
        rows_ref[...] = rows
        logits = dot(rows, wr_ref[...])
        probs = jnp.exp(logits - jnp.max(logits, axis=1, keepdims=True))
        column = lax.broadcasted_iota(jnp.int32, probs.shape, 1)
        gate = jnp.sum(jnp.where(column == id_ref[0] + e, probs, 0.0), axis=1, keepdims=True) / jnp.sum(probs, axis=1, keepdims=True)
        part = wg_ref.shape[1] // 4
        share = 0.0
        for c in range(4):
            cols = slice(c * part, (c + 1) * part)
            a = dot(rows, wg_ref[:, cols])
            b = dot(rows, wu_ref[:, cols])
            raw = raw_ref[:, cols]
            sig = 1.0 / (1.0 + jnp.exp(-a))
            silu = a * sig
            hid = silu * b
            share += jnp.sum(hid * raw, axis=1, keepdims=True)
            raw = raw * gate
            hid_ref[:, cols] = (hid * gate).astype(BF)
            da_ref[:, cols] = (raw * b * (sig * (1.0 + a * (1.0 - sig)))).astype(BF)
            db_ref[:, cols] = (raw * silu).astype(BF)
        share_ref[...] = share
        dh_ref[...] = (dot(da_ref[...], wg_ref[...], NT) + dot(db_ref[...], wu_ref[...], NT)).astype(BF)
    @pl.when(i >= tiles_ref[e])
    def _():
        for ref in (rows_ref, hid_ref, da_ref, db_ref, dh_ref, share_ref):
            ref[...] = jnp.zeros_like(ref)

def expert_rows(tiles, lo, win, first_id, tok, h, wr, wg, wu, raw):
    total, width = h.shape
    experts, _, ff = wg.shape
    nt = tok.shape[0] // (experts * TILE)
    spec = lambda n: pl.BlockSpec((None, TILE, n), lambda e, i, t, a, b, d: (e, i, 0))
    shp = lambda n, dt=BF: jax.ShapeDtypeStruct((experts, nt * TILE, n), dt)
    return pl.pallas_call(
        functools.partial(expert_kernel, total, experts),
        out_shape=[shp(width), shp(ff), shp(ff), shp(ff), shp(width), shp(1, F32)],
        grid_spec=pltpu.PrefetchScalarGridSpec(
            num_scalar_prefetch=4, grid=(experts, nt),
            in_specs=[
                pl.BlockSpec((TILE, 1), lambda e, i, t, a, b, d: (e * nt + i, 0)),
                pl.BlockSpec((total, width), lambda e, i, t, a, b, d: (0, 0), pipeline_mode=pl.Buffered(1)),
                pl.BlockSpec(wr.shape, lambda e, i, t, a, b, d: (0, 0), pipeline_mode=pl.Buffered(1)),
                pl.BlockSpec((None, width, ff), lambda e, i, t, a, b, d: (e, 0, 0)),
                pl.BlockSpec((None, width, ff), lambda e, i, t, a, b, d: (e, 0, 0)),
                pl.BlockSpec((None, TILE, ff), lambda e, i, t, a, b, d: (e, jnp.minimum(i, jnp.maximum(t[e] - 1, 0)), 0)),
            ],
            out_specs=[spec(width), spec(ff), spec(ff), spec(ff), spec(width), spec(1)],
            scratch_shapes=[pltpu.VMEM((TILE, width), F32)],
        ),
        compiler_params=pltpu.CompilerParams(vmem_limit_bytes=60 << 20),
        cost_estimate=pl.CostEstimate(flops=experts*total*(4*width*ff+WIN*width), bytes_accessed=4*total*width+4*experts*ff*width+experts*total*(4*width+10*ff)//2, transcendentals=experts*total*ff//2),
    )(tiles, lo, win, first_id, tok, h, wr, wg, wu, raw)

def combine_kernel(
    experts, start_ref, more_ref, wide_ref, pos_ref, rows_ref, share_ref, out_ref, own_ref, acc_ref
):
    i = pl.program_id(0)
    span = lax.broadcasted_iota(jnp.int32, (TILE, TILE), 1)
    wide_span = lax.broadcasted_iota(jnp.int32, (TILE, 384), 1)
    last = rows_ref.shape[1] - TILE

    def window(e, j):
        base = start_ref[e, i] + j * TILE
        start = pl.multiple_of(jnp.minimum(base, last), 16)
        pos = pos_ref[:, e : e + 1]
        match = (pos - start == span) & (pos >= base)
        return dot(match.astype(F32).astype(BF), rows_ref[e, pl.ds(start, TILE), :])

    acc_ref[...] = sum(window(e, 0) for e in range(experts))
    for e in range(experts):
        wide = pl.multiple_of(wide_ref[e, i], 128)
        match = pos_ref[:, e : e + 1] - wide == wide_span
        share = share_ref[e, :, pl.ds(wide, 384)]
        own_ref[:, e : e + 1] = jnp.sum(jnp.where(match, share, 0.0), axis=1, keepdims=True)

        @pl.when(more_ref[e, i] > 0)
        def _():
            acc_ref[...] += window(e, 1)

    out_ref[...] = acc_ref[...].astype(BF)


def combine_rows(start, more, wide, pos, rows, share):
    experts, capacity, width = rows.shape
    total = pos.shape[0]
    return pl.pallas_call(
        functools.partial(combine_kernel, experts),
        out_shape=[
            jax.ShapeDtypeStruct((total, width), BF),
            jax.ShapeDtypeStruct((total, experts), F32),
        ],
        grid_spec=pltpu.PrefetchScalarGridSpec(
            num_scalar_prefetch=3,
            grid=(total // TILE,),
            in_specs=[
                pl.BlockSpec((TILE, experts), lambda i, *_: (i, 0)),
                pl.BlockSpec(rows.shape, lambda i, *_: (0, 0, 0), pipeline_mode=pl.Buffered(1)),
                pl.BlockSpec(share.shape, lambda i, *_: (0, 0, 0), pipeline_mode=pl.Buffered(1)),
            ],
            out_specs=[
                pl.BlockSpec((TILE, width), lambda i, *_: (i, 0)),
                pl.BlockSpec((TILE, experts), lambda i, *_: (i, 0)),
            ],
            scratch_shapes=[pltpu.VMEM((TILE, width), F32)],
        ),
        compiler_params=pltpu.CompilerParams(vmem_limit_bytes=48 << 20),
        cost_estimate=pl.CostEstimate(
            flops=2 * experts * total * TILE * width,
            bytes_accessed=2 * (experts * capacity + total) * width,
            transcendentals=0,
        ),
    )(start, more, wide, pos, rows, share)


def local(
    tokens,
    cotangent,
    routes,
    block_of_slot,
    cont_seg,
    w_query,
    w_key,
    w_value,
    w_out,
    w_router,
    attn_gain,
    query_gain,
    key_gain,
    ffn_gain,
    w_gate,
    w_up,
    w_down,
):
    ctx_size = lax.axis_size("ctx")
    exp_size = lax.axis_size("exp")
    me = lax.axis_index("ctx")
    exp_index = lax.axis_index("exp")
    tok_rows = tokens.shape[0]
    part_rows = w_query.shape[0]
    own_width = D // ctx_size
    own_heads = HEADS // ctx_size
    experts = w_router.shape[1]
    own_experts = w_gate.shape[0]
    slot_table = block_of_slot[0]
    seg_row = cont_seg[0]
    group_rows = ctx_size * tok_rows
    factor = 1.0 / math.sqrt(HD)

    tokens_group, tokens_there = gather_group(tokens, slot_table, me)
    small = jnp.concatenate(
        [w_router] + [g[:, None] for g in (attn_gain, query_gain, key_gain, ffn_gain)], axis=1
    )
    small = jnp.pad(small, ((0, 0), (0, 128 - small.shape[1])))
    by_owner = jnp.stack(
        [w.reshape(part_rows, ctx_size, own_width) for w in (w_query, w_key, w_value)], axis=2
    )
    by_owner = jnp.swapaxes(by_owner, 0, 1).reshape(ctx_size, part_rows, 3 * own_width)
    by_owner = jnp.concatenate(
        [by_owner, jnp.broadcast_to(small, (ctx_size,) + small.shape)], axis=2
    )
    own_columns = exchange(by_owner, me)
    packed = lax.all_gather(own_columns, "exp", axis=1, tiled=True).reshape(D, 3 * own_width + 128)
    small_full = packed[:, 3 * own_width :]
    router_full = small_full[:, :experts]
    gains = small_full[:, experts : experts + 4].astype(F32)
    gain_attn, gain_ffn = gains[:, 0], gains[:, 3]
    own_gains = lax.dynamic_slice(gains, (me * own_width, 0), (own_width, 4))
    gain_query, gain_key = own_gains[:, 1], own_gains[:, 2]
    out_full = lax.all_gather(w_out, "exp", axis=0, tiled=True)
    routes_all = lax.all_to_all(
        jnp.broadcast_to(routes[None], (exp_size,) + routes.shape),
        "exp",
        split_axis=0,
        concat_axis=0,
        tiled=True,
    ).reshape(exp_size * tok_rows, TOP)
    upstream_all = lax.all_gather(cotangent, "exp", axis=0, tiled=True)
    gate_full = gather_rows(after(w_gate, tokens_there), me)
    up_full = gather_rows(after(w_up, tokens_there), me)
    down_full = gather_rows(after(w_down, tokens_there), me)

    own_ids = exp_index * own_experts + jnp.arange(own_experts, dtype=jnp.int32)
    member = jnp.any(routes_all[:, :, None] == own_ids[None, None, :], axis=1)
    place_of = prefix_count(member)
    capacity = exp_size * 8 * ((5 * tok_rows * TOP // (4 * experts) + 7) // 8)
    row_tiles = (capacity + TILE - 1) // TILE
    capacity = row_tiles * TILE
    all_rows = exp_size * tok_rows
    row_ids = jnp.arange(capacity, dtype=jnp.int32)
    hit = (place_of.T[:, None, :] == row_ids[None, :, None]) & member.T[:, None, :]
    token_ids = jnp.arange(all_rows, dtype=jnp.int32)
    token_of_row = jnp.max(jnp.where(hit, token_ids[None, None, :], -1), axis=2)
    counts = jnp.sum(member.astype(jnp.int32), axis=0)
    used_tiles = (counts + TILE - 1) // TILE
    by_tile = token_of_row.reshape(own_experts * row_tiles, TILE)
    low_token = jnp.maximum(by_tile[:, 0], 0) // 128 * 128
    windows = jnp.maximum((jnp.max(by_tile, axis=1) - low_token) // WIN + 1, 1)
    token_column = token_of_row.reshape(-1, 1)
    place_column = jnp.where(member, place_of, NOWHERE)
    first_place = place_of[::TILE].T
    in_tile = jnp.sum(member.reshape(-1, TILE, own_experts).astype(jnp.int32), axis=1).T
    first_row = first_place // 16 * 16
    more_rows = (first_place + in_tile - first_row > TILE).astype(jnp.int32)
    share_row_start = jnp.minimum(first_place // 128 * 128, capacity - 384)

    seg_ids = jnp.concatenate([jnp.full((PROMPT,), -1, jnp.int32), seg_row])
    starts = jnp.sum(
        (seg_row[None, :] < jnp.arange(CONT, dtype=jnp.int32)[:, None]).astype(jnp.int32), axis=1
    )
    first_pos = jnp.sum(
        jnp.where(
            seg_row[:, None] == jnp.arange(CONT, dtype=jnp.int32)[None, :], starts[None, :], 0
        ),
        axis=1,
    )
    cont_pos = PROMPT + jnp.arange(CTOK, dtype=jnp.int32) - first_pos
    position = jnp.concatenate([jnp.arange(PROMPT, dtype=jnp.int32), cont_pos])
    cos_part, sin_part = angles(position)
    group_inputs = tokens_group.astype(F32)
    hidden_one = (group_inputs * inverse_root(group_inputs) * gain_attn).astype(BF)
    projected = jnp.dot(hidden_one, packed, preferred_element_type=F32)
    query_pre = projected[:, :own_width]
    key_pre = projected[:, own_width : 2 * own_width]
    value_low = projected[:, 2 * own_width : 3 * own_width].astype(BF)
    squares = jnp.stack([jnp.sum(query_pre * query_pre, axis=1), jnp.sum(key_pre * key_pre, axis=1)])
    roots = lax.rsqrt(sum_over_ctx(squares) / D + epsilon)
    root_query, root_key = roots[0][:, None], roots[1][:, None]
    normed_query = query_pre * root_query
    normed_key = key_pre * root_key

    def turn(values, turning):
        heads = values.reshape(group_rows, own_heads, HD)
        return turning(heads, cos_part, sin_part).reshape(group_rows, own_width)

    query_rot = turn(normed_query * gain_query, rotate).astype(BF)
    key_rot = turn(normed_key * gain_key, rotate).astype(BF)
    context_low = attend(query_rot, key_rot, value_low, seg_ids)
    branch_part = jnp.dot(context_low, out_full, preferred_element_type=F32)
    branch = scatter_group(branch_part, slot_table, me)
    inputs = tokens.astype(F32)
    middle = inputs + branch
    root_two = inverse_root(middle)
    normed_two = middle * root_two
    hidden_two = (normed_two * gain_ffn).astype(BF)
    hidden_all = lax.all_gather(hidden_two, "exp", axis=0, tiled=True)
    logits = jnp.dot(hidden_two, router_full, preferred_element_type=F32)
    router_prob = jax.nn.softmax(logits, axis=-1)

    upstream_rows, grad_raw = back_rows(
        used_tiles, low_token, windows, token_column, upstream_all, down_full
    )
    arrived, hidden_gated, grad_gate_pre, grad_up_pre, grad_rows, share_row = expert_rows(
        used_tiles,
        low_token,
        windows,
        own_ids[:1],
        token_column,
        hidden_all,
        router_full,
        gate_full,
        up_full,
        grad_raw,
    )
    grad_two_part, share_token = combine_rows(
        first_row,
        more_rows,
        share_row_start,
        place_column,
        grad_rows,
        share_row.reshape(own_experts, 1, capacity),
    )
    grad_two = lax.psum_scatter(
        grad_two_part, "exp", scatter_dimension=0, tiled=True
    ).astype(F32)
    share_back = lax.all_to_all(
        share_token.reshape(exp_size, tok_rows, own_experts),
        "exp",
        split_axis=0,
        concat_axis=0,
        tiled=True,
    )
    grad_prob = jnp.swapaxes(share_back, 0, 1).reshape(tok_rows, experts)
    result = jnp.einsum(
        "erf,efd->erd", hidden_gated, down_full, preferred_element_type=F32
    ).astype(BF)
    mixture_part, unused = combine_rows(
        first_row,
        more_rows,
        share_row_start,
        place_column,
        result,
        share_row.reshape(own_experts, 1, capacity),
    )
    mixture = lax.psum_scatter(mixture_part, "exp", scatter_dimension=0, tiled=True).astype(F32)
    output = (middle + mixture).astype(BF)

    def weight_grad(left, right):
        return jnp.einsum("era,erb->eab", left, right, preferred_element_type=F32).astype(BF)

    gate_grad = scatter_rows(weight_grad(arrived, grad_gate_pre), me)
    up_grad = scatter_rows(weight_grad(arrived, grad_up_pre), me)
    down_grad = scatter_rows(weight_grad(hidden_gated, upstream_rows), me)

    grad_logits = (
        router_prob * (grad_prob - jnp.sum(router_prob * grad_prob, axis=-1, keepdims=True))
    ).astype(BF)
    grad_router = jnp.einsum("td,te->de", hidden_two, grad_logits, preferred_element_type=F32)
    grad_two = grad_two + jnp.einsum(
        "te,de->td", grad_logits, router_full, preferred_element_type=F32
    )
    grad_ffn_gain = jnp.sum(grad_two * normed_two, axis=0)
    grad_middle = cotangent.astype(F32) + norm_back(grad_two * gain_ffn, normed_two, root_two)

    branch_grad, unused = gather_group(grad_middle.astype(BF), slot_table, me)
    grad_context = lax.dot_general(branch_grad, out_full, NT, preferred_element_type=F32).astype(BF)
    out_grad = jnp.einsum("td,te->de", context_low, branch_grad, preferred_element_type=F32)
    grad_query_rot, grad_key_rot, grad_value = attend_back(
        query_rot, key_rot, value_low, grad_context, seg_ids
    )
    grad_query_norm = turn(grad_query_rot, rotate_back)
    grad_key_norm = turn(grad_key_rot, rotate_back)
    grad_query_gain = jnp.sum(grad_query_norm * normed_query, axis=0)
    grad_key_gain = jnp.sum(grad_key_norm * normed_key, axis=0)
    scaled_query = grad_query_norm * gain_query
    scaled_key = grad_key_norm * gain_key
    means = (
        sum_over_ctx(
            jnp.stack(
                [
                    jnp.sum(scaled_query * normed_query, axis=1),
                    jnp.sum(scaled_key * normed_key, axis=1),
                ]
            )
        )
        / D
    )
    grad_projected = jnp.concatenate(
        [
            root_query * (scaled_query - normed_query * means[0][:, None]),
            root_key * (scaled_key - normed_key * means[1][:, None]),
            grad_value,
        ],
        axis=1,
    ).astype(BF)
    grad_packed = jnp.pad(grad_projected, ((0, 0), (0, 128)))
    grad_one_part = lax.dot_general(grad_packed, packed, NT, preferred_element_type=F32)
    grad_one = scatter_group(grad_one_part, slot_table, me)
    qkv_grad = jnp.einsum("td,te->de", hidden_one, grad_projected, preferred_element_type=F32)
    out_sum = lax.psum_scatter(
        out_grad.astype(BF), "exp", scatter_dimension=0, tiled=True
    ).astype(F32)
    qkv_sum = lax.psum_scatter(
        qkv_grad.astype(BF).reshape(ctx_size, exp_size * part_rows, 3 * own_width),
        "exp",
        scatter_dimension=1,
        tiled=True,
    )
    qkv_own = exchange(qkv_sum, me).astype(F32)
    projection_grads = [
        jnp.swapaxes(qkv_own[:, :, i * own_width : (i + 1) * own_width], 0, 1).reshape(part_rows, D)
        for i in range(3)
    ]
    root_one = inverse_root(inputs)
    normed_one = inputs * root_one
    grad_attn_gain = jnp.sum(grad_one * normed_one, axis=0)
    grad_input = grad_middle + norm_back(grad_one * gain_attn, normed_one, root_one)
    early_sums = lax.psum_scatter(
        jnp.concatenate([grad_router, grad_ffn_gain[:, None]], axis=1),
        BOTH,
        scatter_dimension=0,
        tiled=True,
    )
    head_gains = lax.dynamic_update_slice(
        jnp.zeros((2, D), F32), jnp.stack([grad_query_gain, grad_key_gain]), (0, me * own_width)
    )
    late_sums = lax.dynamic_slice(
        lax.psum(jnp.concatenate([grad_attn_gain[None], head_gains]), BOTH),
        (0, (me * exp_size + exp_index) * part_rows),
        (3, part_rows),
    )
    return (
        output,
        grad_input,
        projection_grads[0],
        projection_grads[1],
        projection_grads[2],
        out_sum,
        early_sums[:, :experts],
        late_sums[0],
        late_sums[1],
        late_sums[2],
        early_sums[:, experts],
        gate_grad,
        up_grad,
        down_grad,
    )


def solution(mesh):
    rows = P(BOTH, None)
    weights = P("exp", "ctx", None)
    in_specs = (
        (rows, rows, rows, P("exp", None), P("exp", None))
        + (rows,) * 5
        + (P(BOTH),) * 4
        + (weights,) * 3
    )
    out_specs = (rows,) * 7 + (P(BOTH),) * 4 + (weights,) * 3
    return jax.shard_map(local, mesh=mesh, in_specs=in_specs, out_specs=out_specs, check_vma=False)
```

```python
import functools
import math

import jax
import jax.numpy as jnp
from jax import lax
from jax.experimental import pallas as pl
from jax.experimental.pallas import tpu as pltpu
from jax.sharding import PartitionSpec as P

D = 2048
HEADS = 16
HD = 128
TOP = 8
PROMPT = 1024
CONT = 2
CTOK = 512

epsilon = 1e-05
rope_base = 10000.0
BF = jnp.bfloat16
F32 = jnp.float32
BOTH = ("ctx", "exp")
X_PAIRS = [(i, i ^ 1) for i in range(4)]
Y_PAIRS = [(i, i ^ 2) for i in range(4)]
XY_PAIRS = [(i, i ^ 3) for i in range(4)]
NT = (((1,), (1,)), ((), ()))
TN = (((0,), (0,)), ((), ()))
TILE = 256
WIN = 512
NOWHERE = -(1 << 20)


def inverse_root(values):
    return lax.rsqrt(jnp.mean(values * values, axis=-1, keepdims=True) + epsilon)


def norm_back(gradient, normed, root_part):
    return root_part * (gradient - normed * jnp.mean(gradient * normed, axis=-1, keepdims=True))


def angles(position):
    half_dim = HD // 2
    inverse = rope_base ** (-2.0 * jnp.arange(half_dim, dtype=F32) / HD)
    phases = position.astype(F32)[:, None] * inverse[None, :]
    cosine, sine = jnp.cos(phases), jnp.sin(phases)
    return jnp.concatenate([cosine, cosine], axis=1), jnp.concatenate([-sine, sine], axis=1)


def send_x(value):
    return lax.ppermute(value, "ctx", X_PAIRS)


def send_y(value):
    return lax.ppermute(value, "ctx", Y_PAIRS)


def send_xy(value):
    return lax.ppermute(value, "ctx", XY_PAIRS)


def after(value, *others):
    return lax.optimization_barrier((value,) + others)[0]


def after_all(values, *others):
    return lax.optimization_barrier(tuple(values) + others)[: len(values)]


def gather_pieces(value, half):
    from_x = send_x(value)
    from_y = send_y(value)
    far_low = send_y(from_x[:half])
    far_high = send_x(from_y[half:])
    return from_x, from_y, far_low, far_high


def scatter_payload(take, me):
    low = jnp.stack([take(me ^ 1, 0), take(me ^ 3, 0)]).astype(BF)
    high = jnp.stack([take(me ^ 2, 1), take(me ^ 3, 1)]).astype(BF)
    return low, high


def scatter_first(take, me):
    low, high = scatter_payload(take, me)
    return send_x(low), send_y(high)


def scatter_second(take, me, low, high):
    low_next = send_y((take(me ^ 2, 0).astype(F32) + low[1].astype(F32)).astype(BF))
    high_next = send_x((take(me ^ 1, 1).astype(F32) + high[1].astype(F32)).astype(BF))
    return low_next, high_next


def scatter_end(take, me, low, high, low_next, high_next):
    first = take(me, 0).astype(F32) + low[0].astype(F32) + low_next.astype(F32)
    second = take(me, 1).astype(F32) + high[0].astype(F32) + high_next.astype(F32)
    return first, second


def exchange(blocks, me):
    if lax.axis_size("ctx") != 4:
        return lax.all_to_all(blocks, "ctx", split_axis=0, concat_axis=0, tiled=True)
    sends = (lambda part: part, send_x, send_y, send_xy)
    whole = jnp.zeros_like(blocks)
    for away, send in enumerate(sends):
        part = send(lax.dynamic_slice_in_dim(blocks, me ^ away, 1, 0))
        whole = lax.dynamic_update_slice_in_dim(whole, part, me ^ away, 0)
    return whole


def sum_over_ctx(value):
    if lax.axis_size("ctx") != 4:
        return lax.psum(value, "ctx")
    value = value + send_x(value)
    return value + send_y(value)


def sum_to_rows(values, me):
    ctx_size, exp_size = lax.axis_size("ctx"), lax.axis_size("exp")
    count, width = values.shape
    parts = values.reshape(count, ctx_size, exp_size, width // (ctx_size * exp_size))
    parts = jnp.transpose(parts, (2, 1, 0, 3))
    parts = jnp.sum(lax.all_to_all(parts, "exp", split_axis=0, concat_axis=0, tiled=True), axis=0)
    return jnp.sum(exchange(parts, me), axis=0)


def gather_expert(w_gate, w_up, w_down, me):
    if lax.axis_size("ctx") != 4:
        return (
            lax.all_gather(jnp.stack([w_gate, w_up]), "ctx", axis=1, tiled=True),
            lax.all_gather(w_down, "ctx", axis=0, tiled=True),
        )
    width = w_gate.shape[1]
    packed = jnp.concatenate([w_gate, w_up, w_down[:, :width], w_down[:, width:]], axis=0)
    return packed, send_x(packed), send_y(packed)


def gather_expert_far(near):
    if lax.axis_size("ctx") != 4:
        return ()
    half = near[1].shape[0] // 2
    return send_y(near[1][:half]), send_x(near[2][half:])


def build_expert(w_gate, w_down, near, far, me):
    if lax.axis_size("ctx") != 4:
        return near
    rows, width = w_gate.shape
    half = rows // 2
    both = jnp.zeros((2, 4 * rows, width), BF)
    down = jnp.zeros((2 * rows, 2 * width), BF)

    def put_both(whole, part, owner, which, first):
        return lax.dynamic_update_slice(whole, part[None], (which, owner * rows + first, 0))

    def put_down(whole, part, owner, which):
        return lax.dynamic_update_slice(whole, part, (owner * half, which * width))

    for away, part in enumerate(near):
        both = put_both(both, part[:rows], me ^ away, 0, 0)
        both = put_both(both, part[rows : 2 * rows], me ^ away, 1, 0)
        down = put_down(down, part[2 * rows : 2 * rows + half], me ^ away, 0)
        down = put_down(down, part[2 * rows + half :], me ^ away, 1)
    low, high = far
    both = put_both(both, low[:rows], me ^ 3, 0, 0)
    both = put_both(both, low[rows:], me ^ 3, 1, 0)
    both = put_both(both, high[:half], me ^ 3, 1, half)
    down = put_down(down, high[half:rows], me ^ 3, 0)
    down = put_down(down, high[rows:], me ^ 3, 1)
    return both, down


def expert_take(grads):
    gate_up, down = grads
    rows, width = gate_up.shape[0] // 4, gate_up.shape[1] // 2
    half = down.shape[0] // 8

    def take(owner, part):
        first = (2 * owner + part) * half
        return jnp.concatenate(
            [
                lax.dynamic_slice(gate_up, (owner * rows, part * width), (rows, width)),
                lax.dynamic_slice(down, (first, 0), (half, width)),
                lax.dynamic_slice(down, (first, width), (half, width)),
            ],
            axis=0,
        )

    return take


def scatter_expert_first(grads, me):
    if lax.axis_size("ctx") != 4:
        return tuple(
            lax.psum_scatter(grad, "ctx", scatter_dimension=0, tiled=True) for grad in grads
        )
    return scatter_first(expert_take(grads), me)


def scatter_expert_second(grads, sums, me):
    if lax.axis_size("ctx") != 4:
        return ()
    return scatter_second(expert_take(grads), me, *sums)


def scatter_expert_end(grads, sums, more, me):
    if lax.axis_size("ctx") != 4:
        gate_up, down = (part.astype(F32) for part in sums)
        width = gate_up.shape[1] // 2
        return gate_up[:, :width], gate_up[:, width:], down
    first, second = scatter_end(expert_take(grads), me, *sums, *more)
    rows, half = grads[0].shape[0] // 4, grads[1].shape[0] // 8
    down = [
        jnp.concatenate([part[rows : rows + half], part[rows + half :]], axis=1)
        for part in (first, second)
    ]
    return first[:rows], second[:rows], jnp.concatenate(down, axis=0)


def pick_blocks(blocks, order):
    return jnp.concatenate(
        [
            lax.dynamic_index_in_dim(blocks, order[i], 0, keepdims=False)
            for i in range(order.shape[0])
        ],
        axis=0,
    )


def gather_group(rows, slot_table, me):
    block = rows.shape[0] // 2
    if lax.axis_size("ctx") != 4:
        blocks = slot_table.shape[0]
        whole = lax.all_gather(rows, "ctx", axis=0, tiled=True).reshape(blocks, block, -1)
        match = slot_table[None, :] == jnp.arange(blocks, dtype=jnp.int32)[:, None]
        order = jnp.sum(jnp.where(match, jnp.arange(blocks, dtype=jnp.int32)[None, :], 0), axis=1)
        return pick_blocks(whole, order), ()
    from_x, from_y, far_low, far_high = gather_pieces(rows, block)
    parts = (
        (rows[:block], me, 0),
        (rows[block:], me, 1),
        (from_x[:block], me ^ 1, 0),
        (from_x[block:], me ^ 1, 1),
        (from_y[:block], me ^ 2, 0),
        (from_y[block:], me ^ 2, 1),
        (far_low, me ^ 3, 0),
        (far_high, me ^ 3, 1),
    )
    whole = jnp.zeros((8 * block, rows.shape[1]), rows.dtype)
    for part, owner, slot in parts:
        start = slot_table[2 * owner + slot] * block
        whole = lax.dynamic_update_slice(whole, part, (start, 0))
    return whole, (far_low, far_high)


def scatter_group(partial, slot_table, me):
    blocks = slot_table.shape[0]
    block = partial.shape[0] // blocks
    if lax.axis_size("ctx") != 4:
        ordered = pick_blocks(partial.reshape(blocks, block, -1), slot_table).astype(BF)
        whole = lax.psum_scatter(ordered, "ctx", scatter_dimension=0, tiled=True)
        return whole.astype(F32), (ordered,), (whole,)

    def take(owner, part):
        start = slot_table[2 * owner + part] * block
        return lax.dynamic_slice(partial, (start, 0), (block, partial.shape[1]))

    sent = scatter_payload(take, me)
    near = send_x(sent[0]), send_y(sent[1])
    far = scatter_second(take, me, *near)
    return jnp.concatenate(scatter_end(take, me, *near, *far), axis=0), sent, far


def prefix_count(member):
    rows, columns = member.shape
    width = 128
    blocks = rows // width
    ones = member.astype(BF).reshape(blocks, width, columns)
    lower = (
        jnp.arange(width)[:, None] > jnp.arange(width)[None, :]
    ).astype(BF)
    inner = jnp.einsum("pq,bqc->bpc", lower, ones, preferred_element_type=F32)
    totals = jnp.sum(ones.astype(F32), axis=1)
    before = (jnp.arange(blocks)[:, None] > jnp.arange(blocks)[None, :]).astype(F32)
    outer = jnp.sum(before[:, :, None] * totals[None, :, :], axis=1)
    return (inner + outer[:, None, :]).reshape(rows, columns).astype(jnp.int32)


def dot(left, right, dims=(((1,), (0,)), ((), ()))):
    return lax.dot_general(left, right, dims, preferred_element_type=F32)


def turned(values, cosine, sine):
    return values * cosine + pltpu.roll(values, HD // 2, 1) * sine


def tile_weights(query, key, seg_q, seg_k, first, factor):
    rows, width = query.shape[0], key.shape[0]
    scores = dot(query, key, NT) * factor
    q_place = first + lax.broadcasted_iota(jnp.int32, (rows, width), 0)
    k_place = lax.broadcasted_iota(jnp.int32, (rows, width), 1)
    allowed = k_place <= q_place
    if first >= PROMPT:
        allowed = allowed & ((seg_k < 0) | (seg_k == seg_q))
    scores = jnp.where(allowed, scores, -1e30)
    weights = jnp.exp(scores - jnp.max(scores, axis=1, keepdims=True))
    return weights, jnp.sum(weights, axis=1, keepdims=True)


def attend_kernel(
    tiles,
    factor,
    qp_ref,
    kp_ref,
    vp_ref,
    root_ref,
    key_root_ref,
    gain_ref,
    cos_ref,
    sin_ref,
    sq_ref,
    sk_ref,
    q_ref,
    k_ref,
    v_ref,
    o_ref,
):
    at = pl.program_id(1)
    tile = qp_ref.shape[0]

    @pl.when(at == 0)
    def _():
        keys = kp_ref[...] * key_root_ref[:, 1:2] * gain_ref[1:2]
        k_ref[...] = turned(keys, cos_ref[...], sin_ref[...]).astype(BF)
        v_ref[...] = vp_ref[...].astype(BF)

    for i in range(tiles):

        @pl.when(at == i)
        def _():
            own = slice(i * tile, (i + 1) * tile)
            width = (i + 1) * tile
            queries = qp_ref[...] * root_ref[:, 0:1] * gain_ref[0:1]
            query = turned(queries, cos_ref[own], sin_ref[own]).astype(BF)
            q_ref[...] = query
            weights, total = tile_weights(
                query, k_ref[:width], sq_ref[...], sk_ref[:, :width], i * tile, factor
            )
            o_ref[...] = (dot(weights.astype(BF), v_ref[:width]) / total).astype(BF)


def attend(projected, roots, gains, cosine, sine, seg, width, tile=512):
    rows = projected.shape[0]
    heads, tiles = width // HD, rows // tile
    own = pl.BlockSpec((tile, HD), lambda h, i: (i, h))
    whole = pl.BlockSpec((rows, HD), lambda h, i: (0, h))
    pairs = heads * rows * rows * (tiles + 1) // (2 * tiles)
    return pl.pallas_call(
        functools.partial(attend_kernel, tiles, 1.0 / math.sqrt(HD)),
        out_shape=[jax.ShapeDtypeStruct((rows, width), BF)] * 4,
        grid=(heads, tiles),
        in_specs=[
            own,
            pl.BlockSpec((rows, HD), lambda h, i: (0, heads + h)),
            pl.BlockSpec((rows, HD), lambda h, i: (0, 2 * heads + h)),
            pl.BlockSpec((tile, 2), lambda h, i: (i, 0)),
            pl.BlockSpec((rows, 2), lambda h, i: (0, 0)),
            pl.BlockSpec((2, HD), lambda h, i: (0, h)),
            pl.BlockSpec((rows, HD), lambda h, i: (0, 0)),
            pl.BlockSpec((rows, HD), lambda h, i: (0, 0)),
            pl.BlockSpec((tile, 1), lambda h, i: (i, 0)),
            pl.BlockSpec((1, rows), lambda h, i: (0, 0)),
        ],
        out_specs=[own, whole, whole, own],
        compiler_params=pltpu.CompilerParams(vmem_limit_bytes=48 << 20),
        cost_estimate=pl.CostEstimate(
            flops=4 * pairs * HD, bytes_accessed=20 * rows * width, transcendentals=pairs
        ),
    )(
        projected,
        projected,
        projected,
        roots,
        roots,
        gains,
        cosine,
        sine,
        seg[:, None],
        seg[None, :],
    )


def attend_back_kernel(
    tiles,
    factor,
    q_ref,
    k_ref,
    v_ref,
    d_ref,
    cos_ref,
    sin_ref,
    sq_ref,
    sk_ref,
    dq_ref,
    dk_ref,
    dv_ref,
):
    at = pl.program_id(1)
    tile = q_ref.shape[0]

    @pl.when(at == 0)
    def _():
        dk_ref[...] = jnp.zeros_like(dk_ref)
        dv_ref[...] = jnp.zeros_like(dv_ref)

    for i in range(tiles):

        @pl.when(at == i)
        def _():
            own = slice(i * tile, (i + 1) * tile)
            width = (i + 1) * tile
            query, grad = q_ref[...], d_ref[...]
            weights, total = tile_weights(
                query, k_ref[:width], sq_ref[...], sk_ref[:, :width], i * tile, factor
            )
            weights = weights / total
            grad_weights = dot(grad, v_ref[:width], NT)
            delta = jnp.sum(weights * grad_weights, axis=1, keepdims=True)
            grad_scores = (weights * (grad_weights - delta)).astype(BF)
            grad_query = dot(grad_scores, k_ref[:width]) * factor
            dq_ref[...] = turned(grad_query, cos_ref[own], -sin_ref[own])
            dk_ref[:width] += dot(grad_scores, query, TN)
            dv_ref[:width] += dot(weights.astype(BF), grad, TN)

    @pl.when(at == tiles - 1)
    def _():
        dk_ref[...] = turned(dk_ref[...] * factor, cos_ref[...], -sin_ref[...])


def attend_back(q, k, v, grad, cosine, sine, seg, tile=512):
    rows, width = q.shape
    heads, tiles = width // HD, rows // tile
    own = pl.BlockSpec((tile, HD), lambda h, i: (i, h))
    whole = pl.BlockSpec((rows, HD), lambda h, i: (0, h))
    table = pl.BlockSpec((rows, HD), lambda h, i: (0, 0))
    pairs = heads * rows * rows * (tiles + 1) // (2 * tiles)
    return pl.pallas_call(
        functools.partial(attend_back_kernel, tiles, 1.0 / math.sqrt(HD)),
        out_shape=[jax.ShapeDtypeStruct((rows, width), F32)] * 3,
        grid=(heads, tiles),
        in_specs=[
            own,
            whole,
            whole,
            own,
            table,
            table,
            pl.BlockSpec((tile, 1), lambda h, i: (i, 0)),
            pl.BlockSpec((1, rows), lambda h, i: (0, 0)),
        ],
        out_specs=[own, whole, whole],
        compiler_params=pltpu.CompilerParams(vmem_limit_bytes=48 << 20),
        cost_estimate=pl.CostEstimate(
            flops=10 * pairs * HD, bytes_accessed=20 * rows * width, transcendentals=pairs
        ),
    )(q, k, v, grad, cosine, sine, seg[:, None], seg[None, :])


def pick_rows(tok, low, windows, source_ref, acc_ref):
    last = source_ref.shape[0] - WIN
    span = lax.broadcasted_iota(jnp.int32, (TILE, WIN), 1)

    def window(j):
        base = low + j * WIN
        start = pl.multiple_of(jnp.minimum(base, last), 128)
        match = (tok - start == span) & (tok >= base)
        return dot(match.astype(F32).astype(BF), source_ref[pl.ds(start, WIN), :])

    acc_ref[...] = window(0)

    @pl.loop(1, windows)
    def _(j):
        acc_ref[...] += window(j)

    return acc_ref[...].astype(BF)


def back_rows_kernel(
    tiles_ref, low_ref, windows_ref, tok_ref, dy_ref, wd_ref, rows_ref, raw_ref, acc_ref
):
    i = pl.program_id(0)

    @pl.when(i < tiles_ref[0])
    def _():
        rows = pick_rows(tok_ref[...], low_ref[i], windows_ref[i], dy_ref, acc_ref)
        rows_ref[...] = rows
        raw_ref[...] = dot(rows, wd_ref[...], NT)

    @pl.when(i >= tiles_ref[0])
    def _():
        rows_ref[...] = jnp.zeros_like(rows_ref)
        raw_ref[...] = jnp.zeros_like(raw_ref)


def back_rows(tables, upstream, w_down):
    total, width = upstream.shape
    ff = w_down.shape[0]
    capacity = tables[3].shape[0]
    tile = lambda n: pl.BlockSpec((TILE, n), lambda i, *_: (i, 0))
    once = lambda shape: pl.BlockSpec(shape, lambda i, *_: (0, 0), pipeline_mode=pl.Buffered(1))
    return pl.pallas_call(
        back_rows_kernel,
        out_shape=[
            jax.ShapeDtypeStruct((capacity, width), BF),
            jax.ShapeDtypeStruct((capacity, ff), F32),
        ],
        grid_spec=pltpu.PrefetchScalarGridSpec(
            num_scalar_prefetch=3,
            grid=(capacity // TILE,),
            in_specs=[tile(1), once((total, width)), once((ff, width))],
            out_specs=[tile(width), tile(ff)],
            scratch_shapes=[pltpu.VMEM((TILE, width), F32)],
        ),
        compiler_params=pltpu.CompilerParams(vmem_limit_bytes=48 << 20),
        cost_estimate=pl.CostEstimate(
            flops=total * (width * ff + WIN * width),
            bytes_accessed=2 * total * width + 2 * ff * width + capacity * (2 * width + 4 * ff),
            transcendentals=0,
        ),
    )(*tables, upstream, w_down)


def expert_kernel(
    own,
    tiles_ref,
    low_ref,
    windows_ref,
    id_ref,
    tok_ref,
    h_ref,
    router_ref,
    wg_ref,
    wu_ref,
    raw_ref,
    rows_ref,
    hid_ref,
    dab_ref,
    dh_ref,
    share_ref,
    acc_ref,
):
    i = pl.program_id(0)
    ff = wg_ref.shape[1]

    @pl.when(i < tiles_ref[0])
    def _():
        rows = pick_rows(tok_ref[...], low_ref[i], windows_ref[i], h_ref, acc_ref)
        rows_ref[...] = rows
        logits = dot(rows, router_ref[...])
        probs = jnp.exp(logits - jnp.max(logits, axis=1, keepdims=True))
        column = lax.broadcasted_iota(jnp.int32, probs.shape, 1)
        mine = jnp.sum(jnp.where(column == id_ref[0] + own, probs, 0.0), axis=1, keepdims=True)
        gate = mine / jnp.sum(probs, axis=1, keepdims=True)
        share = 0.0
        part = ff // 4
        for c in range(4):
            cols = slice(c * part, (c + 1) * part)
            a = dot(rows, wg_ref[:, cols])
            b = dot(rows, wu_ref[:, cols])
            raw = raw_ref[:, cols]
            sig = 1.0 / (1.0 + jnp.exp(-a))
            silu = a * sig
            hid = silu * b
            share += jnp.sum(hid * raw, axis=1, keepdims=True)
            raw = raw * gate
            hid_ref[:, cols] = (hid * gate).astype(BF)
            dab_ref[:, cols] = (raw * b * (sig * (1.0 + a * (1.0 - sig)))).astype(BF)
            dab_ref[:, ff + c * part : ff + (c + 1) * part] = (raw * silu).astype(BF)
        share_ref[...] = share
        dh = dot(dab_ref[:, :ff], wg_ref[...], NT) + dot(dab_ref[:, ff:], wu_ref[...], NT)
        dh_ref[...] = dh.astype(BF)

    @pl.when(i >= tiles_ref[0])
    def _():
        for ref in (rows_ref, hid_ref, dab_ref, dh_ref, share_ref):
            ref[...] = jnp.zeros_like(ref)


def expert_rows(tables, own, first_id, hidden, router, gate_up, raw):
    total, width = hidden.shape
    ff = gate_up.shape[2]
    capacity = tables[3].shape[0]
    tile = lambda n: pl.BlockSpec((TILE, n), lambda i, *_: (i, 0))
    once = lambda shape: pl.BlockSpec(shape, lambda i, *_: (0, 0), pipeline_mode=pl.Buffered(1))
    half = lambda k: pl.BlockSpec(
        (None, width, ff), lambda i, *_: (k, 0, 0), pipeline_mode=pl.Buffered(1)
    )
    made = lambda n, dtype=BF: jax.ShapeDtypeStruct((capacity, n), dtype)
    return pl.pallas_call(
        functools.partial(expert_kernel, own),
        out_shape=[made(width), made(ff), made(2 * ff), made(width), made(1, F32)],
        grid_spec=pltpu.PrefetchScalarGridSpec(
            num_scalar_prefetch=4,
            grid=(capacity // TILE,),
            in_specs=[
                tile(1),
                once((total, width)),
                once(router.shape),
                half(0),
                half(1),
                tile(ff),
            ],
            out_specs=[tile(width), tile(ff), tile(2 * ff), tile(width), tile(1)],
            scratch_shapes=[pltpu.VMEM((TILE, width), F32)],
        ),
        compiler_params=pltpu.CompilerParams(vmem_limit_bytes=56 << 20),
        cost_estimate=pl.CostEstimate(
            flops=total * (4 * width * ff + WIN * width),
            bytes_accessed=2 * total * width + 4 * ff * width + capacity * (4 * width + 10 * ff),
            transcendentals=total * ff,
        ),
    )(*tables[:3], first_id, tables[3], hidden, router, gate_up, gate_up, raw)


def combine_kernel(experts, start_ref, more_ref, wide_ref, pos_ref, *refs):
    rows_refs, share_refs = refs[:experts], refs[experts : 2 * experts]
    out_ref, own_ref, acc_ref = refs[2 * experts :]
    i = pl.program_id(0)
    span = lax.broadcasted_iota(jnp.int32, (TILE, TILE), 1)
    wide_span = lax.broadcasted_iota(jnp.int32, (TILE, 384), 1)
    last = rows_refs[0].shape[0] - TILE

    def window(e, j):
        base = start_ref[e, i] + j * TILE
        start = pl.multiple_of(jnp.minimum(base, last), 16)
        pos = pos_ref[:, e : e + 1]
        match = (pos - start == span) & (pos >= base)
        return dot(match.astype(F32).astype(BF), rows_refs[e][pl.ds(start, TILE), :])

    acc_ref[...] = sum(window(e, 0) for e in range(experts))
    for e in range(experts):
        wide = pl.multiple_of(wide_ref[e, i], 128)
        match = pos_ref[:, e : e + 1] - wide == wide_span
        share = share_refs[e][:, pl.ds(wide, 384)]
        own_ref[:, e : e + 1] = jnp.sum(jnp.where(match, share, 0.0), axis=1, keepdims=True)

        @pl.when(more_ref[e, i] > 0)
        def _():
            acc_ref[...] += window(e, 1)

    out_ref[...] = acc_ref[...].astype(BF)


def combine_rows(tables, rows, shares):
    experts, (capacity, width) = len(rows), rows[0].shape
    total = tables[3].shape[0]
    once = lambda shape: pl.BlockSpec(shape, lambda i, *_: (0, 0), pipeline_mode=pl.Buffered(1))
    tile = lambda n: pl.BlockSpec((TILE, n), lambda i, *_: (i, 0))
    return pl.pallas_call(
        functools.partial(combine_kernel, experts),
        out_shape=[
            jax.ShapeDtypeStruct((total, width), BF),
            jax.ShapeDtypeStruct((total, experts), F32),
        ],
        grid_spec=pltpu.PrefetchScalarGridSpec(
            num_scalar_prefetch=3,
            grid=(total // TILE,),
            in_specs=[tile(experts)]
            + [once((capacity, width))] * experts
            + [once((1, capacity))] * experts,
            out_specs=[tile(width), tile(experts)],
            scratch_shapes=[pltpu.VMEM((TILE, width), F32)],
        ),
        compiler_params=pltpu.CompilerParams(vmem_limit_bytes=48 << 20),
        cost_estimate=pl.CostEstimate(
            flops=2 * experts * total * TILE * width,
            bytes_accessed=2 * (experts * capacity + total) * width,
            transcendentals=0,
        ),
    )(*tables, *rows, *shares)


def local(
    tokens,
    cotangent,
    routes,
    block_of_slot,
    cont_seg,
    w_query,
    w_key,
    w_value,
    w_out,
    w_router,
    attn_gain,
    query_gain,
    key_gain,
    ffn_gain,
    w_gate,
    w_up,
    w_down,
):
    ctx_size = lax.axis_size("ctx")
    exp_size = lax.axis_size("exp")
    me = lax.axis_index("ctx")
    exp_index = lax.axis_index("exp")
    tok_rows = tokens.shape[0]
    part_rows = w_query.shape[0]
    own_width = D // ctx_size
    own_heads = HEADS // ctx_size
    experts = w_router.shape[1]
    own_experts = w_gate.shape[0]
    slot_table = block_of_slot[0]
    seg_row = cont_seg[0]
    group_rows = ctx_size * tok_rows
    factor = 1.0 / math.sqrt(HD)

    tokens_group, tokens_there = gather_group(tokens, slot_table, me)
    small = jnp.concatenate(
        [w_router] + [g[:, None] for g in (attn_gain, query_gain, key_gain, ffn_gain)], axis=1
    )
    small = jnp.pad(small, ((0, 0), (0, 128 - small.shape[1])))
    by_owner = jnp.stack(
        [w.reshape(part_rows, ctx_size, own_width) for w in (w_query, w_key, w_value)], axis=2
    )
    by_owner = jnp.swapaxes(by_owner, 0, 1).reshape(ctx_size, part_rows, 3 * own_width)
    by_owner = jnp.concatenate(
        [by_owner, jnp.broadcast_to(small, (ctx_size,) + small.shape)], axis=2
    )
    own_columns = exchange(by_owner, me)
    packed = lax.all_gather(own_columns, "exp", axis=1, tiled=True).reshape(D, 3 * own_width + 128)
    small_full = packed[:, 3 * own_width :]
    router_full = small_full[:, :experts]
    gains = small_full[:, experts : experts + 4].astype(F32)
    gain_attn, gain_ffn = gains[:, 0], gains[:, 3]
    own_gains = lax.dynamic_slice(gains, (me * own_width, 0), (own_width, 4))
    gain_query, gain_key = own_gains[:, 1], own_gains[:, 2]
    out_full = lax.all_gather(w_out, "exp", axis=0, tiled=True)
    routes_all = lax.all_to_all(
        jnp.broadcast_to(routes[None], (exp_size,) + routes.shape),
        "exp",
        split_axis=0,
        concat_axis=0,
        tiled=True,
    ).reshape(exp_size * tok_rows, TOP)
    upstream_all = lax.all_gather(cotangent, "exp", axis=0, tiled=True)
    first_near = gather_expert(*after_all((w_gate[0], w_up[0], w_down[0]), *tokens_there), me)

    own_ids = exp_index * own_experts + jnp.arange(own_experts, dtype=jnp.int32)
    member = jnp.any(routes_all[:, :, None] == own_ids[None, None, :], axis=1)
    place_of = prefix_count(member)
    capacity = exp_size * 8 * ((5 * tok_rows * TOP // (4 * experts) + 7) // 8)
    row_tiles = (capacity + TILE - 1) // TILE
    capacity = row_tiles * TILE
    all_rows = exp_size * tok_rows
    row_ids = jnp.arange(capacity, dtype=jnp.int32)
    hit = (place_of.T[:, None, :] == row_ids[None, :, None]) & member.T[:, None, :]
    token_ids = jnp.arange(all_rows, dtype=jnp.int32)
    token_of_row = jnp.max(jnp.where(hit, token_ids[None, None, :], -1), axis=2)
    counts = jnp.sum(member.astype(jnp.int32), axis=0)
    used_tiles = (counts + TILE - 1) // TILE
    by_tile = token_of_row.reshape(own_experts * row_tiles, TILE)
    low_token = jnp.maximum(by_tile[:, 0], 0) // 128 * 128
    windows = jnp.maximum((jnp.max(by_tile, axis=1) - low_token) // WIN + 1, 1)
    low_token = low_token.reshape(own_experts, row_tiles)
    windows = windows.reshape(own_experts, row_tiles)
    row_tables = [
        (used_tiles[e : e + 1], low_token[e], windows[e], token_of_row[e][:, None])
        for e in range(own_experts)
    ]
    place_column = jnp.where(member, place_of, NOWHERE)
    first_place = place_of[::TILE].T
    in_tile = jnp.sum(member.reshape(-1, TILE, own_experts).astype(jnp.int32), axis=1).T
    first_row = first_place // 16 * 16
    more_rows = (first_place + in_tile - first_row > TILE).astype(jnp.int32)
    share_row_start = jnp.minimum(first_place // 128 * 128, capacity - 384)
    token_tables = (first_row, more_rows, share_row_start, place_column)

    seg_ids = jnp.concatenate([jnp.full((PROMPT,), -1, jnp.int32), seg_row])
    starts = jnp.sum(
        (seg_row[None, :] < jnp.arange(CONT, dtype=jnp.int32)[:, None]).astype(jnp.int32), axis=1
    )
    first_pos = jnp.sum(
        jnp.where(
            seg_row[:, None] == jnp.arange(CONT, dtype=jnp.int32)[None, :], starts[None, :], 0
        ),
        axis=1,
    )
    cont_pos = PROMPT + jnp.arange(CTOK, dtype=jnp.int32) - first_pos
    position = jnp.concatenate([jnp.arange(PROMPT, dtype=jnp.int32), cont_pos])
    cos_part, sin_part = angles(position)
    group_inputs = after(
        tokens_group, token_of_row, place_column, first_row, more_rows, share_row_start, used_tiles, windows
    ).astype(F32)
    normed_group = group_inputs * inverse_root(group_inputs)
    hidden_one = (normed_group * gain_attn).astype(BF)
    projected = jnp.dot(hidden_one, packed, preferred_element_type=F32)
    query_pre = projected[:, :own_width]
    key_pre = projected[:, own_width : 2 * own_width]
    squares = jnp.stack([jnp.sum(query_pre * query_pre, axis=1), jnp.sum(key_pre * key_pre, axis=1)])
    roots = lax.rsqrt(sum_over_ctx(squares) / D + epsilon)
    root_query, root_key = roots[0][:, None], roots[1][:, None]
    normed_query = query_pre * root_query
    normed_key = key_pre * root_key
    query_rot, key_rot, value_low, context_low = attend(
        projected,
        roots.T,
        jnp.stack([gain_query, gain_key]),
        cos_part,
        sin_part,
        seg_ids,
        own_width,
    )
    branch_part = jnp.dot(context_low, out_full, preferred_element_type=F32)
    branch, unused, branch_there = scatter_group(after(branch_part, *first_near), slot_table, me)
    first_far = gather_expert_far(after_all(first_near, *branch_there))
    expert_weights = [build_expert(w_gate[0], w_down[0], first_near, first_far, me)]
    backs = [back_rows(row_tables[0], upstream_all, expert_weights[0][1])]
    for e in range(1, own_experts):
        near = gather_expert(*after_all((w_gate[e], w_up[e], w_down[e]), *branch_there), me)
        far = gather_expert_far(after_all(near, backs[e - 1][1]))
        expert_weights.append(build_expert(w_gate[e], w_down[e], near, far, me))
        backs.append(back_rows(row_tables[e], upstream_all, expert_weights[e][1]))

    inputs = tokens.astype(F32)
    middle = inputs + branch
    root_two = inverse_root(middle)
    normed_two = middle * root_two
    hidden_two = (normed_two * gain_ffn).astype(BF)
    hidden_all = lax.all_gather(hidden_two, "exp", axis=0, tiled=True)
    logits = jnp.dot(hidden_two, router_full, preferred_element_type=F32)
    router_prob = jax.nn.softmax(logits, axis=-1)

    every = range(own_experts)
    made = [
        expert_rows(
            row_tables[e],
            e,
            own_ids[:1],
            hidden_all,
            router_full,
            expert_weights[e][0],
            backs[e][1],
        )
        for e in every
    ]
    shares = [m[4].reshape(1, capacity) for m in made]
    grad_two_part, share_token = combine_rows(token_tables, [m[3] for m in made], shares)
    grad_two = lax.psum_scatter(grad_two_part, "exp", scatter_dimension=0, tiled=True)
    share_back = lax.all_to_all(
        share_token.reshape(exp_size, tok_rows, own_experts),
        "exp",
        split_axis=0,
        concat_axis=0,
        tiled=True,
    )
    grad_prob = jnp.swapaxes(share_back, 0, 1).reshape(tok_rows, experts)
    expert_grads = []
    for e in every:
        rows, hidden, grad_hidden = after_all(made[e][:3], grad_two_part)
        expert_grads.append(
            (
                lax.dot_general(rows, grad_hidden, TN, preferred_element_type=F32).astype(BF),
                lax.dot_general(hidden, backs[e][0], TN, preferred_element_type=F32).astype(BF),
            )
        )
    results = [
        jnp.dot(made[e][1], expert_weights[e][1], preferred_element_type=F32).astype(BF)
        for e in every
    ]
    grad_two = after(
        grad_two, *results, *(part for grads in expert_grads[1:] for part in grads)
    ).astype(F32)
    grad_logits = (
        router_prob * (grad_prob - jnp.sum(router_prob * grad_prob, axis=-1, keepdims=True))
    ).astype(BF)
    grad_router = jnp.einsum("td,te->ed", hidden_two, grad_logits, preferred_element_type=F32)
    grad_two = grad_two + jnp.einsum(
        "te,de->td", grad_logits, router_full, preferred_element_type=F32
    )
    grad_ffn_gain = jnp.sum(grad_two * normed_two, axis=0)
    grad_middle = cotangent.astype(F32) + norm_back(grad_two * gain_ffn, normed_two, root_two)

    sums = [scatter_expert_first(expert_grads[0], me)]
    more = [scatter_expert_second(expert_grads[0], after_all(sums[0], *results), me)]
    own_grad = after(grad_middle.astype(BF), *more[0])
    branch_grad, grad_there = gather_group(own_grad, slot_table, me)
    mixture_part, unused = combine_rows(token_tables, after_all(results, own_grad), shares)
    mixture = lax.psum_scatter(mixture_part, "exp", scatter_dimension=0, tiled=True).astype(F32)
    output = (middle + mixture).astype(BF)
    for e in range(1, own_experts):
        sums.append(scatter_expert_first(after_all(expert_grads[e], *grad_there), me))
    early_sums = sum_to_rows(jnp.concatenate([grad_router, grad_ffn_gain[None]]), me)
    branch_grad = after(branch_grad, mixture_part, early_sums)
    grad_context = lax.dot_general(branch_grad, out_full, NT, preferred_element_type=F32).astype(BF)
    out_grad = jnp.einsum("td,te->de", context_low, branch_grad, preferred_element_type=F32)
    grad_query_norm, grad_key_norm, grad_value = attend_back(
        query_rot, key_rot, value_low, grad_context, cos_part, sin_part, seg_ids
    )
    grad_query_gain = jnp.sum(grad_query_norm * normed_query, axis=0)
    grad_key_gain = jnp.sum(grad_key_norm * normed_key, axis=0)
    scaled_query = grad_query_norm * gain_query
    scaled_key = grad_key_norm * gain_key
    means = (
        sum_over_ctx(
            jnp.stack(
                [
                    jnp.sum(scaled_query * normed_query, axis=1),
                    jnp.sum(scaled_key * normed_key, axis=1),
                ]
            )
        )
        / D
    )
    grad_projected = jnp.concatenate(
        [
            root_query * (scaled_query - normed_query * means[0][:, None]),
            root_key * (scaled_key - normed_key * means[1][:, None]),
            grad_value,
        ],
        axis=1,
    ).astype(BF)
    grad_projected = after(grad_projected, *(piece for pieces in sums[1:] for piece in pieces))
    grad_packed = jnp.pad(grad_projected, ((0, 0), (0, 128)))
    grad_one_part = lax.dot_general(grad_packed, packed, NT, preferred_element_type=F32)
    grad_attn_gain = jnp.sum(grad_one_part * normed_group, axis=0)
    grad_one, one_sent, one_there = scatter_group(grad_one_part, slot_table, me)
    for e in range(1, own_experts):
        more.append(scatter_expert_second(expert_grads[e], after_all(sums[e], *one_there), me))
    weight_sums = [scatter_expert_end(expert_grads[e], sums[e], more[e], me) for e in every]
    gate_grad, up_grad, down_grad = (jnp.stack(parts) for parts in zip(*weight_sums))
    left, right = after_all((hidden_one, grad_projected), *one_sent)
    qkv_grad = lax.dot_general(left, right, TN, preferred_element_type=F32)
    out_sum = lax.psum_scatter(
        out_grad.astype(BF), "exp", scatter_dimension=0, tiled=True
    ).astype(F32)
    qkv_sum = lax.psum_scatter(
        qkv_grad.astype(BF).reshape(ctx_size, exp_size * part_rows, 3 * own_width),
        "exp",
        scatter_dimension=1,
        tiled=True,
    )
    qkv_own = exchange(qkv_sum, me).astype(F32)
    projection_grads = [
        jnp.swapaxes(qkv_own[:, :, i * own_width : (i + 1) * own_width], 0, 1).reshape(part_rows, D)
        for i in range(3)
    ]
    root_one = inverse_root(inputs)
    normed_one = inputs * root_one
    grad_input = grad_middle + norm_back(grad_one * gain_attn, normed_one, root_one)
    head_gains = lax.dynamic_update_slice(
        jnp.zeros((2, D), F32), jnp.stack([grad_query_gain, grad_key_gain]), (0, me * own_width)
    )
    late_sums = sum_to_rows(jnp.concatenate([grad_attn_gain[None], head_gains]), me)
    return (
        output,
        grad_input,
        projection_grads[0],
        projection_grads[1],
        projection_grads[2],
        out_sum,
        early_sums[:experts].T,
        late_sums[0],
        late_sums[1],
        late_sums[2],
        early_sums[experts],
        gate_grad,
        up_grad,
        down_grad,
    )


def solution(mesh):
    rows = P(BOTH, None)
    weights = P("exp", "ctx", None)
    in_specs = (
        (rows, rows, rows, P("exp", None), P("exp", None))
        + (rows,) * 5
        + (P(BOTH),) * 4
        + (weights,) * 3
    )
    out_specs = (rows,) * 7 + (P(BOTH),) * 4 + (weights,) * 3
    return jax.shard_map(local, mesh=mesh, in_specs=in_specs, out_specs=out_specs, check_vma=False)
```

```python
import functools
import math

import jax
import jax.numpy as jnp
from jax import lax
from jax.experimental import pallas as pl
from jax.experimental.pallas import tpu as pltpu
from jax.sharding import PartitionSpec as P

D = 2048
HEADS = 16
HD = 128
TOP = 8
PROMPT = 1024
CONT = 2
CTOK = 512

epsilon = 1e-05
rope_base = 10000.0
BF = jnp.bfloat16
F32 = jnp.float32
BOTH = ("ctx", "exp")
X_PAIRS = [(i, i ^ 1) for i in range(4)]
Y_PAIRS = [(i, i ^ 2) for i in range(4)]
XY_PAIRS = [(i, i ^ 3) for i in range(4)]
NT = (((1,), (1,)), ((), ()))
TN = (((0,), (0,)), ((), ()))
TILE = 256
WIN = 512
NOWHERE = -(1 << 20)


def inverse_root(values):
    return lax.rsqrt(jnp.mean(values * values, axis=-1, keepdims=True) + epsilon)


def norm_back(gradient, normed, root_part):
    return root_part * (gradient - normed * jnp.mean(gradient * normed, axis=-1, keepdims=True))


def angles(position):
    half_dim = HD // 2
    inverse = rope_base ** (-2.0 * jnp.arange(half_dim, dtype=F32) / HD)
    phases = position.astype(F32)[:, None] * inverse[None, :]
    cosine, sine = jnp.cos(phases), jnp.sin(phases)
    return jnp.concatenate([cosine, cosine], axis=1), jnp.concatenate([-sine, sine], axis=1)


def send_x(value):
    return lax.ppermute(value, "ctx", X_PAIRS)


def send_y(value):
    return lax.ppermute(value, "ctx", Y_PAIRS)


def send_xy(value):
    return lax.ppermute(value, "ctx", XY_PAIRS)


def after(value, *others):
    return lax.optimization_barrier((value,) + others)[0]


def after_all(values, *others):
    return lax.optimization_barrier(tuple(values) + others)[: len(values)]


def gather_pieces(value, half):
    from_x = send_x(value)
    from_y = send_y(value)
    far_low = send_y(from_x[:half])
    far_high = send_x(from_y[half:])
    return from_x, from_y, far_low, far_high


def scatter_payload(take, me):
    low = jnp.stack([take(me ^ 1, 0), take(me ^ 3, 0)]).astype(BF)
    high = jnp.stack([take(me ^ 2, 1), take(me ^ 3, 1)]).astype(BF)
    return low, high


def scatter_first(take, me):
    low, high = scatter_payload(take, me)
    return send_x(low), send_y(high)


def scatter_second(take, me, low, high):
    low_next = send_y((take(me ^ 2, 0).astype(F32) + low[1].astype(F32)).astype(BF))
    high_next = send_x((take(me ^ 1, 1).astype(F32) + high[1].astype(F32)).astype(BF))
    return low_next, high_next


def scatter_end(take, me, low, high, low_next, high_next):
    first = take(me, 0).astype(F32) + low[0].astype(F32) + low_next.astype(F32)
    second = take(me, 1).astype(F32) + high[0].astype(F32) + high_next.astype(F32)
    return first, second


def exchange(blocks, me):
    if lax.axis_size("ctx") != 4:
        return lax.all_to_all(blocks, "ctx", split_axis=0, concat_axis=0, tiled=True)
    sends = (lambda part: part, send_x, send_y, send_xy)
    parts = [
        send(lax.dynamic_index_in_dim(blocks, me ^ away, 0, keepdims=False))
        for away, send in enumerate(sends)
    ]

    def from_ctx(c):
        chosen = parts[0]
        for away in range(1, 4):
            chosen = jnp.where((me ^ c) == away, parts[away], chosen)
        return chosen

    return jnp.stack([from_ctx(c) for c in range(4)])


def sum_over_ctx(value):
    if lax.axis_size("ctx") != 4:
        return lax.psum(value, "ctx")
    value = value + send_x(value)
    return value + send_y(value)


def sum_to_rows(values, me):
    ctx_size, exp_size = lax.axis_size("ctx"), lax.axis_size("exp")
    count, width = values.shape
    parts = values.reshape(count, ctx_size, exp_size, width // (ctx_size * exp_size))
    parts = jnp.transpose(parts, (2, 1, 0, 3))
    parts = jnp.sum(lax.all_to_all(parts, "exp", split_axis=0, concat_axis=0, tiled=True), axis=0)
    return jnp.sum(exchange(parts, me), axis=0)


def gather_expert(w_gate, w_up, w_down, me):
    if lax.axis_size("ctx") != 4:
        return (
            lax.all_gather(jnp.stack([w_gate, w_up]), "ctx", axis=1, tiled=True),
            lax.all_gather(w_down, "ctx", axis=0, tiled=True),
        )
    width = w_gate.shape[1]
    half = (w_gate.shape[0] + w_up.shape[0] + 2 * w_down.shape[0]) // 2
    packed = jnp.concatenate([w_gate, w_up, w_down[:, :width], w_down[:, width:]], axis=0)
    low, high = packed[:half], packed[half:]
    return (low, high), (send_x(low), send_y(low)), None


def gather_expert_more(near, *others):
    if lax.axis_size("ctx") != 4:
        return near
    high = after(near[0][1], *others)
    return near[0], near[1], (send_x(high), send_y(high))


def gather_expert_far(near, *others):
    if lax.axis_size("ctx") != 4:
        return ()
    low, high = after_all((near[1][0], near[2][1]), *others)
    return send_y(low), send_x(high)


def build_expert(w_gate, w_down, near, far, me):
    if lax.axis_size("ctx") != 4:
        return near
    rows, width = w_gate.shape
    half = rows // 2
    both = jnp.zeros((2, 4 * rows, width), BF)
    down = jnp.zeros((2 * rows, 2 * width), BF)

    def put_both(whole, part, owner, which, first):
        return lax.dynamic_update_slice(whole, part[None], (which, owner * rows + first, 0))

    def put_down(whole, part, owner, which):
        return lax.dynamic_update_slice(whole, part, (owner * half, which * width))

    lows = (near[0][0],) + near[1] + (far[0],)
    highs = (near[0][1],) + near[2] + (far[1],)
    for away in range(4):
        low, high, owner = lows[away], highs[away], me ^ away
        both = put_both(both, low[:rows], owner, 0, 0)
        both = put_both(both, low[rows:], owner, 1, 0)
        both = put_both(both, high[:half], owner, 1, half)
        down = put_down(down, high[half:rows], owner, 0)
        down = put_down(down, high[rows:], owner, 1)
    return both, down


def expert_take(grads):
    gate_up, down = grads
    rows, width = gate_up.shape[0] // 4, gate_up.shape[1] // 2
    half = down.shape[0] // 8

    def take(owner, part):
        first = (2 * owner + part) * half
        return jnp.concatenate(
            [
                lax.dynamic_slice(gate_up, (owner * rows, part * width), (rows, width)),
                lax.dynamic_slice(down, (first, 0), (half, width)),
                lax.dynamic_slice(down, (first, width), (half, width)),
            ],
            axis=0,
        )

    return take


def scatter_expert_first(grads, me):
    if lax.axis_size("ctx") != 4:
        return tuple(
            lax.psum_scatter(grad, "ctx", scatter_dimension=0, tiled=True) for grad in grads
        )
    return scatter_first(expert_take(grads), me)


def scatter_expert_second(grads, sums, me):
    if lax.axis_size("ctx") != 4:
        return ()
    return scatter_second(expert_take(grads), me, *sums)


def scatter_expert_end(grads, sums, more, me):
    if lax.axis_size("ctx") != 4:
        gate_up, down = (part.astype(F32) for part in sums)
        width = gate_up.shape[1] // 2
        return gate_up[:, :width], gate_up[:, width:], down
    first, second = scatter_end(expert_take(grads), me, *sums, *more)
    rows, half = grads[0].shape[0] // 4, grads[1].shape[0] // 8
    down = [
        jnp.concatenate([part[rows : rows + half], part[rows + half :]], axis=1)
        for part in (first, second)
    ]
    return first[:rows], second[:rows], jnp.concatenate(down, axis=0)


def pick_blocks(blocks, order):
    return jnp.concatenate(
        [
            lax.dynamic_index_in_dim(blocks, order[i], 0, keepdims=False)
            for i in range(order.shape[0])
        ],
        axis=0,
    )


def gather_group(rows, slot_table, me):
    block = rows.shape[0] // 2
    if lax.axis_size("ctx") != 4:
        blocks = slot_table.shape[0]
        whole = lax.all_gather(rows, "ctx", axis=0, tiled=True).reshape(blocks, block, -1)
        match = slot_table[None, :] == jnp.arange(blocks, dtype=jnp.int32)[:, None]
        order = jnp.sum(jnp.where(match, jnp.arange(blocks, dtype=jnp.int32)[None, :], 0), axis=1)
        return pick_blocks(whole, order), ()
    from_x, from_y, far_low, far_high = gather_pieces(rows, block)
    parts = (
        (rows[:block], me, 0),
        (rows[block:], me, 1),
        (from_x[:block], me ^ 1, 0),
        (from_x[block:], me ^ 1, 1),
        (from_y[:block], me ^ 2, 0),
        (from_y[block:], me ^ 2, 1),
        (far_low, me ^ 3, 0),
        (far_high, me ^ 3, 1),
    )
    whole = jnp.zeros((8 * block, rows.shape[1]), rows.dtype)
    for part, owner, slot in parts:
        start = slot_table[2 * owner + slot] * block
        whole = lax.dynamic_update_slice(whole, part, (start, 0))
    return whole, (far_low, far_high)


def scatter_group(partial, slot_table, me):
    blocks = slot_table.shape[0]
    block = partial.shape[0] // blocks
    if lax.axis_size("ctx") != 4:
        ordered = pick_blocks(partial.reshape(blocks, block, -1), slot_table).astype(BF)
        whole = lax.psum_scatter(ordered, "ctx", scatter_dimension=0, tiled=True)
        return whole.astype(F32), (ordered,), (whole,), (whole,)

    def take(owner, part):
        start = slot_table[2 * owner + part] * block
        return lax.dynamic_slice(partial, (start, 0), (block, partial.shape[1]))

    sent = scatter_payload(take, me)
    near = send_x(sent[0]), send_y(sent[1])
    far = scatter_second(take, me, *near)
    return jnp.concatenate(scatter_end(take, me, *near, *far), axis=0), sent, near, far


def prefix_count(member):
    rows, columns = member.shape
    width = 128
    blocks = rows // width
    ones = member.astype(BF).reshape(blocks, width, columns)
    lower = (
        jnp.arange(width)[:, None] > jnp.arange(width)[None, :]
    ).astype(BF)
    inner = jnp.einsum("pq,bqc->bpc", lower, ones, preferred_element_type=F32)
    totals = jnp.sum(ones.astype(F32), axis=1)
    before = (jnp.arange(blocks)[:, None] > jnp.arange(blocks)[None, :]).astype(F32)
    outer = jnp.sum(before[:, :, None] * totals[None, :, :], axis=1)
    return (inner + outer[:, None, :]).reshape(rows, columns).astype(jnp.int32)


def dot(left, right, dims=(((1,), (0,)), ((), ()))):
    return lax.dot_general(left, right, dims, preferred_element_type=F32)


def turned(values, cosine, sine):
    return values * cosine + pltpu.roll(values, HD // 2, 1) * sine


def tile_weights(query, key, seg_q, seg_k, first, factor):
    rows, width = query.shape[0], key.shape[0]
    scores = dot(query, key, NT) * factor
    q_place = first + lax.broadcasted_iota(jnp.int32, (rows, width), 0)
    k_place = lax.broadcasted_iota(jnp.int32, (rows, width), 1)
    allowed = k_place <= q_place
    if first >= PROMPT:
        allowed = allowed & ((seg_k < 0) | (seg_k == seg_q))
    scores = jnp.where(allowed, scores, -1e30)
    weights = jnp.exp(scores - jnp.max(scores, axis=1, keepdims=True))
    return weights, jnp.sum(weights, axis=1, keepdims=True)


def attend_kernel(
    tiles,
    factor,
    qp_ref,
    kp_ref,
    vp_ref,
    root_ref,
    key_root_ref,
    gain_ref,
    cos_ref,
    sin_ref,
    sq_ref,
    sk_ref,
    q_ref,
    k_ref,
    v_ref,
    o_ref,
):
    at = pl.program_id(1)
    tile = qp_ref.shape[0]

    @pl.when(at == 0)
    def _():
        keys = kp_ref[...] * key_root_ref[:, 1:2] * gain_ref[1:2]
        k_ref[...] = turned(keys, cos_ref[...], sin_ref[...]).astype(BF)
        v_ref[...] = vp_ref[...].astype(BF)

    for i in range(tiles):

        @pl.when(at == i)
        def _():
            own = slice(i * tile, (i + 1) * tile)
            width = (i + 1) * tile
            queries = qp_ref[...] * root_ref[:, 0:1] * gain_ref[0:1]
            query = turned(queries, cos_ref[own], sin_ref[own]).astype(BF)
            q_ref[...] = query
            weights, total = tile_weights(
                query, k_ref[:width], sq_ref[...], sk_ref[:, :width], i * tile, factor
            )
            o_ref[...] = (dot(weights.astype(BF), v_ref[:width]) / total).astype(BF)


def attend(projected, roots, gains, cosine, sine, seg, width, tile=512):
    rows = projected.shape[0]
    heads, tiles = width // HD, rows // tile
    own = pl.BlockSpec((tile, HD), lambda h, i: (i, h))
    whole = pl.BlockSpec((rows, HD), lambda h, i: (0, h))
    pairs = heads * rows * rows * (tiles + 1) // (2 * tiles)
    return pl.pallas_call(
        functools.partial(attend_kernel, tiles, 1.0 / math.sqrt(HD)),
        out_shape=[jax.ShapeDtypeStruct((rows, width), BF)] * 4,
        grid=(heads, tiles),
        in_specs=[
            own,
            pl.BlockSpec((rows, HD), lambda h, i: (0, heads + h)),
            pl.BlockSpec((rows, HD), lambda h, i: (0, 2 * heads + h)),
            pl.BlockSpec((tile, 2), lambda h, i: (i, 0)),
            pl.BlockSpec((rows, 2), lambda h, i: (0, 0)),
            pl.BlockSpec((2, HD), lambda h, i: (0, h)),
            pl.BlockSpec((rows, HD), lambda h, i: (0, 0)),
            pl.BlockSpec((rows, HD), lambda h, i: (0, 0)),
            pl.BlockSpec((tile, 1), lambda h, i: (i, 0)),
            pl.BlockSpec((1, rows), lambda h, i: (0, 0)),
        ],
        out_specs=[own, whole, whole, own],
        compiler_params=pltpu.CompilerParams(vmem_limit_bytes=48 << 20),
        cost_estimate=pl.CostEstimate(
            flops=4 * pairs * HD, bytes_accessed=20 * rows * width, transcendentals=pairs
        ),
    )(
        projected,
        projected,
        projected,
        roots,
        roots,
        gains,
        cosine,
        sine,
        seg[:, None],
        seg[None, :],
    )


def attend_back_kernel(
    tiles,
    factor,
    q_ref,
    k_ref,
    v_ref,
    d_ref,
    cos_ref,
    sin_ref,
    sq_ref,
    sk_ref,
    dq_ref,
    dk_ref,
    dv_ref,
):
    at = pl.program_id(1)
    tile = q_ref.shape[0]

    @pl.when(at == 0)
    def _():
        dk_ref[...] = jnp.zeros_like(dk_ref)
        dv_ref[...] = jnp.zeros_like(dv_ref)

    for i in range(tiles):

        @pl.when(at == i)
        def _():
            own = slice(i * tile, (i + 1) * tile)
            width = (i + 1) * tile
            query, grad = q_ref[...], d_ref[...]
            weights, total = tile_weights(
                query, k_ref[:width], sq_ref[...], sk_ref[:, :width], i * tile, factor
            )
            weights = weights / total
            grad_weights = dot(grad, v_ref[:width], NT)
            delta = jnp.sum(weights * grad_weights, axis=1, keepdims=True)
            grad_scores = (weights * (grad_weights - delta)).astype(BF)
            grad_query = dot(grad_scores, k_ref[:width]) * factor
            dq_ref[...] = turned(grad_query, cos_ref[own], -sin_ref[own])
            dk_ref[:width] += dot(grad_scores, query, TN)
            dv_ref[:width] += dot(weights.astype(BF), grad, TN)

    @pl.when(at == tiles - 1)
    def _():
        dk_ref[...] = turned(dk_ref[...] * factor, cos_ref[...], -sin_ref[...])


def attend_back(q, k, v, grad, cosine, sine, seg, tile=512):
    rows, width = q.shape
    heads, tiles = width // HD, rows // tile
    own = pl.BlockSpec((tile, HD), lambda h, i: (i, h))
    whole = pl.BlockSpec((rows, HD), lambda h, i: (0, h))
    table = pl.BlockSpec((rows, HD), lambda h, i: (0, 0))
    pairs = heads * rows * rows * (tiles + 1) // (2 * tiles)
    return pl.pallas_call(
        functools.partial(attend_back_kernel, tiles, 1.0 / math.sqrt(HD)),
        out_shape=[jax.ShapeDtypeStruct((rows, width), F32)] * 3,
        grid=(heads, tiles),
        in_specs=[
            own,
            whole,
            whole,
            own,
            table,
            table,
            pl.BlockSpec((tile, 1), lambda h, i: (i, 0)),
            pl.BlockSpec((1, rows), lambda h, i: (0, 0)),
        ],
        out_specs=[own, whole, whole],
        compiler_params=pltpu.CompilerParams(vmem_limit_bytes=48 << 20),
        cost_estimate=pl.CostEstimate(
            flops=10 * pairs * HD, bytes_accessed=20 * rows * width, transcendentals=pairs
        ),
    )(q, k, v, grad, cosine, sine, seg[:, None], seg[None, :])


def pick_rows(tok, low, windows, source_ref, acc_ref):
    last = source_ref.shape[0] - WIN
    span = lax.broadcasted_iota(jnp.int32, (TILE, WIN), 1)

    def window(j):
        base = low + j * WIN
        start = pl.multiple_of(jnp.minimum(base, last), 128)
        match = (tok - start == span) & (tok >= base)
        return dot(match.astype(F32).astype(BF), source_ref[pl.ds(start, WIN), :])

    acc_ref[...] = window(0)

    @pl.loop(1, windows)
    def _(j):
        acc_ref[...] += window(j)

    return acc_ref[...].astype(BF)


def back_rows_kernel(
    tiles_ref, low_ref, windows_ref, tok_ref, dy_ref, wd_ref, rows_ref, raw_ref, acc_ref
):
    i = pl.program_id(0)

    @pl.when(i < tiles_ref[0])
    def _():
        rows = pick_rows(tok_ref[...], low_ref[i], windows_ref[i], dy_ref, acc_ref)
        rows_ref[...] = rows
        raw_ref[...] = dot(rows, wd_ref[...], NT)

    @pl.when(i >= tiles_ref[0])
    def _():
        rows_ref[...] = jnp.zeros_like(rows_ref)
        raw_ref[...] = jnp.zeros_like(raw_ref)


def back_rows(tables, upstream, w_down):
    total, width = upstream.shape
    ff = w_down.shape[0]
    capacity = tables[3].shape[0]
    tile = lambda n: pl.BlockSpec((TILE, n), lambda i, *_: (i, 0))
    once = lambda shape: pl.BlockSpec(shape, lambda i, *_: (0, 0), pipeline_mode=pl.Buffered(1))
    return pl.pallas_call(
        back_rows_kernel,
        out_shape=[
            jax.ShapeDtypeStruct((capacity, width), BF),
            jax.ShapeDtypeStruct((capacity, ff), F32),
        ],
        grid_spec=pltpu.PrefetchScalarGridSpec(
            num_scalar_prefetch=3,
            grid=(capacity // TILE,),
            in_specs=[tile(1), once((total, width)), once((ff, width))],
            out_specs=[tile(width), tile(ff)],
            scratch_shapes=[pltpu.VMEM((TILE, width), F32)],
        ),
        compiler_params=pltpu.CompilerParams(vmem_limit_bytes=48 << 20),
        cost_estimate=pl.CostEstimate(
            flops=total * (width * ff + WIN * width),
            bytes_accessed=2 * total * width + 2 * ff * width + capacity * (2 * width + 4 * ff),
            transcendentals=0,
        ),
    )(*tables, upstream, w_down)


def expert_kernel(
    own,
    tiles_ref,
    low_ref,
    windows_ref,
    id_ref,
    tok_ref,
    h_ref,
    router_ref,
    wg_ref,
    wu_ref,
    raw_ref,
    rows_ref,
    hid_ref,
    dab_ref,
    dh_ref,
    share_ref,
    acc_ref,
):
    i = pl.program_id(0)
    ff = wg_ref.shape[1]

    @pl.when(i < tiles_ref[0])
    def _():
        rows = pick_rows(tok_ref[...], low_ref[i], windows_ref[i], h_ref, acc_ref)
        rows_ref[...] = rows
        logits = dot(rows, router_ref[...])
        probs = jnp.exp(logits - jnp.max(logits, axis=1, keepdims=True))
        column = lax.broadcasted_iota(jnp.int32, probs.shape, 1)
        mine = jnp.sum(jnp.where(column == id_ref[0] + own, probs, 0.0), axis=1, keepdims=True)
        gate = mine / jnp.sum(probs, axis=1, keepdims=True)
        share = 0.0
        part = ff // 4
        for c in range(4):
            cols = slice(c * part, (c + 1) * part)
            a = dot(rows, wg_ref[:, cols])
            b = dot(rows, wu_ref[:, cols])
            raw = raw_ref[:, cols]
            sig = 1.0 / (1.0 + jnp.exp(-a))
            silu = a * sig
            hid = silu * b
            share += jnp.sum(hid * raw, axis=1, keepdims=True)
            raw = raw * gate
            hid_ref[:, cols] = (hid * gate).astype(BF)
            dab_ref[:, cols] = (raw * b * (sig * (1.0 + a * (1.0 - sig)))).astype(BF)
            dab_ref[:, ff + c * part : ff + (c + 1) * part] = (raw * silu).astype(BF)
        share_ref[...] = share
        dh = dot(dab_ref[:, :ff], wg_ref[...], NT) + dot(dab_ref[:, ff:], wu_ref[...], NT)
        dh_ref[...] = dh.astype(BF)

    @pl.when(i >= tiles_ref[0])
    def _():
        for ref in (rows_ref, hid_ref, dab_ref, dh_ref, share_ref):
            ref[...] = jnp.zeros_like(ref)


def expert_rows(tables, own, first_id, hidden, router, gate_up, raw):
    total, width = hidden.shape
    ff = gate_up.shape[2]
    capacity = tables[3].shape[0]
    tile = lambda n: pl.BlockSpec((TILE, n), lambda i, *_: (i, 0))
    once = lambda shape: pl.BlockSpec(shape, lambda i, *_: (0, 0), pipeline_mode=pl.Buffered(1))
    half = lambda k: pl.BlockSpec(
        (None, width, ff), lambda i, *_: (k, 0, 0), pipeline_mode=pl.Buffered(1)
    )
    made = lambda n, dtype=BF: jax.ShapeDtypeStruct((capacity, n), dtype)
    return pl.pallas_call(
        functools.partial(expert_kernel, own),
        out_shape=[made(width), made(ff), made(2 * ff), made(width), made(1, F32)],
        grid_spec=pltpu.PrefetchScalarGridSpec(
            num_scalar_prefetch=4,
            grid=(capacity // TILE,),
            in_specs=[
                tile(1),
                once((total, width)),
                once(router.shape),
                half(0),
                half(1),
                tile(ff),
            ],
            out_specs=[tile(width), tile(ff), tile(2 * ff), tile(width), tile(1)],
            scratch_shapes=[pltpu.VMEM((TILE, width), F32)],
        ),
        compiler_params=pltpu.CompilerParams(vmem_limit_bytes=56 << 20),
        cost_estimate=pl.CostEstimate(
            flops=total * (4 * width * ff + WIN * width),
            bytes_accessed=2 * total * width + 4 * ff * width + capacity * (4 * width + 10 * ff),
            transcendentals=total * ff,
        ),
    )(*tables[:3], first_id, tables[3], hidden, router, gate_up, gate_up, raw)


def combine_kernel(experts, start_ref, more_ref, wide_ref, pos_ref, *refs):
    rows_refs, share_refs = refs[:experts], refs[experts : 2 * experts]
    out_ref, own_ref, acc_ref = refs[2 * experts :]
    i = pl.program_id(0)
    span = lax.broadcasted_iota(jnp.int32, (TILE, TILE), 1)
    wide_span = lax.broadcasted_iota(jnp.int32, (TILE, 384), 1)
    last = rows_refs[0].shape[0] - TILE

    def window(e, j):
        base = start_ref[e, i] + j * TILE
        start = pl.multiple_of(jnp.minimum(base, last), 16)
        pos = pos_ref[:, e : e + 1]
        match = (pos - start == span) & (pos >= base)
        return dot(match.astype(F32).astype(BF), rows_refs[e][pl.ds(start, TILE), :])

    acc_ref[...] = sum(window(e, 0) for e in range(experts))
    for e in range(experts):
        wide = pl.multiple_of(wide_ref[e, i], 128)
        match = pos_ref[:, e : e + 1] - wide == wide_span
        share = share_refs[e][:, pl.ds(wide, 384)]
        own_ref[:, e : e + 1] = jnp.sum(jnp.where(match, share, 0.0), axis=1, keepdims=True)

        @pl.when(more_ref[e, i] > 0)
        def _():
            acc_ref[...] += window(e, 1)

    out_ref[...] = acc_ref[...].astype(BF)


def combine_rows(tables, rows, shares):
    experts, (capacity, width) = len(rows), rows[0].shape
    total = tables[3].shape[0]
    once = lambda shape: pl.BlockSpec(shape, lambda i, *_: (0, 0), pipeline_mode=pl.Buffered(1))
    tile = lambda n: pl.BlockSpec((TILE, n), lambda i, *_: (i, 0))
    return pl.pallas_call(
        functools.partial(combine_kernel, experts),
        out_shape=[
            jax.ShapeDtypeStruct((total, width), BF),
            jax.ShapeDtypeStruct((total, experts), F32),
        ],
        grid_spec=pltpu.PrefetchScalarGridSpec(
            num_scalar_prefetch=3,
            grid=(total // TILE,),
            in_specs=[tile(experts)]
            + [once((capacity, width))] * experts
            + [once((1, capacity))] * experts,
            out_specs=[tile(width), tile(experts)],
            scratch_shapes=[pltpu.VMEM((TILE, width), F32)],
        ),
        compiler_params=pltpu.CompilerParams(vmem_limit_bytes=48 << 20),
        cost_estimate=pl.CostEstimate(
            flops=2 * experts * total * TILE * width,
            bytes_accessed=2 * (experts * capacity + total) * width,
            transcendentals=0,
        ),
    )(*tables, *rows, *shares)


def local(
    tokens,
    cotangent,
    routes,
    block_of_slot,
    cont_seg,
    w_query,
    w_key,
    w_value,
    w_out,
    w_router,
    attn_gain,
    query_gain,
    key_gain,
    ffn_gain,
    w_gate,
    w_up,
    w_down,
):
    ctx_size = lax.axis_size("ctx")
    exp_size = lax.axis_size("exp")
    me = lax.axis_index("ctx")
    exp_index = lax.axis_index("exp")
    tok_rows = tokens.shape[0]
    part_rows = w_query.shape[0]
    own_width = D // ctx_size
    own_heads = HEADS // ctx_size
    experts = w_router.shape[1]
    own_experts = w_gate.shape[0]
    slot_table = block_of_slot[0]
    seg_row = cont_seg[0]
    group_rows = ctx_size * tok_rows
    factor = 1.0 / math.sqrt(HD)

    tokens_group, tokens_there = gather_group(tokens, slot_table, me)
    small = jnp.concatenate(
        [w_router] + [g[:, None] for g in (attn_gain, query_gain, key_gain, ffn_gain)], axis=1
    )
    small = jnp.pad(small, ((0, 0), (0, 128 - small.shape[1])))
    by_owner = jnp.stack(
        [w.reshape(part_rows, ctx_size, own_width) for w in (w_query, w_key, w_value)], axis=2
    )
    by_owner = jnp.swapaxes(by_owner, 0, 1).reshape(ctx_size, part_rows, 3 * own_width)
    by_owner = jnp.concatenate(
        [by_owner, jnp.broadcast_to(small, (ctx_size,) + small.shape)], axis=2
    )
    own_columns = exchange(by_owner, me)
    packed = lax.all_gather(own_columns, "exp", axis=1, tiled=True).reshape(D, 3 * own_width + 128)
    small_full = packed[:, 3 * own_width :]
    router_full = small_full[:, :experts]
    gains = small_full[:, experts : experts + 4].astype(F32)
    gain_attn, gain_ffn = gains[:, 0], gains[:, 3]
    own_gains = lax.dynamic_slice(gains, (me * own_width, 0), (own_width, 4))
    gain_query, gain_key = own_gains[:, 1], own_gains[:, 2]
    out_full = lax.all_gather(w_out, "exp", axis=0, tiled=True)
    routes_all = lax.all_to_all(
        jnp.broadcast_to(routes[None], (exp_size,) + routes.shape),
        "exp",
        split_axis=0,
        concat_axis=0,
        tiled=True,
    ).reshape(exp_size * tok_rows, TOP)
    upstream_all = lax.all_gather(cotangent, "exp", axis=0, tiled=True)
    first_near = gather_expert(*after_all((w_gate[0], w_up[0], w_down[0]), *tokens_there), me)

    own_ids = exp_index * own_experts + jnp.arange(own_experts, dtype=jnp.int32)
    member = jnp.any(routes_all[:, :, None] == own_ids[None, None, :], axis=1)
    place_of = prefix_count(member)
    capacity = exp_size * 8 * ((5 * tok_rows * TOP // (4 * experts) + 7) // 8)
    row_tiles = (capacity + TILE - 1) // TILE
    capacity = row_tiles * TILE
    all_rows = exp_size * tok_rows
    row_ids = jnp.arange(capacity, dtype=jnp.int32)
    hit = (place_of.T[:, None, :] == row_ids[None, :, None]) & member.T[:, None, :]
    token_ids = jnp.arange(all_rows, dtype=jnp.int32)
    token_of_row = jnp.max(jnp.where(hit, token_ids[None, None, :], -1), axis=2)
    counts = jnp.sum(member.astype(jnp.int32), axis=0)
    used_tiles = (counts + TILE - 1) // TILE
    by_tile = token_of_row.reshape(own_experts * row_tiles, TILE)
    low_token = jnp.maximum(by_tile[:, 0], 0) // 128 * 128
    windows = jnp.maximum((jnp.max(by_tile, axis=1) - low_token) // WIN + 1, 1)
    low_token = low_token.reshape(own_experts, row_tiles)
    windows = windows.reshape(own_experts, row_tiles)
    row_tables = [
        (used_tiles[e : e + 1], low_token[e], windows[e], token_of_row[e][:, None])
        for e in range(own_experts)
    ]
    place_column = jnp.where(member, place_of, NOWHERE)
    first_place = place_of[::TILE].T
    in_tile = jnp.sum(member.reshape(-1, TILE, own_experts).astype(jnp.int32), axis=1).T
    first_row = first_place // 16 * 16
    more_rows = (first_place + in_tile - first_row > TILE).astype(jnp.int32)
    share_row_start = jnp.minimum(first_place // 128 * 128, capacity - 384)
    token_tables = (first_row, more_rows, share_row_start, place_column)

    seg_ids = jnp.concatenate([jnp.full((PROMPT,), -1, jnp.int32), seg_row])
    starts = jnp.sum(
        (seg_row[None, :] < jnp.arange(CONT, dtype=jnp.int32)[:, None]).astype(jnp.int32), axis=1
    )
    first_pos = jnp.sum(
        jnp.where(
            seg_row[:, None] == jnp.arange(CONT, dtype=jnp.int32)[None, :], starts[None, :], 0
        ),
        axis=1,
    )
    cont_pos = PROMPT + jnp.arange(CTOK, dtype=jnp.int32) - first_pos
    position = jnp.concatenate([jnp.arange(PROMPT, dtype=jnp.int32), cont_pos])
    cos_part, sin_part = angles(position)
    group_inputs = after(
        tokens_group, token_of_row, place_column, first_row, more_rows, share_row_start, used_tiles, windows
    ).astype(F32)
    normed_group = group_inputs * inverse_root(group_inputs)
    hidden_one = (normed_group * gain_attn).astype(BF)
    projected = jnp.dot(hidden_one, packed, preferred_element_type=F32)
    query_pre = projected[:, :own_width]
    key_pre = projected[:, own_width : 2 * own_width]
    squares = jnp.stack([jnp.sum(query_pre * query_pre, axis=1), jnp.sum(key_pre * key_pre, axis=1)])
    if ctx_size == 4:
        squares = after(squares, *first_near[1])
    squares = sum_over_ctx(squares)
    first_near = gather_expert_more(first_near, squares)
    roots = lax.rsqrt(squares / D + epsilon)
    root_query, root_key = roots[0][:, None], roots[1][:, None]
    normed_query = query_pre * root_query
    normed_key = key_pre * root_key
    query_rot, key_rot, value_low, context_low = attend(
        projected,
        roots.T,
        jnp.stack([gain_query, gain_key]),
        cos_part,
        sin_part,
        seg_ids,
        own_width,
    )
    branch_part = jnp.dot(context_low, out_full, preferred_element_type=F32)
    if ctx_size == 4:
        branch_part = after(branch_part, *first_near[1], *first_near[2])
    branch, unused, unused, branch_there = scatter_group(branch_part, slot_table, me)
    far = gather_expert_far(first_near, *branch_there)
    expert_weights = [build_expert(w_gate[0], w_down[0], first_near, far, me)]
    backs = [back_rows(row_tables[0], upstream_all, expert_weights[0][1])]
    for e in range(1, own_experts):
        gates = far if ctx_size == 4 else branch_there
        near = gather_expert(*after_all((w_gate[e], w_up[e], w_down[e]), *gates), me)
        near = gather_expert_more(near)
        far = gather_expert_far(near, backs[0][1])
        expert_weights.append(build_expert(w_gate[e], w_down[e], near, far, me))

    inputs = tokens.astype(F32)
    middle = inputs + branch
    root_two = inverse_root(middle)
    normed_two = middle * root_two
    hidden_two = (normed_two * gain_ffn).astype(BF)
    hidden_all = lax.all_gather(hidden_two, "exp", axis=0, tiled=True)
    logits = jnp.dot(hidden_two, router_full, preferred_element_type=F32)
    router_prob = jax.nn.softmax(logits, axis=-1)

    every = range(own_experts)
    made = []
    for e in every:
        if e > 0:
            upstream = after(upstream_all, made[-1][3])
            backs.append(back_rows(row_tables[e], upstream, expert_weights[e][1]))
        made.append(
            expert_rows(
                row_tables[e],
                e,
                own_ids[:1],
                hidden_all,
                router_full,
                expert_weights[e][0],
                backs[e][1],
            )
        )
    shares = [m[4].reshape(1, capacity) for m in made]
    grad_two_part, share_token = combine_rows(token_tables, [m[3] for m in made], shares)
    grad_two = lax.psum_scatter(grad_two_part, "exp", scatter_dimension=0, tiled=True)
    share_back = lax.all_to_all(
        share_token.reshape(exp_size, tok_rows, own_experts),
        "exp",
        split_axis=0,
        concat_axis=0,
        tiled=True,
    )
    grad_prob = jnp.swapaxes(share_back, 0, 1).reshape(tok_rows, experts)
    expert_grads = []
    results, mixture_part = [], grad_two_part
    for e in every:
        rows, hidden, grad_hidden = after_all(made[e][:3], mixture_part)
        expert_grads.append(
            (
                lax.dot_general(rows, grad_hidden, TN, preferred_element_type=F32).astype(BF),
                lax.dot_general(hidden, backs[e][0], TN, preferred_element_type=F32).astype(BF),
            )
        )
        if e == 0:
            results = [
                jnp.dot(
                    after(made[k][1], *expert_grads[0]),
                    expert_weights[k][1],
                    preferred_element_type=F32,
                ).astype(BF)
                for k in every
            ]
            mixture_part, unused = combine_rows(token_tables, results, shares)
    mixture = lax.psum_scatter(mixture_part, "exp", scatter_dimension=0, tiled=True)
    output = (middle + mixture.astype(F32)).astype(BF)

    grad_two = after(
        grad_two, mixture_part, *(part for grads in expert_grads[1:] for part in grads)
    ).astype(F32)
    grad_logits = (
        router_prob * (grad_prob - jnp.sum(router_prob * grad_prob, axis=-1, keepdims=True))
    ).astype(BF)
    grad_router = jnp.einsum("td,te->ed", hidden_two, grad_logits, preferred_element_type=F32)
    grad_two = grad_two + jnp.einsum(
        "te,de->td", grad_logits, router_full, preferred_element_type=F32
    )
    grad_ffn_gain = jnp.sum(grad_two * normed_two, axis=0)
    grad_middle = cotangent.astype(F32) + norm_back(grad_two * gain_ffn, normed_two, root_two)

    sums = [scatter_expert_first(expert_grads[0], me)]
    more = [scatter_expert_second(expert_grads[0], after_all(sums[0], mixture_part), me)]
    own_grad = after(grad_middle.astype(BF), *more[0])
    branch_grad, grad_there = gather_group(own_grad, slot_table, me)
    for e in range(1, own_experts):
        sums.append(scatter_expert_first(after_all(expert_grads[e], *grad_there), me))
    early_sums = sum_to_rows(jnp.concatenate([grad_router, grad_ffn_gain[None]]), me)
    branch_grad = after(branch_grad, early_sums)
    grad_context = lax.dot_general(branch_grad, out_full, NT, preferred_element_type=F32).astype(BF)
    out_grad = jnp.einsum("td,te->de", context_low, branch_grad, preferred_element_type=F32)
    grad_query_norm, grad_key_norm, grad_value = attend_back(
        query_rot, key_rot, value_low, grad_context, cos_part, sin_part, seg_ids
    )
    grad_query_gain = jnp.sum(grad_query_norm * normed_query, axis=0)
    grad_key_gain = jnp.sum(grad_key_norm * normed_key, axis=0)
    scaled_query = grad_query_norm * gain_query
    scaled_key = grad_key_norm * gain_key
    products = jnp.stack(
        [jnp.sum(scaled_query * normed_query, axis=1), jnp.sum(scaled_key * normed_key, axis=1)]
    )
    products = after(products, *(piece for pieces in sums[1:] for piece in pieces))
    means = sum_over_ctx(products) / D
    for e in range(1, own_experts):
        more.append(scatter_expert_second(expert_grads[e], after_all(sums[e], means), me))
    grad_projected = jnp.concatenate(
        [
            root_query * (scaled_query - normed_query * means[0][:, None]),
            root_key * (scaled_key - normed_key * means[1][:, None]),
            grad_value,
        ],
        axis=1,
    ).astype(BF)
    grad_packed = jnp.pad(grad_projected, ((0, 0), (0, 128)))
    grad_one_part = lax.dot_general(grad_packed, packed, NT, preferred_element_type=F32)
    grad_attn_gain = jnp.sum(grad_one_part * normed_group, axis=0)
    grad_one, one_sent, one_near, unused = scatter_group(
        after(grad_one_part, *(piece for pieces in more[1:] for piece in pieces)), slot_table, me
    )
    weight_sums = [scatter_expert_end(expert_grads[e], sums[e], more[e], me) for e in every]
    gate_grad, up_grad, down_grad = (jnp.stack(parts) for parts in zip(*weight_sums))
    left, right = after_all((hidden_one, grad_projected), *one_sent)
    qkv_grad = lax.dot_general(left, right, TN, preferred_element_type=F32)
    out_sum = lax.psum_scatter(
        after(out_grad.astype(BF), mixture), "exp", scatter_dimension=0, tiled=True
    ).astype(F32)
    qkv_sum = lax.psum_scatter(
        qkv_grad.astype(BF).reshape(ctx_size, exp_size * part_rows, 3 * own_width),
        "exp",
        scatter_dimension=1,
        tiled=True,
    )
    qkv_own = exchange(qkv_sum, me).astype(F32)
    projection_grads = [
        jnp.swapaxes(qkv_own[:, :, i * own_width : (i + 1) * own_width], 0, 1).reshape(part_rows, D)
        for i in range(3)
    ]
    root_one = inverse_root(inputs)
    normed_one = inputs * root_one
    grad_input = grad_middle + norm_back(grad_one * gain_attn, normed_one, root_one)
    head_gains = lax.dynamic_update_slice(
        jnp.zeros((2, D), F32), jnp.stack([grad_query_gain, grad_key_gain]), (0, me * own_width)
    )
    late_sums = sum_to_rows(
        after(jnp.concatenate([grad_attn_gain[None], head_gains]), *one_near), me
    )
    return (
        output,
        grad_input,
        projection_grads[0],
        projection_grads[1],
        projection_grads[2],
        out_sum,
        early_sums[:experts].T,
        late_sums[0],
        late_sums[1],
        late_sums[2],
        early_sums[experts],
        gate_grad,
        up_grad,
        down_grad,
    )


def solution(mesh):
    rows = P(BOTH, None)
    weights = P("exp", "ctx", None)
    in_specs = (
        (rows, rows, rows, P("exp", None), P("exp", None))
        + (rows,) * 5
        + (P(BOTH),) * 4
        + (weights,) * 3
    )
    out_specs = (rows,) * 7 + (P(BOTH),) * 4 + (weights,) * 3
    return jax.shard_map(local, mesh=mesh, in_specs=in_specs, out_specs=out_specs, check_vma=False)
```

```python
import functools
import math

import jax
import jax.numpy as jnp
from jax import lax
from jax.experimental import pallas as pl
from jax.experimental.pallas import tpu as pltpu
from jax.sharding import PartitionSpec as P

D = 2048
HEADS = 16
HD = 128
TOP = 8
PROMPT = 1024
CONT = 2
CTOK = 512

epsilon = 1e-05
rope_base = 10000.0
BF = jnp.bfloat16
F32 = jnp.float32
BOTH = ("ctx", "exp")
X_PAIRS = [(i, i ^ 1) for i in range(4)]
Y_PAIRS = [(i, i ^ 2) for i in range(4)]
XY_PAIRS = [(i, i ^ 3) for i in range(4)]
NT = (((1,), (1,)), ((), ()))
TN = (((0,), (0,)), ((), ()))
TILE = 256
WIN = 512
NOWHERE = -(1 << 20)


def inverse_root(values):
    return lax.rsqrt(jnp.mean(values * values, axis=-1, keepdims=True) + epsilon)


def norm_back(gradient, normed, root_part):
    return root_part * (gradient - normed * jnp.mean(gradient * normed, axis=-1, keepdims=True))


def angles(position):
    half_dim = HD // 2
    inverse = rope_base ** (-2.0 * jnp.arange(half_dim, dtype=F32) / HD)
    phases = position.astype(F32)[:, None] * inverse[None, :]
    cosine, sine = jnp.cos(phases), jnp.sin(phases)
    return jnp.concatenate([cosine, cosine], axis=1), jnp.concatenate([-sine, sine], axis=1)


def send_x(value):
    return lax.ppermute(value, "ctx", X_PAIRS)


def send_y(value):
    return lax.ppermute(value, "ctx", Y_PAIRS)


def send_xy(value):
    return lax.ppermute(value, "ctx", XY_PAIRS)


def after(value, *others):
    return lax.optimization_barrier((value,) + others)[0]


def after_all(values, *others):
    return lax.optimization_barrier(tuple(values) + others)[: len(values)]


def gather_pieces(low, high):
    low_x, high_y = send_x(low), send_y(high)
    high_x, low_y = send_x(high), send_y(low)
    return (low_x, low_y, send_y(low_x)), (high_x, high_y, send_x(high_y))


def scatter_ahead(take, me):
    return send_x(take(me ^ 3, 0).astype(BF)), send_y(take(me ^ 3, 1).astype(BF))


def scatter_direct(take, me, *others):
    low, high = take(me ^ 1, 0).astype(BF), take(me ^ 2, 1).astype(BF)
    if others:
        low, high = after_all((low, high), *others)
    return send_x(low), send_y(high)


def scatter_last(take, me, ahead):
    low = (take(me ^ 2, 0).astype(F32) + ahead[0].astype(F32)).astype(BF)
    high = (take(me ^ 1, 1).astype(F32) + ahead[1].astype(F32)).astype(BF)
    return send_y(low), send_x(high)


def scatter_end(take, me, direct, last):
    return [
        take(me, part).astype(F32) + direct[part].astype(F32) + last[part].astype(F32)
        for part in range(2)
    ]


def exchange(blocks, me):
    if lax.axis_size("ctx") != 4:
        return lax.all_to_all(blocks, "ctx", split_axis=0, concat_axis=0, tiled=True)
    sends = (lambda part: part, send_x, send_y, send_xy)
    parts = [
        send(lax.dynamic_index_in_dim(blocks, me ^ away, 0, keepdims=False))
        for away, send in enumerate(sends)
    ]

    def from_ctx(c):
        chosen = parts[0]
        for away in range(1, 4):
            chosen = jnp.where((me ^ c) == away, parts[away], chosen)
        return chosen

    return jnp.stack([from_ctx(c) for c in range(4)])


def sum_over_ctx(value):
    if lax.axis_size("ctx") != 4:
        return lax.psum(value, "ctx")
    value = value + send_x(value)
    return value + send_y(value)


def sum_to_rows(values, me):
    ctx_size, exp_size = lax.axis_size("ctx"), lax.axis_size("exp")
    count, width = values.shape
    parts = values.reshape(count, ctx_size, exp_size, width // (ctx_size * exp_size))
    parts = jnp.transpose(parts, (2, 1, 0, 3))
    parts = jnp.sum(lax.all_to_all(parts, "exp", split_axis=0, concat_axis=0, tiled=True), axis=0)
    return jnp.sum(exchange(parts, me), axis=0)


def pack_expert(w_gate, w_up, w_down):
    half, width = w_up.shape[0] // 2, w_up.shape[1]
    low = jnp.concatenate([w_gate, w_up[:half]], axis=0)
    high = jnp.concatenate([w_up[half:], w_down[:, :width], w_down[:, width:]], axis=0)
    return low, high


def whole_expert(w_gate, w_up, w_down):
    return (
        lax.all_gather(jnp.stack([w_gate, w_up]), "ctx", axis=1, tiled=True),
        lax.all_gather(w_down, "ctx", axis=0, tiled=True),
    )


def expert_take(grads):
    gate_up, down = grads
    rows, width = gate_up.shape[0] // 4, gate_up.shape[1] // 2
    half = down.shape[0] // 8

    def take(owner, part):
        first = (2 * owner + part) * half
        return jnp.concatenate(
            [
                lax.dynamic_slice(gate_up, (owner * rows, part * width), (rows, width)),
                lax.dynamic_slice(down, (first, 0), (half, width)),
                lax.dynamic_slice(down, (first, width), (half, width)),
            ],
            axis=0,
        )

    return take


def scatter_expert_first(grads, me):
    if lax.axis_size("ctx") != 4:
        return tuple(
            lax.psum_scatter(grad, "ctx", scatter_dimension=0, tiled=True) for grad in grads
        )
    take = expert_take(grads)
    low = send_x(jnp.stack([take(me ^ 1, 0), take(me ^ 3, 0)]).astype(BF))
    high = send_y(jnp.stack([take(me ^ 2, 1), take(me ^ 3, 1)]).astype(BF))
    return low, high


def split_sums(sums):
    if lax.axis_size("ctx") != 4:
        return sums, sums
    return (sums[0][1], sums[1][1]), (sums[0][0], sums[1][0])


def scatter_expert_end(grads, direct, last, me):
    if lax.axis_size("ctx") != 4:
        gate_up, down = (part.astype(F32) for part in direct)
        width = gate_up.shape[1] // 2
        return gate_up[:, :width], gate_up[:, width:], down
    first, second = scatter_end(expert_take(grads), me, direct, last)
    rows, half = grads[0].shape[0] // 4, grads[1].shape[0] // 8
    down = [
        jnp.concatenate([part[rows : rows + half], part[rows + half :]], axis=1)
        for part in (first, second)
    ]
    return first[:rows], second[:rows], jnp.concatenate(down, axis=0)


def pick_blocks(blocks, order):
    return jnp.concatenate(
        [
            lax.dynamic_index_in_dim(blocks, order[i], 0, keepdims=False)
            for i in range(order.shape[0])
        ],
        axis=0,
    )


def gather_group(rows, slot_table, me):
    block = rows.shape[0] // 2
    if lax.axis_size("ctx") != 4:
        blocks = slot_table.shape[0]
        whole = lax.all_gather(rows, "ctx", axis=0, tiled=True).reshape(blocks, block, -1)
        match = slot_table[None, :] == jnp.arange(blocks, dtype=jnp.int32)[:, None]
        order = jnp.sum(jnp.where(match, jnp.arange(blocks, dtype=jnp.int32)[None, :], 0), axis=1)
        return pick_blocks(whole, order), ()
    pieces = gather_pieces(rows[:block], rows[block:])
    whole = jnp.zeros((8 * block, rows.shape[1]), rows.dtype)
    for slot in range(2):
        for away in range(4):
            part = pieces[slot][away - 1] if away else rows[slot * block : (slot + 1) * block]
            start = slot_table[2 * (me ^ away) + slot] * block
            whole = lax.dynamic_update_slice(whole, part, (start, 0))
    return whole, (pieces[0][2], pieces[1][2])


def scatter_group(partial, slot_table, me):
    blocks = slot_table.shape[0]
    block = partial.shape[0] // blocks
    if lax.axis_size("ctx") != 4:
        ordered = pick_blocks(partial.reshape(blocks, block, -1), slot_table).astype(BF)
        whole = lax.psum_scatter(ordered, "ctx", scatter_dimension=0, tiled=True)
        return whole.astype(F32), (whole,), (whole,)

    def take(owner, part):
        start = slot_table[2 * owner + part] * block
        return lax.dynamic_slice(partial, (start, 0), (block, partial.shape[1]))

    ahead = scatter_ahead(take, me)
    direct = scatter_direct(take, me)
    last = scatter_last(take, me, ahead)
    return jnp.concatenate(scatter_end(take, me, direct, last), axis=0), ahead, last


def prefix_count(member):
    rows, columns = member.shape
    width = 128
    blocks = rows // width
    ones = member.astype(BF).reshape(blocks, width, columns)
    lower = (
        jnp.arange(width)[:, None] > jnp.arange(width)[None, :]
    ).astype(BF)
    inner = jnp.einsum("pq,bqc->bpc", lower, ones, preferred_element_type=F32)
    totals = jnp.sum(ones.astype(F32), axis=1)
    before = (jnp.arange(blocks)[:, None] > jnp.arange(blocks)[None, :]).astype(F32)
    outer = jnp.sum(before[:, :, None] * totals[None, :, :], axis=1)
    return (inner + outer[:, None, :]).reshape(rows, columns).astype(jnp.int32)


def dot(left, right, dims=(((1,), (0,)), ((), ()))):
    return lax.dot_general(left, right, dims, preferred_element_type=F32)


def turned(values, cosine, sine):
    return values * cosine + pltpu.roll(values, HD // 2, 1) * sine


def tile_weights(query, key, seg_q, seg_k, first, factor):
    rows, width = query.shape[0], key.shape[0]
    scores = dot(query, key, NT) * factor
    q_place = first + lax.broadcasted_iota(jnp.int32, (rows, width), 0)
    k_place = lax.broadcasted_iota(jnp.int32, (rows, width), 1)
    allowed = k_place <= q_place
    if first >= PROMPT:
        allowed = allowed & ((seg_k < 0) | (seg_k == seg_q))
    scores = jnp.where(allowed, scores, -1e30)
    weights = jnp.exp(scores - jnp.max(scores, axis=1, keepdims=True))
    return weights, jnp.sum(weights, axis=1, keepdims=True)


def attend_kernel(
    tiles,
    factor,
    qp_ref,
    kp_ref,
    vp_ref,
    root_ref,
    key_root_ref,
    gain_ref,
    cos_ref,
    sin_ref,
    sq_ref,
    sk_ref,
    q_ref,
    k_ref,
    v_ref,
    o_ref,
):
    at = pl.program_id(1)
    tile = qp_ref.shape[0]

    @pl.when(at == 0)
    def _():
        keys = kp_ref[...] * key_root_ref[:, 1:2] * gain_ref[1:2]
        k_ref[...] = turned(keys, cos_ref[...], sin_ref[...]).astype(BF)
        v_ref[...] = vp_ref[...].astype(BF)

    for i in range(tiles):

        @pl.when(at == i)
        def _():
            own = slice(i * tile, (i + 1) * tile)
            width = (i + 1) * tile
            queries = qp_ref[...] * root_ref[:, 0:1] * gain_ref[0:1]
            query = turned(queries, cos_ref[own], sin_ref[own]).astype(BF)
            q_ref[...] = query
            weights, total = tile_weights(
                query, k_ref[:width], sq_ref[...], sk_ref[:, :width], i * tile, factor
            )
            o_ref[...] = (dot(weights.astype(BF), v_ref[:width]) / total).astype(BF)


def attend(projected, roots, gains, cosine, sine, seg, width, tile=512):
    rows = projected.shape[0]
    heads, tiles = width // HD, rows // tile
    own = pl.BlockSpec((tile, HD), lambda h, i: (i, h))
    whole = pl.BlockSpec((rows, HD), lambda h, i: (0, h))
    pairs = heads * rows * rows * (tiles + 1) // (2 * tiles)
    return pl.pallas_call(
        functools.partial(attend_kernel, tiles, 1.0 / math.sqrt(HD)),
        out_shape=[jax.ShapeDtypeStruct((rows, width), BF)] * 4,
        grid=(heads, tiles),
        in_specs=[
            own,
            pl.BlockSpec((rows, HD), lambda h, i: (0, heads + h)),
            pl.BlockSpec((rows, HD), lambda h, i: (0, 2 * heads + h)),
            pl.BlockSpec((tile, 2), lambda h, i: (i, 0)),
            pl.BlockSpec((rows, 2), lambda h, i: (0, 0)),
            pl.BlockSpec((2, HD), lambda h, i: (0, h)),
            pl.BlockSpec((rows, HD), lambda h, i: (0, 0)),
            pl.BlockSpec((rows, HD), lambda h, i: (0, 0)),
            pl.BlockSpec((tile, 1), lambda h, i: (i, 0)),
            pl.BlockSpec((1, rows), lambda h, i: (0, 0)),
        ],
        out_specs=[own, whole, whole, own],
        compiler_params=pltpu.CompilerParams(vmem_limit_bytes=48 << 20),
        cost_estimate=pl.CostEstimate(
            flops=4 * pairs * HD, bytes_accessed=20 * rows * width, transcendentals=pairs
        ),
    )(
        projected,
        projected,
        projected,
        roots,
        roots,
        gains,
        cosine,
        sine,
        seg[:, None],
        seg[None, :],
    )


def attend_back_kernel(
    tiles,
    factor,
    q_ref,
    k_ref,
    v_ref,
    d_ref,
    cos_ref,
    sin_ref,
    sq_ref,
    sk_ref,
    dq_ref,
    dk_ref,
    dv_ref,
):
    at = pl.program_id(1)
    tile = q_ref.shape[0]

    @pl.when(at == 0)
    def _():
        dk_ref[...] = jnp.zeros_like(dk_ref)
        dv_ref[...] = jnp.zeros_like(dv_ref)

    for i in range(tiles):

        @pl.when(at == i)
        def _():
            own = slice(i * tile, (i + 1) * tile)
            width = (i + 1) * tile
            query, grad = q_ref[...], d_ref[...]
            weights, total = tile_weights(
                query, k_ref[:width], sq_ref[...], sk_ref[:, :width], i * tile, factor
            )
            weights = weights / total
            grad_weights = dot(grad, v_ref[:width], NT)
            delta = jnp.sum(weights * grad_weights, axis=1, keepdims=True)
            grad_scores = (weights * (grad_weights - delta)).astype(BF)
            grad_query = dot(grad_scores, k_ref[:width]) * factor
            dq_ref[...] = turned(grad_query, cos_ref[own], -sin_ref[own])
            dk_ref[:width] += dot(grad_scores, query, TN)
            dv_ref[:width] += dot(weights.astype(BF), grad, TN)

    @pl.when(at == tiles - 1)
    def _():
        dk_ref[...] = turned(dk_ref[...] * factor, cos_ref[...], -sin_ref[...])


def attend_back(q, k, v, grad, cosine, sine, seg, tile=512):
    rows, width = q.shape
    heads, tiles = width // HD, rows // tile
    own = pl.BlockSpec((tile, HD), lambda h, i: (i, h))
    whole = pl.BlockSpec((rows, HD), lambda h, i: (0, h))
    table = pl.BlockSpec((rows, HD), lambda h, i: (0, 0))
    pairs = heads * rows * rows * (tiles + 1) // (2 * tiles)
    return pl.pallas_call(
        functools.partial(attend_back_kernel, tiles, 1.0 / math.sqrt(HD)),
        out_shape=[jax.ShapeDtypeStruct((rows, width), F32)] * 3,
        grid=(heads, tiles),
        in_specs=[
            own,
            whole,
            whole,
            own,
            table,
            table,
            pl.BlockSpec((tile, 1), lambda h, i: (i, 0)),
            pl.BlockSpec((1, rows), lambda h, i: (0, 0)),
        ],
        out_specs=[own, whole, whole],
        compiler_params=pltpu.CompilerParams(vmem_limit_bytes=48 << 20),
        cost_estimate=pl.CostEstimate(
            flops=10 * pairs * HD, bytes_accessed=20 * rows * width, transcendentals=pairs
        ),
    )(q, k, v, grad, cosine, sine, seg[:, None], seg[None, :])


def pick_rows(tok, low, windows, source_ref, acc_ref):
    last = source_ref.shape[0] - WIN
    span = lax.broadcasted_iota(jnp.int32, (TILE, WIN), 1)

    def window(j):
        base = low + j * WIN
        start = pl.multiple_of(jnp.minimum(base, last), 128)
        match = (tok - start == span) & (tok >= base)
        return dot(match.astype(F32).astype(BF), source_ref[pl.ds(start, WIN), :])

    acc_ref[...] = window(0)

    @pl.loop(1, windows)
    def _(j):
        acc_ref[...] += window(j)

    return acc_ref[...].astype(BF)


def copy_all(copies):
    for copy in copies:
        copy.start()
    for copy in copies:
        copy.wait()


def back_rows_kernel(tiles_ref, low_ref, windows_ref, me_ref, tok_ref, dy_ref, *refs):
    parts, (rows_ref, raw_ref, down_ref, acc_ref, sems) = refs[:-5], refs[-5:]
    i = pl.program_id(0)

    @pl.when(i == 0)
    def _():
        if len(parts) == 1:
            copy_all([pltpu.make_async_copy(parts[0], down_ref, sems.at[0])])
            return
        rows, width = down_ref.shape[0] // 4, down_ref.shape[1] // 2
        copies = []
        for away, part in enumerate(parts):
            owner = pl.multiple_of((me_ref[0] ^ away) * rows, rows)
            for k in range(2):
                copies.append(
                    pltpu.make_async_copy(
                        part.at[pl.ds((k + 1) * rows, rows)],
                        down_ref.at[pl.ds(owner, rows), pl.ds(k * width, width)],
                        sems.at[len(copies)],
                    )
                )
        copy_all(copies)

    @pl.when(i < tiles_ref[0])
    def _():
        rows = pick_rows(tok_ref[...], low_ref[i], windows_ref[i], dy_ref, acc_ref)
        rows_ref[...] = rows
        raw_ref[...] = dot(rows, down_ref[...], NT)

    @pl.when(i >= tiles_ref[0])
    def _():
        rows_ref[...] = jnp.zeros_like(rows_ref)
        raw_ref[...] = jnp.zeros_like(raw_ref)


def back_rows(tables, me, upstream, parts, ff):
    total, width = upstream.shape
    capacity = tables[3].shape[0]
    tile = lambda n: pl.BlockSpec((TILE, n), lambda i, *_: (i, 0))
    once = lambda shape: pl.BlockSpec(shape, lambda i, *_: (0, 0), pipeline_mode=pl.Buffered(1))
    return pl.pallas_call(
        back_rows_kernel,
        out_shape=[
            jax.ShapeDtypeStruct((capacity, width), BF),
            jax.ShapeDtypeStruct((capacity, ff), F32),
            jax.ShapeDtypeStruct((ff, width), BF),
        ],
        grid_spec=pltpu.PrefetchScalarGridSpec(
            num_scalar_prefetch=4,
            grid=(capacity // TILE,),
            in_specs=[tile(1), once((total, width))]
            + [pl.BlockSpec(memory_space=pl.ANY)] * len(parts),
            out_specs=[tile(width), tile(ff), pl.BlockSpec((ff, width), lambda i, *_: (0, 0))],
            scratch_shapes=[
                pltpu.VMEM((TILE, width), F32),
                pltpu.SemaphoreType.DMA((2 * len(parts),)),
            ],
        ),
        compiler_params=pltpu.CompilerParams(vmem_limit_bytes=48 << 20),
        cost_estimate=pl.CostEstimate(
            flops=total * (width * ff + WIN * width),
            bytes_accessed=2 * total * width + 4 * ff * width + capacity * (2 * width + 4 * ff),
            transcendentals=0,
        ),
    )(*tables[:3], me, tables[3], upstream, *parts)


def expert_kernel(
    own, tiles_ref, low_ref, windows_ref, ids_ref, tok_ref, h_ref, router_ref, raw_ref, *refs
):
    parts = refs[:-8]
    rows_ref, hid_ref, dab_ref, dh_ref, share_ref, both_ref, acc_ref, sems = refs[-8:]
    wg_ref, wu_ref = both_ref.at[0], both_ref.at[1]
    i = pl.program_id(0)
    ff = wg_ref.shape[1]

    @pl.when(i == 0)
    def _():
        if len(parts) == 1:
            copy_all([pltpu.make_async_copy(parts[0], both_ref, sems.at[0])])
            return
        rows = wg_ref.shape[0] // 4
        half = rows // 2
        copies = []
        for away in range(4):
            owner = pl.multiple_of((ids_ref[1] ^ away) * rows, rows)
            for part, first, count, which, shift in (
                (parts[away], 0, rows, 0, 0),
                (parts[away], rows, half, 1, 0),
                (parts[4 + away], 0, half, 1, half),
            ):
                copies.append(
                    pltpu.make_async_copy(
                        part.at[pl.ds(first, count)],
                        both_ref.at[which, pl.ds(owner + shift, count)],
                        sems.at[len(copies)],
                    )
                )
        copy_all(copies)

    @pl.when(i < tiles_ref[0])
    def _():
        rows = pick_rows(tok_ref[...], low_ref[i], windows_ref[i], h_ref, acc_ref)
        rows_ref[...] = rows
        logits = dot(rows, router_ref[...])
        probs = jnp.exp(logits - jnp.max(logits, axis=1, keepdims=True))
        column = lax.broadcasted_iota(jnp.int32, probs.shape, 1)
        mine = jnp.sum(jnp.where(column == ids_ref[0] + own, probs, 0.0), axis=1, keepdims=True)
        gate = mine / jnp.sum(probs, axis=1, keepdims=True)
        share = 0.0
        part = ff // 4
        for c in range(4):
            cols = slice(c * part, (c + 1) * part)
            a = dot(rows, wg_ref[:, cols])
            b = dot(rows, wu_ref[:, cols])
            raw = raw_ref[:, cols]
            sig = 1.0 / (1.0 + jnp.exp(-a))
            silu = a * sig
            hid = silu * b
            share += jnp.sum(hid * raw, axis=1, keepdims=True)
            raw = raw * gate
            hid_ref[:, cols] = (hid * gate).astype(BF)
            dab_ref[:, cols] = (raw * b * (sig * (1.0 + a * (1.0 - sig)))).astype(BF)
            dab_ref[:, ff + c * part : ff + (c + 1) * part] = (raw * silu).astype(BF)
        share_ref[...] = share
        dh = dot(dab_ref[:, :ff], wg_ref[...], NT) + dot(dab_ref[:, ff:], wu_ref[...], NT)
        dh_ref[...] = dh.astype(BF)

    @pl.when(i >= tiles_ref[0])
    def _():
        for ref in (rows_ref, hid_ref, dab_ref, dh_ref, share_ref):
            ref[...] = jnp.zeros_like(ref)


def expert_rows(tables, own, ids, hidden, router, parts, raw):
    total, width = hidden.shape
    capacity, ff = raw.shape
    tile = lambda n: pl.BlockSpec((TILE, n), lambda i, *_: (i, 0))
    once = lambda shape: pl.BlockSpec(shape, lambda i, *_: (0, 0), pipeline_mode=pl.Buffered(1))
    made = lambda n, dtype=BF: jax.ShapeDtypeStruct((capacity, n), dtype)
    return pl.pallas_call(
        functools.partial(expert_kernel, own),
        out_shape=[made(width), made(ff), made(2 * ff), made(width), made(1, F32)],
        grid_spec=pltpu.PrefetchScalarGridSpec(
            num_scalar_prefetch=4,
            grid=(capacity // TILE,),
            in_specs=[tile(1), once((total, width)), once(router.shape), tile(ff)]
            + [pl.BlockSpec(memory_space=pl.ANY)] * len(parts),
            out_specs=[tile(width), tile(ff), tile(2 * ff), tile(width), tile(1)],
            scratch_shapes=[
                pltpu.VMEM((2, width, ff), BF),
                pltpu.VMEM((TILE, width), F32),
                pltpu.SemaphoreType.DMA((12,)),
            ],
        ),
        compiler_params=pltpu.CompilerParams(vmem_limit_bytes=56 << 20),
        cost_estimate=pl.CostEstimate(
            flops=total * (4 * width * ff + WIN * width),
            bytes_accessed=2 * total * width + 4 * ff * width + capacity * (4 * width + 10 * ff),
            transcendentals=total * ff,
        ),
    )(*tables[:3], ids, tables[3], hidden, router, raw, *parts)


def combine_kernel(experts, start_ref, more_ref, wide_ref, pos_ref, *refs):
    rows_refs, share_refs = refs[:experts], refs[experts : 2 * experts]
    out_ref, own_ref, acc_ref = refs[2 * experts :]
    i = pl.program_id(0)
    span = lax.broadcasted_iota(jnp.int32, (TILE, TILE), 1)
    wide_span = lax.broadcasted_iota(jnp.int32, (TILE, 384), 1)
    last = rows_refs[0].shape[0] - TILE

    def window(e, j):
        base = start_ref[e, i] + j * TILE
        start = pl.multiple_of(jnp.minimum(base, last), 16)
        pos = pos_ref[:, e : e + 1]
        match = (pos - start == span) & (pos >= base)
        return dot(match.astype(F32).astype(BF), rows_refs[e][pl.ds(start, TILE), :])

    acc_ref[...] = sum(window(e, 0) for e in range(experts))
    for e in range(experts):
        wide = pl.multiple_of(wide_ref[e, i], 128)
        match = pos_ref[:, e : e + 1] - wide == wide_span
        share = share_refs[e][:, pl.ds(wide, 384)]
        own_ref[:, e : e + 1] = jnp.sum(jnp.where(match, share, 0.0), axis=1, keepdims=True)

        @pl.when(more_ref[e, i] > 0)
        def _():
            acc_ref[...] += window(e, 1)

    out_ref[...] = acc_ref[...].astype(BF)


def combine_rows(tables, rows, shares):
    experts, (capacity, width) = len(rows), rows[0].shape
    total = tables[3].shape[0]
    once = lambda shape: pl.BlockSpec(shape, lambda i, *_: (0, 0), pipeline_mode=pl.Buffered(1))
    tile = lambda n: pl.BlockSpec((TILE, n), lambda i, *_: (i, 0))
    return pl.pallas_call(
        functools.partial(combine_kernel, experts),
        out_shape=[
            jax.ShapeDtypeStruct((total, width), BF),
            jax.ShapeDtypeStruct((total, experts), F32),
        ],
        grid_spec=pltpu.PrefetchScalarGridSpec(
            num_scalar_prefetch=3,
            grid=(total // TILE,),
            in_specs=[tile(experts)]
            + [once((capacity, width))] * experts
            + [once((1, capacity))] * experts,
            out_specs=[tile(width), tile(experts)],
            scratch_shapes=[pltpu.VMEM((TILE, width), F32)],
        ),
        compiler_params=pltpu.CompilerParams(vmem_limit_bytes=48 << 20),
        cost_estimate=pl.CostEstimate(
            flops=2 * experts * total * TILE * width,
            bytes_accessed=2 * (experts * capacity + total) * width,
            transcendentals=0,
        ),
    )(*tables, *rows, *shares)


def local(
    tokens,
    cotangent,
    routes,
    block_of_slot,
    cont_seg,
    w_query,
    w_key,
    w_value,
    w_out,
    w_router,
    attn_gain,
    query_gain,
    key_gain,
    ffn_gain,
    w_gate,
    w_up,
    w_down,
):
    ctx_size = lax.axis_size("ctx")
    exp_size = lax.axis_size("exp")
    me = lax.axis_index("ctx")
    exp_index = lax.axis_index("exp")
    tok_rows = tokens.shape[0]
    part_rows = w_query.shape[0]
    own_width = D // ctx_size
    own_heads = HEADS // ctx_size
    experts = w_router.shape[1]
    own_experts = w_gate.shape[0]
    slot_table = block_of_slot[0]
    seg_row = cont_seg[0]
    group_rows = ctx_size * tok_rows
    factor = 1.0 / math.sqrt(HD)

    tokens_group, tokens_there = gather_group(tokens, slot_table, me)
    small = jnp.concatenate(
        [w_router] + [g[:, None] for g in (attn_gain, query_gain, key_gain, ffn_gain)], axis=1
    )
    small = jnp.pad(small, ((0, 0), (0, 128 - small.shape[1])))
    by_owner = jnp.stack(
        [w.reshape(part_rows, ctx_size, own_width) for w in (w_query, w_key, w_value)], axis=2
    )
    by_owner = jnp.swapaxes(by_owner, 0, 1).reshape(ctx_size, part_rows, 3 * own_width)
    by_owner = jnp.concatenate(
        [by_owner, jnp.broadcast_to(small, (ctx_size,) + small.shape)], axis=2
    )
    own_columns = exchange(by_owner, me)
    packed = lax.all_gather(own_columns, "exp", axis=1, tiled=True).reshape(D, 3 * own_width + 128)
    small_full = packed[:, 3 * own_width :]
    router_full = small_full[:, :experts]
    gains = small_full[:, experts : experts + 4].astype(F32)
    gain_attn, gain_ffn = gains[:, 0], gains[:, 3]
    own_gains = lax.dynamic_slice(gains, (me * own_width, 0), (own_width, 4))
    gain_query, gain_key = own_gains[:, 1], own_gains[:, 2]
    out_full = lax.all_gather(w_out, "exp", axis=0, tiled=True)
    routes_all = lax.all_to_all(
        jnp.broadcast_to(routes[None], (exp_size,) + routes.shape),
        "exp",
        split_axis=0,
        concat_axis=0,
        tiled=True,
    ).reshape(exp_size * tok_rows, TOP)
    upstream_all = lax.all_gather(cotangent, "exp", axis=0, tiled=True)
    packs = [pack_expert(w_gate[e], w_up[e], w_down[e]) for e in range(own_experts)]
    if ctx_size == 4:
        ahead = after_all(packs[0], *tokens_there)
        ahead = send_x(ahead[0]), send_y(ahead[1])

    own_ids = exp_index * own_experts + jnp.arange(own_experts, dtype=jnp.int32)
    member = jnp.any(routes_all[:, :, None] == own_ids[None, None, :], axis=1)
    place_of = prefix_count(member)
    capacity = exp_size * 8 * ((5 * tok_rows * TOP // (4 * experts) + 7) // 8)
    row_tiles = (capacity + TILE - 1) // TILE
    capacity = row_tiles * TILE
    all_rows = exp_size * tok_rows
    row_ids = jnp.arange(capacity, dtype=jnp.int32)
    hit = (place_of.T[:, None, :] == row_ids[None, :, None]) & member.T[:, None, :]
    token_ids = jnp.arange(all_rows, dtype=jnp.int32)
    token_of_row = jnp.max(jnp.where(hit, token_ids[None, None, :], -1), axis=2)
    counts = jnp.sum(member.astype(jnp.int32), axis=0)
    used_tiles = (counts + TILE - 1) // TILE
    by_tile = token_of_row.reshape(own_experts * row_tiles, TILE)
    low_token = jnp.maximum(by_tile[:, 0], 0) // 128 * 128
    windows = jnp.maximum((jnp.max(by_tile, axis=1) - low_token) // WIN + 1, 1)
    low_token = low_token.reshape(own_experts, row_tiles)
    windows = windows.reshape(own_experts, row_tiles)
    row_tables = [
        (used_tiles[e : e + 1], low_token[e], windows[e], token_of_row[e][:, None])
        for e in range(own_experts)
    ]
    place_column = jnp.where(member, place_of, NOWHERE)
    first_place = place_of[::TILE].T
    in_tile = jnp.sum(member.reshape(-1, TILE, own_experts).astype(jnp.int32), axis=1).T
    first_row = first_place // 16 * 16
    more_rows = (first_place + in_tile - first_row > TILE).astype(jnp.int32)
    share_row_start = jnp.minimum(first_place // 128 * 128, capacity - 384)
    token_tables = (first_row, more_rows, share_row_start, place_column)

    seg_ids = jnp.concatenate([jnp.full((PROMPT,), -1, jnp.int32), seg_row])
    starts = jnp.sum(
        (seg_row[None, :] < jnp.arange(CONT, dtype=jnp.int32)[:, None]).astype(jnp.int32), axis=1
    )
    first_pos = jnp.sum(
        jnp.where(
            seg_row[:, None] == jnp.arange(CONT, dtype=jnp.int32)[None, :], starts[None, :], 0
        ),
        axis=1,
    )
    cont_pos = PROMPT + jnp.arange(CTOK, dtype=jnp.int32) - first_pos
    position = jnp.concatenate([jnp.arange(PROMPT, dtype=jnp.int32), cont_pos])
    cos_part, sin_part = angles(position)
    group_inputs = after(
        tokens_group, token_of_row, place_column, first_row, more_rows, share_row_start, used_tiles, windows
    ).astype(F32)
    normed_group = group_inputs * inverse_root(group_inputs)
    hidden_one = (normed_group * gain_attn).astype(BF)
    projected = jnp.dot(hidden_one, packed, preferred_element_type=F32)
    query_pre = projected[:, :own_width]
    key_pre = projected[:, own_width : 2 * own_width]
    squares = jnp.stack([jnp.sum(query_pre * query_pre, axis=1), jnp.sum(key_pre * key_pre, axis=1)])
    if ctx_size == 4:
        squares = after(squares, *ahead)
    squares = sum_over_ctx(squares)
    if ctx_size == 4:
        direct = after_all(packs[0], squares)
        direct = send_x(direct[1]), send_y(direct[0])
    roots = lax.rsqrt(squares / D + epsilon)
    root_query, root_key = roots[0][:, None], roots[1][:, None]
    normed_query = query_pre * root_query
    normed_key = key_pre * root_key
    query_rot, key_rot, value_low, context_low = attend(
        projected,
        roots.T,
        jnp.stack([gain_query, gain_key]),
        cos_part,
        sin_part,
        seg_ids,
        own_width,
    )
    branch_part = jnp.dot(context_low, out_full, preferred_element_type=F32)
    if ctx_size == 4:
        branch_part = after(branch_part, *direct)
    branch, unused, branch_there = scatter_group(branch_part, slot_table, me)
    me_table = jnp.reshape(me, (1,)).astype(jnp.int32)
    ids = jnp.stack([own_ids[0], me.astype(jnp.int32)])
    width = w_gate.shape[2]
    lows, highs, backs = [], [], []
    if ctx_size == 4:
        passed = after_all(ahead, *branch_there)
        passed = send_y(passed[0]), send_x(passed[1])
        lows.append((packs[0][0], ahead[0], direct[1], passed[0]))
        highs.append((packs[0][1], direct[0], ahead[1], passed[1]))
        upstream = upstream_all
        for e in range(1, own_experts):
            low, high = after_all(packs[e], *passed)
            ahead = send_x(low), send_y(high)
            direct = send_x(high), send_y(low)
            passed = send_y(ahead[0]), send_x(ahead[1])
            lows.append((packs[e][0], ahead[0], direct[1], passed[0]))
            highs.append((packs[e][1], direct[0], ahead[1], passed[1]))
            upstream = after(upstream, *ahead)
        backs.append(back_rows(row_tables[0], me_table, upstream, highs[0], width))
    else:
        for e in range(own_experts):
            both, down = whole_expert(*after_all((w_gate[e], w_up[e], w_down[e]), *branch_there))
            lows.append((both,))
            highs.append((down,))
        backs.append(back_rows(row_tables[0], me_table, upstream_all, highs[0], width))

    inputs = tokens.astype(F32)
    middle = inputs + branch
    root_two = inverse_root(middle)
    normed_two = middle * root_two
    hidden_two = (normed_two * gain_ffn).astype(BF)
    hidden_all = lax.all_gather(hidden_two, "exp", axis=0, tiled=True)
    logits = jnp.dot(hidden_two, router_full, preferred_element_type=F32)
    router_prob = jax.nn.softmax(logits, axis=-1)

    every = range(own_experts)
    made = []
    for e in every:
        if e > 0:
            upstream = after(upstream_all, made[-1][3])
            highs[e] = after_all(highs[e], made[-1][3])
            backs.append(back_rows(row_tables[e], me_table, upstream, highs[e], width))
        parts = tuple(lows[e]) + tuple(highs[e]) if ctx_size == 4 else lows[e]
        made.append(
            expert_rows(row_tables[e], e, ids, hidden_all, router_full, parts, backs[e][1])
        )
    shares = [m[4].reshape(1, capacity) for m in made]
    grad_two_part, share_token = combine_rows(token_tables, [m[3] for m in made], shares)
    grad_two = lax.psum_scatter(grad_two_part, "exp", scatter_dimension=0, tiled=True)
    share_back = lax.all_to_all(
        share_token.reshape(exp_size, tok_rows, own_experts),
        "exp",
        split_axis=0,
        concat_axis=0,
        tiled=True,
    )
    grad_prob = jnp.swapaxes(share_back, 0, 1).reshape(tok_rows, experts)
    expert_grads = []
    mixture_part = grad_two_part
    for e in every:
        rows, hidden, grad_hidden = after_all(made[e][:3], mixture_part)
        expert_grads.append(
            (
                lax.dot_general(rows, grad_hidden, TN, preferred_element_type=F32).astype(BF),
                lax.dot_general(hidden, backs[e][0], TN, preferred_element_type=F32).astype(BF),
            )
        )
        if e == 0:
            results = [
                jnp.dot(
                    after(made[k][1], *expert_grads[0]), backs[k][2], preferred_element_type=F32
                ).astype(BF)
                for k in every
            ]
            if ctx_size == 4:
                take = expert_take(expert_grads[0])
                ahead = scatter_ahead(take, me)
                results = after_all(results, *ahead)
                direct = scatter_direct(take, me, *ahead)
                last = scatter_last(take, me, ahead)
            else:
                direct, last = scatter_expert_first(expert_grads[0], me), ()
            mixture_part, unused = combine_rows(token_tables, results, shares)
    directs, lasts = [direct], [last]
    mixture = lax.psum_scatter(mixture_part, "exp", scatter_dimension=0, tiled=True)
    output = (middle + mixture.astype(F32)).astype(BF)

    grad_two = after(
        grad_two, mixture_part, *(part for grads in expert_grads[1:] for part in grads)
    ).astype(F32)
    grad_logits = (
        router_prob * (grad_prob - jnp.sum(router_prob * grad_prob, axis=-1, keepdims=True))
    ).astype(BF)
    grad_router = jnp.einsum("td,te->ed", hidden_two, grad_logits, preferred_element_type=F32)
    grad_two = grad_two + jnp.einsum(
        "te,de->td", grad_logits, router_full, preferred_element_type=F32
    )
    grad_ffn_gain = jnp.sum(grad_two * normed_two, axis=0)
    grad_middle = cotangent.astype(F32) + norm_back(grad_two * gain_ffn, normed_two, root_two)

    own_grad = after(grad_middle.astype(BF), *directs[0], *lasts[0])
    branch_grad, grad_there = gather_group(own_grad, slot_table, me)
    sums = []
    for e in range(1, own_experts):
        sums.append(scatter_expert_first(after_all(expert_grads[e], *grad_there), me))
    grad_context = lax.dot_general(branch_grad, out_full, NT, preferred_element_type=F32).astype(BF)
    out_grad = lax.dot_general(
        context_low, branch_grad, TN, preferred_element_type=F32
    ).astype(BF)
    grad_query_norm, grad_key_norm, grad_value = attend_back(
        query_rot, key_rot, value_low, grad_context, cos_part, sin_part, seg_ids
    )
    grad_query_gain = jnp.sum(grad_query_norm * normed_query, axis=0)
    grad_key_gain = jnp.sum(grad_key_norm * normed_key, axis=0)
    scaled_query = grad_query_norm * gain_query
    scaled_key = grad_key_norm * gain_key
    products = jnp.stack(
        [jnp.sum(scaled_query * normed_query, axis=1), jnp.sum(scaled_key * normed_key, axis=1)]
    )
    products = after(products, out_grad, *(piece for pieces in sums for piece in pieces))
    means = sum_over_ctx(products) / D
    for e in range(1, own_experts):
        ahead, direct = split_sums(sums[e - 1])
        directs.append(direct)
        ahead = after_all(ahead, means)
        take = expert_take(expert_grads[e])
        lasts.append(scatter_last(take, me, ahead) if ctx_size == 4 else ())
    grad_projected = jnp.concatenate(
        [
            root_query * (scaled_query - normed_query * means[0][:, None]),
            root_key * (scaled_key - normed_key * means[1][:, None]),
            grad_value,
        ],
        axis=1,
    ).astype(BF)
    grad_packed = jnp.pad(grad_projected, ((0, 0), (0, 128)))
    grad_one_part = lax.dot_general(grad_packed, packed, NT, preferred_element_type=F32)
    grad_attn_gain = jnp.sum(grad_one_part * normed_group, axis=0)
    qkv_grad = lax.dot_general(hidden_one, grad_projected, TN, preferred_element_type=F32).astype(BF)
    grad_one, one_ahead, unused = scatter_group(
        after(grad_one_part, *(piece for pieces in lasts[1:] for piece in pieces)), slot_table, me
    )
    weight_sums = [
        scatter_expert_end(
            expert_grads[e], after_all(directs[e], *one_ahead), after_all(lasts[e], *one_ahead), me
        )
        for e in every
    ]
    gate_grad, up_grad, down_grad = (jnp.stack(parts) for parts in zip(*weight_sums))
    out_sum = lax.psum_scatter(
        after(out_grad, mixture), "exp", scatter_dimension=0, tiled=True
    ).astype(F32)
    qkv_sum = lax.psum_scatter(
        qkv_grad.reshape(ctx_size, exp_size * part_rows, 3 * own_width),
        "exp",
        scatter_dimension=1,
        tiled=True,
    )
    qkv_own = exchange(qkv_sum, me).astype(F32)
    projection_grads = [
        jnp.swapaxes(qkv_own[:, :, i * own_width : (i + 1) * own_width], 0, 1).reshape(part_rows, D)
        for i in range(3)
    ]
    root_one = inverse_root(inputs)
    normed_one = inputs * root_one
    grad_input = grad_middle + norm_back(grad_one * gain_attn, normed_one, root_one)
    head_gains = lax.dynamic_update_slice(
        jnp.zeros((2, D), F32), jnp.stack([grad_query_gain, grad_key_gain]), (0, me * own_width)
    )
    small_sums = jnp.concatenate(
        [grad_router, jnp.stack([grad_ffn_gain, grad_attn_gain]), head_gains]
    )
    small_sums = sum_to_rows(after(small_sums, *one_ahead), me)
    return (
        output,
        grad_input,
        projection_grads[0],
        projection_grads[1],
        projection_grads[2],
        out_sum,
        small_sums[:experts].T,
        small_sums[experts + 1],
        small_sums[experts + 2],
        small_sums[experts + 3],
        small_sums[experts],
        gate_grad,
        up_grad,
        down_grad,
    )


def solution(mesh):
    rows = P(BOTH, None)
    weights = P("exp", "ctx", None)
    in_specs = (
        (rows, rows, rows, P("exp", None), P("exp", None))
        + (rows,) * 5
        + (P(BOTH),) * 4
        + (weights,) * 3
    )
    out_specs = (rows,) * 7 + (P(BOTH),) * 4 + (weights,) * 3
    return jax.shard_map(local, mesh=mesh, in_specs=in_specs, out_specs=out_specs, check_vma=False)
```

```python
import functools
import math

import jax
import jax.numpy as jnp
from jax import lax
from jax.experimental import pallas as pl
from jax.experimental.pallas import tpu as pltpu
from jax.sharding import PartitionSpec as P

D = 2048
HEADS = 16
HD = 128
TOP = 8
PROMPT = 1024
CONT = 2
CTOK = 512

epsilon = 1e-05
rope_base = 10000.0
BF = jnp.bfloat16
F32 = jnp.float32
BOTH = ("ctx", "exp")
X_PAIRS = [(i, i ^ 1) for i in range(4)]
Y_PAIRS = [(i, i ^ 2) for i in range(4)]
XY_PAIRS = [(i, i ^ 3) for i in range(4)]
NT = (((1,), (1,)), ((), ()))
TN = (((0,), (0,)), ((), ()))
TILE = 256
WIN = 768
NOWHERE = -(1 << 20)


def inverse_root(values):
    return lax.rsqrt(jnp.mean(values * values, axis=-1, keepdims=True) + epsilon)


def norm_back(gradient, normed, root_part):
    return root_part * (gradient - normed * jnp.mean(gradient * normed, axis=-1, keepdims=True))


def angles(position):
    half_dim = HD // 2
    inverse = rope_base ** (-2.0 * jnp.arange(half_dim, dtype=F32) / HD)
    phases = position.astype(F32)[:, None] * inverse[None, :]
    cosine, sine = jnp.cos(phases), jnp.sin(phases)
    return jnp.concatenate([cosine, cosine], axis=1), jnp.concatenate([-sine, sine], axis=1)


def send_x(value):
    return lax.ppermute(value, "ctx", X_PAIRS)


def send_y(value):
    return lax.ppermute(value, "ctx", Y_PAIRS)


def send_xy(value):
    return lax.ppermute(value, "ctx", XY_PAIRS)


def after(value, *others):
    return lax.optimization_barrier((value,) + others)[0]


def after_all(values, *others):
    return lax.optimization_barrier(tuple(values) + others)[: len(values)]


def gather_pieces(low, high):
    low_x, high_y = send_x(low), send_y(high)
    high_x, low_y = send_x(high), send_y(low)
    return (low_x, low_y, send_y(low_x)), (high_x, high_y, send_x(high_y))


def scatter_ahead(take, me):
    return send_x(take(me ^ 3, 0).astype(BF)), send_y(take(me ^ 3, 1).astype(BF))


def scatter_direct(take, me, *others):
    low, high = take(me ^ 1, 0).astype(BF), take(me ^ 2, 1).astype(BF)
    if others:
        low, high = after_all((low, high), *others)
    return send_x(low), send_y(high)


def scatter_last_payload(take, me, ahead):
    low = (take(me ^ 2, 0).astype(F32) + ahead[0].astype(F32)).astype(BF)
    high = (take(me ^ 1, 1).astype(F32) + ahead[1].astype(F32)).astype(BF)
    return low, high


def scatter_last(take, me, ahead):
    low, high = scatter_last_payload(take, me, ahead)
    return send_y(low), send_x(high)


def scatter_end(take, me, direct, last):
    return [
        take(me, part).astype(F32) + direct[part].astype(F32) + last[part].astype(F32)
        for part in range(2)
    ]


def exchange(blocks, me):
    if lax.axis_size("ctx") != 4:
        return lax.all_to_all(blocks, "ctx", split_axis=0, concat_axis=0, tiled=True)
    sends = (lambda part: part, send_x, send_y, send_xy)
    parts = [
        send(lax.dynamic_index_in_dim(blocks, me ^ away, 0, keepdims=False))
        for away, send in enumerate(sends)
    ]

    def from_ctx(c):
        chosen = parts[0]
        for away in range(1, 4):
            chosen = jnp.where((me ^ c) == away, parts[away], chosen)
        return chosen

    return jnp.stack([from_ctx(c) for c in range(4)])


def sum_over_ctx(value):
    if lax.axis_size("ctx") != 4:
        return lax.psum(value, "ctx")
    value = value + send_x(value)
    return value + send_y(value)


def sum_to_rows(values, me):
    ctx_size, exp_size = lax.axis_size("ctx"), lax.axis_size("exp")
    count, width = values.shape
    parts = values.reshape(count, ctx_size, exp_size, width // (ctx_size * exp_size))
    parts = jnp.transpose(parts, (2, 1, 0, 3))
    parts = jnp.sum(lax.all_to_all(parts, "exp", split_axis=0, concat_axis=0, tiled=True), axis=0)
    return jnp.sum(exchange(parts, me), axis=0)


def pack_expert(w_gate, w_up, w_down):
    half, width = w_up.shape[0] // 2, w_up.shape[1]
    low = jnp.concatenate([w_gate, w_up[:half]], axis=0)
    high = jnp.concatenate([w_up[half:], w_down[:, :width], w_down[:, width:]], axis=0)
    return low, high


def whole_expert(w_gate, w_up, w_down):
    return (
        lax.all_gather(jnp.stack([w_gate, w_up]), "ctx", axis=1, tiled=True),
        lax.all_gather(w_down, "ctx", axis=0, tiled=True),
    )


def expert_take(grads):
    gate_up, down = grads
    rows, width = gate_up.shape[0] // 4, gate_up.shape[1] // 2
    half = down.shape[0] // 8

    def take(owner, part):
        first = (2 * owner + part) * half
        return jnp.concatenate(
            [
                lax.dynamic_slice(gate_up, (owner * rows, part * width), (rows, width)),
                lax.dynamic_slice(down, (first, 0), (half, width)),
                lax.dynamic_slice(down, (first, width), (half, width)),
            ],
            axis=0,
        )

    return take


def scatter_expert_first(grads, me):
    if lax.axis_size("ctx") != 4:
        return tuple(
            lax.psum_scatter(grad, "ctx", scatter_dimension=0, tiled=True) for grad in grads
        )
    return scatter_joined(expert_take(grads), me)


def scatter_joined(take, me):
    low = send_x(jnp.stack([take(me ^ 1, 0), take(me ^ 3, 0)]).astype(BF))
    high = send_y(jnp.stack([take(me ^ 2, 1), take(me ^ 3, 1)]).astype(BF))
    return low, high


def split_sums(sums):
    if lax.axis_size("ctx") != 4:
        return sums, sums
    return (sums[0][1], sums[1][1]), (sums[0][0], sums[1][0])


def scatter_expert_end(grads, direct, last, me):
    if lax.axis_size("ctx") != 4:
        gate_up, down = (part.astype(F32) for part in direct)
        width = gate_up.shape[1] // 2
        return gate_up[:, :width], gate_up[:, width:], down
    first, second = scatter_end(expert_take(grads), me, direct, last)
    rows, half = grads[0].shape[0] // 4, grads[1].shape[0] // 8
    down = [
        jnp.concatenate([part[rows : rows + half], part[rows + half :]], axis=1)
        for part in (first, second)
    ]
    return first[:rows], second[:rows], jnp.concatenate(down, axis=0)


def pick_blocks(blocks, order):
    return jnp.concatenate(
        [
            lax.dynamic_index_in_dim(blocks, order[i], 0, keepdims=False)
            for i in range(order.shape[0])
        ],
        axis=0,
    )


def gather_group(rows, slot_table, me):
    block = rows.shape[0] // 2
    if lax.axis_size("ctx") != 4:
        blocks = slot_table.shape[0]
        whole = lax.all_gather(rows, "ctx", axis=0, tiled=True).reshape(blocks, block, -1)
        match = slot_table[None, :] == jnp.arange(blocks, dtype=jnp.int32)[:, None]
        order = jnp.sum(jnp.where(match, jnp.arange(blocks, dtype=jnp.int32)[None, :], 0), axis=1)
        return pick_blocks(whole, order), ()
    pieces = gather_pieces(rows[:block], rows[block:])
    whole = jnp.zeros((8 * block, rows.shape[1]), rows.dtype)
    for slot in range(2):
        for away in range(4):
            part = pieces[slot][away - 1] if away else rows[slot * block : (slot + 1) * block]
            start = slot_table[2 * (me ^ away) + slot] * block
            whole = lax.dynamic_update_slice(whole, part, (start, 0))
    return whole, (pieces[0][2], pieces[1][2])


def scatter_group(partial, slot_table, me, joined=False):
    blocks = slot_table.shape[0]
    block = partial.shape[0] // blocks
    if lax.axis_size("ctx") != 4:
        ordered = pick_blocks(partial.reshape(blocks, block, -1), slot_table).astype(BF)
        whole = lax.psum_scatter(ordered, "ctx", scatter_dimension=0, tiled=True)
        return whole.astype(F32), (whole,), (whole,), (whole,)

    def take(owner, part):
        start = slot_table[2 * owner + part] * block
        return lax.dynamic_slice(partial, (start, 0), (block, partial.shape[1]))

    if joined:
        ahead, direct = split_sums(scatter_joined(take, me))
    else:
        ahead, direct = scatter_ahead(take, me), scatter_direct(take, me)
    sent = scatter_last_payload(take, me, ahead)
    last = send_y(sent[0]), send_x(sent[1])
    return jnp.concatenate(scatter_end(take, me, direct, last), axis=0), ahead, sent, last


def prefix_count(member):
    rows, columns = member.shape
    width = 128
    blocks = rows // width
    ones = member.astype(BF).reshape(blocks, width, columns)
    lower = (
        jnp.arange(width)[:, None] > jnp.arange(width)[None, :]
    ).astype(BF)
    inner = jnp.einsum("pq,bqc->bpc", lower, ones, preferred_element_type=F32)
    totals = jnp.sum(ones.astype(F32), axis=1)
    before = (jnp.arange(blocks)[:, None] > jnp.arange(blocks)[None, :]).astype(F32)
    outer = jnp.sum(before[:, :, None] * totals[None, :, :], axis=1)
    return (inner + outer[:, None, :]).reshape(rows, columns).astype(jnp.int32)


def dot(left, right, dims=(((1,), (0,)), ((), ()))):
    return lax.dot_general(left, right, dims, preferred_element_type=F32)


def turned(values, cosine, sine):
    return values * cosine + pltpu.roll(values, HD // 2, 1) * sine


def tile_weights(query, key, seg_q, seg_k, first, factor):
    rows, width = query.shape[0], key.shape[0]
    scores = dot(query, key, NT) * factor
    q_place = first + lax.broadcasted_iota(jnp.int32, (rows, width), 0)
    k_place = lax.broadcasted_iota(jnp.int32, (rows, width), 1)
    allowed = k_place <= q_place
    if first >= PROMPT:
        allowed = allowed & ((seg_k < 0) | (seg_k == seg_q))
    scores = jnp.where(allowed, scores, -1e30)
    weights = jnp.exp(scores - jnp.max(scores, axis=1, keepdims=True))
    return weights, jnp.sum(weights, axis=1, keepdims=True)


def attend_kernel(
    tiles,
    factor,
    qp_ref,
    kp_ref,
    vp_ref,
    root_ref,
    key_root_ref,
    gain_ref,
    cos_ref,
    sin_ref,
    sq_ref,
    sk_ref,
    q_ref,
    k_ref,
    v_ref,
    o_ref,
):
    at = pl.program_id(1)
    tile = qp_ref.shape[0]

    @pl.when(at == 0)
    def _():
        keys = kp_ref[...] * key_root_ref[:, 1:2] * gain_ref[1:2]
        k_ref[...] = turned(keys, cos_ref[...], sin_ref[...]).astype(BF)
        v_ref[...] = vp_ref[...].astype(BF)

    for i in range(tiles):

        @pl.when(at == i)
        def _():
            own = slice(i * tile, (i + 1) * tile)
            width = (i + 1) * tile
            queries = qp_ref[...] * root_ref[:, 0:1] * gain_ref[0:1]
            query = turned(queries, cos_ref[own], sin_ref[own]).astype(BF)
            q_ref[...] = query
            weights, total = tile_weights(
                query, k_ref[:width], sq_ref[...], sk_ref[:, :width], i * tile, factor
            )
            o_ref[...] = (dot(weights.astype(BF), v_ref[:width]) / total).astype(BF)


def attend(projected, roots, gains, cosine, sine, seg, width, tile=512):
    rows = projected.shape[0]
    heads, tiles = width // HD, rows // tile
    own = pl.BlockSpec((tile, HD), lambda h, i: (i, h))
    whole = pl.BlockSpec((rows, HD), lambda h, i: (0, h))
    pairs = heads * rows * rows * (tiles + 1) // (2 * tiles)
    return pl.pallas_call(
        functools.partial(attend_kernel, tiles, 1.0 / math.sqrt(HD)),
        out_shape=[jax.ShapeDtypeStruct((rows, width), BF)] * 4,
        grid=(heads, tiles),
        in_specs=[
            own,
            pl.BlockSpec((rows, HD), lambda h, i: (0, heads + h)),
            pl.BlockSpec((rows, HD), lambda h, i: (0, 2 * heads + h)),
            pl.BlockSpec((tile, 2), lambda h, i: (i, 0)),
            pl.BlockSpec((rows, 2), lambda h, i: (0, 0)),
            pl.BlockSpec((2, HD), lambda h, i: (0, h)),
            pl.BlockSpec((rows, HD), lambda h, i: (0, 0)),
            pl.BlockSpec((rows, HD), lambda h, i: (0, 0)),
            pl.BlockSpec((tile, 1), lambda h, i: (i, 0)),
            pl.BlockSpec((1, rows), lambda h, i: (0, 0)),
        ],
        out_specs=[own, whole, whole, own],
        compiler_params=pltpu.CompilerParams(vmem_limit_bytes=48 << 20),
        cost_estimate=pl.CostEstimate(
            flops=4 * pairs * HD, bytes_accessed=20 * rows * width, transcendentals=pairs
        ),
    )(
        projected,
        projected,
        projected,
        roots,
        roots,
        gains,
        cosine,
        sine,
        seg[:, None],
        seg[None, :],
    )


def attend_back_kernel(
    tiles,
    factor,
    q_ref,
    k_ref,
    v_ref,
    d_ref,
    cos_ref,
    sin_ref,
    sq_ref,
    sk_ref,
    dq_ref,
    dk_ref,
    dv_ref,
):
    at = pl.program_id(1)
    tile = q_ref.shape[0]

    @pl.when(at == 0)
    def _():
        dk_ref[...] = jnp.zeros_like(dk_ref)
        dv_ref[...] = jnp.zeros_like(dv_ref)

    for i in range(tiles):

        @pl.when(at == i)
        def _():
            own = slice(i * tile, (i + 1) * tile)
            width = (i + 1) * tile
            query, grad = q_ref[...], d_ref[...]
            weights, total = tile_weights(
                query, k_ref[:width], sq_ref[...], sk_ref[:, :width], i * tile, factor
            )
            weights = weights / total
            grad_weights = dot(grad, v_ref[:width], NT)
            delta = jnp.sum(weights * grad_weights, axis=1, keepdims=True)
            grad_scores = (weights * (grad_weights - delta)).astype(BF)
            grad_query = dot(grad_scores, k_ref[:width]) * factor
            dq_ref[...] = turned(grad_query, cos_ref[own], -sin_ref[own])
            dk_ref[:width] += dot(grad_scores, query, TN)
            dv_ref[:width] += dot(weights.astype(BF), grad, TN)

    @pl.when(at == tiles - 1)
    def _():
        dk_ref[...] = turned(dk_ref[...] * factor, cos_ref[...], -sin_ref[...])


def attend_back(q, k, v, grad, cosine, sine, seg, tile=512):
    rows, width = q.shape
    heads, tiles = width // HD, rows // tile
    own = pl.BlockSpec((tile, HD), lambda h, i: (i, h))
    whole = pl.BlockSpec((rows, HD), lambda h, i: (0, h))
    table = pl.BlockSpec((rows, HD), lambda h, i: (0, 0))
    pairs = heads * rows * rows * (tiles + 1) // (2 * tiles)
    return pl.pallas_call(
        functools.partial(attend_back_kernel, tiles, 1.0 / math.sqrt(HD)),
        out_shape=[jax.ShapeDtypeStruct((rows, width), F32)] * 3,
        grid=(heads, tiles),
        in_specs=[
            own,
            whole,
            whole,
            own,
            table,
            table,
            pl.BlockSpec((tile, 1), lambda h, i: (i, 0)),
            pl.BlockSpec((1, rows), lambda h, i: (0, 0)),
        ],
        out_specs=[own, whole, whole],
        compiler_params=pltpu.CompilerParams(vmem_limit_bytes=48 << 20),
        cost_estimate=pl.CostEstimate(
            flops=10 * pairs * HD, bytes_accessed=20 * rows * width, transcendentals=pairs
        ),
    )(q, k, v, grad, cosine, sine, seg[:, None], seg[None, :])


def pick_rows(tok, low, windows, source_ref, acc_ref):
    last = source_ref.shape[0] - WIN
    span = lax.broadcasted_iota(jnp.int32, (TILE, WIN), 1)

    def window(j):
        base = low + j * WIN
        start = pl.multiple_of(jnp.minimum(base, last), 128)
        match = (tok - start == span) & (tok >= base)
        return dot(match.astype(F32).astype(BF), source_ref[pl.ds(start, WIN), :])

    acc_ref[...] = window(0)

    @pl.loop(1, windows)
    def _(j):
        acc_ref[...] += window(j)

    return acc_ref[...].astype(BF)


def copy_all(copies):
    for copy in copies:
        copy.start()
    for copy in copies:
        copy.wait()


def back_rows_kernel(tiles_ref, low_ref, windows_ref, me_ref, tok_ref, dy_ref, *refs):
    parts, (rows_ref, raw_ref, down_ref, acc_ref, sems) = refs[:-5], refs[-5:]
    i = pl.program_id(0)

    @pl.when(i == 0)
    def _():
        if len(parts) == 1:
            copy_all([pltpu.make_async_copy(parts[0], down_ref, sems.at[0])])
            return
        rows, width = down_ref.shape[0] // 4, down_ref.shape[1] // 2
        copies = []
        for away, part in enumerate(parts):
            owner = pl.multiple_of((me_ref[0] ^ away) * rows, rows)
            for k in range(2):
                copies.append(
                    pltpu.make_async_copy(
                        part.at[pl.ds((k + 1) * rows, rows)],
                        down_ref.at[pl.ds(owner, rows), pl.ds(k * width, width)],
                        sems.at[len(copies)],
                    )
                )
        copy_all(copies)

    @pl.when(i < tiles_ref[0])
    def _():
        rows = pick_rows(tok_ref[...], low_ref[i], windows_ref[i], dy_ref, acc_ref)
        rows_ref[...] = rows
        raw_ref[...] = dot(rows, down_ref[...], NT)

    @pl.when(i >= tiles_ref[0])
    def _():
        rows_ref[...] = jnp.zeros_like(rows_ref)
        raw_ref[...] = jnp.zeros_like(raw_ref)


def back_rows(tables, me, upstream, parts, ff):
    total, width = upstream.shape
    capacity = tables[3].shape[0]
    tile = lambda n: pl.BlockSpec((TILE, n), lambda i, *_: (i, 0))
    once = lambda shape: pl.BlockSpec(shape, lambda i, *_: (0, 0), pipeline_mode=pl.Buffered(1))
    return pl.pallas_call(
        back_rows_kernel,
        out_shape=[
            jax.ShapeDtypeStruct((capacity, width), BF),
            jax.ShapeDtypeStruct((capacity, ff), F32),
            jax.ShapeDtypeStruct((ff, width), BF),
        ],
        grid_spec=pltpu.PrefetchScalarGridSpec(
            num_scalar_prefetch=4,
            grid=(capacity // TILE,),
            in_specs=[tile(1), once((total, width))]
            + [pl.BlockSpec(memory_space=pl.ANY)] * len(parts),
            out_specs=[tile(width), tile(ff), pl.BlockSpec((ff, width), lambda i, *_: (0, 0))],
            scratch_shapes=[
                pltpu.VMEM((TILE, width), F32),
                pltpu.SemaphoreType.DMA((2 * len(parts),)),
            ],
        ),
        compiler_params=pltpu.CompilerParams(vmem_limit_bytes=48 << 20),
        cost_estimate=pl.CostEstimate(
            flops=total * (width * ff + WIN * width),
            bytes_accessed=2 * total * width + 4 * ff * width + capacity * (2 * width + 4 * ff),
            transcendentals=0,
        ),
    )(*tables[:3], me, tables[3], upstream, *parts)


def expert_kernel(
    own, tiles_ref, low_ref, windows_ref, ids_ref, tok_ref, h_ref, router_ref, raw_ref, *refs
):
    parts = refs[:-8]
    rows_ref, hid_ref, dab_ref, dh_ref, share_ref, both_ref, acc_ref, sems = refs[-8:]
    wg_ref, wu_ref = both_ref.at[0], both_ref.at[1]
    i = pl.program_id(0)
    ff = wg_ref.shape[1]

    @pl.when(i == 0)
    def _():
        if len(parts) == 1:
            copy_all([pltpu.make_async_copy(parts[0], both_ref, sems.at[0])])
            return
        rows = wg_ref.shape[0] // 4
        half = rows // 2
        copies = []
        for away in range(4):
            owner = pl.multiple_of((ids_ref[1] ^ away) * rows, rows)
            for part, first, count, which, shift in (
                (parts[away], 0, rows, 0, 0),
                (parts[away], rows, half, 1, 0),
                (parts[4 + away], 0, half, 1, half),
            ):
                copies.append(
                    pltpu.make_async_copy(
                        part.at[pl.ds(first, count)],
                        both_ref.at[which, pl.ds(owner + shift, count)],
                        sems.at[len(copies)],
                    )
                )
        copy_all(copies)

    @pl.when(i < tiles_ref[0])
    def _():
        rows = pick_rows(tok_ref[...], low_ref[i], windows_ref[i], h_ref, acc_ref)
        rows_ref[...] = rows
        logits = dot(rows, router_ref[...])
        probs = jnp.exp(logits - jnp.max(logits, axis=1, keepdims=True))
        column = lax.broadcasted_iota(jnp.int32, probs.shape, 1)
        mine = jnp.sum(jnp.where(column == ids_ref[0] + own, probs, 0.0), axis=1, keepdims=True)
        gate = mine / jnp.sum(probs, axis=1, keepdims=True)
        share = 0.0
        part = ff // 4
        for c in range(4):
            cols = slice(c * part, (c + 1) * part)
            a = dot(rows, wg_ref[:, cols])
            b = dot(rows, wu_ref[:, cols])
            raw = raw_ref[:, cols]
            sig = 1.0 / (1.0 + jnp.exp(-a))
            silu = a * sig
            hid = silu * b
            share += jnp.sum(hid * raw, axis=1, keepdims=True)
            raw = raw * gate
            hid_ref[:, cols] = (hid * gate).astype(BF)
            dab_ref[:, cols] = (raw * b * (sig * (1.0 + a * (1.0 - sig)))).astype(BF)
            dab_ref[:, ff + c * part : ff + (c + 1) * part] = (raw * silu).astype(BF)
        share_ref[...] = share
        dh = dot(dab_ref[:, :ff], wg_ref[...], NT) + dot(dab_ref[:, ff:], wu_ref[...], NT)
        dh_ref[...] = dh.astype(BF)

    @pl.when(i >= tiles_ref[0])
    def _():
        for ref in (rows_ref, hid_ref, dab_ref, dh_ref, share_ref):
            ref[...] = jnp.zeros_like(ref)


def expert_rows(tables, own, ids, hidden, router, parts, raw):
    total, width = hidden.shape
    capacity, ff = raw.shape
    tile = lambda n: pl.BlockSpec((TILE, n), lambda i, *_: (i, 0))
    once = lambda shape: pl.BlockSpec(shape, lambda i, *_: (0, 0), pipeline_mode=pl.Buffered(1))
    made = lambda n, dtype=BF: jax.ShapeDtypeStruct((capacity, n), dtype)
    return pl.pallas_call(
        functools.partial(expert_kernel, own),
        out_shape=[made(width), made(ff), made(2 * ff), made(width), made(1, F32)],
        grid_spec=pltpu.PrefetchScalarGridSpec(
            num_scalar_prefetch=4,
            grid=(capacity // TILE,),
            in_specs=[tile(1), once((total, width)), once(router.shape), tile(ff)]
            + [pl.BlockSpec(memory_space=pl.ANY)] * len(parts),
            out_specs=[tile(width), tile(ff), tile(2 * ff), tile(width), tile(1)],
            scratch_shapes=[
                pltpu.VMEM((2, width, ff), BF),
                pltpu.VMEM((TILE, width), F32),
                pltpu.SemaphoreType.DMA((12,)),
            ],
        ),
        compiler_params=pltpu.CompilerParams(vmem_limit_bytes=56 << 20),
        cost_estimate=pl.CostEstimate(
            flops=total * (4 * width * ff + WIN * width),
            bytes_accessed=2 * total * width + 4 * ff * width + capacity * (4 * width + 10 * ff),
            transcendentals=total * ff,
        ),
    )(*tables[:3], ids, tables[3], hidden, router, raw, *parts)


def combine_kernel(experts, start_ref, more_ref, wide_ref, pos_ref, *refs):
    rows_refs, share_refs = refs[:experts], refs[experts : 2 * experts]
    out_ref, own_ref, acc_ref = refs[2 * experts :]
    i = pl.program_id(0)
    span = lax.broadcasted_iota(jnp.int32, (TILE, TILE), 1)
    wide_span = lax.broadcasted_iota(jnp.int32, (TILE, 384), 1)
    last = rows_refs[0].shape[0] - TILE

    def window(e, j):
        base = start_ref[e, i] + j * TILE
        start = pl.multiple_of(jnp.minimum(base, last), 16)
        pos = pos_ref[:, e : e + 1]
        match = (pos - start == span) & (pos >= base)
        return dot(match.astype(F32).astype(BF), rows_refs[e][pl.ds(start, TILE), :])

    acc_ref[...] = sum(window(e, 0) for e in range(experts))
    for e in range(experts):
        wide = pl.multiple_of(wide_ref[e, i], 128)
        match = pos_ref[:, e : e + 1] - wide == wide_span
        share = share_refs[e][:, pl.ds(wide, 384)]
        own_ref[:, e : e + 1] = jnp.sum(jnp.where(match, share, 0.0), axis=1, keepdims=True)

        @pl.when(more_ref[e, i] > 0)
        def _():
            acc_ref[...] += window(e, 1)

    out_ref[...] = acc_ref[...].astype(BF)


def combine_rows(tables, rows, shares):
    experts, (capacity, width) = len(rows), rows[0].shape
    total = tables[3].shape[0]
    once = lambda shape: pl.BlockSpec(shape, lambda i, *_: (0, 0), pipeline_mode=pl.Buffered(1))
    tile = lambda n: pl.BlockSpec((TILE, n), lambda i, *_: (i, 0))
    return pl.pallas_call(
        functools.partial(combine_kernel, experts),
        out_shape=[
            jax.ShapeDtypeStruct((total, width), BF),
            jax.ShapeDtypeStruct((total, experts), F32),
        ],
        grid_spec=pltpu.PrefetchScalarGridSpec(
            num_scalar_prefetch=3,
            grid=(total // TILE,),
            in_specs=[tile(experts)]
            + [once((capacity, width))] * experts
            + [once((1, capacity))] * experts,
            out_specs=[tile(width), tile(experts)],
            scratch_shapes=[pltpu.VMEM((TILE, width), F32)],
        ),
        compiler_params=pltpu.CompilerParams(vmem_limit_bytes=48 << 20),
        cost_estimate=pl.CostEstimate(
            flops=2 * experts * total * TILE * width,
            bytes_accessed=2 * (experts * capacity + total) * width,
            transcendentals=0,
        ),
    )(*tables, *rows, *shares)


def local(
    tokens,
    cotangent,
    routes,
    block_of_slot,
    cont_seg,
    w_query,
    w_key,
    w_value,
    w_out,
    w_router,
    attn_gain,
    query_gain,
    key_gain,
    ffn_gain,
    w_gate,
    w_up,
    w_down,
):
    ctx_size = lax.axis_size("ctx")
    exp_size = lax.axis_size("exp")
    me = lax.axis_index("ctx")
    exp_index = lax.axis_index("exp")
    tok_rows = tokens.shape[0]
    part_rows = w_query.shape[0]
    own_width = D // ctx_size
    own_heads = HEADS // ctx_size
    experts = w_router.shape[1]
    own_experts = w_gate.shape[0]
    slot_table = block_of_slot[0]
    seg_row = cont_seg[0]
    group_rows = ctx_size * tok_rows
    factor = 1.0 / math.sqrt(HD)

    tokens_group, tokens_there = gather_group(tokens, slot_table, me)
    small = jnp.concatenate(
        [w_router] + [g[:, None] for g in (attn_gain, query_gain, key_gain, ffn_gain)], axis=1
    )
    small = jnp.pad(small, ((0, 0), (0, 128 - small.shape[1])))
    by_owner = jnp.stack(
        [w.reshape(part_rows, ctx_size, own_width) for w in (w_query, w_key, w_value)], axis=2
    )
    by_owner = jnp.swapaxes(by_owner, 0, 1).reshape(ctx_size, part_rows, 3 * own_width)
    by_owner = jnp.concatenate(
        [by_owner, jnp.broadcast_to(small, (ctx_size,) + small.shape)], axis=2
    )
    own_columns = exchange(by_owner, me)
    packed = lax.all_gather(own_columns, "exp", axis=1, tiled=True).reshape(D, 3 * own_width + 128)
    small_full = packed[:, 3 * own_width :]
    router_full = small_full[:, :experts]
    gains = small_full[:, experts : experts + 4].astype(F32)
    gain_attn, gain_ffn = gains[:, 0], gains[:, 3]
    own_gains = lax.dynamic_slice(gains, (me * own_width, 0), (own_width, 4))
    gain_query, gain_key = own_gains[:, 1], own_gains[:, 2]
    out_full = lax.all_gather(w_out, "exp", axis=0, tiled=True)
    routes_all = lax.all_to_all(
        jnp.broadcast_to(routes[None], (exp_size,) + routes.shape),
        "exp",
        split_axis=0,
        concat_axis=0,
        tiled=True,
    ).reshape(exp_size * tok_rows, TOP)
    upstream_all = lax.all_gather(cotangent, "exp", axis=0, tiled=True)
    packs = [pack_expert(w_gate[e], w_up[e], w_down[e]) for e in range(own_experts)]
    if ctx_size == 4:
        ahead = after_all(packs[0], *tokens_there)
        ahead = send_x(ahead[0]), send_y(ahead[1])

    seg_ids = jnp.concatenate([jnp.full((PROMPT,), -1, jnp.int32), seg_row])
    starts = jnp.sum(
        (seg_row[None, :] < jnp.arange(CONT, dtype=jnp.int32)[:, None]).astype(jnp.int32), axis=1
    )
    first_pos = jnp.sum(
        jnp.where(
            seg_row[:, None] == jnp.arange(CONT, dtype=jnp.int32)[None, :], starts[None, :], 0
        ),
        axis=1,
    )
    cont_pos = PROMPT + jnp.arange(CTOK, dtype=jnp.int32) - first_pos
    position = jnp.concatenate([jnp.arange(PROMPT, dtype=jnp.int32), cont_pos])
    cos_part, sin_part = angles(position)
    group_inputs = tokens_group.astype(F32)
    normed_group = group_inputs * inverse_root(group_inputs)
    hidden_one = (normed_group * gain_attn).astype(BF)
    projected = jnp.dot(hidden_one, packed, preferred_element_type=F32)
    query_pre = projected[:, :own_width]
    key_pre = projected[:, own_width : 2 * own_width]
    squares = jnp.stack([jnp.sum(query_pre * query_pre, axis=1), jnp.sum(key_pre * key_pre, axis=1)])
    if ctx_size == 4:
        squares = after(squares, *ahead)
    squares = sum_over_ctx(squares)
    if ctx_size == 4:
        direct = after_all(packs[0], squares)
        direct = send_x(direct[1]), send_y(direct[0])
    roots = lax.rsqrt(squares / D + epsilon)
    root_query, root_key = roots[0][:, None], roots[1][:, None]
    normed_query = query_pre * root_query
    normed_key = key_pre * root_key
    query_rot, key_rot, value_low, context_low = attend(
        projected,
        roots.T,
        jnp.stack([gain_query, gain_key]),
        cos_part,
        sin_part,
        seg_ids,
        own_width,
    )
    branch_part = jnp.dot(context_low, out_full, preferred_element_type=F32)
    if ctx_size == 4:
        branch_part = after(branch_part, *direct)
    branch, unused, unused, branch_there = scatter_group(branch_part, slot_table, me)
    me_table = jnp.reshape(me, (1,)).astype(jnp.int32)
    width = w_gate.shape[2]
    lows, highs, backs = [], [], []
    if ctx_size == 4:
        passed = after_all(ahead, *branch_there)
        passed = send_y(passed[0]), send_x(passed[1])
        lows.append((packs[0][0], ahead[0], direct[1], passed[0]))
        highs.append((packs[0][1], direct[0], ahead[1], passed[1]))
        upstream, first_passed = upstream_all, passed
        for e in range(1, own_experts):
            low, high = after_all(packs[e], *passed)
            ahead = send_x(low), send_y(high)
            direct = send_x(high), send_y(low)
            passed = send_y(ahead[0]), send_x(ahead[1])
            lows.append((packs[e][0], ahead[0], direct[1], passed[0]))
            highs.append((packs[e][1], direct[0], ahead[1], passed[1]))
            upstream = after(upstream, *ahead)
    else:
        for e in range(own_experts):
            both, down = whole_expert(*after_all((w_gate[e], w_up[e], w_down[e]), *branch_there))
            lows.append((both,))
            highs.append((down,))
        upstream = upstream_all
        first_passed = branch_there

    own_ids = exp_index * own_experts + jnp.arange(own_experts, dtype=jnp.int32)
    member = jnp.any(after(routes_all, *first_passed)[:, :, None] == own_ids[None, None, :], axis=1)
    place_of = prefix_count(member)
    capacity = exp_size * 8 * ((5 * tok_rows * TOP // (4 * experts) + 7) // 8)
    row_tiles = (capacity + TILE - 1) // TILE
    capacity = row_tiles * TILE
    all_rows = exp_size * tok_rows
    row_ids = jnp.arange(capacity, dtype=jnp.int32)
    hit = (place_of.T[:, None, :] == row_ids[None, :, None]) & member.T[:, None, :]
    token_ids = jnp.arange(all_rows, dtype=jnp.int32)
    token_of_row = jnp.max(jnp.where(hit, token_ids[None, None, :], -1), axis=2)
    counts = jnp.sum(member.astype(jnp.int32), axis=0)
    used_tiles = (counts + TILE - 1) // TILE
    by_tile = token_of_row.reshape(own_experts * row_tiles, TILE)
    low_token = jnp.maximum(by_tile[:, 0], 0) // 128 * 128
    windows = jnp.maximum((jnp.max(by_tile, axis=1) - low_token) // WIN + 1, 1)
    low_token = low_token.reshape(own_experts, row_tiles)
    windows = windows.reshape(own_experts, row_tiles)
    row_tables = [
        (used_tiles[e : e + 1], low_token[e], windows[e], token_of_row[e][:, None])
        for e in range(own_experts)
    ]
    place_column = jnp.where(member, place_of, NOWHERE)
    first_place = place_of[::TILE].T
    in_tile = jnp.sum(member.reshape(-1, TILE, own_experts).astype(jnp.int32), axis=1).T
    first_row = first_place // 16 * 16
    more_rows = (first_place + in_tile - first_row > TILE).astype(jnp.int32)
    share_row_start = jnp.minimum(first_place // 128 * 128, capacity - 384)
    token_tables = (first_row, more_rows, share_row_start, place_column)

    ids = jnp.stack([own_ids[0], me.astype(jnp.int32)])
    backs.append(back_rows(row_tables[0], me_table, upstream, highs[0], width))

    inputs = tokens.astype(F32)
    middle = inputs + branch
    root_two = inverse_root(middle)
    normed_two = middle * root_two
    hidden_two = (normed_two * gain_ffn).astype(BF)
    hidden_all = lax.all_gather(hidden_two, "exp", axis=0, tiled=True)
    logits = jnp.dot(hidden_two, router_full, preferred_element_type=F32)
    router_prob = jax.nn.softmax(logits, axis=-1)

    every = range(own_experts)
    made = []
    for e in every:
        if e > 0:
            upstream = after(upstream_all, made[-1][3])
            highs[e] = after_all(highs[e], made[-1][3])
            backs.append(back_rows(row_tables[e], me_table, upstream, highs[e], width))
        parts = tuple(lows[e]) + tuple(highs[e]) if ctx_size == 4 else lows[e]
        made.append(
            expert_rows(row_tables[e], e, ids, hidden_all, router_full, parts, backs[e][1])
        )
    shares = [m[4].reshape(1, capacity) for m in made]
    grad_two_part, share_token = combine_rows(token_tables, [m[3] for m in made], shares)
    grad_two = lax.psum_scatter(grad_two_part, "exp", scatter_dimension=0, tiled=True)
    share_back = lax.all_to_all(
        share_token.reshape(exp_size, tok_rows, own_experts),
        "exp",
        split_axis=0,
        concat_axis=0,
        tiled=True,
    )
    grad_prob = jnp.swapaxes(share_back, 0, 1).reshape(tok_rows, experts)
    def weight_grads(e, *others):
        rows, hidden, grad_hidden = after_all(made[e][:3], *others)
        return (
            lax.dot_general(rows, grad_hidden, TN, preferred_element_type=F32).astype(BF),
            lax.dot_general(hidden, backs[e][0], TN, preferred_element_type=F32).astype(BF),
        )

    expert_grads = [weight_grads(0, grad_two_part)]
    results = [
        jnp.dot(
            after(made[e][1], share_back, *expert_grads[0]),
            backs[e][2],
            preferred_element_type=F32,
        ).astype(BF)
        for e in every
    ]
    if ctx_size == 4:
        take = expert_take(expert_grads[0])
        ahead = scatter_ahead(take, me)
        results = after_all(results, *ahead)
    mixture_part, unused = combine_rows(token_tables, results, shares)
    if ctx_size == 4:
        direct = scatter_direct(take, me, mixture_part)
        last = scatter_last(take, me, after_all(ahead, mixture_part))
    else:
        direct, last = scatter_expert_first(expert_grads[0], me), ()
    directs, lasts = [direct], [last]

    mixture = lax.psum_scatter(mixture_part, "exp", scatter_dimension=0, tiled=True)
    output = (middle + mixture.astype(F32)).astype(BF)
    grad_two = after(grad_two, mixture_part).astype(F32)
    grad_logits = (
        router_prob * (grad_prob - jnp.sum(router_prob * grad_prob, axis=-1, keepdims=True))
    ).astype(BF)
    grad_router = jnp.einsum("td,te->ed", hidden_two, grad_logits, preferred_element_type=F32)
    grad_two = grad_two + jnp.einsum(
        "te,de->td", grad_logits, router_full, preferred_element_type=F32
    )
    grad_ffn_gain = jnp.sum(grad_two * normed_two, axis=0)
    grad_middle = cotangent.astype(F32) + norm_back(grad_two * gain_ffn, normed_two, root_two)

    own_grad = after(grad_middle.astype(BF), *directs[0], *lasts[0])
    branch_grad, grad_there = gather_group(own_grad, slot_table, me)
    sums = []
    for e in range(1, own_experts):
        expert_grads.append(weight_grads(e, own_grad))
        sums.append(scatter_expert_first(after_all(expert_grads[e], *grad_there), me))
    grad_context = lax.dot_general(branch_grad, out_full, NT, preferred_element_type=F32).astype(BF)
    out_grad = lax.dot_general(
        context_low, branch_grad, TN, preferred_element_type=F32
    ).astype(BF)
    grad_query_norm, grad_key_norm, grad_value = attend_back(
        query_rot, key_rot, value_low, grad_context, cos_part, sin_part, seg_ids
    )
    grad_query_gain = jnp.sum(grad_query_norm * normed_query, axis=0)
    grad_key_gain = jnp.sum(grad_key_norm * normed_key, axis=0)
    scaled_query = grad_query_norm * gain_query
    scaled_key = grad_key_norm * gain_key
    products = jnp.stack(
        [jnp.sum(scaled_query * normed_query, axis=1), jnp.sum(scaled_key * normed_key, axis=1)]
    )
    products = after(products, out_grad, *(piece for pieces in sums for piece in pieces))
    means = sum_over_ctx(products) / D
    for e in range(1, own_experts):
        ahead, direct = split_sums(sums[e - 1])
        directs.append(direct)
        ahead = after_all(ahead, means)
        take = expert_take(expert_grads[e])
        lasts.append(scatter_last(take, me, ahead) if ctx_size == 4 else ())
    grad_projected = jnp.concatenate(
        [
            root_query * (scaled_query - normed_query * means[0][:, None]),
            root_key * (scaled_key - normed_key * means[1][:, None]),
            grad_value,
        ],
        axis=1,
    ).astype(BF)
    grad_packed = jnp.pad(grad_projected, ((0, 0), (0, 128)))
    grad_one_part = lax.dot_general(grad_packed, packed, NT, preferred_element_type=F32)
    grad_attn_gain = jnp.sum(grad_one_part * normed_group, axis=0)
    qkv_grad = lax.dot_general(hidden_one, grad_projected, TN, preferred_element_type=F32).astype(BF)
    grad_one, one_ahead, one_sent, unused = scatter_group(
        after(grad_one_part, *(piece for pieces in lasts[1:] for piece in pieces)),
        slot_table,
        me,
        joined=True,
    )
    weight_sums = [
        scatter_expert_end(
            expert_grads[e], after_all(directs[e], *one_sent), after_all(lasts[e], *one_sent), me
        )
        for e in every
    ]
    gate_grad, up_grad, down_grad = (jnp.stack(parts) for parts in zip(*weight_sums))
    out_sum = lax.psum_scatter(
        out_grad, "exp", scatter_dimension=0, tiled=True
    ).astype(F32)
    qkv_sum = lax.psum_scatter(
        after(qkv_grad, mixture).reshape(ctx_size, exp_size * part_rows, 3 * own_width),
        "exp",
        scatter_dimension=1,
        tiled=True,
    )
    qkv_own = exchange(qkv_sum, me).astype(F32)
    projection_grads = [
        jnp.swapaxes(qkv_own[:, :, i * own_width : (i + 1) * own_width], 0, 1).reshape(part_rows, D)
        for i in range(3)
    ]
    root_one = inverse_root(inputs)
    normed_one = inputs * root_one
    grad_input = grad_middle + norm_back(grad_one * gain_attn, normed_one, root_one)
    head_gains = lax.dynamic_update_slice(
        jnp.zeros((2, D), F32), jnp.stack([grad_query_gain, grad_key_gain]), (0, me * own_width)
    )
    small_sums = jnp.concatenate(
        [grad_router, jnp.stack([grad_ffn_gain, grad_attn_gain]), head_gains]
    )
    small_sums = sum_to_rows(after(small_sums, *one_sent), me)
    return (
        output,
        grad_input,
        projection_grads[0],
        projection_grads[1],
        projection_grads[2],
        out_sum,
        small_sums[:experts].T,
        small_sums[experts + 1],
        small_sums[experts + 2],
        small_sums[experts + 3],
        small_sums[experts],
        gate_grad,
        up_grad,
        down_grad,
    )


def solution(mesh):
    rows = P(BOTH, None)
    weights = P("exp", "ctx", None)
    in_specs = (
        (rows, rows, rows, P("exp", None), P("exp", None))
        + (rows,) * 5
        + (P(BOTH),) * 4
        + (weights,) * 3
    )
    out_specs = (rows,) * 7 + (P(BOTH),) * 4 + (weights,) * 3
    return jax.shard_map(local, mesh=mesh, in_specs=in_specs, out_specs=out_specs, check_vma=False)
```

```python
import functools
import math

import jax
import jax.numpy as jnp
from jax import lax
from jax.experimental import pallas as pl
from jax.experimental.pallas import tpu as pltpu
from jax.sharding import PartitionSpec as P

D = 2048
HEADS = 16
HD = 128
TOP = 8
PROMPT = 1024
CONT = 2
CTOK = 512

epsilon = 1e-05
rope_base = 10000.0
BF = jnp.bfloat16
F32 = jnp.float32
BOTH = ("ctx", "exp")
X_PAIRS = [(i, i ^ 1) for i in range(4)]
Y_PAIRS = [(i, i ^ 2) for i in range(4)]
XY_PAIRS = [(i, i ^ 3) for i in range(4)]
NT = (((1,), (1,)), ((), ()))
TN = (((0,), (0,)), ((), ()))
TILE = 256
WIN = 768
NOWHERE = -(1 << 20)


def inverse_root(values):
    return lax.rsqrt(jnp.mean(values * values, axis=-1, keepdims=True) + epsilon)


def norm_back(gradient, normed, root_part):
    return root_part * (gradient - normed * jnp.mean(gradient * normed, axis=-1, keepdims=True))


def angles(position):
    half_dim = HD // 2
    inverse = rope_base ** (-2.0 * jnp.arange(half_dim, dtype=F32) / HD)
    phases = position.astype(F32)[:, None] * inverse[None, :]
    cosine, sine = jnp.cos(phases), jnp.sin(phases)
    return jnp.concatenate([cosine, cosine], axis=1), jnp.concatenate([-sine, sine], axis=1)


def send_x(value):
    return lax.ppermute(value, "ctx", X_PAIRS)


def send_y(value):
    return lax.ppermute(value, "ctx", Y_PAIRS)


def send_xy(value):
    return lax.ppermute(value, "ctx", XY_PAIRS)


def after(value, *others):
    return lax.optimization_barrier((value,) + others)[0]


def after_all(values, *others):
    return lax.optimization_barrier(tuple(values) + others)[: len(values)]


def gather_pieces(low, high):
    low_x, high_y = send_x(low), send_y(high)
    high_x, low_y = send_x(high), send_y(low)
    return (low_x, low_y, send_y(low_x)), (high_x, high_y, send_x(high_y))


def scatter_ahead(take, me):
    return send_x(take(me ^ 3, 0).astype(BF)), send_y(take(me ^ 3, 1).astype(BF))


def scatter_direct(take, me, *others):
    low, high = take(me ^ 1, 0).astype(BF), take(me ^ 2, 1).astype(BF)
    if others:
        low, high = after_all((low, high), *others)
    return send_x(low), send_y(high)


def scatter_last_payload(take, me, ahead):
    low = (take(me ^ 2, 0).astype(F32) + ahead[0].astype(F32)).astype(BF)
    high = (take(me ^ 1, 1).astype(F32) + ahead[1].astype(F32)).astype(BF)
    return low, high


def scatter_last(take, me, ahead):
    low, high = scatter_last_payload(take, me, ahead)
    return send_y(low), send_x(high)


def scatter_end(take, me, direct, last):
    return [
        take(me, part).astype(F32) + direct[part].astype(F32) + last[part].astype(F32)
        for part in range(2)
    ]


def exchange(blocks, me):
    if lax.axis_size("ctx") != 4:
        return lax.all_to_all(blocks, "ctx", split_axis=0, concat_axis=0, tiled=True)
    sends = (lambda part: part, send_x, send_y, send_xy)
    parts = [
        send(lax.dynamic_index_in_dim(blocks, me ^ away, 0, keepdims=False))
        for away, send in enumerate(sends)
    ]

    def from_ctx(c):
        chosen = parts[0]
        for away in range(1, 4):
            chosen = jnp.where((me ^ c) == away, parts[away], chosen)
        return chosen

    return jnp.stack([from_ctx(c) for c in range(4)])


def sum_over_ctx(value):
    if lax.axis_size("ctx") != 4:
        return lax.psum(value, "ctx")
    value = value + send_x(value)
    return value + send_y(value)


def sum_to_rows(values, me, *others):
    ctx_size, exp_size = lax.axis_size("ctx"), lax.axis_size("exp")
    count, width = values.shape
    parts = values.reshape(count, ctx_size, exp_size, width // (ctx_size * exp_size))
    parts = jnp.transpose(parts, (2, 1, 0, 3))
    parts = lax.all_to_all(parts, "exp", split_axis=0, concat_axis=0, tiled=True)
    parts = jnp.sum(after(parts, *others), axis=0)
    return jnp.sum(exchange(parts, me), axis=0)


def pack_expert(w_gate, w_up, w_down):
    half, width = w_up.shape[0] // 2, w_up.shape[1]
    low = jnp.concatenate([w_gate, w_up[:half]], axis=0)
    high = jnp.concatenate([w_up[half:], w_down[:, :width], w_down[:, width:]], axis=0)
    return low, high


def whole_expert(w_gate, w_up, w_down):
    return (
        lax.all_gather(jnp.stack([w_gate, w_up]), "ctx", axis=1, tiled=True),
        lax.all_gather(w_down, "ctx", axis=0, tiled=True),
    )


def expert_take(grads):
    gate_up, down = grads
    rows, width = gate_up.shape[0] // 4, gate_up.shape[1] // 2
    half = down.shape[0] // 8

    def take(owner, part):
        first = (2 * owner + part) * half
        return jnp.concatenate(
            [
                lax.dynamic_slice(gate_up, (owner * rows, part * width), (rows, width)),
                lax.dynamic_slice(down, (first, 0), (half, width)),
                lax.dynamic_slice(down, (first, width), (half, width)),
            ],
            axis=0,
        )

    return take


def scatter_expert_first(grads, me):
    if lax.axis_size("ctx") != 4:
        return tuple(
            lax.psum_scatter(grad, "ctx", scatter_dimension=0, tiled=True) for grad in grads
        )
    return scatter_joined(expert_take(grads), me)


def scatter_joined(take, me):
    low, high = joined_payload(take, me)
    return send_x(low), send_y(high)


def joined_payload(take, me):
    low = jnp.stack([take(me ^ 1, 0), take(me ^ 3, 0)]).astype(BF)
    high = jnp.stack([take(me ^ 2, 1), take(me ^ 3, 1)]).astype(BF)
    return low, high


def split_sums(sums):
    if lax.axis_size("ctx") != 4:
        return sums, sums
    return (sums[0][1], sums[1][1]), (sums[0][0], sums[1][0])


def scatter_expert_end(grads, direct, last, me):
    if lax.axis_size("ctx") != 4:
        gate_up, down = (part.astype(F32) for part in direct)
        width = gate_up.shape[1] // 2
        return gate_up[:, :width], gate_up[:, width:], down
    first, second = scatter_end(expert_take(grads), me, direct, last)
    rows, half = grads[0].shape[0] // 4, grads[1].shape[0] // 8
    down = [
        jnp.concatenate([part[rows : rows + half], part[rows + half :]], axis=1)
        for part in (first, second)
    ]
    return first[:rows], second[:rows], jnp.concatenate(down, axis=0)


def pick_blocks(blocks, order):
    return jnp.concatenate(
        [
            lax.dynamic_index_in_dim(blocks, order[i], 0, keepdims=False)
            for i in range(order.shape[0])
        ],
        axis=0,
    )


def gather_group(rows, slot_table, me):
    block = rows.shape[0] // 2
    if lax.axis_size("ctx") != 4:
        blocks = slot_table.shape[0]
        whole = lax.all_gather(rows, "ctx", axis=0, tiled=True).reshape(blocks, block, -1)
        match = slot_table[None, :] == jnp.arange(blocks, dtype=jnp.int32)[:, None]
        order = jnp.sum(jnp.where(match, jnp.arange(blocks, dtype=jnp.int32)[None, :], 0), axis=1)
        return pick_blocks(whole, order), ()
    pieces = gather_pieces(rows[:block], rows[block:])
    whole = jnp.zeros((8 * block, rows.shape[1]), rows.dtype)
    for slot in range(2):
        for away in range(4):
            part = pieces[slot][away - 1] if away else rows[slot * block : (slot + 1) * block]
            start = slot_table[2 * (me ^ away) + slot] * block
            whole = lax.dynamic_update_slice(whole, part, (start, 0))
    return whole, (pieces[0][2], pieces[1][2])


def scatter_group(partial, slot_table, me, joined=False):
    blocks = slot_table.shape[0]
    block = partial.shape[0] // blocks
    if lax.axis_size("ctx") != 4:
        ordered = pick_blocks(partial.reshape(blocks, block, -1), slot_table).astype(BF)
        whole = lax.psum_scatter(ordered, "ctx", scatter_dimension=0, tiled=True)
        return whole.astype(F32), (whole,), (whole,), (whole,)

    def take(owner, part):
        start = slot_table[2 * owner + part] * block
        return lax.dynamic_slice(partial, (start, 0), (block, partial.shape[1]))

    first = ()
    if joined:
        first = joined_payload(take, me)
        ahead, direct = split_sums((send_x(first[0]), send_y(first[1])))
    else:
        ahead, direct = scatter_ahead(take, me), scatter_direct(take, me)
    sent = scatter_last_payload(take, me, ahead)
    last = send_y(sent[0]), send_x(sent[1])
    return jnp.concatenate(scatter_end(take, me, direct, last), axis=0), first, sent, last


def prefix_count(member):
    rows, columns = member.shape
    width = 128
    blocks = rows // width
    ones = member.astype(BF).reshape(blocks, width, columns)
    lower = (
        jnp.arange(width)[:, None] > jnp.arange(width)[None, :]
    ).astype(BF)
    inner = jnp.einsum("pq,bqc->bpc", lower, ones, preferred_element_type=F32)
    totals = jnp.sum(ones.astype(F32), axis=1)
    before = (jnp.arange(blocks)[:, None] > jnp.arange(blocks)[None, :]).astype(F32)
    outer = jnp.sum(before[:, :, None] * totals[None, :, :], axis=1)
    return (inner + outer[:, None, :]).reshape(rows, columns).astype(jnp.int32)


def dot(left, right, dims=(((1,), (0,)), ((), ()))):
    return lax.dot_general(left, right, dims, preferred_element_type=F32)


def turned(values, cosine, sine):
    return values * cosine + pltpu.roll(values, HD // 2, 1) * sine


def tile_weights(query, key, seg_q, seg_k, first, factor):
    rows, width = query.shape[0], key.shape[0]
    scores = dot(query, key, NT) * factor
    q_place = first + lax.broadcasted_iota(jnp.int32, (rows, width), 0)
    k_place = lax.broadcasted_iota(jnp.int32, (rows, width), 1)
    allowed = k_place <= q_place
    if first >= PROMPT:
        allowed = allowed & ((seg_k < 0) | (seg_k == seg_q))
    scores = jnp.where(allowed, scores, -1e30)
    weights = jnp.exp(scores - jnp.max(scores, axis=1, keepdims=True))
    return weights, jnp.sum(weights, axis=1, keepdims=True)


def attend_kernel(
    tiles,
    factor,
    qp_ref,
    kp_ref,
    vp_ref,
    root_ref,
    key_root_ref,
    gain_ref,
    cos_ref,
    sin_ref,
    sq_ref,
    sk_ref,
    q_ref,
    k_ref,
    v_ref,
    o_ref,
):
    at = pl.program_id(1)
    tile = qp_ref.shape[0]

    @pl.when(at == 0)
    def _():
        keys = kp_ref[...] * key_root_ref[:, 1:2] * gain_ref[1:2]
        k_ref[...] = turned(keys, cos_ref[...], sin_ref[...]).astype(BF)
        v_ref[...] = vp_ref[...].astype(BF)

    for i in range(tiles):

        @pl.when(at == i)
        def _():
            own = slice(i * tile, (i + 1) * tile)
            width = (i + 1) * tile
            queries = qp_ref[...] * root_ref[:, 0:1] * gain_ref[0:1]
            query = turned(queries, cos_ref[own], sin_ref[own]).astype(BF)
            q_ref[...] = query
            weights, total = tile_weights(
                query, k_ref[:width], sq_ref[...], sk_ref[:, :width], i * tile, factor
            )
            o_ref[...] = (dot(weights.astype(BF), v_ref[:width]) / total).astype(BF)


def attend(projected, roots, gains, cosine, sine, seg, width, tile=512):
    rows = projected.shape[0]
    heads, tiles = width // HD, rows // tile
    own = pl.BlockSpec((tile, HD), lambda h, i: (i, h))
    whole = pl.BlockSpec((rows, HD), lambda h, i: (0, h))
    pairs = heads * rows * rows * (tiles + 1) // (2 * tiles)
    return pl.pallas_call(
        functools.partial(attend_kernel, tiles, 1.0 / math.sqrt(HD)),
        out_shape=[jax.ShapeDtypeStruct((rows, width), BF)] * 4,
        grid=(heads, tiles),
        in_specs=[
            own,
            pl.BlockSpec((rows, HD), lambda h, i: (0, heads + h)),
            pl.BlockSpec((rows, HD), lambda h, i: (0, 2 * heads + h)),
            pl.BlockSpec((tile, 2), lambda h, i: (i, 0)),
            pl.BlockSpec((rows, 2), lambda h, i: (0, 0)),
            pl.BlockSpec((2, HD), lambda h, i: (0, h)),
            pl.BlockSpec((rows, HD), lambda h, i: (0, 0)),
            pl.BlockSpec((rows, HD), lambda h, i: (0, 0)),
            pl.BlockSpec((tile, 1), lambda h, i: (i, 0)),
            pl.BlockSpec((1, rows), lambda h, i: (0, 0)),
        ],
        out_specs=[own, whole, whole, own],
        compiler_params=pltpu.CompilerParams(vmem_limit_bytes=48 << 20),
        cost_estimate=pl.CostEstimate(
            flops=4 * pairs * HD, bytes_accessed=20 * rows * width, transcendentals=pairs
        ),
    )(
        projected,
        projected,
        projected,
        roots,
        roots,
        gains,
        cosine,
        sine,
        seg[:, None],
        seg[None, :],
    )


def attend_back_kernel(
    tiles,
    factor,
    q_ref,
    k_ref,
    v_ref,
    d_ref,
    cos_ref,
    sin_ref,
    sq_ref,
    sk_ref,
    dq_ref,
    dk_ref,
    dv_ref,
):
    at = pl.program_id(1)
    tile = q_ref.shape[0]

    @pl.when(at == 0)
    def _():
        dk_ref[...] = jnp.zeros_like(dk_ref)
        dv_ref[...] = jnp.zeros_like(dv_ref)

    for i in range(tiles):

        @pl.when(at == i)
        def _():
            own = slice(i * tile, (i + 1) * tile)
            width = (i + 1) * tile
            query, grad = q_ref[...], d_ref[...]
            weights, total = tile_weights(
                query, k_ref[:width], sq_ref[...], sk_ref[:, :width], i * tile, factor
            )
            weights = weights / total
            grad_weights = dot(grad, v_ref[:width], NT)
            delta = jnp.sum(weights * grad_weights, axis=1, keepdims=True)
            grad_scores = (weights * (grad_weights - delta)).astype(BF)
            grad_query = dot(grad_scores, k_ref[:width]) * factor
            dq_ref[...] = turned(grad_query, cos_ref[own], -sin_ref[own])
            dk_ref[:width] += dot(grad_scores, query, TN)
            dv_ref[:width] += dot(weights.astype(BF), grad, TN)

    @pl.when(at == tiles - 1)
    def _():
        dk_ref[...] = turned(dk_ref[...] * factor, cos_ref[...], -sin_ref[...])


def attend_back(q, k, v, grad, cosine, sine, seg, tile=512):
    rows, width = q.shape
    heads, tiles = width // HD, rows // tile
    own = pl.BlockSpec((tile, HD), lambda h, i: (i, h))
    whole = pl.BlockSpec((rows, HD), lambda h, i: (0, h))
    table = pl.BlockSpec((rows, HD), lambda h, i: (0, 0))
    pairs = heads * rows * rows * (tiles + 1) // (2 * tiles)
    return pl.pallas_call(
        functools.partial(attend_back_kernel, tiles, 1.0 / math.sqrt(HD)),
        out_shape=[jax.ShapeDtypeStruct((rows, width), F32)] * 3,
        grid=(heads, tiles),
        in_specs=[
            own,
            whole,
            whole,
            own,
            table,
            table,
            pl.BlockSpec((tile, 1), lambda h, i: (i, 0)),
            pl.BlockSpec((1, rows), lambda h, i: (0, 0)),
        ],
        out_specs=[own, whole, whole],
        compiler_params=pltpu.CompilerParams(vmem_limit_bytes=48 << 20),
        cost_estimate=pl.CostEstimate(
            flops=10 * pairs * HD, bytes_accessed=20 * rows * width, transcendentals=pairs
        ),
    )(q, k, v, grad, cosine, sine, seg[:, None], seg[None, :])


def pick_rows(tok, low, windows, source_ref, acc_ref):
    last = source_ref.shape[0] - WIN
    span = lax.broadcasted_iota(jnp.int32, (TILE, WIN), 1)

    def window(j):
        base = low + j * WIN
        start = pl.multiple_of(jnp.minimum(base, last), 128)
        match = (tok - start == span) & (tok >= base)
        return dot(match.astype(F32).astype(BF), source_ref[pl.ds(start, WIN), :])

    acc_ref[...] = window(0)

    @pl.loop(1, windows)
    def _(j):
        acc_ref[...] += window(j)

    return acc_ref[...].astype(BF)


def copy_all(copies):
    for copy in copies:
        copy.start()
    for copy in copies:
        copy.wait()


def back_rows_kernel(tiles_ref, low_ref, windows_ref, me_ref, tok_ref, dy_ref, *refs):
    parts, (rows_ref, raw_ref, down_ref, acc_ref, sems) = refs[:-5], refs[-5:]
    i = pl.program_id(0)

    @pl.when(i == 0)
    def _():
        if len(parts) == 1:
            copy_all([pltpu.make_async_copy(parts[0], down_ref, sems.at[0])])
            return
        rows, width = down_ref.shape[0] // 4, down_ref.shape[1] // 2
        copies = []
        for away, part in enumerate(parts):
            owner = pl.multiple_of((me_ref[0] ^ away) * rows, rows)
            for k in range(2):
                copies.append(
                    pltpu.make_async_copy(
                        part.at[pl.ds((k + 1) * rows, rows)],
                        down_ref.at[pl.ds(owner, rows), pl.ds(k * width, width)],
                        sems.at[len(copies)],
                    )
                )
        copy_all(copies)

    @pl.when(i < tiles_ref[0])
    def _():
        rows = pick_rows(tok_ref[...], low_ref[i], windows_ref[i], dy_ref, acc_ref)
        rows_ref[...] = rows
        raw_ref[...] = dot(rows, down_ref[...], NT)

    @pl.when(i >= tiles_ref[0])
    def _():
        rows_ref[...] = jnp.zeros_like(rows_ref)
        raw_ref[...] = jnp.zeros_like(raw_ref)


def back_rows(tables, me, upstream, parts, ff):
    total, width = upstream.shape
    capacity = tables[3].shape[0]
    tile = lambda n: pl.BlockSpec((TILE, n), lambda i, *_: (i, 0))
    once = lambda shape: pl.BlockSpec(shape, lambda i, *_: (0, 0), pipeline_mode=pl.Buffered(1))
    return pl.pallas_call(
        back_rows_kernel,
        out_shape=[
            jax.ShapeDtypeStruct((capacity, width), BF),
            jax.ShapeDtypeStruct((capacity, ff), F32),
            jax.ShapeDtypeStruct((ff, width), BF),
        ],
        grid_spec=pltpu.PrefetchScalarGridSpec(
            num_scalar_prefetch=4,
            grid=(capacity // TILE,),
            in_specs=[tile(1), once((total, width))]
            + [pl.BlockSpec(memory_space=pl.ANY)] * len(parts),
            out_specs=[tile(width), tile(ff), pl.BlockSpec((ff, width), lambda i, *_: (0, 0))],
            scratch_shapes=[
                pltpu.VMEM((TILE, width), F32),
                pltpu.SemaphoreType.DMA((2 * len(parts),)),
            ],
        ),
        compiler_params=pltpu.CompilerParams(vmem_limit_bytes=48 << 20),
        cost_estimate=pl.CostEstimate(
            flops=total * (width * ff + WIN * width),
            bytes_accessed=2 * total * width + 4 * ff * width + capacity * (2 * width + 4 * ff),
            transcendentals=0,
        ),
    )(*tables[:3], me, tables[3], upstream, *parts)


def expert_kernel(
    own, tiles_ref, low_ref, windows_ref, ids_ref, tok_ref, h_ref, router_ref, raw_ref, *refs
):
    parts = refs[:-8]
    rows_ref, hid_ref, dab_ref, dh_ref, share_ref, both_ref, acc_ref, sems = refs[-8:]
    wg_ref, wu_ref = both_ref.at[0], both_ref.at[1]
    i = pl.program_id(0)
    ff = wg_ref.shape[1]

    @pl.when(i == 0)
    def _():
        if len(parts) == 1:
            copy_all([pltpu.make_async_copy(parts[0], both_ref, sems.at[0])])
            return
        rows = wg_ref.shape[0] // 4
        half = rows // 2
        copies = []
        for away in range(4):
            owner = pl.multiple_of((ids_ref[1] ^ away) * rows, rows)
            for part, first, count, which, shift in (
                (parts[away], 0, rows, 0, 0),
                (parts[away], rows, half, 1, 0),
                (parts[4 + away], 0, half, 1, half),
            ):
                copies.append(
                    pltpu.make_async_copy(
                        part.at[pl.ds(first, count)],
                        both_ref.at[which, pl.ds(owner + shift, count)],
                        sems.at[len(copies)],
                    )
                )
        copy_all(copies)

    @pl.when(i < tiles_ref[0])
    def _():
        rows = pick_rows(tok_ref[...], low_ref[i], windows_ref[i], h_ref, acc_ref)
        rows_ref[...] = rows
        logits = dot(rows, router_ref[...])
        probs = jnp.exp(logits - jnp.max(logits, axis=1, keepdims=True))
        column = lax.broadcasted_iota(jnp.int32, probs.shape, 1)
        mine = jnp.sum(jnp.where(column == ids_ref[0] + own, probs, 0.0), axis=1, keepdims=True)
        gate = mine / jnp.sum(probs, axis=1, keepdims=True)
        share = 0.0
        part = ff // 4
        for c in range(4):
            cols = slice(c * part, (c + 1) * part)
            a = dot(rows, wg_ref[:, cols])
            b = dot(rows, wu_ref[:, cols])
            raw = raw_ref[:, cols]
            sig = 1.0 / (1.0 + jnp.exp(-a))
            silu = a * sig
            hid = silu * b
            share += jnp.sum(hid * raw, axis=1, keepdims=True)
            raw = raw * gate
            hid_ref[:, cols] = (hid * gate).astype(BF)
            dab_ref[:, cols] = (raw * b * (sig * (1.0 + a * (1.0 - sig)))).astype(BF)
            dab_ref[:, ff + c * part : ff + (c + 1) * part] = (raw * silu).astype(BF)
        share_ref[...] = share
        dh = dot(dab_ref[:, :ff], wg_ref[...], NT) + dot(dab_ref[:, ff:], wu_ref[...], NT)
        dh_ref[...] = dh.astype(BF)

    @pl.when(i >= tiles_ref[0])
    def _():
        for ref in (rows_ref, hid_ref, dab_ref, dh_ref, share_ref):
            ref[...] = jnp.zeros_like(ref)


def expert_rows(tables, own, ids, hidden, router, parts, raw):
    total, width = hidden.shape
    capacity, ff = raw.shape
    tile = lambda n: pl.BlockSpec((TILE, n), lambda i, *_: (i, 0))
    once = lambda shape: pl.BlockSpec(shape, lambda i, *_: (0, 0), pipeline_mode=pl.Buffered(1))
    made = lambda n, dtype=BF: jax.ShapeDtypeStruct((capacity, n), dtype)
    return pl.pallas_call(
        functools.partial(expert_kernel, own),
        out_shape=[made(width), made(ff), made(2 * ff), made(width), made(1, F32)],
        grid_spec=pltpu.PrefetchScalarGridSpec(
            num_scalar_prefetch=4,
            grid=(capacity // TILE,),
            in_specs=[tile(1), once((total, width)), once(router.shape), tile(ff)]
            + [pl.BlockSpec(memory_space=pl.ANY)] * len(parts),
            out_specs=[tile(width), tile(ff), tile(2 * ff), tile(width), tile(1)],
            scratch_shapes=[
                pltpu.VMEM((2, width, ff), BF),
                pltpu.VMEM((TILE, width), F32),
                pltpu.SemaphoreType.DMA((12,)),
            ],
        ),
        compiler_params=pltpu.CompilerParams(vmem_limit_bytes=56 << 20),
        cost_estimate=pl.CostEstimate(
            flops=total * (4 * width * ff + WIN * width),
            bytes_accessed=2 * total * width + 4 * ff * width + capacity * (4 * width + 10 * ff),
            transcendentals=total * ff,
        ),
    )(*tables[:3], ids, tables[3], hidden, router, raw, *parts)


def combine_kernel(experts, start_ref, more_ref, wide_ref, pos_ref, *refs):
    rows_refs, share_refs = refs[:experts], refs[experts : 2 * experts]
    out_ref, own_ref, acc_ref = refs[2 * experts :]
    i = pl.program_id(0)
    span = lax.broadcasted_iota(jnp.int32, (TILE, TILE), 1)
    wide_span = lax.broadcasted_iota(jnp.int32, (TILE, 384), 1)
    last = rows_refs[0].shape[0] - TILE

    def window(e, j):
        base = start_ref[e, i] + j * TILE
        start = pl.multiple_of(jnp.minimum(base, last), 16)
        pos = pos_ref[:, e : e + 1]
        match = (pos - start == span) & (pos >= base)
        return dot(match.astype(F32).astype(BF), rows_refs[e][pl.ds(start, TILE), :])

    acc_ref[...] = sum(window(e, 0) for e in range(experts))
    for e in range(experts):
        wide = pl.multiple_of(wide_ref[e, i], 128)
        match = pos_ref[:, e : e + 1] - wide == wide_span
        share = share_refs[e][:, pl.ds(wide, 384)]
        own_ref[:, e : e + 1] = jnp.sum(jnp.where(match, share, 0.0), axis=1, keepdims=True)

        @pl.when(more_ref[e, i] > 0)
        def _():
            acc_ref[...] += window(e, 1)

    out_ref[...] = acc_ref[...].astype(BF)


def combine_rows(tables, rows, shares):
    experts, (capacity, width) = len(rows), rows[0].shape
    total = tables[3].shape[0]
    once = lambda shape: pl.BlockSpec(shape, lambda i, *_: (0, 0), pipeline_mode=pl.Buffered(1))
    tile = lambda n: pl.BlockSpec((TILE, n), lambda i, *_: (i, 0))
    return pl.pallas_call(
        functools.partial(combine_kernel, experts),
        out_shape=[
            jax.ShapeDtypeStruct((total, width), BF),
            jax.ShapeDtypeStruct((total, experts), F32),
        ],
        grid_spec=pltpu.PrefetchScalarGridSpec(
            num_scalar_prefetch=3,
            grid=(total // TILE,),
            in_specs=[tile(experts)]
            + [once((capacity, width))] * experts
            + [once((1, capacity))] * experts,
            out_specs=[tile(width), tile(experts)],
            scratch_shapes=[pltpu.VMEM((TILE, width), F32)],
        ),
        compiler_params=pltpu.CompilerParams(vmem_limit_bytes=48 << 20),
        cost_estimate=pl.CostEstimate(
            flops=2 * experts * total * TILE * width,
            bytes_accessed=2 * (experts * capacity + total) * width,
            transcendentals=0,
        ),
    )(*tables, *rows, *shares)


def local(
    tokens,
    cotangent,
    routes,
    block_of_slot,
    cont_seg,
    w_query,
    w_key,
    w_value,
    w_out,
    w_router,
    attn_gain,
    query_gain,
    key_gain,
    ffn_gain,
    w_gate,
    w_up,
    w_down,
):
    ctx_size = lax.axis_size("ctx")
    exp_size = lax.axis_size("exp")
    me = lax.axis_index("ctx")
    exp_index = lax.axis_index("exp")
    tok_rows = tokens.shape[0]
    part_rows = w_query.shape[0]
    own_width = D // ctx_size
    own_heads = HEADS // ctx_size
    experts = w_router.shape[1]
    own_experts = w_gate.shape[0]
    slot_table = block_of_slot[0]
    seg_row = cont_seg[0]
    group_rows = ctx_size * tok_rows
    factor = 1.0 / math.sqrt(HD)

    tokens_group, tokens_there = gather_group(tokens, slot_table, me)
    small = jnp.concatenate(
        [w_router] + [g[:, None] for g in (attn_gain, query_gain, key_gain, ffn_gain)], axis=1
    )
    small = jnp.pad(small, ((0, 0), (0, 128 - small.shape[1])))
    by_owner = jnp.stack(
        [w.reshape(part_rows, ctx_size, own_width) for w in (w_query, w_key, w_value)], axis=2
    )
    by_owner = jnp.swapaxes(by_owner, 0, 1).reshape(ctx_size, part_rows, 3 * own_width)
    by_owner = jnp.concatenate(
        [by_owner, jnp.broadcast_to(small, (ctx_size,) + small.shape)], axis=2
    )
    own_columns = exchange(by_owner, me)
    packed = lax.all_gather(own_columns, "exp", axis=1, tiled=True).reshape(D, 3 * own_width + 128)
    small_full = packed[:, 3 * own_width :]
    router_full = small_full[:, :experts]
    gains = small_full[:, experts : experts + 4].astype(F32)
    gain_attn, gain_ffn = gains[:, 0], gains[:, 3]
    own_gains = lax.dynamic_slice(gains, (me * own_width, 0), (own_width, 4))
    gain_query, gain_key = own_gains[:, 1], own_gains[:, 2]
    out_full = lax.all_gather(w_out, "exp", axis=0, tiled=True)
    routes_all = lax.all_to_all(
        jnp.broadcast_to(routes[None], (exp_size,) + routes.shape),
        "exp",
        split_axis=0,
        concat_axis=0,
        tiled=True,
    ).reshape(exp_size * tok_rows, TOP)
    upstream_all = lax.all_gather(cotangent, "exp", axis=0, tiled=True)
    packs = [pack_expert(w_gate[e], w_up[e], w_down[e]) for e in range(own_experts)]
    if ctx_size == 4:
        ahead = after_all(packs[0], *tokens_there)
        ahead = send_x(ahead[0]), send_y(ahead[1])

    seg_ids = jnp.concatenate([jnp.full((PROMPT,), -1, jnp.int32), seg_row])
    starts = jnp.sum(
        (seg_row[None, :] < jnp.arange(CONT, dtype=jnp.int32)[:, None]).astype(jnp.int32), axis=1
    )
    first_pos = jnp.sum(
        jnp.where(
            seg_row[:, None] == jnp.arange(CONT, dtype=jnp.int32)[None, :], starts[None, :], 0
        ),
        axis=1,
    )
    cont_pos = PROMPT + jnp.arange(CTOK, dtype=jnp.int32) - first_pos
    position = jnp.concatenate([jnp.arange(PROMPT, dtype=jnp.int32), cont_pos])
    cos_part, sin_part = angles(position)
    group_inputs = tokens_group.astype(F32)
    normed_group = group_inputs * inverse_root(group_inputs)
    hidden_one = (normed_group * gain_attn).astype(BF)
    projected = jnp.dot(hidden_one, packed, preferred_element_type=F32)
    query_pre = projected[:, :own_width]
    key_pre = projected[:, own_width : 2 * own_width]
    squares = jnp.stack([jnp.sum(query_pre * query_pre, axis=1), jnp.sum(key_pre * key_pre, axis=1)])
    if ctx_size == 4:
        squares = after(squares, *ahead)
    squares = sum_over_ctx(squares)
    if ctx_size == 4:
        direct = after_all(packs[0], squares)
        direct = send_x(direct[1]), send_y(direct[0])
    roots = lax.rsqrt(squares / D + epsilon)
    root_query, root_key = roots[0][:, None], roots[1][:, None]
    normed_query = query_pre * root_query
    normed_key = key_pre * root_key
    query_rot, key_rot, value_low, context_low = attend(
        projected,
        roots.T,
        jnp.stack([gain_query, gain_key]),
        cos_part,
        sin_part,
        seg_ids,
        own_width,
    )
    branch_part = jnp.dot(context_low, out_full, preferred_element_type=F32)
    if ctx_size == 4:
        branch_part = after(branch_part, *direct)
    branch, unused, unused, branch_there = scatter_group(branch_part, slot_table, me)
    me_table = jnp.reshape(me, (1,)).astype(jnp.int32)
    width = w_gate.shape[2]
    lows, highs, backs = [], [], []
    if ctx_size == 4:
        passed = after_all(ahead, *branch_there)
        passed = send_y(passed[0]), send_x(passed[1])
        lows.append((packs[0][0], ahead[0], direct[1], passed[0]))
        highs.append((packs[0][1], direct[0], ahead[1], passed[1]))
        upstream, first_passed = upstream_all, passed
        for e in range(1, own_experts):
            low, high = after_all(packs[e], *passed)
            ahead = send_x(low), send_y(high)
            low, high = after_all((low, high), *ahead)
            direct = send_x(high), send_y(low)
            passed = send_y(ahead[0]), send_x(ahead[1])
            lows.append((packs[e][0], ahead[0], direct[1], passed[0]))
            highs.append((packs[e][1], direct[0], ahead[1], passed[1]))
            upstream = after(upstream, *ahead)
    else:
        for e in range(own_experts):
            both, down = whole_expert(*after_all((w_gate[e], w_up[e], w_down[e]), *branch_there))
            lows.append((both,))
            highs.append((down,))
        upstream = upstream_all
        first_passed = branch_there

    own_ids = exp_index * own_experts + jnp.arange(own_experts, dtype=jnp.int32)
    member = jnp.any(after(routes_all, *first_passed)[:, :, None] == own_ids[None, None, :], axis=1)
    place_of = prefix_count(member)
    capacity = exp_size * 8 * ((5 * tok_rows * TOP // (4 * experts) + 7) // 8)
    row_tiles = (capacity + TILE - 1) // TILE
    capacity = row_tiles * TILE
    all_rows = exp_size * tok_rows
    row_ids = jnp.arange(capacity, dtype=jnp.int32)
    hit = (place_of.T[:, None, :] == row_ids[None, :, None]) & member.T[:, None, :]
    token_ids = jnp.arange(all_rows, dtype=jnp.int32)
    token_of_row = jnp.max(jnp.where(hit, token_ids[None, None, :], -1), axis=2)
    counts = jnp.sum(member.astype(jnp.int32), axis=0)
    used_tiles = (counts + TILE - 1) // TILE
    by_tile = token_of_row.reshape(own_experts * row_tiles, TILE)
    low_token = jnp.maximum(by_tile[:, 0], 0) // 128 * 128
    windows = jnp.maximum((jnp.max(by_tile, axis=1) - low_token) // WIN + 1, 1)
    low_token = low_token.reshape(own_experts, row_tiles)
    windows = windows.reshape(own_experts, row_tiles)
    row_tables = [
        (used_tiles[e : e + 1], low_token[e], windows[e], token_of_row[e][:, None])
        for e in range(own_experts)
    ]
    place_column = jnp.where(member, place_of, NOWHERE)
    first_place = place_of[::TILE].T
    in_tile = jnp.sum(member.reshape(-1, TILE, own_experts).astype(jnp.int32), axis=1).T
    first_row = first_place // 16 * 16
    more_rows = (first_place + in_tile - first_row > TILE).astype(jnp.int32)
    share_row_start = jnp.minimum(first_place // 128 * 128, capacity - 384)
    token_tables = (first_row, more_rows, share_row_start, place_column)

    ids = jnp.stack([own_ids[0], me.astype(jnp.int32)])
    backs.append(back_rows(row_tables[0], me_table, upstream, highs[0], width))

    inputs = tokens.astype(F32)
    middle = inputs + branch
    root_two = inverse_root(middle)
    normed_two = middle * root_two
    hidden_two = (normed_two * gain_ffn).astype(BF)
    hidden_all = lax.all_gather(hidden_two, "exp", axis=0, tiled=True)
    logits = jnp.dot(hidden_two, router_full, preferred_element_type=F32)
    router_prob = jax.nn.softmax(logits, axis=-1)

    every = range(own_experts)
    made = []
    for e in every:
        if e > 0:
            upstream = after(upstream_all, made[-1][3])
            highs[e] = after_all(highs[e], made[-1][3])
            backs.append(back_rows(row_tables[e], me_table, upstream, highs[e], width))
        parts = tuple(lows[e]) + tuple(highs[e]) if ctx_size == 4 else lows[e]
        made.append(
            expert_rows(row_tables[e], e, ids, hidden_all, router_full, parts, backs[e][1])
        )
    shares = [m[4].reshape(1, capacity) for m in made]
    grad_two_part, share_token = combine_rows(token_tables, [m[3] for m in made], shares)
    grad_two = lax.psum_scatter(grad_two_part, "exp", scatter_dimension=0, tiled=True)
    share_back = lax.all_to_all(
        share_token.reshape(exp_size, tok_rows, own_experts),
        "exp",
        split_axis=0,
        concat_axis=0,
        tiled=True,
    )
    grad_prob = jnp.swapaxes(share_back, 0, 1).reshape(tok_rows, experts)
    def weight_grads(e, *others):
        rows, hidden, grad_hidden = after_all(made[e][:3], *others)
        return (
            lax.dot_general(rows, grad_hidden, TN, preferred_element_type=F32).astype(BF),
            lax.dot_general(hidden, backs[e][0], TN, preferred_element_type=F32).astype(BF),
        )

    expert_grads = [weight_grads(0, grad_two_part)]
    if ctx_size == 4:
        take = expert_take(expert_grads[0])
        payload = joined_payload(take, me)
    else:
        payload = expert_grads[0]
    results = [
        jnp.dot(
            after(made[e][1], share_back, *payload), backs[e][2], preferred_element_type=F32
        ).astype(BF)
        for e in every
    ]
    if ctx_size == 4:
        ahead, direct = split_sums((send_x(payload[0]), send_y(payload[1])))
        last = scatter_last_payload(take, me, ahead)
        results = after_all(results, *last)
        last = send_y(last[0]), send_x(last[1])
    else:
        direct, last = scatter_expert_first(expert_grads[0], me), ()
    mixture_part, unused = combine_rows(token_tables, results, shares)
    directs, lasts = [direct], [last]

    mixture = lax.psum_scatter(mixture_part, "exp", scatter_dimension=0, tiled=True)
    output = (middle + mixture.astype(F32)).astype(BF)
    grad_two = after(grad_two, mixture_part).astype(F32)
    grad_logits = (
        router_prob * (grad_prob - jnp.sum(router_prob * grad_prob, axis=-1, keepdims=True))
    ).astype(BF)
    grad_router = jnp.einsum("td,te->ed", hidden_two, grad_logits, preferred_element_type=F32)
    grad_two = grad_two + jnp.einsum(
        "te,de->td", grad_logits, router_full, preferred_element_type=F32
    )
    grad_ffn_gain = jnp.sum(grad_two * normed_two, axis=0)
    grad_middle = cotangent.astype(F32) + norm_back(grad_two * gain_ffn, normed_two, root_two)

    own_grad = after(grad_middle.astype(BF), *directs[0], *lasts[0])
    branch_grad, grad_there = gather_group(own_grad, slot_table, me)
    sums = []
    for e in range(1, own_experts):
        expert_grads.append(weight_grads(e, own_grad))
        sums.append(scatter_expert_first(after_all(expert_grads[e], *grad_there), me))
    grad_context = lax.dot_general(branch_grad, out_full, NT, preferred_element_type=F32).astype(BF)
    out_grad = lax.dot_general(
        context_low, branch_grad, TN, preferred_element_type=F32
    ).astype(BF)
    grad_query_norm, grad_key_norm, grad_value = attend_back(
        query_rot, key_rot, value_low, grad_context, cos_part, sin_part, seg_ids
    )
    grad_query_gain = jnp.sum(grad_query_norm * normed_query, axis=0)
    grad_key_gain = jnp.sum(grad_key_norm * normed_key, axis=0)
    scaled_query = grad_query_norm * gain_query
    scaled_key = grad_key_norm * gain_key
    products = jnp.stack(
        [jnp.sum(scaled_query * normed_query, axis=1), jnp.sum(scaled_key * normed_key, axis=1)]
    )
    weight_sums = [scatter_expert_end(expert_grads[0], directs[0], lasts[0], me)]
    products = after(
        products, out_grad, *weight_sums[0], *(piece for pieces in sums for piece in pieces)
    )
    means = sum_over_ctx(products) / D
    for e in range(1, own_experts):
        ahead, direct = split_sums(sums[e - 1])
        directs.append(direct)
        ahead = after_all(ahead, means)
        take = expert_take(expert_grads[e])
        lasts.append(scatter_last(take, me, ahead) if ctx_size == 4 else ())
    grad_projected = jnp.concatenate(
        [
            root_query * (scaled_query - normed_query * means[0][:, None]),
            root_key * (scaled_key - normed_key * means[1][:, None]),
            grad_value,
        ],
        axis=1,
    ).astype(BF)
    grad_packed = jnp.pad(grad_projected, ((0, 0), (0, 128)))
    grad_one_part = lax.dot_general(grad_packed, packed, NT, preferred_element_type=F32)
    grad_attn_gain = jnp.sum(grad_one_part * normed_group, axis=0)
    qkv_grad = lax.dot_general(hidden_one, grad_projected, TN, preferred_element_type=F32).astype(BF)
    grad_one, one_first, one_sent, unused = scatter_group(
        after(grad_one_part, *(piece for pieces in lasts[1:] for piece in pieces)),
        slot_table,
        me,
        joined=True,
    )
    for e in range(1, own_experts):
        direct, last = after_all(directs[e], *one_sent), after_all(lasts[e], *one_sent)
        weight_sums.append(scatter_expert_end(expert_grads[e], direct, last, me))
    gate_grad, up_grad, down_grad = (jnp.stack(parts) for parts in zip(*weight_sums))
    out_sum = lax.psum_scatter(
        out_grad, "exp", scatter_dimension=0, tiled=True
    ).astype(F32)
    qkv_sum = lax.psum_scatter(
        after(qkv_grad, mixture).reshape(ctx_size, exp_size * part_rows, 3 * own_width),
        "exp",
        scatter_dimension=1,
        tiled=True,
    )
    qkv_own = exchange(qkv_sum, me).astype(F32)
    projection_grads = [
        jnp.swapaxes(qkv_own[:, :, i * own_width : (i + 1) * own_width], 0, 1).reshape(part_rows, D)
        for i in range(3)
    ]
    root_one = inverse_root(inputs)
    normed_one = inputs * root_one
    grad_input = grad_middle + norm_back(grad_one * gain_attn, normed_one, root_one)
    head_gains = lax.dynamic_update_slice(
        jnp.zeros((2, D), F32), jnp.stack([grad_query_gain, grad_key_gain]), (0, me * own_width)
    )
    small_sums = jnp.concatenate(
        [grad_router, jnp.stack([grad_ffn_gain, grad_attn_gain]), head_gains]
    )
    small_sums = sum_to_rows(after(small_sums, *one_first), me, *one_sent)
    return (
        output,
        grad_input,
        projection_grads[0],
        projection_grads[1],
        projection_grads[2],
        out_sum,
        small_sums[:experts].T,
        small_sums[experts + 1],
        small_sums[experts + 2],
        small_sums[experts + 3],
        small_sums[experts],
        gate_grad,
        up_grad,
        down_grad,
    )


def solution(mesh):
    rows = P(BOTH, None)
    weights = P("exp", "ctx", None)
    in_specs = (
        (rows, rows, rows, P("exp", None), P("exp", None))
        + (rows,) * 5
        + (P(BOTH),) * 4
        + (weights,) * 3
    )
    out_specs = (rows,) * 7 + (P(BOTH),) * 4 + (weights,) * 3
    return jax.shard_map(local, mesh=mesh, in_specs=in_specs, out_specs=out_specs, check_vma=False)
```

```python
import functools
import math

import jax
import jax.numpy as jnp
from jax import lax
from jax.experimental import pallas as pl
from jax.experimental.pallas import tpu as pltpu
from jax.sharding import PartitionSpec as P

D = 2048
HEADS = 16
HD = 128
TOP = 8
PROMPT = 1024
CONT = 2
CTOK = 512

epsilon = 1e-05
rope_base = 10000.0
BF = jnp.bfloat16
F32 = jnp.float32
BOTH = ("ctx", "exp")
X_PAIRS = [(i, i ^ 1) for i in range(4)]
Y_PAIRS = [(i, i ^ 2) for i in range(4)]
XY_PAIRS = [(i, i ^ 3) for i in range(4)]
NT = (((1,), (1,)), ((), ()))
TN = (((0,), (0,)), ((), ()))
TILE = 256
WIN = 768
NOWHERE = -(1 << 20)


def inverse_root(values):
    return lax.rsqrt(jnp.mean(values * values, axis=-1, keepdims=True) + epsilon)


def norm_back(gradient, normed, root_part):
    return root_part * (gradient - normed * jnp.mean(gradient * normed, axis=-1, keepdims=True))


def angles(position):
    half_dim = HD // 2
    inverse = rope_base ** (-2.0 * jnp.arange(half_dim, dtype=F32) / HD)
    phases = position.astype(F32)[:, None] * inverse[None, :]
    cosine, sine = jnp.cos(phases), jnp.sin(phases)
    return jnp.concatenate([cosine, cosine], axis=1), jnp.concatenate([-sine, sine], axis=1)


def send_x(value):
    return lax.ppermute(value, "ctx", X_PAIRS)


def send_y(value):
    return lax.ppermute(value, "ctx", Y_PAIRS)


def send_xy(value):
    return lax.ppermute(value, "ctx", XY_PAIRS)


def after(value, *others):
    return lax.optimization_barrier((value,) + others)[0]


def after_all(values, *others):
    return lax.optimization_barrier(tuple(values) + others)[: len(values)]


def gather_pieces(low, high):
    low_x, high_y = send_x(low), send_y(high)
    high_x, low_y = send_x(high), send_y(low)
    return (low_x, low_y, send_y(low_x)), (high_x, high_y, send_x(high_y))


def scatter_ahead(take, me):
    return send_x(take(me ^ 3, 0).astype(BF)), send_y(take(me ^ 3, 1).astype(BF))


def scatter_direct(take, me, *others):
    low, high = take(me ^ 1, 0).astype(BF), take(me ^ 2, 1).astype(BF)
    if others:
        low, high = after_all((low, high), *others)
    return send_x(low), send_y(high)


def scatter_last_payload(take, me, ahead):
    low = (take(me ^ 2, 0).astype(F32) + ahead[0].astype(F32)).astype(BF)
    high = (take(me ^ 1, 1).astype(F32) + ahead[1].astype(F32)).astype(BF)
    return low, high


def scatter_last(take, me, ahead):
    low, high = scatter_last_payload(take, me, ahead)
    return send_y(low), send_x(high)


def scatter_end(take, me, direct, last):
    return [
        take(me, part).astype(F32) + direct[part].astype(F32) + last[part].astype(F32)
        for part in range(2)
    ]


def exchange(blocks, me):
    if lax.axis_size("ctx") != 4:
        return lax.all_to_all(blocks, "ctx", split_axis=0, concat_axis=0, tiled=True)
    sends = (lambda part: part, send_x, send_y, send_xy)
    parts = [
        send(lax.dynamic_index_in_dim(blocks, me ^ away, 0, keepdims=False))
        for away, send in enumerate(sends)
    ]

    def from_ctx(c):
        chosen = parts[0]
        for away in range(1, 4):
            chosen = jnp.where((me ^ c) == away, parts[away], chosen)
        return chosen

    return jnp.stack([from_ctx(c) for c in range(4)])


def sum_over_ctx(value):
    if lax.axis_size("ctx") != 4:
        return lax.psum(value, "ctx")
    value = value + send_x(value)
    return value + send_y(value)


def sum_to_rows(values, me, *others):
    ctx_size, exp_size = lax.axis_size("ctx"), lax.axis_size("exp")
    count, width = values.shape
    parts = values.reshape(count, ctx_size, exp_size, width // (ctx_size * exp_size))
    parts = jnp.transpose(parts, (2, 1, 0, 3))
    parts = lax.all_to_all(parts, "exp", split_axis=0, concat_axis=0, tiled=True)
    parts = jnp.sum(after(parts, *others), axis=0)
    return jnp.sum(exchange(parts, me), axis=0)


def pack_expert(w_gate, w_up, w_down):
    half, width = w_up.shape[0] // 2, w_up.shape[1]
    low = jnp.concatenate([w_gate, w_up[:half]], axis=0)
    high = jnp.concatenate([w_up[half:], w_down[:, :width], w_down[:, width:]], axis=0)
    return low, high


def whole_expert(w_gate, w_up, w_down):
    return (
        lax.all_gather(jnp.stack([w_gate, w_up]), "ctx", axis=1, tiled=True),
        lax.all_gather(w_down, "ctx", axis=0, tiled=True),
    )


def expert_take(grads):
    gate_up, down = grads
    rows, width = gate_up.shape[0] // 4, gate_up.shape[1] // 2
    half = down.shape[0] // 8

    def take(owner, part):
        first = (2 * owner + part) * half
        return jnp.concatenate(
            [
                lax.dynamic_slice(gate_up, (owner * rows, part * width), (rows, width)),
                lax.dynamic_slice(down, (first, 0), (half, width)),
                lax.dynamic_slice(down, (first, width), (half, width)),
            ],
            axis=0,
        )

    return take


def scatter_expert_first(grads, me):
    if lax.axis_size("ctx") != 4:
        return tuple(
            lax.psum_scatter(grad, "ctx", scatter_dimension=0, tiled=True) for grad in grads
        )
    return scatter_joined(expert_take(grads), me)


def scatter_joined(take, me):
    low, high = joined_payload(take, me)
    return send_x(low), send_y(high)


def joined_payload(take, me):
    low = jnp.stack([take(me ^ 1, 0), take(me ^ 3, 0)]).astype(BF)
    high = jnp.stack([take(me ^ 2, 1), take(me ^ 3, 1)]).astype(BF)
    return low, high


def split_sums(sums):
    if lax.axis_size("ctx") != 4:
        return sums, sums
    return (sums[0][1], sums[1][1]), (sums[0][0], sums[1][0])


def scatter_expert_end(grads, direct, last, me):
    if lax.axis_size("ctx") != 4:
        gate_up, down = (part.astype(F32) for part in direct)
        width = gate_up.shape[1] // 2
        return gate_up[:, :width], gate_up[:, width:], down
    first, second = scatter_end(expert_take(grads), me, direct, last)
    rows, half = grads[0].shape[0] // 4, grads[1].shape[0] // 8
    down = [
        jnp.concatenate([part[rows : rows + half], part[rows + half :]], axis=1)
        for part in (first, second)
    ]
    return first[:rows], second[:rows], jnp.concatenate(down, axis=0)


def pick_blocks(blocks, order):
    return jnp.concatenate(
        [
            lax.dynamic_index_in_dim(blocks, order[i], 0, keepdims=False)
            for i in range(order.shape[0])
        ],
        axis=0,
    )


def gather_group(rows, slot_table, me):
    block = rows.shape[0] // 2
    if lax.axis_size("ctx") != 4:
        blocks = slot_table.shape[0]
        whole = lax.all_gather(rows, "ctx", axis=0, tiled=True).reshape(blocks, block, -1)
        match = slot_table[None, :] == jnp.arange(blocks, dtype=jnp.int32)[:, None]
        order = jnp.sum(jnp.where(match, jnp.arange(blocks, dtype=jnp.int32)[None, :], 0), axis=1)
        return pick_blocks(whole, order), ()
    pieces = gather_pieces(rows[:block], rows[block:])
    whole = jnp.zeros((8 * block, rows.shape[1]), rows.dtype)
    for slot in range(2):
        for away in range(4):
            part = pieces[slot][away - 1] if away else rows[slot * block : (slot + 1) * block]
            start = slot_table[2 * (me ^ away) + slot] * block
            whole = lax.dynamic_update_slice(whole, part, (start, 0))
    return whole, (pieces[0][2], pieces[1][2])


def scatter_group(partial, slot_table, me, joined=False):
    blocks = slot_table.shape[0]
    block = partial.shape[0] // blocks
    if lax.axis_size("ctx") != 4:
        ordered = pick_blocks(partial.reshape(blocks, block, -1), slot_table).astype(BF)
        whole = lax.psum_scatter(ordered, "ctx", scatter_dimension=0, tiled=True)
        return whole.astype(F32), (whole,), (whole,), (whole,)

    def take(owner, part):
        start = slot_table[2 * owner + part] * block
        return lax.dynamic_slice(partial, (start, 0), (block, partial.shape[1]))

    first = ()
    if joined:
        first = joined_payload(take, me)
        ahead, direct = split_sums((send_x(first[0]), send_y(first[1])))
    else:
        ahead, direct = scatter_ahead(take, me), scatter_direct(take, me)
    sent = scatter_last_payload(take, me, ahead)
    last = send_y(sent[0]), send_x(sent[1])
    return jnp.concatenate(scatter_end(take, me, direct, last), axis=0), first, sent, last


def prefix_count(member):
    rows, columns = member.shape
    width = 128
    blocks = rows // width
    ones = member.astype(BF).reshape(blocks, width, columns)
    lower = (
        jnp.arange(width)[:, None] > jnp.arange(width)[None, :]
    ).astype(BF)
    inner = jnp.einsum("pq,bqc->bpc", lower, ones, preferred_element_type=F32)
    totals = jnp.sum(ones.astype(F32), axis=1)
    before = (jnp.arange(blocks)[:, None] > jnp.arange(blocks)[None, :]).astype(F32)
    outer = jnp.sum(before[:, :, None] * totals[None, :, :], axis=1)
    return (inner + outer[:, None, :]).reshape(rows, columns).astype(jnp.int32)


def dot(left, right, dims=(((1,), (0,)), ((), ()))):
    return lax.dot_general(left, right, dims, preferred_element_type=F32)


def turned(values, cosine, sine):
    return values * cosine + pltpu.roll(values, HD // 2, 1) * sine


def tile_weights(query, key, seg_q, seg_k, first, factor):
    rows, width = query.shape[0], key.shape[0]
    scores = dot(query, key, NT) * factor
    q_place = first + lax.broadcasted_iota(jnp.int32, (rows, width), 0)
    k_place = lax.broadcasted_iota(jnp.int32, (rows, width), 1)
    allowed = k_place <= q_place
    if first >= PROMPT:
        allowed = allowed & ((seg_k < 0) | (seg_k == seg_q))
    scores = jnp.where(allowed, scores, -1e30)
    weights = jnp.exp(scores - jnp.max(scores, axis=1, keepdims=True))
    return weights, jnp.sum(weights, axis=1, keepdims=True)


def attend_kernel(
    tiles,
    factor,
    qp_ref,
    kp_ref,
    vp_ref,
    root_ref,
    key_root_ref,
    gain_ref,
    cos_ref,
    sin_ref,
    sq_ref,
    sk_ref,
    q_ref,
    k_ref,
    v_ref,
    o_ref,
):
    at = pl.program_id(1)
    tile = qp_ref.shape[0]

    @pl.when(at == 0)
    def _():
        keys = kp_ref[...] * key_root_ref[:, 1:2] * gain_ref[1:2]
        k_ref[...] = turned(keys, cos_ref[...], sin_ref[...]).astype(BF)
        v_ref[...] = vp_ref[...].astype(BF)

    for i in range(tiles):

        @pl.when(at == i)
        def _():
            own = slice(i * tile, (i + 1) * tile)
            width = (i + 1) * tile
            queries = qp_ref[...] * root_ref[:, 0:1] * gain_ref[0:1]
            query = turned(queries, cos_ref[own], sin_ref[own]).astype(BF)
            q_ref[...] = query
            weights, total = tile_weights(
                query, k_ref[:width], sq_ref[...], sk_ref[:, :width], i * tile, factor
            )
            o_ref[...] = (dot(weights.astype(BF), v_ref[:width]) / total).astype(BF)


def attend(projected, roots, gains, cosine, sine, seg, width, tile=512):
    rows = projected.shape[0]
    heads, tiles = width // HD, rows // tile
    own = pl.BlockSpec((tile, HD), lambda h, i: (i, h))
    whole = pl.BlockSpec((rows, HD), lambda h, i: (0, h))
    pairs = heads * rows * rows * (tiles + 1) // (2 * tiles)
    return pl.pallas_call(
        functools.partial(attend_kernel, tiles, 1.0 / math.sqrt(HD)),
        out_shape=[jax.ShapeDtypeStruct((rows, width), BF)] * 4,
        grid=(heads, tiles),
        in_specs=[
            own,
            pl.BlockSpec((rows, HD), lambda h, i: (0, heads + h)),
            pl.BlockSpec((rows, HD), lambda h, i: (0, 2 * heads + h)),
            pl.BlockSpec((tile, 2), lambda h, i: (i, 0)),
            pl.BlockSpec((rows, 2), lambda h, i: (0, 0)),
            pl.BlockSpec((2, HD), lambda h, i: (0, h)),
            pl.BlockSpec((rows, HD), lambda h, i: (0, 0)),
            pl.BlockSpec((rows, HD), lambda h, i: (0, 0)),
            pl.BlockSpec((tile, 1), lambda h, i: (i, 0)),
            pl.BlockSpec((1, rows), lambda h, i: (0, 0)),
        ],
        out_specs=[own, whole, whole, own],
        compiler_params=pltpu.CompilerParams(vmem_limit_bytes=48 << 20),
        cost_estimate=pl.CostEstimate(
            flops=4 * pairs * HD, bytes_accessed=20 * rows * width, transcendentals=pairs
        ),
    )(
        projected,
        projected,
        projected,
        roots,
        roots,
        gains,
        cosine,
        sine,
        seg[:, None],
        seg[None, :],
    )


def attend_back_kernel(
    tiles,
    factor,
    q_ref,
    k_ref,
    v_ref,
    d_ref,
    cos_ref,
    sin_ref,
    sq_ref,
    sk_ref,
    dq_ref,
    dk_ref,
    dv_ref,
):
    at = pl.program_id(1)
    tile = q_ref.shape[0]

    @pl.when(at == 0)
    def _():
        dk_ref[...] = jnp.zeros_like(dk_ref)
        dv_ref[...] = jnp.zeros_like(dv_ref)

    for i in range(tiles):

        @pl.when(at == i)
        def _():
            own = slice(i * tile, (i + 1) * tile)
            width = (i + 1) * tile
            query, grad = q_ref[...], d_ref[...]
            weights, total = tile_weights(
                query, k_ref[:width], sq_ref[...], sk_ref[:, :width], i * tile, factor
            )
            weights = weights / total
            grad_weights = dot(grad, v_ref[:width], NT)
            delta = jnp.sum(weights * grad_weights, axis=1, keepdims=True)
            grad_scores = (weights * (grad_weights - delta)).astype(BF)
            grad_query = dot(grad_scores, k_ref[:width]) * factor
            dq_ref[...] = turned(grad_query, cos_ref[own], -sin_ref[own])
            dk_ref[:width] += dot(grad_scores, query, TN)
            dv_ref[:width] += dot(weights.astype(BF), grad, TN)

    @pl.when(at == tiles - 1)
    def _():
        dk_ref[...] = turned(dk_ref[...] * factor, cos_ref[...], -sin_ref[...])


def attend_back(q, k, v, grad, cosine, sine, seg, tile=512):
    rows, width = q.shape
    heads, tiles = width // HD, rows // tile
    own = pl.BlockSpec((tile, HD), lambda h, i: (i, h))
    whole = pl.BlockSpec((rows, HD), lambda h, i: (0, h))
    table = pl.BlockSpec((rows, HD), lambda h, i: (0, 0))
    pairs = heads * rows * rows * (tiles + 1) // (2 * tiles)
    return pl.pallas_call(
        functools.partial(attend_back_kernel, tiles, 1.0 / math.sqrt(HD)),
        out_shape=[jax.ShapeDtypeStruct((rows, width), F32)] * 3,
        grid=(heads, tiles),
        in_specs=[
            own,
            whole,
            whole,
            own,
            table,
            table,
            pl.BlockSpec((tile, 1), lambda h, i: (i, 0)),
            pl.BlockSpec((1, rows), lambda h, i: (0, 0)),
        ],
        out_specs=[own, whole, whole],
        compiler_params=pltpu.CompilerParams(vmem_limit_bytes=48 << 20),
        cost_estimate=pl.CostEstimate(
            flops=10 * pairs * HD, bytes_accessed=20 * rows * width, transcendentals=pairs
        ),
    )(q, k, v, grad, cosine, sine, seg[:, None], seg[None, :])


def pick_rows(tok, low, windows, source_ref, acc_ref):
    last = source_ref.shape[0] - WIN
    span = lax.broadcasted_iota(jnp.int32, (TILE, WIN), 1)

    def window(j):
        base = low + j * WIN
        start = pl.multiple_of(jnp.minimum(base, last), 128)
        match = (tok - start == span) & (tok >= base)
        return dot(match.astype(F32).astype(BF), source_ref[pl.ds(start, WIN), :])

    acc_ref[...] = window(0)

    @pl.loop(1, windows)
    def _(j):
        acc_ref[...] += window(j)

    return acc_ref[...].astype(BF)


def copy_all(copies):
    for copy in copies:
        copy.start()
    for copy in copies:
        copy.wait()


def back_rows_kernel(tiles_ref, low_ref, windows_ref, me_ref, tok_ref, dy_ref, *refs):
    parts, (rows_ref, raw_ref, down_ref, acc_ref, sems) = refs[:-5], refs[-5:]
    i = pl.program_id(0)

    @pl.when(i == 0)
    def _():
        if len(parts) == 1:
            copy_all([pltpu.make_async_copy(parts[0], down_ref, sems.at[0])])
            return
        rows, width = down_ref.shape[0] // 4, down_ref.shape[1] // 2
        copies = []
        for away, part in enumerate(parts):
            owner = pl.multiple_of((me_ref[0] ^ away) * rows, rows)
            for k in range(2):
                copies.append(
                    pltpu.make_async_copy(
                        part.at[pl.ds((k + 1) * rows, rows)],
                        down_ref.at[pl.ds(owner, rows), pl.ds(k * width, width)],
                        sems.at[len(copies)],
                    )
                )
        copy_all(copies)

    @pl.when(i < tiles_ref[0])
    def _():
        rows = pick_rows(tok_ref[...], low_ref[i], windows_ref[i], dy_ref, acc_ref)
        rows_ref[...] = rows
        raw_ref[...] = dot(rows, down_ref[...], NT)

    @pl.when(i >= tiles_ref[0])
    def _():
        rows_ref[...] = jnp.zeros_like(rows_ref)
        raw_ref[...] = jnp.zeros_like(raw_ref)


def back_rows(tables, me, upstream, parts, ff):
    total, width = upstream.shape
    capacity = tables[3].shape[0]
    tile = lambda n: pl.BlockSpec((TILE, n), lambda i, *_: (i, 0))
    once = lambda shape: pl.BlockSpec(shape, lambda i, *_: (0, 0), pipeline_mode=pl.Buffered(1))
    return pl.pallas_call(
        back_rows_kernel,
        out_shape=[
            jax.ShapeDtypeStruct((capacity, width), BF),
            jax.ShapeDtypeStruct((capacity, ff), F32),
            jax.ShapeDtypeStruct((ff, width), BF),
        ],
        grid_spec=pltpu.PrefetchScalarGridSpec(
            num_scalar_prefetch=4,
            grid=(capacity // TILE,),
            in_specs=[tile(1), once((total, width))]
            + [pl.BlockSpec(memory_space=pl.ANY)] * len(parts),
            out_specs=[tile(width), tile(ff), pl.BlockSpec((ff, width), lambda i, *_: (0, 0))],
            scratch_shapes=[
                pltpu.VMEM((TILE, width), F32),
                pltpu.SemaphoreType.DMA((2 * len(parts),)),
            ],
        ),
        compiler_params=pltpu.CompilerParams(vmem_limit_bytes=48 << 20),
        cost_estimate=pl.CostEstimate(
            flops=total * (width * ff + WIN * width),
            bytes_accessed=2 * total * width + 4 * ff * width + capacity * (2 * width + 4 * ff),
            transcendentals=0,
        ),
    )(*tables[:3], me, tables[3], upstream, *parts)


def expert_kernel(
    own, tiles_ref, low_ref, windows_ref, ids_ref, tok_ref, h_ref, router_ref, raw_ref, *refs
):
    parts = refs[:-8]
    rows_ref, hid_ref, dab_ref, dh_ref, share_ref, both_ref, acc_ref, sems = refs[-8:]
    wg_ref, wu_ref = both_ref.at[0], both_ref.at[1]
    i = pl.program_id(0)
    ff = wg_ref.shape[1]

    @pl.when(i == 0)
    def _():
        if len(parts) == 1:
            copy_all([pltpu.make_async_copy(parts[0], both_ref, sems.at[0])])
            return
        rows = wg_ref.shape[0] // 4
        half = rows // 2
        copies = []
        for away in range(4):
            owner = pl.multiple_of((ids_ref[1] ^ away) * rows, rows)
            for part, first, count, which, shift in (
                (parts[away], 0, rows, 0, 0),
                (parts[away], rows, half, 1, 0),
                (parts[4 + away], 0, half, 1, half),
            ):
                copies.append(
                    pltpu.make_async_copy(
                        part.at[pl.ds(first, count)],
                        both_ref.at[which, pl.ds(owner + shift, count)],
                        sems.at[len(copies)],
                    )
                )
        copy_all(copies)

    @pl.when(i < tiles_ref[0])
    def _():
        rows = pick_rows(tok_ref[...], low_ref[i], windows_ref[i], h_ref, acc_ref)
        rows_ref[...] = rows
        logits = dot(rows, router_ref[...])
        probs = jnp.exp(logits - jnp.max(logits, axis=1, keepdims=True))
        column = lax.broadcasted_iota(jnp.int32, probs.shape, 1)
        mine = jnp.sum(jnp.where(column == ids_ref[0] + own, probs, 0.0), axis=1, keepdims=True)
        gate = mine / jnp.sum(probs, axis=1, keepdims=True)
        share = 0.0
        part = ff // 4
        for c in range(4):
            cols = slice(c * part, (c + 1) * part)
            a = dot(rows, wg_ref[:, cols])
            b = dot(rows, wu_ref[:, cols])
            raw = raw_ref[:, cols]
            sig = 1.0 / (1.0 + jnp.exp(-a))
            silu = a * sig
            hid = silu * b
            share += jnp.sum(hid * raw, axis=1, keepdims=True)
            raw = raw * gate
            hid_ref[:, cols] = (hid * gate).astype(BF)
            dab_ref[:, cols] = (raw * b * (sig * (1.0 + a * (1.0 - sig)))).astype(BF)
            dab_ref[:, ff + c * part : ff + (c + 1) * part] = (raw * silu).astype(BF)
        share_ref[...] = share
        dh = dot(dab_ref[:, :ff], wg_ref[...], NT) + dot(dab_ref[:, ff:], wu_ref[...], NT)
        dh_ref[...] = dh.astype(BF)

    @pl.when(i >= tiles_ref[0])
    def _():
        for ref in (rows_ref, hid_ref, dab_ref, dh_ref, share_ref):
            ref[...] = jnp.zeros_like(ref)


def expert_rows(tables, own, ids, hidden, router, parts, raw):
    total, width = hidden.shape
    capacity, ff = raw.shape
    tile = lambda n: pl.BlockSpec((TILE, n), lambda i, *_: (i, 0))
    once = lambda shape: pl.BlockSpec(shape, lambda i, *_: (0, 0), pipeline_mode=pl.Buffered(1))
    made = lambda n, dtype=BF: jax.ShapeDtypeStruct((capacity, n), dtype)
    return pl.pallas_call(
        functools.partial(expert_kernel, own),
        out_shape=[made(width), made(ff), made(2 * ff), made(width), made(1, F32)],
        grid_spec=pltpu.PrefetchScalarGridSpec(
            num_scalar_prefetch=4,
            grid=(capacity // TILE,),
            in_specs=[tile(1), once((total, width)), once(router.shape), tile(ff)]
            + [pl.BlockSpec(memory_space=pl.ANY)] * len(parts),
            out_specs=[tile(width), tile(ff), tile(2 * ff), tile(width), tile(1)],
            scratch_shapes=[
                pltpu.VMEM((2, width, ff), BF),
                pltpu.VMEM((TILE, width), F32),
                pltpu.SemaphoreType.DMA((12,)),
            ],
        ),
        compiler_params=pltpu.CompilerParams(vmem_limit_bytes=56 << 20),
        cost_estimate=pl.CostEstimate(
            flops=total * (4 * width * ff + WIN * width),
            bytes_accessed=2 * total * width + 4 * ff * width + capacity * (4 * width + 10 * ff),
            transcendentals=total * ff,
        ),
    )(*tables[:3], ids, tables[3], hidden, router, raw, *parts)


def combine_kernel(experts, start_ref, more_ref, wide_ref, pos_ref, *refs):
    rows_refs, share_refs = refs[:experts], refs[experts : 2 * experts]
    out_ref, own_ref, acc_ref = refs[2 * experts :]
    i = pl.program_id(0)
    span = lax.broadcasted_iota(jnp.int32, (TILE, TILE), 1)
    wide_span = lax.broadcasted_iota(jnp.int32, (TILE, 384), 1)
    last = rows_refs[0].shape[0] - TILE

    def window(e, j):
        base = start_ref[e, i] + j * TILE
        start = pl.multiple_of(jnp.minimum(base, last), 16)
        pos = pos_ref[:, e : e + 1]
        match = (pos - start == span) & (pos >= base)
        return dot(match.astype(F32).astype(BF), rows_refs[e][pl.ds(start, TILE), :])

    acc_ref[...] = sum(window(e, 0) for e in range(experts))
    for e in range(experts):
        wide = pl.multiple_of(wide_ref[e, i], 128)
        match = pos_ref[:, e : e + 1] - wide == wide_span
        share = share_refs[e][:, pl.ds(wide, 384)]
        own_ref[:, e : e + 1] = jnp.sum(jnp.where(match, share, 0.0), axis=1, keepdims=True)

        @pl.when(more_ref[e, i] > 0)
        def _():
            acc_ref[...] += window(e, 1)

    out_ref[...] = acc_ref[...].astype(BF)


def combine_rows(tables, rows, shares):
    experts, (capacity, width) = len(rows), rows[0].shape
    total = tables[3].shape[0]
    once = lambda shape: pl.BlockSpec(shape, lambda i, *_: (0, 0), pipeline_mode=pl.Buffered(1))
    tile = lambda n: pl.BlockSpec((TILE, n), lambda i, *_: (i, 0))
    return pl.pallas_call(
        functools.partial(combine_kernel, experts),
        out_shape=[
            jax.ShapeDtypeStruct((total, width), BF),
            jax.ShapeDtypeStruct((total, experts), F32),
        ],
        grid_spec=pltpu.PrefetchScalarGridSpec(
            num_scalar_prefetch=3,
            grid=(total // TILE,),
            in_specs=[tile(experts)]
            + [once((capacity, width))] * experts
            + [once((1, capacity))] * experts,
            out_specs=[tile(width), tile(experts)],
            scratch_shapes=[pltpu.VMEM((TILE, width), F32)],
        ),
        compiler_params=pltpu.CompilerParams(vmem_limit_bytes=48 << 20),
        cost_estimate=pl.CostEstimate(
            flops=2 * experts * total * TILE * width,
            bytes_accessed=2 * (experts * capacity + total) * width,
            transcendentals=0,
        ),
    )(*tables, *rows, *shares)


def local(
    tokens,
    cotangent,
    routes,
    block_of_slot,
    cont_seg,
    w_query,
    w_key,
    w_value,
    w_out,
    w_router,
    attn_gain,
    query_gain,
    key_gain,
    ffn_gain,
    w_gate,
    w_up,
    w_down,
):
    ctx_size = lax.axis_size("ctx")
    exp_size = lax.axis_size("exp")
    me = lax.axis_index("ctx")
    exp_index = lax.axis_index("exp")
    tok_rows = tokens.shape[0]
    part_rows = w_query.shape[0]
    own_width = D // ctx_size
    own_heads = HEADS // ctx_size
    experts = w_router.shape[1]
    own_experts = w_gate.shape[0]
    slot_table = block_of_slot[0]
    seg_row = cont_seg[0]
    group_rows = ctx_size * tok_rows
    factor = 1.0 / math.sqrt(HD)

    tokens_group, tokens_there = gather_group(tokens, slot_table, me)
    small = jnp.concatenate(
        [w_router] + [g[:, None] for g in (attn_gain, query_gain, key_gain, ffn_gain)], axis=1
    )
    small = jnp.pad(small, ((0, 0), (0, 128 - small.shape[1])))
    by_owner = jnp.stack(
        [w.reshape(part_rows, ctx_size, own_width) for w in (w_query, w_key, w_value)], axis=2
    )
    by_owner = jnp.swapaxes(by_owner, 0, 1).reshape(ctx_size, part_rows, 3 * own_width)
    by_owner = jnp.concatenate(
        [by_owner, jnp.broadcast_to(small, (ctx_size,) + small.shape)], axis=2
    )
    out_full = lax.all_gather(w_out, "exp", axis=0, tiled=True)
    own_columns, out_full = after_all((exchange(by_owner, me), out_full))
    packed = lax.all_gather(own_columns, "exp", axis=1, tiled=True).reshape(D, 3 * own_width + 128)
    small_full = packed[:, 3 * own_width :]
    router_full = small_full[:, :experts]
    gains = small_full[:, experts : experts + 4].astype(F32)
    gain_attn, gain_ffn = gains[:, 0], gains[:, 3]
    own_gains = lax.dynamic_slice(gains, (me * own_width, 0), (own_width, 4))
    gain_query, gain_key = own_gains[:, 1], own_gains[:, 2]
    routes_all = lax.all_to_all(
        jnp.broadcast_to(routes[None], (exp_size,) + routes.shape),
        "exp",
        split_axis=0,
        concat_axis=0,
        tiled=True,
    ).reshape(exp_size * tok_rows, TOP)
    upstream_all = lax.all_gather(cotangent, "exp", axis=0, tiled=True)
    packs = [pack_expert(w_gate[e], w_up[e], w_down[e]) for e in range(own_experts)]
    if ctx_size == 4:
        ahead = after_all(packs[0], *tokens_there)
        ahead = send_x(ahead[0]), send_y(ahead[1])

    seg_ids = jnp.concatenate([jnp.full((PROMPT,), -1, jnp.int32), seg_row])
    starts = jnp.sum(
        (seg_row[None, :] < jnp.arange(CONT, dtype=jnp.int32)[:, None]).astype(jnp.int32), axis=1
    )
    first_pos = jnp.sum(
        jnp.where(
            seg_row[:, None] == jnp.arange(CONT, dtype=jnp.int32)[None, :], starts[None, :], 0
        ),
        axis=1,
    )
    cont_pos = PROMPT + jnp.arange(CTOK, dtype=jnp.int32) - first_pos
    position = jnp.concatenate([jnp.arange(PROMPT, dtype=jnp.int32), cont_pos])
    cos_part, sin_part = angles(position)
    group_inputs = tokens_group.astype(F32)
    normed_group = group_inputs * inverse_root(group_inputs)
    hidden_one = (normed_group * gain_attn).astype(BF)
    projected = jnp.dot(hidden_one, packed, preferred_element_type=F32)
    query_pre = projected[:, :own_width]
    key_pre = projected[:, own_width : 2 * own_width]
    squares = jnp.stack([jnp.sum(query_pre * query_pre, axis=1), jnp.sum(key_pre * key_pre, axis=1)])
    if ctx_size == 4:
        squares = after(squares, *ahead)
    squares = sum_over_ctx(squares)
    if ctx_size == 4:
        direct = after_all(packs[0], squares)
        direct = send_x(direct[1]), send_y(direct[0])
    roots = lax.rsqrt(squares / D + epsilon)
    root_query, root_key = roots[0][:, None], roots[1][:, None]
    normed_query = query_pre * root_query
    normed_key = key_pre * root_key
    query_rot, key_rot, value_low, context_low = attend(
        projected,
        roots.T,
        jnp.stack([gain_query, gain_key]),
        cos_part,
        sin_part,
        seg_ids,
        own_width,
    )
    branch_part = jnp.dot(context_low, out_full, preferred_element_type=F32)
    if ctx_size == 4:
        branch_part = after(branch_part, *direct)
    branch, unused, unused, branch_there = scatter_group(branch_part, slot_table, me)
    me_table = jnp.reshape(me, (1,)).astype(jnp.int32)
    width = w_gate.shape[2]
    lows, highs, backs = [], [], []
    if ctx_size == 4:
        passed = after_all(ahead, *branch_there)
        passed = send_y(passed[0]), send_x(passed[1])
        lows.append((packs[0][0], ahead[0], direct[1], passed[0]))
        highs.append((packs[0][1], direct[0], ahead[1], passed[1]))
        upstream, first_passed = upstream_all, passed
        for e in range(1, own_experts):
            low, high = after_all(packs[e], *passed)
            ahead = send_x(low), send_y(high)
            low, high = after_all((low, high), *ahead)
            direct = send_x(high), send_y(low)
            passed = send_y(ahead[0]), send_x(ahead[1])
            lows.append((packs[e][0], ahead[0], direct[1], passed[0]))
            highs.append((packs[e][1], direct[0], ahead[1], passed[1]))
            upstream = after(upstream, *ahead)
    else:
        for e in range(own_experts):
            both, down = whole_expert(*after_all((w_gate[e], w_up[e], w_down[e]), *branch_there))
            lows.append((both,))
            highs.append((down,))
        upstream = upstream_all
        first_passed = branch_there

    own_ids = exp_index * own_experts + jnp.arange(own_experts, dtype=jnp.int32)
    member = jnp.any(after(routes_all, *first_passed)[:, :, None] == own_ids[None, None, :], axis=1)
    place_of = prefix_count(member)
    capacity = exp_size * 8 * ((5 * tok_rows * TOP // (4 * experts) + 7) // 8)
    row_tiles = (capacity + TILE - 1) // TILE
    capacity = row_tiles * TILE
    all_rows = exp_size * tok_rows
    row_ids = jnp.arange(capacity, dtype=jnp.int32)
    hit = (place_of.T[:, None, :] == row_ids[None, :, None]) & member.T[:, None, :]
    token_ids = jnp.arange(all_rows, dtype=jnp.int32)
    token_of_row = jnp.max(jnp.where(hit, token_ids[None, None, :], -1), axis=2)
    counts = jnp.sum(member.astype(jnp.int32), axis=0)
    used_tiles = (counts + TILE - 1) // TILE
    by_tile = token_of_row.reshape(own_experts * row_tiles, TILE)
    low_token = jnp.maximum(by_tile[:, 0], 0) // 128 * 128
    windows = jnp.maximum((jnp.max(by_tile, axis=1) - low_token) // WIN + 1, 1)
    low_token = low_token.reshape(own_experts, row_tiles)
    windows = windows.reshape(own_experts, row_tiles)
    row_tables = [
        (used_tiles[e : e + 1], low_token[e], windows[e], token_of_row[e][:, None])
        for e in range(own_experts)
    ]
    place_column = jnp.where(member, place_of, NOWHERE)
    first_place = place_of[::TILE].T
    in_tile = jnp.sum(member.reshape(-1, TILE, own_experts).astype(jnp.int32), axis=1).T
    first_row = first_place // 16 * 16
    more_rows = (first_place + in_tile - first_row > TILE).astype(jnp.int32)
    share_row_start = jnp.minimum(first_place // 128 * 128, capacity - 384)
    token_tables = (first_row, more_rows, share_row_start, place_column)

    ids = jnp.stack([own_ids[0], me.astype(jnp.int32)])
    backs.append(back_rows(row_tables[0], me_table, upstream, highs[0], width))

    inputs = tokens.astype(F32)
    middle = inputs + branch
    root_two = inverse_root(middle)
    normed_two = middle * root_two
    hidden_two = (normed_two * gain_ffn).astype(BF)
    hidden_all = lax.all_gather(hidden_two, "exp", axis=0, tiled=True)
    logits = jnp.dot(hidden_two, router_full, preferred_element_type=F32)
    router_prob = jax.nn.softmax(logits, axis=-1)

    every = range(own_experts)
    made = []
    for e in every:
        if e > 0:
            upstream = after(upstream_all, made[-1][3])
            highs[e] = after_all(highs[e], made[-1][3])
            backs.append(back_rows(row_tables[e], me_table, upstream, highs[e], width))
        parts = tuple(lows[e]) + tuple(highs[e]) if ctx_size == 4 else lows[e]
        made.append(
            expert_rows(row_tables[e], e, ids, hidden_all, router_full, parts, backs[e][1])
        )
    shares = [m[4].reshape(1, capacity) for m in made]
    grad_two_part, share_token = combine_rows(token_tables, [m[3] for m in made], shares)
    grad_two = lax.psum_scatter(grad_two_part, "exp", scatter_dimension=0, tiled=True)
    def weight_grads(e, *others):
        rows, hidden, grad_hidden = after_all(made[e][:3], *others)
        return (
            lax.dot_general(rows, grad_hidden, TN, preferred_element_type=F32).astype(BF),
            lax.dot_general(hidden, backs[e][0], TN, preferred_element_type=F32).astype(BF),
        )

    expert_grads = [weight_grads(0, grad_two_part)]
    if ctx_size == 4:
        take = expert_take(expert_grads[0])
        payload = joined_payload(take, me)
    else:
        payload = expert_grads[0]
    results = [
        jnp.dot(
            after(made[e][1], *payload), backs[e][2], preferred_element_type=F32
        ).astype(BF)
        for e in every
    ]
    share_back = lax.all_to_all(
        after(share_token, *results).reshape(exp_size, tok_rows, own_experts),
        "exp",
        split_axis=0,
        concat_axis=0,
        tiled=True,
    )
    grad_prob = jnp.swapaxes(share_back, 0, 1).reshape(tok_rows, experts)
    if ctx_size == 4:
        ahead, direct = split_sums((send_x(payload[0]), send_y(payload[1])))
        last = scatter_last_payload(take, me, ahead)
        results = after_all(results, *last)
        last = send_y(last[0]), send_x(last[1])
    else:
        direct, last = scatter_expert_first(expert_grads[0], me), ()
    mixture_part, unused = combine_rows(token_tables, results, shares)
    directs, lasts = [direct], [last]

    mixture = lax.psum_scatter(mixture_part, "exp", scatter_dimension=0, tiled=True)
    output = (middle + mixture.astype(F32)).astype(BF)
    grad_two = after(grad_two, mixture_part).astype(F32)
    grad_logits = (
        router_prob * (grad_prob - jnp.sum(router_prob * grad_prob, axis=-1, keepdims=True))
    ).astype(BF)
    grad_router = jnp.einsum("td,te->ed", hidden_two, grad_logits, preferred_element_type=F32)
    grad_two = grad_two + jnp.einsum(
        "te,de->td", grad_logits, router_full, preferred_element_type=F32
    )
    grad_ffn_gain = jnp.sum(grad_two * normed_two, axis=0)
    grad_middle = cotangent.astype(F32) + norm_back(grad_two * gain_ffn, normed_two, root_two)

    own_grad = after(grad_middle.astype(BF), *directs[0], *lasts[0])
    branch_grad, grad_there = gather_group(own_grad, slot_table, me)
    sums = []
    for e in range(1, own_experts):
        expert_grads.append(weight_grads(e, own_grad))
        sums.append(scatter_expert_first(after_all(expert_grads[e], *grad_there), me))
    grad_context = lax.dot_general(branch_grad, out_full, NT, preferred_element_type=F32).astype(BF)
    out_grad = lax.dot_general(
        context_low, branch_grad, TN, preferred_element_type=F32
    ).astype(BF)
    grad_query_norm, grad_key_norm, grad_value = attend_back(
        query_rot, key_rot, value_low, grad_context, cos_part, sin_part, seg_ids
    )
    grad_query_gain = jnp.sum(grad_query_norm * normed_query, axis=0)
    grad_key_gain = jnp.sum(grad_key_norm * normed_key, axis=0)
    scaled_query = grad_query_norm * gain_query
    scaled_key = grad_key_norm * gain_key
    products = jnp.stack(
        [jnp.sum(scaled_query * normed_query, axis=1), jnp.sum(scaled_key * normed_key, axis=1)]
    )
    weight_sums = [scatter_expert_end(expert_grads[0], directs[0], lasts[0], me)]
    *weight_sums[0], products = after_all(
        (*weight_sums[0], products), out_grad, *(piece for pieces in sums for piece in pieces)
    )
    means = sum_over_ctx(products) / D
    for e in range(1, own_experts):
        ahead, direct = split_sums(sums[e - 1])
        directs.append(direct)
        ahead = after_all(ahead, means)
        take = expert_take(expert_grads[e])
        if ctx_size == 4:
            last_sent = scatter_last_payload(take, me, ahead)
            lasts.append((send_y(last_sent[0]), send_x(last_sent[1])))
        else:
            last_sent = direct
            lasts.append(())
    grad_projected = jnp.concatenate(
        [
            root_query * (scaled_query - normed_query * means[0][:, None]),
            root_key * (scaled_key - normed_key * means[1][:, None]),
            grad_value,
        ],
        axis=1,
    ).astype(BF)
    grad_packed = jnp.pad(grad_projected, ((0, 0), (0, 128)))
    grad_one_part = lax.dot_general(grad_packed, packed, NT, preferred_element_type=F32)
    grad_attn_gain = jnp.sum(grad_one_part * normed_group, axis=0)
    left, right = after_all((hidden_one, grad_projected), *last_sent)
    qkv_grad = lax.dot_general(left, right, TN, preferred_element_type=F32).astype(BF)
    grad_one, one_first, one_sent, unused = scatter_group(
        after(grad_one_part, *(piece for pieces in lasts[1:] for piece in pieces)),
        slot_table,
        me,
        joined=True,
    )
    for e in range(1, own_experts):
        direct, last = after_all(directs[e], *one_sent), after_all(lasts[e], *one_sent)
        weight_sums.append(scatter_expert_end(expert_grads[e], direct, last, me))
    gate_grad, up_grad, down_grad = (jnp.stack(parts) for parts in zip(*weight_sums))
    out_sum = lax.psum_scatter(
        out_grad, "exp", scatter_dimension=0, tiled=True
    ).astype(F32)
    qkv_sum = lax.psum_scatter(
        after(qkv_grad, mixture).reshape(ctx_size, exp_size * part_rows, 3 * own_width),
        "exp",
        scatter_dimension=1,
        tiled=True,
    )
    qkv_own = exchange(qkv_sum, me).astype(F32)
    projection_grads = [
        jnp.swapaxes(qkv_own[:, :, i * own_width : (i + 1) * own_width], 0, 1).reshape(part_rows, D)
        for i in range(3)
    ]
    root_one = inverse_root(inputs)
    normed_one = inputs * root_one
    grad_input = grad_middle + norm_back(grad_one * gain_attn, normed_one, root_one)
    head_gains = lax.dynamic_update_slice(
        jnp.zeros((2, D), F32), jnp.stack([grad_query_gain, grad_key_gain]), (0, me * own_width)
    )
    small_sums = jnp.concatenate(
        [grad_router, jnp.stack([grad_ffn_gain, grad_attn_gain]), head_gains]
    )
    small_sums = sum_to_rows(after(small_sums, *one_first), me, *one_sent)
    return (
        output,
        grad_input,
        projection_grads[0],
        projection_grads[1],
        projection_grads[2],
        out_sum,
        small_sums[:experts].T,
        small_sums[experts + 1],
        small_sums[experts + 2],
        small_sums[experts + 3],
        small_sums[experts],
        gate_grad,
        up_grad,
        down_grad,
    )


def solution(mesh):
    rows = P(BOTH, None)
    weights = P("exp", "ctx", None)
    in_specs = (
        (rows, rows, rows, P("exp", None), P("exp", None))
        + (rows,) * 5
        + (P(BOTH),) * 4
        + (weights,) * 3
    )
    out_specs = (rows,) * 7 + (P(BOTH),) * 4 + (weights,) * 3
    return jax.shard_map(local, mesh=mesh, in_specs=in_specs, out_specs=out_specs, check_vma=False)
```

```python
import functools
import math

import jax
import jax.numpy as jnp
from jax import lax
from jax.experimental import pallas as pl
from jax.experimental.pallas import tpu as pltpu
from jax.sharding import PartitionSpec as P

D = 2048
HEADS = 16
HD = 128
TOP = 8
PROMPT = 1024
CONT = 2
CTOK = 512

epsilon = 1e-05
rope_base = 10000.0
BF = jnp.bfloat16
F32 = jnp.float32
BOTH = ("ctx", "exp")
X_PAIRS = [(i, i ^ 1) for i in range(4)]
Y_PAIRS = [(i, i ^ 2) for i in range(4)]
XY_PAIRS = [(i, i ^ 3) for i in range(4)]
NT = (((1,), (1,)), ((), ()))
TN = (((0,), (0,)), ((), ()))
TILE = 256
WIN = 768
NOWHERE = -(1 << 20)


def inverse_root(values):
    return lax.rsqrt(jnp.mean(values * values, axis=-1, keepdims=True) + epsilon)


def norm_back(gradient, normed, root_part):
    return root_part * (gradient - normed * jnp.mean(gradient * normed, axis=-1, keepdims=True))


def angles(position):
    half_dim = HD // 2
    inverse = rope_base ** (-2.0 * jnp.arange(half_dim, dtype=F32) / HD)
    phases = position.astype(F32)[:, None] * inverse[None, :]
    cosine, sine = jnp.cos(phases), jnp.sin(phases)
    return jnp.concatenate([cosine, cosine], axis=1), jnp.concatenate([-sine, sine], axis=1)


def send_x(value):
    return lax.ppermute(value, "ctx", X_PAIRS)


def send_y(value):
    return lax.ppermute(value, "ctx", Y_PAIRS)


def send_xy(value):
    return lax.ppermute(value, "ctx", XY_PAIRS)


def after(value, *others):
    return lax.optimization_barrier((value,) + others)[0]


def after_all(values, *others):
    return lax.optimization_barrier(tuple(values) + others)[: len(values)]


def gather_pieces(low, high):
    low_x, high_y = send_x(low), send_y(high)
    high_x, low_y = send_x(high), send_y(low)
    return (low_x, low_y, send_y(low_x)), (high_x, high_y, send_x(high_y))


def scatter_ahead(take, me):
    return send_x(take(me ^ 3, 0).astype(BF)), send_y(take(me ^ 3, 1).astype(BF))


def scatter_direct(take, me, *others):
    low, high = take(me ^ 1, 0).astype(BF), take(me ^ 2, 1).astype(BF)
    if others:
        low, high = after_all((low, high), *others)
    return send_x(low), send_y(high)


def scatter_last_payload(take, me, ahead):
    low = (take(me ^ 2, 0).astype(F32) + ahead[0].astype(F32)).astype(BF)
    high = (take(me ^ 1, 1).astype(F32) + ahead[1].astype(F32)).astype(BF)
    return low, high


def scatter_last(take, me, ahead):
    low, high = scatter_last_payload(take, me, ahead)
    return send_y(low), send_x(high)


def scatter_end(take, me, direct, last):
    return [
        take(me, part).astype(F32) + direct[part].astype(F32) + last[part].astype(F32)
        for part in range(2)
    ]


def exchange(blocks, me):
    if lax.axis_size("ctx") != 4:
        return lax.all_to_all(blocks, "ctx", split_axis=0, concat_axis=0, tiled=True)
    sends = (lambda part: part, send_x, send_y, send_xy)
    parts = [
        send(lax.dynamic_index_in_dim(blocks, me ^ away, 0, keepdims=False))
        for away, send in enumerate(sends)
    ]

    def from_ctx(c):
        chosen = parts[0]
        for away in range(1, 4):
            chosen = jnp.where((me ^ c) == away, parts[away], chosen)
        return chosen

    return jnp.stack([from_ctx(c) for c in range(4)])


def sum_over_ctx(value):
    if lax.axis_size("ctx") != 4:
        return lax.psum(value, "ctx")
    value = value + send_x(value)
    return value + send_y(value)


def sum_to_rows(values, me, *others):
    ctx_size, exp_size = lax.axis_size("ctx"), lax.axis_size("exp")
    count, width = values.shape
    parts = values.reshape(count, ctx_size, exp_size, width // (ctx_size * exp_size))
    parts = jnp.transpose(parts, (2, 1, 0, 3))
    exp_index, step = lax.axis_index("exp"), exp_size // 2
    while step:
        upper = (exp_index // step) % 2
        kept = lax.dynamic_slice_in_dim(parts, upper * step, step, 0)
        sent = lax.dynamic_slice_in_dim(parts, (1 - upper) * step, step, 0)
        parts = kept + lax.ppermute(sent, "exp", [(i, i ^ step) for i in range(exp_size)])
        step //= 2
    parts = after(parts[0], *others)
    return jnp.sum(exchange(parts, me), axis=0)


def pack_expert(w_gate, w_up, w_down):
    half, width = w_up.shape[0] // 2, w_up.shape[1]
    low = jnp.concatenate([w_gate, w_up[:half]], axis=0)
    high = jnp.concatenate([w_up[half:], w_down[:, :width], w_down[:, width:]], axis=0)
    return low, high


def whole_expert(w_gate, w_up, w_down):
    return (
        lax.all_gather(jnp.stack([w_gate, w_up]), "ctx", axis=1, tiled=True),
        lax.all_gather(w_down, "ctx", axis=0, tiled=True),
    )


def expert_take(grads):
    gate_up, down = grads
    rows, width = gate_up.shape[0] // 4, gate_up.shape[1] // 2
    half = down.shape[0] // 8

    def take(owner, part):
        first = (2 * owner + part) * half
        return jnp.concatenate(
            [
                lax.dynamic_slice(gate_up, (owner * rows, part * width), (rows, width)),
                lax.dynamic_slice(down, (first, 0), (half, width)),
                lax.dynamic_slice(down, (first, width), (half, width)),
            ],
            axis=0,
        )

    return take


def scatter_expert_first(grads, me):
    if lax.axis_size("ctx") != 4:
        return tuple(
            lax.psum_scatter(grad, "ctx", scatter_dimension=0, tiled=True) for grad in grads
        )
    return scatter_joined(expert_take(grads), me)


def scatter_joined(take, me):
    low, high = joined_payload(take, me)
    return send_x(low), send_y(high)


def joined_payload(take, me):
    low = jnp.stack([take(me ^ 1, 0), take(me ^ 3, 0)]).astype(BF)
    high = jnp.stack([take(me ^ 2, 1), take(me ^ 3, 1)]).astype(BF)
    return low, high


def split_sums(sums):
    if lax.axis_size("ctx") != 4:
        return sums, sums
    return (sums[0][1], sums[1][1]), (sums[0][0], sums[1][0])


def scatter_expert_end(grads, direct, last, me):
    if lax.axis_size("ctx") != 4:
        gate_up, down = (part.astype(F32) for part in direct)
        width = gate_up.shape[1] // 2
        return gate_up[:, :width], gate_up[:, width:], down
    first, second = scatter_end(expert_take(grads), me, direct, last)
    rows, half = grads[0].shape[0] // 4, grads[1].shape[0] // 8
    down = [
        jnp.concatenate([part[rows : rows + half], part[rows + half :]], axis=1)
        for part in (first, second)
    ]
    return first[:rows], second[:rows], jnp.concatenate(down, axis=0)


def pick_blocks(blocks, order):
    return jnp.concatenate(
        [
            lax.dynamic_index_in_dim(blocks, order[i], 0, keepdims=False)
            for i in range(order.shape[0])
        ],
        axis=0,
    )


def gather_group(rows, slot_table, me):
    block = rows.shape[0] // 2
    if lax.axis_size("ctx") != 4:
        blocks = slot_table.shape[0]
        whole = lax.all_gather(rows, "ctx", axis=0, tiled=True).reshape(blocks, block, -1)
        match = slot_table[None, :] == jnp.arange(blocks, dtype=jnp.int32)[:, None]
        order = jnp.sum(jnp.where(match, jnp.arange(blocks, dtype=jnp.int32)[None, :], 0), axis=1)
        return pick_blocks(whole, order), ()
    pieces = gather_pieces(rows[:block], rows[block:])
    whole = jnp.zeros((8 * block, rows.shape[1]), rows.dtype)
    for slot in range(2):
        for away in range(4):
            part = pieces[slot][away - 1] if away else rows[slot * block : (slot + 1) * block]
            start = slot_table[2 * (me ^ away) + slot] * block
            whole = lax.dynamic_update_slice(whole, part, (start, 0))
    return whole, (pieces[0][2], pieces[1][2])


def scatter_group(partial, slot_table, me, joined=False):
    blocks = slot_table.shape[0]
    block = partial.shape[0] // blocks
    if lax.axis_size("ctx") != 4:
        ordered = pick_blocks(partial.reshape(blocks, block, -1), slot_table).astype(BF)
        whole = lax.psum_scatter(ordered, "ctx", scatter_dimension=0, tiled=True)
        return whole.astype(F32), (whole,), (whole,), (whole,)

    def take(owner, part):
        start = slot_table[2 * owner + part] * block
        return lax.dynamic_slice(partial, (start, 0), (block, partial.shape[1]))

    first = ()
    if joined:
        first = joined_payload(take, me)
        ahead, direct = split_sums((send_x(first[0]), send_y(first[1])))
    else:
        ahead, direct = scatter_ahead(take, me), scatter_direct(take, me)
    sent = scatter_last_payload(take, me, ahead)
    if joined:
        sent = after_all(sent)
    last = send_y(sent[0]), send_x(sent[1])
    return jnp.concatenate(scatter_end(take, me, direct, last), axis=0), first, sent, last


def prefix_count(member):
    rows, columns = member.shape
    width = 128
    blocks = rows // width
    ones = member.astype(BF).reshape(blocks, width, columns)
    lower = (
        jnp.arange(width)[:, None] > jnp.arange(width)[None, :]
    ).astype(BF)
    inner = jnp.einsum("pq,bqc->bpc", lower, ones, preferred_element_type=F32)
    totals = jnp.sum(ones.astype(F32), axis=1)
    before = (jnp.arange(blocks)[:, None] > jnp.arange(blocks)[None, :]).astype(F32)
    outer = jnp.sum(before[:, :, None] * totals[None, :, :], axis=1)
    return (inner + outer[:, None, :]).reshape(rows, columns).astype(jnp.int32)


def dot(left, right, dims=(((1,), (0,)), ((), ()))):
    return lax.dot_general(left, right, dims, preferred_element_type=F32)


def turned(values, cosine, sine):
    return values * cosine + pltpu.roll(values, HD // 2, 1) * sine


def tile_weights(query, key, seg_q, seg_k, first, factor):
    rows, width = query.shape[0], key.shape[0]
    scores = dot(query, key, NT) * factor
    q_place = first + lax.broadcasted_iota(jnp.int32, (rows, width), 0)
    k_place = lax.broadcasted_iota(jnp.int32, (rows, width), 1)
    allowed = k_place <= q_place
    if first >= PROMPT:
        allowed = allowed & ((seg_k < 0) | (seg_k == seg_q))
    scores = jnp.where(allowed, scores, -1e30)
    weights = jnp.exp(scores - jnp.max(scores, axis=1, keepdims=True))
    return weights, jnp.sum(weights, axis=1, keepdims=True)


def attend_kernel(
    tiles,
    factor,
    qp_ref,
    kp_ref,
    vp_ref,
    root_ref,
    key_root_ref,
    gain_ref,
    cos_ref,
    sin_ref,
    sq_ref,
    sk_ref,
    q_ref,
    k_ref,
    v_ref,
    o_ref,
):
    at = pl.program_id(1)
    tile = qp_ref.shape[0]

    @pl.when(at == 0)
    def _():
        keys = kp_ref[...] * key_root_ref[:, 1:2] * gain_ref[1:2]
        k_ref[...] = turned(keys, cos_ref[...], sin_ref[...]).astype(BF)
        v_ref[...] = vp_ref[...].astype(BF)

    for i in range(tiles):

        @pl.when(at == i)
        def _():
            own = slice(i * tile, (i + 1) * tile)
            width = (i + 1) * tile
            queries = qp_ref[...] * root_ref[:, 0:1] * gain_ref[0:1]
            query = turned(queries, cos_ref[own], sin_ref[own]).astype(BF)
            q_ref[...] = query
            weights, total = tile_weights(
                query, k_ref[:width], sq_ref[...], sk_ref[:, :width], i * tile, factor
            )
            o_ref[...] = (dot(weights.astype(BF), v_ref[:width]) / total).astype(BF)


def attend(projected, roots, gains, cosine, sine, seg, width, tile=512):
    rows = projected.shape[0]
    heads, tiles = width // HD, rows // tile
    own = pl.BlockSpec((tile, HD), lambda h, i: (i, h))
    whole = pl.BlockSpec((rows, HD), lambda h, i: (0, h))
    pairs = heads * rows * rows * (tiles + 1) // (2 * tiles)
    return pl.pallas_call(
        functools.partial(attend_kernel, tiles, 1.0 / math.sqrt(HD)),
        out_shape=[jax.ShapeDtypeStruct((rows, width), BF)] * 4,
        grid=(heads, tiles),
        in_specs=[
            own,
            pl.BlockSpec((rows, HD), lambda h, i: (0, heads + h)),
            pl.BlockSpec((rows, HD), lambda h, i: (0, 2 * heads + h)),
            pl.BlockSpec((tile, 2), lambda h, i: (i, 0)),
            pl.BlockSpec((rows, 2), lambda h, i: (0, 0)),
            pl.BlockSpec((2, HD), lambda h, i: (0, h)),
            pl.BlockSpec((rows, HD), lambda h, i: (0, 0)),
            pl.BlockSpec((rows, HD), lambda h, i: (0, 0)),
            pl.BlockSpec((tile, 1), lambda h, i: (i, 0)),
            pl.BlockSpec((1, rows), lambda h, i: (0, 0)),
        ],
        out_specs=[own, whole, whole, own],
        compiler_params=pltpu.CompilerParams(vmem_limit_bytes=48 << 20),
        cost_estimate=pl.CostEstimate(
            flops=4 * pairs * HD, bytes_accessed=20 * rows * width, transcendentals=pairs
        ),
    )(
        projected,
        projected,
        projected,
        roots,
        roots,
        gains,
        cosine,
        sine,
        seg[:, None],
        seg[None, :],
    )


def attend_back_kernel(
    tiles,
    factor,
    q_ref,
    k_ref,
    v_ref,
    d_ref,
    cos_ref,
    sin_ref,
    sq_ref,
    sk_ref,
    dq_ref,
    dk_ref,
    dv_ref,
):
    at = pl.program_id(1)
    tile = q_ref.shape[0]

    @pl.when(at == 0)
    def _():
        dk_ref[...] = jnp.zeros_like(dk_ref)
        dv_ref[...] = jnp.zeros_like(dv_ref)

    for i in range(tiles):

        @pl.when(at == i)
        def _():
            own = slice(i * tile, (i + 1) * tile)
            width = (i + 1) * tile
            query, grad = q_ref[...], d_ref[...]
            weights, total = tile_weights(
                query, k_ref[:width], sq_ref[...], sk_ref[:, :width], i * tile, factor
            )
            weights = weights / total
            grad_weights = dot(grad, v_ref[:width], NT)
            delta = jnp.sum(weights * grad_weights, axis=1, keepdims=True)
            grad_scores = (weights * (grad_weights - delta)).astype(BF)
            grad_query = dot(grad_scores, k_ref[:width]) * factor
            dq_ref[...] = turned(grad_query, cos_ref[own], -sin_ref[own])
            dk_ref[:width] += dot(grad_scores, query, TN)
            dv_ref[:width] += dot(weights.astype(BF), grad, TN)

    @pl.when(at == tiles - 1)
    def _():
        dk_ref[...] = turned(dk_ref[...] * factor, cos_ref[...], -sin_ref[...])


def attend_back(q, k, v, grad, cosine, sine, seg, tile=512):
    rows, width = q.shape
    heads, tiles = width // HD, rows // tile
    own = pl.BlockSpec((tile, HD), lambda h, i: (i, h))
    whole = pl.BlockSpec((rows, HD), lambda h, i: (0, h))
    table = pl.BlockSpec((rows, HD), lambda h, i: (0, 0))
    pairs = heads * rows * rows * (tiles + 1) // (2 * tiles)
    return pl.pallas_call(
        functools.partial(attend_back_kernel, tiles, 1.0 / math.sqrt(HD)),
        out_shape=[jax.ShapeDtypeStruct((rows, width), F32)] * 3,
        grid=(heads, tiles),
        in_specs=[
            own,
            whole,
            whole,
            own,
            table,
            table,
            pl.BlockSpec((tile, 1), lambda h, i: (i, 0)),
            pl.BlockSpec((1, rows), lambda h, i: (0, 0)),
        ],
        out_specs=[own, whole, whole],
        compiler_params=pltpu.CompilerParams(vmem_limit_bytes=48 << 20),
        cost_estimate=pl.CostEstimate(
            flops=10 * pairs * HD, bytes_accessed=20 * rows * width, transcendentals=pairs
        ),
    )(q, k, v, grad, cosine, sine, seg[:, None], seg[None, :])


def pick_rows(tok, low, windows, source_ref, acc_ref):
    last = source_ref.shape[0] - WIN
    span = lax.broadcasted_iota(jnp.int32, (TILE, WIN), 1)

    def window(j):
        base = low + j * WIN
        start = pl.multiple_of(jnp.minimum(base, last), 128)
        match = (tok - start == span) & (tok >= base)
        return dot(match.astype(F32).astype(BF), source_ref[pl.ds(start, WIN), :])

    acc_ref[...] = window(0)

    @pl.loop(1, windows)
    def _(j):
        acc_ref[...] += window(j)

    return acc_ref[...].astype(BF)


def copy_all(copies):
    for copy in copies:
        copy.start()
    for copy in copies:
        copy.wait()


def back_rows_kernel(tiles_ref, low_ref, windows_ref, me_ref, tok_ref, dy_ref, *refs):
    parts, (rows_ref, raw_ref, down_ref, acc_ref, sems) = refs[:-5], refs[-5:]
    i = pl.program_id(0)

    @pl.when(i == 0)
    def _():
        if len(parts) == 1:
            copy_all([pltpu.make_async_copy(parts[0], down_ref, sems.at[0])])
            return
        rows, width = down_ref.shape[0] // 4, down_ref.shape[1] // 2
        copies = []
        for away, part in enumerate(parts):
            owner = pl.multiple_of((me_ref[0] ^ away) * rows, rows)
            for k in range(2):
                copies.append(
                    pltpu.make_async_copy(
                        part.at[pl.ds((k + 1) * rows, rows)],
                        down_ref.at[pl.ds(owner, rows), pl.ds(k * width, width)],
                        sems.at[len(copies)],
                    )
                )
        copy_all(copies)

    @pl.when(i < tiles_ref[0])
    def _():
        rows = pick_rows(tok_ref[...], low_ref[i], windows_ref[i], dy_ref, acc_ref)
        rows_ref[...] = rows
        raw_ref[...] = dot(rows, down_ref[...], NT)

    @pl.when(i >= tiles_ref[0])
    def _():
        rows_ref[...] = jnp.zeros_like(rows_ref)
        raw_ref[...] = jnp.zeros_like(raw_ref)


def back_rows(tables, me, upstream, parts, ff):
    total, width = upstream.shape
    capacity = tables[3].shape[0]
    tile = lambda n: pl.BlockSpec((TILE, n), lambda i, *_: (i, 0))
    once = lambda shape: pl.BlockSpec(shape, lambda i, *_: (0, 0), pipeline_mode=pl.Buffered(1))
    return pl.pallas_call(
        back_rows_kernel,
        out_shape=[
            jax.ShapeDtypeStruct((capacity, width), BF),
            jax.ShapeDtypeStruct((capacity, ff), F32),
            jax.ShapeDtypeStruct((ff, width), BF),
        ],
        grid_spec=pltpu.PrefetchScalarGridSpec(
            num_scalar_prefetch=4,
            grid=(capacity // TILE,),
            in_specs=[tile(1), once((total, width))]
            + [pl.BlockSpec(memory_space=pl.ANY)] * len(parts),
            out_specs=[tile(width), tile(ff), pl.BlockSpec((ff, width), lambda i, *_: (0, 0))],
            scratch_shapes=[
                pltpu.VMEM((TILE, width), F32),
                pltpu.SemaphoreType.DMA((2 * len(parts),)),
            ],
        ),
        compiler_params=pltpu.CompilerParams(vmem_limit_bytes=48 << 20),
        cost_estimate=pl.CostEstimate(
            flops=total * (width * ff + WIN * width),
            bytes_accessed=2 * total * width + 4 * ff * width + capacity * (2 * width + 4 * ff),
            transcendentals=0,
        ),
    )(*tables[:3], me, tables[3], upstream, *parts)


def expert_kernel(
    own, tiles_ref, low_ref, windows_ref, ids_ref, tok_ref, h_ref, router_ref, raw_ref, *refs
):
    parts = refs[:-8]
    rows_ref, hid_ref, dab_ref, dh_ref, share_ref, both_ref, acc_ref, sems = refs[-8:]
    wg_ref, wu_ref = both_ref.at[0], both_ref.at[1]
    i = pl.program_id(0)
    ff = wg_ref.shape[1]

    @pl.when(i == 0)
    def _():
        if len(parts) == 1:
            copy_all([pltpu.make_async_copy(parts[0], both_ref, sems.at[0])])
            return
        rows = wg_ref.shape[0] // 4
        half = rows // 2
        copies = []
        for away in range(4):
            owner = pl.multiple_of((ids_ref[1] ^ away) * rows, rows)
            for part, first, count, which, shift in (
                (parts[away], 0, rows, 0, 0),
                (parts[away], rows, half, 1, 0),
                (parts[4 + away], 0, half, 1, half),
            ):
                copies.append(
                    pltpu.make_async_copy(
                        part.at[pl.ds(first, count)],
                        both_ref.at[which, pl.ds(owner + shift, count)],
                        sems.at[len(copies)],
                    )
                )
        copy_all(copies)

    @pl.when(i < tiles_ref[0])
    def _():
        rows = pick_rows(tok_ref[...], low_ref[i], windows_ref[i], h_ref, acc_ref)
        rows_ref[...] = rows
        logits = dot(rows, router_ref[...])
        probs = jnp.exp(logits - jnp.max(logits, axis=1, keepdims=True))
        column = lax.broadcasted_iota(jnp.int32, probs.shape, 1)
        mine = jnp.sum(jnp.where(column == ids_ref[0] + own, probs, 0.0), axis=1, keepdims=True)
        gate = mine / jnp.sum(probs, axis=1, keepdims=True)
        share = 0.0
        part = ff // 4
        for c in range(4):
            cols = slice(c * part, (c + 1) * part)
            a = dot(rows, wg_ref[:, cols])
            b = dot(rows, wu_ref[:, cols])
            raw = raw_ref[:, cols]
            sig = 1.0 / (1.0 + jnp.exp(-a))
            silu = a * sig
            hid = silu * b
            share += jnp.sum(hid * raw, axis=1, keepdims=True)
            raw = raw * gate
            hid_ref[:, cols] = (hid * gate).astype(BF)
            dab_ref[:, cols] = (raw * b * (sig * (1.0 + a * (1.0 - sig)))).astype(BF)
            dab_ref[:, ff + c * part : ff + (c + 1) * part] = (raw * silu).astype(BF)
        share_ref[...] = share
        dh = dot(dab_ref[:, :ff], wg_ref[...], NT) + dot(dab_ref[:, ff:], wu_ref[...], NT)
        dh_ref[...] = dh.astype(BF)

    @pl.when(i >= tiles_ref[0])
    def _():
        for ref in (rows_ref, hid_ref, dab_ref, dh_ref, share_ref):
            ref[...] = jnp.zeros_like(ref)


def expert_rows(tables, own, ids, hidden, router, parts, raw):
    total, width = hidden.shape
    capacity, ff = raw.shape
    tile = lambda n: pl.BlockSpec((TILE, n), lambda i, *_: (i, 0))
    once = lambda shape: pl.BlockSpec(shape, lambda i, *_: (0, 0), pipeline_mode=pl.Buffered(1))
    made = lambda n, dtype=BF: jax.ShapeDtypeStruct((capacity, n), dtype)
    return pl.pallas_call(
        functools.partial(expert_kernel, own),
        out_shape=[made(width), made(ff), made(2 * ff), made(width), made(1, F32)],
        grid_spec=pltpu.PrefetchScalarGridSpec(
            num_scalar_prefetch=4,
            grid=(capacity // TILE,),
            in_specs=[tile(1), once((total, width)), once(router.shape), tile(ff)]
            + [pl.BlockSpec(memory_space=pl.ANY)] * len(parts),
            out_specs=[tile(width), tile(ff), tile(2 * ff), tile(width), tile(1)],
            scratch_shapes=[
                pltpu.VMEM((2, width, ff), BF),
                pltpu.VMEM((TILE, width), F32),
                pltpu.SemaphoreType.DMA((12,)),
            ],
        ),
        compiler_params=pltpu.CompilerParams(vmem_limit_bytes=56 << 20),
        cost_estimate=pl.CostEstimate(
            flops=total * (4 * width * ff + WIN * width),
            bytes_accessed=2 * total * width + 4 * ff * width + capacity * (4 * width + 10 * ff),
            transcendentals=total * ff,
        ),
    )(*tables[:3], ids, tables[3], hidden, router, raw, *parts)


def combine_kernel(experts, shared, start_ref, more_ref, wide_ref, id_ref, pos_ref, *refs):
    rows_refs, share_refs = refs[:experts], refs[experts:-2]
    out_ref, acc_ref = refs[-2:]
    i = pl.program_id(0)
    span = lax.broadcasted_iota(jnp.int32, (TILE, TILE), 1)
    last, width = rows_refs[0].shape[0] - TILE, rows_refs[0].shape[1]

    def window(e, j):
        base = start_ref[e, i] + j * TILE
        start = pl.multiple_of(jnp.minimum(base, last), 16)
        pos = pos_ref[:, e : e + 1]
        match = (pos - start == span) & (pos >= base)
        return dot(match.astype(F32).astype(BF), rows_refs[e][pl.ds(start, TILE), :])

    acc_ref[...] = sum(window(e, 0) for e in range(experts))
    for e in range(experts):

        @pl.when(more_ref[e, i] > 0)
        def _():
            acc_ref[...] += window(e, 1)

    out_ref[:, :width] = acc_ref[...].astype(BF)
    if shared:
        wide_span = lax.broadcasted_iota(jnp.int32, (TILE, 384), 1)
        column = lax.broadcasted_iota(jnp.int32, (TILE, shared), 1)
        extra = jnp.zeros((TILE, shared), F32)
        for e in range(experts):
            wide = pl.multiple_of(wide_ref[e, i], 128)
            match = pos_ref[:, e : e + 1] - wide == wide_span
            share = share_refs[e][:, pl.ds(wide, 384)]
            own = jnp.sum(jnp.where(match, share, 0.0), axis=1, keepdims=True)
            head = own.astype(BF).astype(F32)
            first = 2 * (id_ref[0] + e)
            extra += jnp.where(column == first, head, 0.0)
            extra += jnp.where(column == first + 1, own - head, 0.0)
        out_ref[:, width:] = extra.astype(BF)


def combine_rows(tables, ids, rows, shares=()):
    experts, (capacity, width) = len(rows), rows[0].shape
    total = tables[3].shape[0]
    shared = 128 if shares else 0
    once = lambda shape: pl.BlockSpec(shape, lambda i, *_: (0, 0), pipeline_mode=pl.Buffered(1))
    tile = lambda n: pl.BlockSpec((TILE, n), lambda i, *_: (i, 0))
    return pl.pallas_call(
        functools.partial(combine_kernel, experts, shared),
        out_shape=jax.ShapeDtypeStruct((total, width + shared), BF),
        grid_spec=pltpu.PrefetchScalarGridSpec(
            num_scalar_prefetch=4,
            grid=(total // TILE,),
            in_specs=[tile(experts)]
            + [once((capacity, width))] * experts
            + [once((1, capacity))] * len(shares),
            out_specs=tile(width + shared),
            scratch_shapes=[pltpu.VMEM((TILE, width), F32)],
        ),
        compiler_params=pltpu.CompilerParams(vmem_limit_bytes=48 << 20),
        cost_estimate=pl.CostEstimate(
            flops=2 * experts * total * TILE * width,
            bytes_accessed=2 * (experts * capacity + total) * width,
            transcendentals=0,
        ),
    )(*tables[:3], ids, tables[3], *rows, *shares)


def local(
    tokens,
    cotangent,
    routes,
    block_of_slot,
    cont_seg,
    w_query,
    w_key,
    w_value,
    w_out,
    w_router,
    attn_gain,
    query_gain,
    key_gain,
    ffn_gain,
    w_gate,
    w_up,
    w_down,
):
    ctx_size = lax.axis_size("ctx")
    exp_size = lax.axis_size("exp")
    me = lax.axis_index("ctx")
    exp_index = lax.axis_index("exp")
    tok_rows = tokens.shape[0]
    part_rows = w_query.shape[0]
    own_width = D // ctx_size
    own_heads = HEADS // ctx_size
    experts = w_router.shape[1]
    own_experts = w_gate.shape[0]
    slot_table = block_of_slot[0]
    seg_row = cont_seg[0]
    group_rows = ctx_size * tok_rows
    factor = 1.0 / math.sqrt(HD)

    tokens_group, tokens_there = gather_group(tokens, slot_table, me)
    small = jnp.concatenate(
        [w_router] + [g[:, None] for g in (attn_gain, query_gain, key_gain, ffn_gain)], axis=1
    )
    small = jnp.pad(small, ((0, 0), (0, 128 - small.shape[1])))
    by_owner = jnp.stack(
        [w.reshape(part_rows, ctx_size, own_width) for w in (w_query, w_key, w_value)], axis=2
    )
    by_owner = jnp.swapaxes(by_owner, 0, 1).reshape(ctx_size, part_rows, 3 * own_width)
    by_owner = jnp.concatenate(
        [by_owner, jnp.broadcast_to(small, (ctx_size,) + small.shape)], axis=2
    )
    out_full = lax.all_gather(w_out, "exp", axis=0, tiled=True)
    own_columns, out_full = after_all((exchange(by_owner, me), out_full))
    packed = lax.all_gather(own_columns, "exp", axis=1, tiled=True).reshape(D, 3 * own_width + 128)
    small_full = packed[:, 3 * own_width :]
    router_full = small_full[:, :experts]
    gains = small_full[:, experts : experts + 4].astype(F32)
    gain_attn, gain_ffn = gains[:, 0], gains[:, 3]
    own_gains = lax.dynamic_slice(gains, (me * own_width, 0), (own_width, 4))
    gain_query, gain_key = own_gains[:, 1], own_gains[:, 2]
    routes_all = lax.all_to_all(
        jnp.broadcast_to(routes[None], (exp_size,) + routes.shape),
        "exp",
        split_axis=0,
        concat_axis=0,
        tiled=True,
    ).reshape(exp_size * tok_rows, TOP)
    upstream_all = lax.all_gather(cotangent, "exp", axis=0, tiled=True)
    packs = [pack_expert(w_gate[e], w_up[e], w_down[e]) for e in range(own_experts)]
    if ctx_size == 4:
        ahead = after_all(packs[0], *tokens_there)
        ahead = send_x(ahead[0]), send_y(ahead[1])

    seg_ids = jnp.concatenate([jnp.full((PROMPT,), -1, jnp.int32), seg_row])
    starts = jnp.sum(
        (seg_row[None, :] < jnp.arange(CONT, dtype=jnp.int32)[:, None]).astype(jnp.int32), axis=1
    )
    first_pos = jnp.sum(
        jnp.where(
            seg_row[:, None] == jnp.arange(CONT, dtype=jnp.int32)[None, :], starts[None, :], 0
        ),
        axis=1,
    )
    cont_pos = PROMPT + jnp.arange(CTOK, dtype=jnp.int32) - first_pos
    position = jnp.concatenate([jnp.arange(PROMPT, dtype=jnp.int32), cont_pos])
    cos_part, sin_part = angles(position)
    group_inputs = tokens_group.astype(F32)
    normed_group = group_inputs * inverse_root(group_inputs)
    hidden_one = (normed_group * gain_attn).astype(BF)
    projected = jnp.dot(hidden_one, packed, preferred_element_type=F32)
    query_pre = projected[:, :own_width]
    key_pre = projected[:, own_width : 2 * own_width]
    squares = jnp.stack([jnp.sum(query_pre * query_pre, axis=1), jnp.sum(key_pre * key_pre, axis=1)])
    if ctx_size == 4:
        squares = after(squares, *ahead)
    squares = sum_over_ctx(squares)
    if ctx_size == 4:
        direct = after_all(packs[0], squares)
        direct = send_x(direct[1]), send_y(direct[0])
    roots = lax.rsqrt(squares / D + epsilon)
    root_query, root_key = roots[0][:, None], roots[1][:, None]
    normed_query = query_pre * root_query
    normed_key = key_pre * root_key
    query_rot, key_rot, value_low, context_low = attend(
        projected,
        roots.T,
        jnp.stack([gain_query, gain_key]),
        cos_part,
        sin_part,
        seg_ids,
        own_width,
    )
    branch_part = jnp.dot(context_low, out_full, preferred_element_type=F32)
    if ctx_size == 4:
        branch_part = after(branch_part, *direct)
    branch, unused, unused, branch_there = scatter_group(branch_part, slot_table, me)
    me_table = jnp.reshape(me, (1,)).astype(jnp.int32)
    width = w_gate.shape[2]
    lows, highs, backs = [], [], []
    if ctx_size == 4:
        passed = after_all(ahead, *branch_there)
        passed = send_y(passed[0]), send_x(passed[1])
        lows.append((packs[0][0], ahead[0], direct[1], passed[0]))
        highs.append((packs[0][1], direct[0], ahead[1], passed[1]))
        upstream, first_passed = upstream_all, passed
        for e in range(1, own_experts):
            low, high = after_all(packs[e], *passed)
            ahead = send_x(low), send_y(high)
            low, high = after_all((low, high), *ahead)
            direct = send_x(high), send_y(low)
            passed = send_y(ahead[0]), send_x(ahead[1])
            lows.append((packs[e][0], ahead[0], direct[1], passed[0]))
            highs.append((packs[e][1], direct[0], ahead[1], passed[1]))
            upstream = after(upstream, *ahead)
    else:
        for e in range(own_experts):
            both, down = whole_expert(*after_all((w_gate[e], w_up[e], w_down[e]), *branch_there))
            lows.append((both,))
            highs.append((down,))
        upstream = upstream_all
        first_passed = branch_there

    own_ids = exp_index * own_experts + jnp.arange(own_experts, dtype=jnp.int32)
    member = jnp.any(after(routes_all, *first_passed)[:, :, None] == own_ids[None, None, :], axis=1)
    place_of = prefix_count(member)
    capacity = exp_size * 8 * ((5 * tok_rows * TOP // (4 * experts) + 7) // 8)
    row_tiles = (capacity + TILE - 1) // TILE
    capacity = row_tiles * TILE
    all_rows = exp_size * tok_rows
    row_ids = jnp.arange(capacity, dtype=jnp.int32)
    hit = (place_of.T[:, None, :] == row_ids[None, :, None]) & member.T[:, None, :]
    token_ids = jnp.arange(all_rows, dtype=jnp.int32)
    token_of_row = jnp.max(jnp.where(hit, token_ids[None, None, :], -1), axis=2)
    counts = jnp.sum(member.astype(jnp.int32), axis=0)
    used_tiles = (counts + TILE - 1) // TILE
    by_tile = token_of_row.reshape(own_experts * row_tiles, TILE)
    low_token = jnp.maximum(by_tile[:, 0], 0) // 128 * 128
    windows = jnp.maximum((jnp.max(by_tile, axis=1) - low_token) // WIN + 1, 1)
    low_token = low_token.reshape(own_experts, row_tiles)
    windows = windows.reshape(own_experts, row_tiles)
    row_tables = [
        (used_tiles[e : e + 1], low_token[e], windows[e], token_of_row[e][:, None])
        for e in range(own_experts)
    ]
    place_column = jnp.where(member, place_of, NOWHERE)
    first_place = place_of[::TILE].T
    in_tile = jnp.sum(member.reshape(-1, TILE, own_experts).astype(jnp.int32), axis=1).T
    first_row = first_place // 16 * 16
    more_rows = (first_place + in_tile - first_row > TILE).astype(jnp.int32)
    share_row_start = jnp.minimum(first_place // 128 * 128, capacity - 384)
    token_tables = (first_row, more_rows, share_row_start, place_column)

    ids = jnp.stack([own_ids[0], me.astype(jnp.int32)])
    backs.append(back_rows(row_tables[0], me_table, upstream, highs[0], width))

    inputs = tokens.astype(F32)
    middle = inputs + branch
    root_two = inverse_root(middle)
    normed_two = middle * root_two
    hidden_two = (normed_two * gain_ffn).astype(BF)
    hidden_all = lax.all_gather(hidden_two, "exp", axis=0, tiled=True)
    logits = jnp.dot(hidden_two, router_full, preferred_element_type=F32)
    router_prob = jax.nn.softmax(logits, axis=-1)

    every = range(own_experts)
    made = []
    for e in every:
        if e > 0:
            upstream = after(upstream_all, made[-1][3])
            highs[e] = after_all(highs[e], made[-1][3])
            backs.append(back_rows(row_tables[e], me_table, upstream, highs[e], width))
        parts = tuple(lows[e]) + tuple(highs[e]) if ctx_size == 4 else lows[e]
        made.append(
            expert_rows(row_tables[e], e, ids, hidden_all, router_full, parts, backs[e][1])
        )
    shares = [m[4].reshape(1, capacity) for m in made]
    grad_two_part = combine_rows(token_tables, ids, [m[3] for m in made], shares)
    grad_two = lax.psum_scatter(grad_two_part, "exp", scatter_dimension=0, tiled=True)
    def weight_grads(e, *others):
        rows, hidden, grad_hidden = after_all(made[e][:3], *others)
        return (
            lax.dot_general(rows, grad_hidden, TN, preferred_element_type=F32).astype(BF),
            lax.dot_general(hidden, backs[e][0], TN, preferred_element_type=F32).astype(BF),
        )

    expert_grads = [weight_grads(0, grad_two_part)]
    if ctx_size == 4:
        take = expert_take(expert_grads[0])
        payload = joined_payload(take, me)
    else:
        payload = expert_grads[0]
    results = [
        jnp.dot(
            after(made[e][1], *payload), backs[e][2], preferred_element_type=F32
        ).astype(BF)
        for e in every
    ]
    if ctx_size == 4:
        ahead, direct = split_sums((send_x(payload[0]), send_y(payload[1])))
        last = scatter_last_payload(take, me, ahead)
        results = after_all(results, *last)
        last = send_y(last[0]), send_x(last[1])
    else:
        direct, last = scatter_expert_first(expert_grads[0], me), ()
    mixture_part = combine_rows(token_tables, ids, results)
    directs, lasts = [direct], [last]

    mixture = lax.psum_scatter(mixture_part, "exp", scatter_dimension=0, tiled=True)
    output = (middle + mixture.astype(F32)).astype(BF)
    grad_two = after(grad_two, mixture_part).astype(F32)
    grad_prob = jnp.sum(
        grad_two[:, D : D + 2 * experts].reshape(tok_rows, experts, 2), axis=2
    )
    grad_two = grad_two[:, :D]
    grad_logits = (
        router_prob * (grad_prob - jnp.sum(router_prob * grad_prob, axis=-1, keepdims=True))
    ).astype(BF)
    grad_router = jnp.einsum("td,te->ed", hidden_two, grad_logits, preferred_element_type=F32)
    grad_two = grad_two + jnp.einsum(
        "te,de->td", grad_logits, router_full, preferred_element_type=F32
    )
    grad_ffn_gain = jnp.sum(grad_two * normed_two, axis=0)
    grad_middle = cotangent.astype(F32) + norm_back(grad_two * gain_ffn, normed_two, root_two)

    own_grad = after(grad_middle.astype(BF), *directs[0], *lasts[0])
    branch_grad, grad_there = gather_group(own_grad, slot_table, me)
    sums = []
    for e in range(1, own_experts):
        expert_grads.append(weight_grads(e, own_grad))
        sums.append(scatter_expert_first(after_all(expert_grads[e], *grad_there), me))
    grad_context = lax.dot_general(branch_grad, out_full, NT, preferred_element_type=F32).astype(BF)
    out_grad = lax.dot_general(
        context_low, branch_grad, TN, preferred_element_type=F32
    ).astype(BF)
    grad_query_norm, grad_key_norm, grad_value = attend_back(
        query_rot, key_rot, value_low, grad_context, cos_part, sin_part, seg_ids
    )
    grad_query_gain = jnp.sum(grad_query_norm * normed_query, axis=0)
    grad_key_gain = jnp.sum(grad_key_norm * normed_key, axis=0)
    scaled_query = grad_query_norm * gain_query
    scaled_key = grad_key_norm * gain_key
    products = jnp.stack(
        [jnp.sum(scaled_query * normed_query, axis=1), jnp.sum(scaled_key * normed_key, axis=1)]
    )
    weight_sums = [scatter_expert_end(expert_grads[0], directs[0], lasts[0], me)]
    *weight_sums[0], products = after_all(
        (*weight_sums[0], products), out_grad, *(piece for pieces in sums for piece in pieces)
    )
    means = sum_over_ctx(products) / D
    for e in range(1, own_experts):
        ahead, direct = split_sums(sums[e - 1])
        directs.append(direct)
        ahead = after_all(ahead, means)
        take = expert_take(expert_grads[e])
        if ctx_size == 4:
            last_sent = scatter_last_payload(take, me, ahead)
            lasts.append((send_y(last_sent[0]), send_x(last_sent[1])))
        else:
            last_sent = direct
            lasts.append(())
    grad_projected = jnp.concatenate(
        [
            root_query * (scaled_query - normed_query * means[0][:, None]),
            root_key * (scaled_key - normed_key * means[1][:, None]),
            grad_value,
        ],
        axis=1,
    ).astype(BF)
    grad_packed = jnp.pad(grad_projected, ((0, 0), (0, 128)))
    grad_one_part = lax.dot_general(grad_packed, packed, NT, preferred_element_type=F32)
    grad_attn_gain = jnp.sum(grad_one_part * normed_group, axis=0)
    left, right = after_all((hidden_one, grad_projected), *last_sent)
    qkv_grad = lax.dot_general(left, right, TN, preferred_element_type=F32).astype(BF)
    grad_one, one_first, one_sent, unused = scatter_group(
        after(grad_one_part, *(piece for pieces in lasts[1:] for piece in pieces)),
        slot_table,
        me,
        joined=True,
    )
    for e in range(1, own_experts):
        direct, last = after_all(directs[e], *one_sent), after_all(lasts[e], *one_sent)
        weight_sums.append(scatter_expert_end(expert_grads[e], direct, last, me))
    gate_grad, up_grad, down_grad = (jnp.stack(parts) for parts in zip(*weight_sums))
    out_sum = lax.psum_scatter(
        out_grad, "exp", scatter_dimension=0, tiled=True
    ).astype(F32)
    qkv_sum = lax.psum_scatter(
        after(qkv_grad, mixture).reshape(ctx_size, exp_size * part_rows, 3 * own_width),
        "exp",
        scatter_dimension=1,
        tiled=True,
    )
    qkv_own = exchange(qkv_sum, me).astype(F32)
    projection_grads = [
        jnp.swapaxes(qkv_own[:, :, i * own_width : (i + 1) * own_width], 0, 1).reshape(part_rows, D)
        for i in range(3)
    ]
    root_one = inverse_root(inputs)
    normed_one = inputs * root_one
    grad_input = grad_middle + norm_back(grad_one * gain_attn, normed_one, root_one)
    head_gains = lax.dynamic_update_slice(
        jnp.zeros((2, D), F32), jnp.stack([grad_query_gain, grad_key_gain]), (0, me * own_width)
    )
    small_sums = jnp.concatenate(
        [grad_router, jnp.stack([grad_ffn_gain, grad_attn_gain]), head_gains]
    )
    small_sums = sum_to_rows(after(small_sums, *one_first), me, *one_sent)
    return (
        output,
        grad_input,
        projection_grads[0],
        projection_grads[1],
        projection_grads[2],
        out_sum,
        small_sums[:experts].T,
        small_sums[experts + 1],
        small_sums[experts + 2],
        small_sums[experts + 3],
        small_sums[experts],
        gate_grad,
        up_grad,
        down_grad,
    )


def solution(mesh):
    rows = P(BOTH, None)
    weights = P("exp", "ctx", None)
    in_specs = (
        (rows, rows, rows, P("exp", None), P("exp", None))
        + (rows,) * 5
        + (P(BOTH),) * 4
        + (weights,) * 3
    )
    out_specs = (rows,) * 7 + (P(BOTH),) * 4 + (weights,) * 3
    return jax.shard_map(local, mesh=mesh, in_specs=in_specs, out_specs=out_specs, check_vma=False)
```

```python
import functools
import math

import jax
import jax.numpy as jnp
from jax import lax
from jax.experimental import pallas as pl
from jax.experimental.pallas import tpu as pltpu
from jax.sharding import PartitionSpec as P

D = 2048
HEADS = 16
HD = 128
TOP = 8
PROMPT = 1024
CONT = 2
CTOK = 512

epsilon = 1e-05
rope_base = 10000.0
BF = jnp.bfloat16
F32 = jnp.float32
BOTH = ("ctx", "exp")
X_PAIRS = [(i, i ^ 1) for i in range(4)]
Y_PAIRS = [(i, i ^ 2) for i in range(4)]
XY_PAIRS = [(i, i ^ 3) for i in range(4)]
NT = (((1,), (1,)), ((), ()))
TN = (((0,), (0,)), ((), ()))
TILE = 256
WIN = 768
NOWHERE = -(1 << 20)


def inverse_root(values):
    return lax.rsqrt(jnp.mean(values * values, axis=-1, keepdims=True) + epsilon)


def norm_back(gradient, normed, root_part):
    return root_part * (gradient - normed * jnp.mean(gradient * normed, axis=-1, keepdims=True))


def angles(position):
    half_dim = HD // 2
    inverse = rope_base ** (-2.0 * jnp.arange(half_dim, dtype=F32) / HD)
    phases = position.astype(F32)[:, None] * inverse[None, :]
    cosine, sine = jnp.cos(phases), jnp.sin(phases)
    return jnp.concatenate([cosine, cosine], axis=1), jnp.concatenate([-sine, sine], axis=1)


def send_x(value):
    return lax.ppermute(value, "ctx", X_PAIRS)


def send_y(value):
    return lax.ppermute(value, "ctx", Y_PAIRS)


def send_xy(value):
    return lax.ppermute(value, "ctx", XY_PAIRS)


def after(value, *others):
    return lax.optimization_barrier((value,) + others)[0]


def after_all(values, *others):
    return lax.optimization_barrier(tuple(values) + others)[: len(values)]


def gather_pieces(low, high):
    low_x, high_y = send_x(low), send_y(high)
    high_x, low_y = send_x(high), send_y(low)
    return (low_x, low_y, send_y(low_x)), (high_x, high_y, send_x(high_y))


def scatter_ahead(take, me):
    return send_x(take(me ^ 3, 0).astype(BF)), send_y(take(me ^ 3, 1).astype(BF))


def scatter_direct(take, me, *others):
    low, high = take(me ^ 1, 0).astype(BF), take(me ^ 2, 1).astype(BF)
    if others:
        low, high = after_all((low, high), *others)
    return send_x(low), send_y(high)


def scatter_last_payload(take, me, ahead):
    low = (take(me ^ 2, 0).astype(F32) + ahead[0].astype(F32)).astype(BF)
    high = (take(me ^ 1, 1).astype(F32) + ahead[1].astype(F32)).astype(BF)
    return low, high


def scatter_last(take, me, ahead):
    low, high = scatter_last_payload(take, me, ahead)
    return send_y(low), send_x(high)


def scatter_end(take, me, direct, last):
    return [
        take(me, part).astype(F32) + direct[part].astype(F32) + last[part].astype(F32)
        for part in range(2)
    ]


def exchange(blocks, me):
    if lax.axis_size("ctx") != 4:
        return lax.all_to_all(blocks, "ctx", split_axis=0, concat_axis=0, tiled=True)
    sends = (lambda part: part, send_x, send_y, send_xy)
    parts = [
        send(lax.dynamic_index_in_dim(blocks, me ^ away, 0, keepdims=False))
        for away, send in enumerate(sends)
    ]

    def from_ctx(c):
        chosen = parts[0]
        for away in range(1, 4):
            chosen = jnp.where((me ^ c) == away, parts[away], chosen)
        return chosen

    return jnp.stack([from_ctx(c) for c in range(4)])


def sum_over_ctx(value):
    if lax.axis_size("ctx") != 4:
        return lax.psum(value, "ctx")
    value = value + send_x(value)
    return value + send_y(value)


def sum_to_rows(values, me, others, late):
    ctx_size, exp_size = lax.axis_size("ctx"), lax.axis_size("exp")
    count, width = values.shape
    parts = values.reshape(count, ctx_size, exp_size, width // (ctx_size * exp_size))
    parts = jnp.transpose(parts, (2, 1, 0, 3))
    exp_index, step = lax.axis_index("exp"), exp_size // 2
    while step:
        upper = (exp_index // step) % 2
        kept = lax.dynamic_slice_in_dim(parts, upper * step, step, 0)
        sent = lax.dynamic_slice_in_dim(parts, (1 - upper) * step, step, 0)
        parts = kept + lax.ppermute(sent, "exp", [(i, i ^ step) for i in range(exp_size)])
        step //= 2
        parts = after(parts, *others)
    return jnp.sum(exchange(after(parts[0], late), me), axis=0)


def pack_expert(w_gate, w_up, w_down):
    half, width = w_up.shape[0] // 2, w_up.shape[1]
    low = jnp.concatenate([w_gate, w_up[:half]], axis=0)
    high = jnp.concatenate([w_up[half:], w_down[:, :width], w_down[:, width:]], axis=0)
    return low, high


def whole_expert(w_gate, w_up, w_down):
    return (
        lax.all_gather(jnp.stack([w_gate, w_up]), "ctx", axis=1, tiled=True),
        lax.all_gather(w_down, "ctx", axis=0, tiled=True),
    )


def expert_take(grads):
    gate_up, down = grads
    rows, width = gate_up.shape[0] // 4, gate_up.shape[1] // 2
    half = down.shape[0] // 8

    def take(owner, part):
        first = (2 * owner + part) * half
        return jnp.concatenate(
            [
                lax.dynamic_slice(gate_up, (owner * rows, part * width), (rows, width)),
                lax.dynamic_slice(down, (first, 0), (half, width)),
                lax.dynamic_slice(down, (first, width), (half, width)),
            ],
            axis=0,
        )

    return take


def scatter_expert_first(grads, me):
    if lax.axis_size("ctx") != 4:
        return tuple(
            lax.psum_scatter(grad, "ctx", scatter_dimension=0, tiled=True) for grad in grads
        )
    return scatter_joined(expert_take(grads), me)


def scatter_joined(take, me):
    low, high = joined_payload(take, me)
    return send_x(low), send_y(high)


def joined_payload(take, me):
    low = jnp.stack([take(me ^ 1, 0), take(me ^ 3, 0)]).astype(BF)
    high = jnp.stack([take(me ^ 2, 1), take(me ^ 3, 1)]).astype(BF)
    return low, high


def split_sums(sums):
    if lax.axis_size("ctx") != 4:
        return sums, sums
    return (sums[0][1], sums[1][1]), (sums[0][0], sums[1][0])


def scatter_expert_end(grads, direct, last, me):
    if lax.axis_size("ctx") != 4:
        gate_up, down = (part.astype(F32) for part in direct)
        width = gate_up.shape[1] // 2
        return gate_up[:, :width], gate_up[:, width:], down
    first, second = scatter_end(expert_take(grads), me, direct, last)
    rows, half = grads[0].shape[0] // 4, grads[1].shape[0] // 8
    down = [
        jnp.concatenate([part[rows : rows + half], part[rows + half :]], axis=1)
        for part in (first, second)
    ]
    return first[:rows], second[:rows], jnp.concatenate(down, axis=0)


def pick_blocks(blocks, order):
    return jnp.concatenate(
        [
            lax.dynamic_index_in_dim(blocks, order[i], 0, keepdims=False)
            for i in range(order.shape[0])
        ],
        axis=0,
    )


def gather_group(rows, slot_table, me):
    block = rows.shape[0] // 2
    if lax.axis_size("ctx") != 4:
        blocks = slot_table.shape[0]
        whole = lax.all_gather(rows, "ctx", axis=0, tiled=True).reshape(blocks, block, -1)
        match = slot_table[None, :] == jnp.arange(blocks, dtype=jnp.int32)[:, None]
        order = jnp.sum(jnp.where(match, jnp.arange(blocks, dtype=jnp.int32)[None, :], 0), axis=1)
        return pick_blocks(whole, order), ()
    pieces = gather_pieces(rows[:block], rows[block:])
    whole = jnp.zeros((8 * block, rows.shape[1]), rows.dtype)
    for slot in range(2):
        for away in range(4):
            part = pieces[slot][away - 1] if away else rows[slot * block : (slot + 1) * block]
            start = slot_table[2 * (me ^ away) + slot] * block
            whole = lax.dynamic_update_slice(whole, part, (start, 0))
    return whole, (pieces[0][2], pieces[1][2])


def scatter_group(partial, slot_table, me, joined=False):
    blocks = slot_table.shape[0]
    block = partial.shape[0] // blocks
    if lax.axis_size("ctx") != 4:
        ordered = pick_blocks(partial.reshape(blocks, block, -1), slot_table).astype(BF)
        whole = lax.psum_scatter(ordered, "ctx", scatter_dimension=0, tiled=True)
        return whole.astype(F32), (whole,), (whole,), (whole,)

    def take(owner, part):
        start = slot_table[2 * owner + part] * block
        return lax.dynamic_slice(partial, (start, 0), (block, partial.shape[1]))

    first = ()
    if joined:
        first = joined_payload(take, me)
        ahead, direct = split_sums((send_x(first[0]), send_y(first[1])))
    else:
        ahead, direct = scatter_ahead(take, me), scatter_direct(take, me)
    sent = scatter_last_payload(take, me, ahead)
    if joined:
        sent = after_all(sent)
    last = send_y(sent[0]), send_x(sent[1])
    return jnp.concatenate(scatter_end(take, me, direct, last), axis=0), first, sent, last


def prefix_count(member):
    rows, columns = member.shape
    width = 128
    blocks = rows // width
    ones = member.astype(BF).reshape(blocks, width, columns)
    lower = (
        jnp.arange(width)[:, None] > jnp.arange(width)[None, :]
    ).astype(BF)
    inner = jnp.einsum("pq,bqc->bpc", lower, ones, preferred_element_type=F32)
    totals = jnp.sum(ones.astype(F32), axis=1)
    before = (jnp.arange(blocks)[:, None] > jnp.arange(blocks)[None, :]).astype(F32)
    outer = jnp.sum(before[:, :, None] * totals[None, :, :], axis=1)
    return (inner + outer[:, None, :]).reshape(rows, columns).astype(jnp.int32)


def dot(left, right, dims=(((1,), (0,)), ((), ()))):
    return lax.dot_general(left, right, dims, preferred_element_type=F32)


def turned(values, cosine, sine):
    return values * cosine + pltpu.roll(values, HD // 2, 1) * sine


def tile_weights(query, key, seg_q, seg_k, first, factor):
    rows, width = query.shape[0], key.shape[0]
    scores = dot(query, key, NT) * factor
    q_place = first + lax.broadcasted_iota(jnp.int32, (rows, width), 0)
    k_place = lax.broadcasted_iota(jnp.int32, (rows, width), 1)
    allowed = k_place <= q_place
    if first >= PROMPT:
        allowed = allowed & ((seg_k < 0) | (seg_k == seg_q))
    scores = jnp.where(allowed, scores, -1e30)
    weights = jnp.exp(scores - jnp.max(scores, axis=1, keepdims=True))
    return weights, jnp.sum(weights, axis=1, keepdims=True)


def attend_kernel(
    tiles,
    factor,
    qp_ref,
    kp_ref,
    vp_ref,
    root_ref,
    key_root_ref,
    gain_ref,
    cos_ref,
    sin_ref,
    sq_ref,
    sk_ref,
    q_ref,
    k_ref,
    v_ref,
    o_ref,
):
    at = pl.program_id(1)
    tile = qp_ref.shape[0]

    @pl.when(at == 0)
    def _():
        keys = kp_ref[...] * key_root_ref[:, 1:2] * gain_ref[1:2]
        k_ref[...] = turned(keys, cos_ref[...], sin_ref[...]).astype(BF)
        v_ref[...] = vp_ref[...].astype(BF)

    for i in range(tiles):

        @pl.when(at == i)
        def _():
            own = slice(i * tile, (i + 1) * tile)
            width = (i + 1) * tile
            queries = qp_ref[...] * root_ref[:, 0:1] * gain_ref[0:1]
            query = turned(queries, cos_ref[own], sin_ref[own]).astype(BF)
            q_ref[...] = query
            weights, total = tile_weights(
                query, k_ref[:width], sq_ref[...], sk_ref[:, :width], i * tile, factor
            )
            o_ref[...] = (dot(weights.astype(BF), v_ref[:width]) / total).astype(BF)


def attend(projected, roots, gains, cosine, sine, seg, width, tile=512):
    rows = projected.shape[0]
    heads, tiles = width // HD, rows // tile
    own = pl.BlockSpec((tile, HD), lambda h, i: (i, h))
    whole = pl.BlockSpec((rows, HD), lambda h, i: (0, h))
    pairs = heads * rows * rows * (tiles + 1) // (2 * tiles)
    return pl.pallas_call(
        functools.partial(attend_kernel, tiles, 1.0 / math.sqrt(HD)),
        out_shape=[jax.ShapeDtypeStruct((rows, width), BF)] * 4,
        grid=(heads, tiles),
        in_specs=[
            own,
            pl.BlockSpec((rows, HD), lambda h, i: (0, heads + h)),
            pl.BlockSpec((rows, HD), lambda h, i: (0, 2 * heads + h)),
            pl.BlockSpec((tile, 2), lambda h, i: (i, 0)),
            pl.BlockSpec((rows, 2), lambda h, i: (0, 0)),
            pl.BlockSpec((2, HD), lambda h, i: (0, h)),
            pl.BlockSpec((rows, HD), lambda h, i: (0, 0)),
            pl.BlockSpec((rows, HD), lambda h, i: (0, 0)),
            pl.BlockSpec((tile, 1), lambda h, i: (i, 0)),
            pl.BlockSpec((1, rows), lambda h, i: (0, 0)),
        ],
        out_specs=[own, whole, whole, own],
        compiler_params=pltpu.CompilerParams(vmem_limit_bytes=48 << 20),
        cost_estimate=pl.CostEstimate(
            flops=4 * pairs * HD, bytes_accessed=20 * rows * width, transcendentals=pairs
        ),
    )(
        projected,
        projected,
        projected,
        roots,
        roots,
        gains,
        cosine,
        sine,
        seg[:, None],
        seg[None, :],
    )


def attend_back_kernel(
    tiles,
    factor,
    q_ref,
    k_ref,
    v_ref,
    d_ref,
    cos_ref,
    sin_ref,
    sq_ref,
    sk_ref,
    dq_ref,
    dk_ref,
    dv_ref,
):
    at = pl.program_id(1)
    tile = q_ref.shape[0]

    @pl.when(at == 0)
    def _():
        dk_ref[...] = jnp.zeros_like(dk_ref)
        dv_ref[...] = jnp.zeros_like(dv_ref)

    for i in range(tiles):

        @pl.when(at == i)
        def _():
            own = slice(i * tile, (i + 1) * tile)
            width = (i + 1) * tile
            query, grad = q_ref[...], d_ref[...]
            weights, total = tile_weights(
                query, k_ref[:width], sq_ref[...], sk_ref[:, :width], i * tile, factor
            )
            weights = weights / total
            grad_weights = dot(grad, v_ref[:width], NT)
            delta = jnp.sum(weights * grad_weights, axis=1, keepdims=True)
            grad_scores = (weights * (grad_weights - delta)).astype(BF)
            grad_query = dot(grad_scores, k_ref[:width]) * factor
            dq_ref[...] = turned(grad_query, cos_ref[own], -sin_ref[own])
            dk_ref[:width] += dot(grad_scores, query, TN)
            dv_ref[:width] += dot(weights.astype(BF), grad, TN)

    @pl.when(at == tiles - 1)
    def _():
        dk_ref[...] = turned(dk_ref[...] * factor, cos_ref[...], -sin_ref[...])


def attend_back(q, k, v, grad, cosine, sine, seg, tile=512):
    rows, width = q.shape
    heads, tiles = width // HD, rows // tile
    own = pl.BlockSpec((tile, HD), lambda h, i: (i, h))
    whole = pl.BlockSpec((rows, HD), lambda h, i: (0, h))
    table = pl.BlockSpec((rows, HD), lambda h, i: (0, 0))
    pairs = heads * rows * rows * (tiles + 1) // (2 * tiles)
    return pl.pallas_call(
        functools.partial(attend_back_kernel, tiles, 1.0 / math.sqrt(HD)),
        out_shape=[jax.ShapeDtypeStruct((rows, width), F32)] * 3,
        grid=(heads, tiles),
        in_specs=[
            own,
            whole,
            whole,
            own,
            table,
            table,
            pl.BlockSpec((tile, 1), lambda h, i: (i, 0)),
            pl.BlockSpec((1, rows), lambda h, i: (0, 0)),
        ],
        out_specs=[own, whole, whole],
        compiler_params=pltpu.CompilerParams(vmem_limit_bytes=48 << 20),
        cost_estimate=pl.CostEstimate(
            flops=10 * pairs * HD, bytes_accessed=20 * rows * width, transcendentals=pairs
        ),
    )(q, k, v, grad, cosine, sine, seg[:, None], seg[None, :])


def pick_rows(tok, low, windows, source_ref, acc_ref):
    last = source_ref.shape[0] - WIN
    span = lax.broadcasted_iota(jnp.int32, (TILE, WIN), 1)

    def window(j):
        base = low + j * WIN
        start = pl.multiple_of(jnp.minimum(base, last), 128)
        match = (tok - start == span) & (tok >= base)
        return dot(match.astype(F32).astype(BF), source_ref[pl.ds(start, WIN), :])

    acc_ref[...] = window(0)

    @pl.loop(1, windows)
    def _(j):
        acc_ref[...] += window(j)

    return acc_ref[...].astype(BF)


def copy_all(copies):
    for copy in copies:
        copy.start()
    for copy in copies:
        copy.wait()


def back_rows_kernel(tiles_ref, low_ref, windows_ref, me_ref, tok_ref, dy_ref, *refs):
    parts, (rows_ref, raw_ref, down_ref, acc_ref, sems) = refs[:-5], refs[-5:]
    i = pl.program_id(0)

    @pl.when(i == 0)
    def _():
        if len(parts) == 1:
            copy_all([pltpu.make_async_copy(parts[0], down_ref, sems.at[0])])
            return
        rows, width = down_ref.shape[0] // 4, down_ref.shape[1] // 2
        copies = []
        for away, part in enumerate(parts):
            owner = pl.multiple_of((me_ref[0] ^ away) * rows, rows)
            for k in range(2):
                copies.append(
                    pltpu.make_async_copy(
                        part.at[pl.ds((k + 1) * rows, rows)],
                        down_ref.at[pl.ds(owner, rows), pl.ds(k * width, width)],
                        sems.at[len(copies)],
                    )
                )
        copy_all(copies)

    @pl.when(i < tiles_ref[0])
    def _():
        rows = pick_rows(tok_ref[...], low_ref[i], windows_ref[i], dy_ref, acc_ref)
        rows_ref[...] = rows
        raw_ref[...] = dot(rows, down_ref[...], NT)

    @pl.when(i >= tiles_ref[0])
    def _():
        rows_ref[...] = jnp.zeros_like(rows_ref)
        raw_ref[...] = jnp.zeros_like(raw_ref)


def back_rows(tables, me, upstream, parts, ff):
    total, width = upstream.shape
    capacity = tables[3].shape[0]
    tile = lambda n: pl.BlockSpec((TILE, n), lambda i, *_: (i, 0))
    once = lambda shape: pl.BlockSpec(shape, lambda i, *_: (0, 0), pipeline_mode=pl.Buffered(1))
    return pl.pallas_call(
        back_rows_kernel,
        out_shape=[
            jax.ShapeDtypeStruct((capacity, width), BF),
            jax.ShapeDtypeStruct((capacity, ff), F32),
            jax.ShapeDtypeStruct((ff, width), BF),
        ],
        grid_spec=pltpu.PrefetchScalarGridSpec(
            num_scalar_prefetch=4,
            grid=(capacity // TILE,),
            in_specs=[tile(1), once((total, width))]
            + [pl.BlockSpec(memory_space=pl.ANY)] * len(parts),
            out_specs=[tile(width), tile(ff), pl.BlockSpec((ff, width), lambda i, *_: (0, 0))],
            scratch_shapes=[
                pltpu.VMEM((TILE, width), F32),
                pltpu.SemaphoreType.DMA((2 * len(parts),)),
            ],
        ),
        compiler_params=pltpu.CompilerParams(vmem_limit_bytes=48 << 20),
        cost_estimate=pl.CostEstimate(
            flops=total * (width * ff + WIN * width),
            bytes_accessed=2 * total * width + 4 * ff * width + capacity * (2 * width + 4 * ff),
            transcendentals=0,
        ),
    )(*tables[:3], me, tables[3], upstream, *parts)


def expert_kernel(
    own, tiles_ref, low_ref, windows_ref, ids_ref, tok_ref, h_ref, router_ref, raw_ref, *refs
):
    parts = refs[:-8]
    rows_ref, hid_ref, dab_ref, dh_ref, share_ref, both_ref, acc_ref, sems = refs[-8:]
    wg_ref, wu_ref = both_ref.at[0], both_ref.at[1]
    i = pl.program_id(0)
    ff = wg_ref.shape[1]

    @pl.when(i == 0)
    def _():
        if len(parts) == 1:
            copy_all([pltpu.make_async_copy(parts[0], both_ref, sems.at[0])])
            return
        rows = wg_ref.shape[0] // 4
        half = rows // 2
        copies = []
        for away in range(4):
            owner = pl.multiple_of((ids_ref[1] ^ away) * rows, rows)
            for part, first, count, which, shift in (
                (parts[away], 0, rows, 0, 0),
                (parts[away], rows, half, 1, 0),
                (parts[4 + away], 0, half, 1, half),
            ):
                copies.append(
                    pltpu.make_async_copy(
                        part.at[pl.ds(first, count)],
                        both_ref.at[which, pl.ds(owner + shift, count)],
                        sems.at[len(copies)],
                    )
                )
        copy_all(copies)

    @pl.when(i < tiles_ref[0])
    def _():
        rows = pick_rows(tok_ref[...], low_ref[i], windows_ref[i], h_ref, acc_ref)
        rows_ref[...] = rows
        logits = dot(rows, router_ref[...])
        probs = jnp.exp(logits - jnp.max(logits, axis=1, keepdims=True))
        column = lax.broadcasted_iota(jnp.int32, probs.shape, 1)
        mine = jnp.sum(jnp.where(column == ids_ref[0] + own, probs, 0.0), axis=1, keepdims=True)
        gate = mine / jnp.sum(probs, axis=1, keepdims=True)
        share = 0.0
        part = ff // 4
        for c in range(4):
            cols = slice(c * part, (c + 1) * part)
            a = dot(rows, wg_ref[:, cols])
            b = dot(rows, wu_ref[:, cols])
            raw = raw_ref[:, cols]
            sig = 1.0 / (1.0 + jnp.exp(-a))
            silu = a * sig
            hid = silu * b
            share += jnp.sum(hid * raw, axis=1, keepdims=True)
            raw = raw * gate
            hid_ref[:, cols] = (hid * gate).astype(BF)
            dab_ref[:, cols] = (raw * b * (sig * (1.0 + a * (1.0 - sig)))).astype(BF)
            dab_ref[:, ff + c * part : ff + (c + 1) * part] = (raw * silu).astype(BF)
        share_ref[...] = share
        dh = dot(dab_ref[:, :ff], wg_ref[...], NT) + dot(dab_ref[:, ff:], wu_ref[...], NT)
        dh_ref[...] = dh.astype(BF)

    @pl.when(i >= tiles_ref[0])
    def _():
        for ref in (rows_ref, hid_ref, dab_ref, dh_ref, share_ref):
            ref[...] = jnp.zeros_like(ref)


def expert_rows(tables, own, ids, hidden, router, parts, raw):
    total, width = hidden.shape
    capacity, ff = raw.shape
    tile = lambda n: pl.BlockSpec((TILE, n), lambda i, *_: (i, 0))
    once = lambda shape: pl.BlockSpec(shape, lambda i, *_: (0, 0), pipeline_mode=pl.Buffered(1))
    made = lambda n, dtype=BF: jax.ShapeDtypeStruct((capacity, n), dtype)
    return pl.pallas_call(
        functools.partial(expert_kernel, own),
        out_shape=[made(width), made(ff), made(2 * ff), made(width), made(1, F32)],
        grid_spec=pltpu.PrefetchScalarGridSpec(
            num_scalar_prefetch=4,
            grid=(capacity // TILE,),
            in_specs=[tile(1), once((total, width)), once(router.shape), tile(ff)]
            + [pl.BlockSpec(memory_space=pl.ANY)] * len(parts),
            out_specs=[tile(width), tile(ff), tile(2 * ff), tile(width), tile(1)],
            scratch_shapes=[
                pltpu.VMEM((2, width, ff), BF),
                pltpu.VMEM((TILE, width), F32),
                pltpu.SemaphoreType.DMA((12,)),
            ],
        ),
        compiler_params=pltpu.CompilerParams(vmem_limit_bytes=56 << 20),
        cost_estimate=pl.CostEstimate(
            flops=total * (4 * width * ff + WIN * width),
            bytes_accessed=2 * total * width + 4 * ff * width + capacity * (4 * width + 10 * ff),
            transcendentals=total * ff,
        ),
    )(*tables[:3], ids, tables[3], hidden, router, raw, *parts)


def combine_kernel(experts, shared, start_ref, more_ref, wide_ref, id_ref, pos_ref, *refs):
    rows_refs, share_refs = refs[:experts], refs[experts:-2]
    out_ref, acc_ref = refs[-2:]
    i = pl.program_id(0)
    span = lax.broadcasted_iota(jnp.int32, (TILE, TILE), 1)
    last, width = rows_refs[0].shape[0] - TILE, rows_refs[0].shape[1]

    def window(e, j):
        base = start_ref[e, i] + j * TILE
        start = pl.multiple_of(jnp.minimum(base, last), 16)
        pos = pos_ref[:, e : e + 1]
        match = (pos - start == span) & (pos >= base)
        return dot(match.astype(F32).astype(BF), rows_refs[e][pl.ds(start, TILE), :])

    acc_ref[...] = sum(window(e, 0) for e in range(experts))
    for e in range(experts):

        @pl.when(more_ref[e, i] > 0)
        def _():
            acc_ref[...] += window(e, 1)

    out_ref[:, :width] = acc_ref[...].astype(BF)
    if shared:
        wide_span = lax.broadcasted_iota(jnp.int32, (TILE, 384), 1)
        column = lax.broadcasted_iota(jnp.int32, (TILE, shared), 1)
        extra = jnp.zeros((TILE, shared), F32)
        for e in range(experts):
            wide = pl.multiple_of(wide_ref[e, i], 128)
            match = pos_ref[:, e : e + 1] - wide == wide_span
            share = share_refs[e][:, pl.ds(wide, 384)]
            own = jnp.sum(jnp.where(match, share, 0.0), axis=1, keepdims=True)
            head = own.astype(BF).astype(F32)
            first = 2 * (id_ref[0] + e)
            extra += jnp.where(column == first, head, 0.0)
            extra += jnp.where(column == first + 1, own - head, 0.0)
        out_ref[:, width:] = extra.astype(BF)


def combine_rows(tables, ids, rows, shares=()):
    experts, (capacity, width) = len(rows), rows[0].shape
    total = tables[3].shape[0]
    shared = 128 if shares else 0
    once = lambda shape: pl.BlockSpec(shape, lambda i, *_: (0, 0), pipeline_mode=pl.Buffered(1))
    tile = lambda n: pl.BlockSpec((TILE, n), lambda i, *_: (i, 0))
    return pl.pallas_call(
        functools.partial(combine_kernel, experts, shared),
        out_shape=jax.ShapeDtypeStruct((total, width + shared), BF),
        grid_spec=pltpu.PrefetchScalarGridSpec(
            num_scalar_prefetch=4,
            grid=(total // TILE,),
            in_specs=[tile(experts)]
            + [once((capacity, width))] * experts
            + [once((1, capacity))] * len(shares),
            out_specs=tile(width + shared),
            scratch_shapes=[pltpu.VMEM((TILE, width), F32)],
        ),
        compiler_params=pltpu.CompilerParams(vmem_limit_bytes=48 << 20),
        cost_estimate=pl.CostEstimate(
            flops=2 * experts * total * TILE * width,
            bytes_accessed=2 * (experts * capacity + total) * width,
            transcendentals=0,
        ),
    )(*tables[:3], ids, tables[3], *rows, *shares)


def local(
    tokens,
    cotangent,
    routes,
    block_of_slot,
    cont_seg,
    w_query,
    w_key,
    w_value,
    w_out,
    w_router,
    attn_gain,
    query_gain,
    key_gain,
    ffn_gain,
    w_gate,
    w_up,
    w_down,
):
    ctx_size = lax.axis_size("ctx")
    exp_size = lax.axis_size("exp")
    me = lax.axis_index("ctx")
    exp_index = lax.axis_index("exp")
    tok_rows = tokens.shape[0]
    part_rows = w_query.shape[0]
    own_width = D // ctx_size
    own_heads = HEADS // ctx_size
    experts = w_router.shape[1]
    own_experts = w_gate.shape[0]
    slot_table = block_of_slot[0]
    seg_row = cont_seg[0]
    group_rows = ctx_size * tok_rows
    factor = 1.0 / math.sqrt(HD)

    tokens_group, tokens_there = gather_group(tokens, slot_table, me)
    small = jnp.concatenate(
        [w_router] + [g[:, None] for g in (attn_gain, query_gain, key_gain, ffn_gain)], axis=1
    )
    small = jnp.pad(small, ((0, 0), (0, 128 - small.shape[1])))
    by_owner = jnp.stack(
        [w.reshape(part_rows, ctx_size, own_width) for w in (w_query, w_key, w_value)], axis=2
    )
    by_owner = jnp.swapaxes(by_owner, 0, 1).reshape(ctx_size, part_rows, 3 * own_width)
    by_owner = jnp.concatenate(
        [by_owner, jnp.broadcast_to(small, (ctx_size,) + small.shape)], axis=2
    )
    out_full = lax.all_gather(w_out, "exp", axis=0, tiled=True)
    own_columns, out_full = after_all((exchange(by_owner, me), out_full))
    packed = lax.all_gather(own_columns, "exp", axis=1, tiled=True).reshape(D, 3 * own_width + 128)
    small_full = packed[:, 3 * own_width :]
    router_full = small_full[:, :experts]
    gains = small_full[:, experts : experts + 4].astype(F32)
    gain_attn, gain_ffn = gains[:, 0], gains[:, 3]
    own_gains = lax.dynamic_slice(gains, (me * own_width, 0), (own_width, 4))
    gain_query, gain_key = own_gains[:, 1], own_gains[:, 2]
    routes_all = lax.all_to_all(
        jnp.broadcast_to(routes[None], (exp_size,) + routes.shape),
        "exp",
        split_axis=0,
        concat_axis=0,
        tiled=True,
    ).reshape(exp_size * tok_rows, TOP)
    upstream_all = lax.all_gather(cotangent, "exp", axis=0, tiled=True)
    packs = [pack_expert(w_gate[e], w_up[e], w_down[e]) for e in range(own_experts)]
    if ctx_size == 4:
        ahead = after_all(packs[0], *tokens_there)
        ahead = send_x(ahead[0]), send_y(ahead[1])

    seg_ids = jnp.concatenate([jnp.full((PROMPT,), -1, jnp.int32), seg_row])
    starts = jnp.sum(
        (seg_row[None, :] < jnp.arange(CONT, dtype=jnp.int32)[:, None]).astype(jnp.int32), axis=1
    )
    first_pos = jnp.sum(
        jnp.where(
            seg_row[:, None] == jnp.arange(CONT, dtype=jnp.int32)[None, :], starts[None, :], 0
        ),
        axis=1,
    )
    cont_pos = PROMPT + jnp.arange(CTOK, dtype=jnp.int32) - first_pos
    position = jnp.concatenate([jnp.arange(PROMPT, dtype=jnp.int32), cont_pos])
    cos_part, sin_part = angles(position)
    group_inputs = tokens_group.astype(F32)
    normed_group = group_inputs * inverse_root(group_inputs)
    hidden_one = (normed_group * gain_attn).astype(BF)
    projected = jnp.dot(hidden_one, packed, preferred_element_type=F32)
    query_pre = projected[:, :own_width]
    key_pre = projected[:, own_width : 2 * own_width]
    squares = jnp.stack([jnp.sum(query_pre * query_pre, axis=1), jnp.sum(key_pre * key_pre, axis=1)])
    if ctx_size == 4:
        squares = after(squares, *ahead)
    squares = sum_over_ctx(squares)
    if ctx_size == 4:
        direct = after_all(packs[0], squares)
        direct = send_x(direct[1]), send_y(direct[0])
    roots = lax.rsqrt(squares / D + epsilon)
    root_query, root_key = roots[0][:, None], roots[1][:, None]
    normed_query = query_pre * root_query
    normed_key = key_pre * root_key
    query_rot, key_rot, value_low, context_low = attend(
        projected,
        roots.T,
        jnp.stack([gain_query, gain_key]),
        cos_part,
        sin_part,
        seg_ids,
        own_width,
    )
    branch_part = jnp.dot(context_low, out_full, preferred_element_type=F32)
    if ctx_size == 4:
        branch_part = after(branch_part, *direct)
    branch, unused, unused, branch_there = scatter_group(branch_part, slot_table, me)
    me_table = jnp.reshape(me, (1,)).astype(jnp.int32)
    width = w_gate.shape[2]
    lows, highs, backs = [], [], []
    if ctx_size == 4:
        passed = after_all(ahead, *branch_there)
        passed = send_y(passed[0]), send_x(passed[1])
        lows.append((packs[0][0], ahead[0], direct[1], passed[0]))
        highs.append((packs[0][1], direct[0], ahead[1], passed[1]))
        upstream, first_passed = upstream_all, passed
        for e in range(1, own_experts):
            low, high = after_all(packs[e], *passed)
            ahead = send_x(low), send_y(high)
            low, high = after_all((low, high), *ahead)
            direct = send_x(high), send_y(low)
            passed = send_y(ahead[0]), send_x(ahead[1])
            lows.append((packs[e][0], ahead[0], direct[1], passed[0]))
            highs.append((packs[e][1], direct[0], ahead[1], passed[1]))
            upstream = after(upstream, *ahead)
    else:
        for e in range(own_experts):
            both, down = whole_expert(*after_all((w_gate[e], w_up[e], w_down[e]), *branch_there))
            lows.append((both,))
            highs.append((down,))
        upstream = upstream_all
        first_passed = branch_there

    own_ids = exp_index * own_experts + jnp.arange(own_experts, dtype=jnp.int32)
    member = jnp.any(after(routes_all, *first_passed)[:, :, None] == own_ids[None, None, :], axis=1)
    place_of = prefix_count(member)
    capacity = exp_size * 8 * ((5 * tok_rows * TOP // (4 * experts) + 7) // 8)
    row_tiles = (capacity + TILE - 1) // TILE
    capacity = row_tiles * TILE
    all_rows = exp_size * tok_rows
    row_ids = jnp.arange(capacity, dtype=jnp.int32)
    hit = (place_of.T[:, None, :] == row_ids[None, :, None]) & member.T[:, None, :]
    token_ids = jnp.arange(all_rows, dtype=jnp.int32)
    token_of_row = jnp.max(jnp.where(hit, token_ids[None, None, :], -1), axis=2)
    counts = jnp.sum(member.astype(jnp.int32), axis=0)
    used_tiles = (counts + TILE - 1) // TILE
    by_tile = token_of_row.reshape(own_experts * row_tiles, TILE)
    low_token = jnp.maximum(by_tile[:, 0], 0) // 128 * 128
    windows = jnp.maximum((jnp.max(by_tile, axis=1) - low_token) // WIN + 1, 1)
    low_token = low_token.reshape(own_experts, row_tiles)
    windows = windows.reshape(own_experts, row_tiles)
    row_tables = [
        (used_tiles[e : e + 1], low_token[e], windows[e], token_of_row[e][:, None])
        for e in range(own_experts)
    ]
    place_column = jnp.where(member, place_of, NOWHERE)
    first_place = place_of[::TILE].T
    in_tile = jnp.sum(member.reshape(-1, TILE, own_experts).astype(jnp.int32), axis=1).T
    first_row = first_place // 16 * 16
    more_rows = (first_place + in_tile - first_row > TILE).astype(jnp.int32)
    share_row_start = jnp.minimum(first_place // 128 * 128, capacity - 384)
    token_tables = (first_row, more_rows, share_row_start, place_column)

    ids = jnp.stack([own_ids[0], me.astype(jnp.int32)])
    backs.append(back_rows(row_tables[0], me_table, upstream, highs[0], width))

    inputs = tokens.astype(F32)
    middle = inputs + branch
    root_two = inverse_root(middle)
    normed_two = middle * root_two
    hidden_two = (normed_two * gain_ffn).astype(BF)
    hidden_all = lax.all_gather(hidden_two, "exp", axis=0, tiled=True)
    logits = jnp.dot(hidden_two, router_full, preferred_element_type=F32)
    router_prob = jax.nn.softmax(logits, axis=-1)

    every = range(own_experts)
    made = []
    for e in every:
        if e > 0:
            upstream = after(upstream_all, made[-1][3])
            highs[e] = after_all(highs[e], made[-1][3])
            backs.append(back_rows(row_tables[e], me_table, upstream, highs[e], width))
        parts = tuple(lows[e]) + tuple(highs[e]) if ctx_size == 4 else lows[e]
        made.append(
            expert_rows(row_tables[e], e, ids, hidden_all, router_full, parts, backs[e][1])
        )
    shares = [m[4].reshape(1, capacity) for m in made]
    grad_two_part = combine_rows(token_tables, ids, [m[3] for m in made], shares)
    grad_two = lax.psum_scatter(grad_two_part, "exp", scatter_dimension=0, tiled=True)
    def weight_grads(e, *others):
        rows, hidden, grad_hidden = after_all(made[e][:3], *others)
        return (
            lax.dot_general(rows, grad_hidden, TN, preferred_element_type=F32).astype(BF),
            lax.dot_general(hidden, backs[e][0], TN, preferred_element_type=F32).astype(BF),
        )

    expert_grads = [weight_grads(0, grad_two_part)]
    if ctx_size == 4:
        take = expert_take(expert_grads[0])
        payload = joined_payload(take, me)
    else:
        payload = expert_grads[0]
    results = [
        jnp.dot(
            after(made[e][1], *payload), backs[e][2], preferred_element_type=F32
        ).astype(BF)
        for e in every
    ]
    if ctx_size == 4:
        ahead, direct = split_sums((send_x(payload[0]), send_y(payload[1])))
        last = scatter_last_payload(take, me, ahead)
        results = after_all(results, *last)
        last = send_y(last[0]), send_x(last[1])
    else:
        direct, last = scatter_expert_first(expert_grads[0], me), ()
    mixture_part = combine_rows(token_tables, ids, results)
    directs, lasts = [direct], [last]

    mixture = lax.psum_scatter(mixture_part, "exp", scatter_dimension=0, tiled=True)
    output = (middle + mixture.astype(F32)).astype(BF)
    grad_two = after(grad_two, mixture_part)
    grad_prob = jnp.sum(
        grad_two[:, D : D + 2 * experts].astype(F32).reshape(tok_rows, experts, 2), axis=2
    )
    grad_two = grad_two[:, :D].astype(F32)
    grad_logits = (
        router_prob * (grad_prob - jnp.sum(router_prob * grad_prob, axis=-1, keepdims=True))
    ).astype(BF)
    grad_router = jnp.einsum("td,te->ed", hidden_two, grad_logits, preferred_element_type=F32)
    grad_two = grad_two + jnp.einsum(
        "te,de->td", grad_logits, router_full, preferred_element_type=F32
    )
    grad_ffn_gain = jnp.sum(grad_two * normed_two, axis=0)
    grad_middle = cotangent.astype(F32) + norm_back(grad_two * gain_ffn, normed_two, root_two)

    own_grad = after(grad_middle.astype(BF), *directs[0], *lasts[0])
    branch_grad, grad_there = gather_group(own_grad, slot_table, me)
    sums = []
    for e in range(1, own_experts):
        expert_grads.append(weight_grads(e, own_grad))
        sums.append(scatter_expert_first(after_all(expert_grads[e], *grad_there), me))
    grad_context = lax.dot_general(branch_grad, out_full, NT, preferred_element_type=F32).astype(BF)
    out_grad = lax.dot_general(
        context_low, branch_grad, TN, preferred_element_type=F32
    ).astype(BF)
    grad_query_norm, grad_key_norm, grad_value = attend_back(
        query_rot, key_rot, value_low, grad_context, cos_part, sin_part, seg_ids
    )
    grad_query_gain = jnp.sum(grad_query_norm * normed_query, axis=0)
    grad_key_gain = jnp.sum(grad_key_norm * normed_key, axis=0)
    scaled_query = grad_query_norm * gain_query
    scaled_key = grad_key_norm * gain_key
    products = jnp.stack(
        [jnp.sum(scaled_query * normed_query, axis=1), jnp.sum(scaled_key * normed_key, axis=1)]
    )
    weight_sums = [scatter_expert_end(expert_grads[0], directs[0], lasts[0], me)]
    *weight_sums[0], products = after_all(
        (*weight_sums[0], products), out_grad, *(piece for pieces in sums for piece in pieces)
    )
    means = sum_over_ctx(products) / D
    for e in range(1, own_experts):
        ahead, direct = split_sums(sums[e - 1])
        directs.append(direct)
        ahead = after_all(ahead, means)
        take = expert_take(expert_grads[e])
        if ctx_size == 4:
            last_sent = scatter_last_payload(take, me, ahead)
            lasts.append((send_y(last_sent[0]), send_x(last_sent[1])))
        else:
            last_sent = direct
            lasts.append(())
    grad_projected = jnp.concatenate(
        [
            root_query * (scaled_query - normed_query * means[0][:, None]),
            root_key * (scaled_key - normed_key * means[1][:, None]),
            grad_value,
        ],
        axis=1,
    ).astype(BF)
    grad_packed = jnp.pad(grad_projected, ((0, 0), (0, 128)))
    grad_one_part = lax.dot_general(grad_packed, packed, NT, preferred_element_type=F32)
    grad_attn_gain = jnp.sum(grad_one_part * normed_group, axis=0)
    left, right = after_all((hidden_one, grad_projected), *last_sent)
    qkv_grad = lax.dot_general(left, right, TN, preferred_element_type=F32).astype(BF)
    grad_one, one_first, one_sent, unused = scatter_group(
        after(grad_one_part, *(piece for pieces in lasts[1:] for piece in pieces)),
        slot_table,
        me,
        joined=True,
    )
    for e in range(1, own_experts):
        direct, last = after_all(directs[e], *one_sent), after_all(lasts[e], *one_sent)
        weight_sums.append(scatter_expert_end(expert_grads[e], direct, last, me))
    gate_grad, up_grad, down_grad = (jnp.stack(parts) for parts in zip(*weight_sums))
    out_sum = lax.psum_scatter(
        out_grad, "exp", scatter_dimension=0, tiled=True
    ).astype(F32)
    qkv_sum = lax.psum_scatter(
        after(qkv_grad, mixture).reshape(ctx_size, exp_size * part_rows, 3 * own_width),
        "exp",
        scatter_dimension=1,
        tiled=True,
    )
    qkv_own = exchange(qkv_sum, me).astype(F32)
    projection_grads = [
        jnp.swapaxes(qkv_own[:, :, i * own_width : (i + 1) * own_width], 0, 1).reshape(part_rows, D)
        for i in range(3)
    ]
    root_one = inverse_root(inputs)
    normed_one = inputs * root_one
    grad_input = grad_middle + norm_back(grad_one * gain_attn, normed_one, root_one)
    head_gains = lax.dynamic_update_slice(
        jnp.zeros((2, D), F32), jnp.stack([grad_query_gain, grad_key_gain]), (0, me * own_width)
    )
    small_sums = jnp.concatenate(
        [grad_router, jnp.stack([grad_ffn_gain, grad_attn_gain]), head_gains]
    )
    small_sums = sum_to_rows(after(small_sums, *one_first), me, one_sent, qkv_sum)
    return (
        output,
        grad_input,
        projection_grads[0],
        projection_grads[1],
        projection_grads[2],
        out_sum,
        small_sums[:experts].T,
        small_sums[experts + 1],
        small_sums[experts + 2],
        small_sums[experts + 3],
        small_sums[experts],
        gate_grad,
        up_grad,
        down_grad,
    )


def solution(mesh):
    rows = P(BOTH, None)
    weights = P("exp", "ctx", None)
    in_specs = (
        (rows, rows, rows, P("exp", None), P("exp", None))
        + (rows,) * 5
        + (P(BOTH),) * 4
        + (weights,) * 3
    )
    out_specs = (rows,) * 7 + (P(BOTH),) * 4 + (weights,) * 3
    return jax.shard_map(local, mesh=mesh, in_specs=in_specs, out_specs=out_specs, check_vma=False)
```

```python
import functools
import math

import jax
import jax.numpy as jnp
from jax import lax
from jax.experimental import pallas as pl
from jax.experimental.pallas import tpu as pltpu
from jax.sharding import PartitionSpec as P

D = 2048
HEADS = 16
HD = 128
TOP = 8
PROMPT = 1024
CONT = 2
CTOK = 512

epsilon = 1e-05
rope_base = 10000.0
BF = jnp.bfloat16
F32 = jnp.float32
BOTH = ("ctx", "exp")
X_PAIRS = [(i, i ^ 1) for i in range(4)]
Y_PAIRS = [(i, i ^ 2) for i in range(4)]
XY_PAIRS = [(i, i ^ 3) for i in range(4)]
NT = (((1,), (1,)), ((), ()))
TN = (((0,), (0,)), ((), ()))
TILE = 256
WIN = 768
NOWHERE = -(1 << 20)


def inverse_root(values):
    return lax.rsqrt(jnp.mean(values * values, axis=-1, keepdims=True) + epsilon)


def norm_back(gradient, normed, root_part):
    return root_part * (gradient - normed * jnp.mean(gradient * normed, axis=-1, keepdims=True))


def angles(position):
    half_dim = HD // 2
    inverse = rope_base ** (-2.0 * jnp.arange(half_dim, dtype=F32) / HD)
    phases = position.astype(F32)[:, None] * inverse[None, :]
    cosine, sine = jnp.cos(phases), jnp.sin(phases)
    return jnp.concatenate([cosine, cosine], axis=1), jnp.concatenate([-sine, sine], axis=1)


def send_x(value):
    return lax.ppermute(value, "ctx", X_PAIRS)


def send_y(value):
    return lax.ppermute(value, "ctx", Y_PAIRS)


def send_xy(value):
    return lax.ppermute(value, "ctx", XY_PAIRS)


def after(value, *others):
    return lax.optimization_barrier((value,) + others)[0]


def after_all(values, *others):
    return lax.optimization_barrier(tuple(values) + others)[: len(values)]


def gather_pieces(low, high):
    low_x, high_y = send_x(low), send_y(high)
    high_x, low_y = send_x(high), send_y(low)
    return (low_x, low_y, send_y(low_x)), (high_x, high_y, send_x(high_y))


def scatter_ahead(take, me):
    return send_x(take(me ^ 3, 0).astype(BF)), send_y(take(me ^ 3, 1).astype(BF))


def scatter_direct(take, me, *others):
    low, high = take(me ^ 1, 0).astype(BF), take(me ^ 2, 1).astype(BF)
    if others:
        low, high = after_all((low, high), *others)
    return send_x(low), send_y(high)


def scatter_last_payload(take, me, ahead):
    low = (take(me ^ 2, 0).astype(F32) + ahead[0].astype(F32)).astype(BF)
    high = (take(me ^ 1, 1).astype(F32) + ahead[1].astype(F32)).astype(BF)
    return low, high


def scatter_last(take, me, ahead):
    low, high = scatter_last_payload(take, me, ahead)
    return send_y(low), send_x(high)


def scatter_end(take, me, direct, last):
    return [
        take(me, part).astype(F32) + direct[part].astype(F32) + last[part].astype(F32)
        for part in range(2)
    ]


def exchange(blocks, me):
    if lax.axis_size("ctx") != 4:
        return lax.all_to_all(blocks, "ctx", split_axis=0, concat_axis=0, tiled=True)
    sends = (lambda part: part, send_x, send_y, send_xy)
    parts = [
        send(lax.dynamic_index_in_dim(blocks, me ^ away, 0, keepdims=False))
        for away, send in enumerate(sends)
    ]

    def from_ctx(c):
        chosen = parts[0]
        for away in range(1, 4):
            chosen = jnp.where((me ^ c) == away, parts[away], chosen)
        return chosen

    return jnp.stack([from_ctx(c) for c in range(4)])


def sum_over_ctx(value):
    if lax.axis_size("ctx") != 4:
        return lax.psum(value, "ctx")
    value = value + send_x(value)
    return value + send_y(value)


def sum_to_rows(values, me, others, late):
    ctx_size, exp_size = lax.axis_size("ctx"), lax.axis_size("exp")
    count, width = values.shape
    parts = values.reshape(count, ctx_size, exp_size, width // (ctx_size * exp_size))
    parts = jnp.transpose(parts, (2, 1, 0, 3))
    exp_index, step = lax.axis_index("exp"), exp_size // 2
    while step:
        upper = (exp_index // step) % 2
        kept = lax.dynamic_slice_in_dim(parts, upper * step, step, 0)
        sent = lax.dynamic_slice_in_dim(parts, (1 - upper) * step, step, 0)
        parts = kept + lax.ppermute(sent, "exp", [(i, i ^ step) for i in range(exp_size)])
        step //= 2
        parts = after(parts, *others)
    return jnp.sum(exchange(after(parts[0], late), me), axis=0)


def pack_expert(w_gate, w_up, w_down):
    half, width = w_up.shape[0] // 2, w_up.shape[1]
    low = jnp.concatenate([w_gate, w_up[:half]], axis=0)
    high = jnp.concatenate([w_up[half:], w_down[:, :width], w_down[:, width:]], axis=0)
    return low, high


def whole_expert(w_gate, w_up, w_down):
    return (
        lax.all_gather(jnp.stack([w_gate, w_up]), "ctx", axis=1, tiled=True),
        lax.all_gather(w_down, "ctx", axis=0, tiled=True),
    )


def expert_take(grads):
    gate_up, down = grads
    rows, width = gate_up.shape[0] // 4, gate_up.shape[1] // 2
    half = down.shape[0] // 8

    def take(owner, part):
        first = (2 * owner + part) * half
        return jnp.concatenate(
            [
                lax.dynamic_slice(gate_up, (owner * rows, part * width), (rows, width)),
                lax.dynamic_slice(down, (first, 0), (half, width)),
                lax.dynamic_slice(down, (first, width), (half, width)),
            ],
            axis=0,
        )

    return take


def scatter_expert_first(grads, me):
    if lax.axis_size("ctx") != 4:
        return tuple(
            lax.psum_scatter(grad, "ctx", scatter_dimension=0, tiled=True) for grad in grads
        )
    return scatter_joined(expert_take(grads), me)


def scatter_joined(take, me):
    low, high = joined_payload(take, me)
    return send_x(low), send_y(high)


def joined_payload(take, me):
    low = jnp.stack([take(me ^ 1, 0), take(me ^ 3, 0)]).astype(BF)
    high = jnp.stack([take(me ^ 2, 1), take(me ^ 3, 1)]).astype(BF)
    return low, high


def split_sums(sums):
    if lax.axis_size("ctx") != 4:
        return sums, sums
    return (sums[0][1], sums[1][1]), (sums[0][0], sums[1][0])


def scatter_expert_end(grads, direct, last, me):
    if lax.axis_size("ctx") != 4:
        gate_up, down = (part.astype(F32) for part in direct)
        width = gate_up.shape[1] // 2
        return gate_up[:, :width], gate_up[:, width:], down
    first, second = scatter_end(expert_take(grads), me, direct, last)
    rows, half = grads[0].shape[0] // 4, grads[1].shape[0] // 8
    down = [
        jnp.concatenate([part[rows : rows + half], part[rows + half :]], axis=1)
        for part in (first, second)
    ]
    return first[:rows], second[:rows], jnp.concatenate(down, axis=0)


def pick_blocks(blocks, order):
    return jnp.concatenate(
        [
            lax.dynamic_index_in_dim(blocks, order[i], 0, keepdims=False)
            for i in range(order.shape[0])
        ],
        axis=0,
    )


def gather_group(rows, slot_table, me):
    block = rows.shape[0] // 2
    if lax.axis_size("ctx") != 4:
        blocks = slot_table.shape[0]
        whole = lax.all_gather(rows, "ctx", axis=0, tiled=True).reshape(blocks, block, -1)
        match = slot_table[None, :] == jnp.arange(blocks, dtype=jnp.int32)[:, None]
        order = jnp.sum(jnp.where(match, jnp.arange(blocks, dtype=jnp.int32)[None, :], 0), axis=1)
        return pick_blocks(whole, order), ()
    pieces = gather_pieces(rows[:block], rows[block:])
    whole = jnp.zeros((8 * block, rows.shape[1]), rows.dtype)
    for slot in range(2):
        for away in range(4):
            part = pieces[slot][away - 1] if away else rows[slot * block : (slot + 1) * block]
            start = slot_table[2 * (me ^ away) + slot] * block
            whole = lax.dynamic_update_slice(whole, part, (start, 0))
    return whole, (pieces[0][2], pieces[1][2])


def scatter_group(partial, slot_table, me, joined=False):
    blocks = slot_table.shape[0]
    block = partial.shape[0] // blocks
    if lax.axis_size("ctx") != 4:
        ordered = pick_blocks(partial.reshape(blocks, block, -1), slot_table).astype(BF)
        whole = lax.psum_scatter(ordered, "ctx", scatter_dimension=0, tiled=True)
        return whole.astype(F32), (whole,), (whole,), (whole,)

    def take(owner, part):
        start = slot_table[2 * owner + part] * block
        return lax.dynamic_slice(partial, (start, 0), (block, partial.shape[1]))

    first = ()
    if joined:
        first = joined_payload(take, me)
        ahead, direct = split_sums((send_x(first[0]), send_y(first[1])))
    else:
        ahead, direct = scatter_ahead(take, me), scatter_direct(take, me)
    sent = scatter_last_payload(take, me, ahead)
    if joined:
        sent = after_all(sent)
    last = send_y(sent[0]), send_x(sent[1])
    return jnp.concatenate(scatter_end(take, me, direct, last), axis=0), first, sent, last


def prefix_count(member):
    rows, columns = member.shape
    width = 128
    blocks = rows // width
    ones = member.astype(BF).reshape(blocks, width, columns)
    lower = (
        jnp.arange(width)[:, None] > jnp.arange(width)[None, :]
    ).astype(BF)
    inner = jnp.einsum("pq,bqc->bpc", lower, ones, preferred_element_type=F32)
    totals = jnp.sum(ones.astype(F32), axis=1)
    before = (jnp.arange(blocks)[:, None] > jnp.arange(blocks)[None, :]).astype(F32)
    outer = jnp.sum(before[:, :, None] * totals[None, :, :], axis=1)
    return (inner + outer[:, None, :]).reshape(rows, columns).astype(jnp.int32)


def dot(left, right, dims=(((1,), (0,)), ((), ()))):
    return lax.dot_general(left, right, dims, preferred_element_type=F32)


def turned(values, cosine, sine):
    return values * cosine + pltpu.roll(values, HD // 2, 1) * sine


def tile_weights(query, key, seg_q, seg_k, first, factor):
    rows, width = query.shape[0], key.shape[0]
    scores = dot(query, key, NT) * factor
    q_place = first + lax.broadcasted_iota(jnp.int32, (rows, width), 0)
    k_place = lax.broadcasted_iota(jnp.int32, (rows, width), 1)
    allowed = k_place <= q_place
    if first >= PROMPT:
        allowed = allowed & ((seg_k < 0) | (seg_k == seg_q))
    scores = jnp.where(allowed, scores, -1e30)
    weights = jnp.exp(scores - jnp.max(scores, axis=1, keepdims=True))
    return weights, jnp.sum(weights, axis=1, keepdims=True)


def attend_kernel(
    tiles,
    factor,
    qp_ref,
    kp_ref,
    vp_ref,
    root_ref,
    key_root_ref,
    gain_ref,
    cos_ref,
    sin_ref,
    sq_ref,
    sk_ref,
    q_ref,
    k_ref,
    v_ref,
    o_ref,
):
    at = pl.program_id(1)
    tile = qp_ref.shape[0]

    @pl.when(at == 0)
    def _():
        keys = kp_ref[...] * key_root_ref[:, 1:2] * gain_ref[1:2]
        k_ref[...] = turned(keys, cos_ref[...], sin_ref[...]).astype(BF)
        v_ref[...] = vp_ref[...].astype(BF)

    for i in range(tiles):

        @pl.when(at == i)
        def _():
            own = slice(i * tile, (i + 1) * tile)
            width = (i + 1) * tile
            queries = qp_ref[...] * root_ref[:, 0:1] * gain_ref[0:1]
            query = turned(queries, cos_ref[own], sin_ref[own]).astype(BF)
            q_ref[...] = query
            weights, total = tile_weights(
                query, k_ref[:width], sq_ref[...], sk_ref[:, :width], i * tile, factor
            )
            o_ref[...] = (dot(weights.astype(BF), v_ref[:width]) / total).astype(BF)


def attend(projected, roots, gains, cosine, sine, seg, width, tile=512):
    rows = projected.shape[0]
    heads, tiles = width // HD, rows // tile
    own = pl.BlockSpec((tile, HD), lambda h, i: (i, h))
    whole = pl.BlockSpec((rows, HD), lambda h, i: (0, h))
    pairs = heads * rows * rows * (tiles + 1) // (2 * tiles)
    return pl.pallas_call(
        functools.partial(attend_kernel, tiles, 1.0 / math.sqrt(HD)),
        out_shape=[jax.ShapeDtypeStruct((rows, width), BF)] * 4,
        grid=(heads, tiles),
        in_specs=[
            own,
            pl.BlockSpec((rows, HD), lambda h, i: (0, heads + h)),
            pl.BlockSpec((rows, HD), lambda h, i: (0, 2 * heads + h)),
            pl.BlockSpec((tile, 2), lambda h, i: (i, 0)),
            pl.BlockSpec((rows, 2), lambda h, i: (0, 0)),
            pl.BlockSpec((2, HD), lambda h, i: (0, h)),
            pl.BlockSpec((rows, HD), lambda h, i: (0, 0)),
            pl.BlockSpec((rows, HD), lambda h, i: (0, 0)),
            pl.BlockSpec((tile, 1), lambda h, i: (i, 0)),
            pl.BlockSpec((1, rows), lambda h, i: (0, 0)),
        ],
        out_specs=[own, whole, whole, own],
        compiler_params=pltpu.CompilerParams(vmem_limit_bytes=48 << 20),
        cost_estimate=pl.CostEstimate(
            flops=4 * pairs * HD, bytes_accessed=20 * rows * width, transcendentals=pairs
        ),
    )(
        projected,
        projected,
        projected,
        roots,
        roots,
        gains,
        cosine,
        sine,
        seg[:, None],
        seg[None, :],
    )


def attend_back_kernel(
    tiles,
    factor,
    q_ref,
    k_ref,
    v_ref,
    d_ref,
    cos_ref,
    sin_ref,
    sq_ref,
    sk_ref,
    dq_ref,
    dk_ref,
    dv_ref,
):
    at = pl.program_id(1)
    tile = q_ref.shape[0]

    @pl.when(at == 0)
    def _():
        dk_ref[...] = jnp.zeros_like(dk_ref)
        dv_ref[...] = jnp.zeros_like(dv_ref)

    for i in range(tiles):

        @pl.when(at == i)
        def _():
            own = slice(i * tile, (i + 1) * tile)
            width = (i + 1) * tile
            query, grad = q_ref[...], d_ref[...]
            weights, total = tile_weights(
                query, k_ref[:width], sq_ref[...], sk_ref[:, :width], i * tile, factor
            )
            weights = weights / total
            grad_weights = dot(grad, v_ref[:width], NT)
            delta = jnp.sum(weights * grad_weights, axis=1, keepdims=True)
            grad_scores = (weights * (grad_weights - delta)).astype(BF)
            grad_query = dot(grad_scores, k_ref[:width]) * factor
            dq_ref[...] = turned(grad_query, cos_ref[own], -sin_ref[own])
            dk_ref[:width] += dot(grad_scores, query, TN)
            dv_ref[:width] += dot(weights.astype(BF), grad, TN)

    @pl.when(at == tiles - 1)
    def _():
        dk_ref[...] = turned(dk_ref[...] * factor, cos_ref[...], -sin_ref[...])


def attend_back(q, k, v, grad, cosine, sine, seg, tile=512):
    rows, width = q.shape
    heads, tiles = width // HD, rows // tile
    own = pl.BlockSpec((tile, HD), lambda h, i: (i, h))
    whole = pl.BlockSpec((rows, HD), lambda h, i: (0, h))
    table = pl.BlockSpec((rows, HD), lambda h, i: (0, 0))
    pairs = heads * rows * rows * (tiles + 1) // (2 * tiles)
    return pl.pallas_call(
        functools.partial(attend_back_kernel, tiles, 1.0 / math.sqrt(HD)),
        out_shape=[jax.ShapeDtypeStruct((rows, width), F32)] * 3,
        grid=(heads, tiles),
        in_specs=[
            own,
            whole,
            whole,
            own,
            table,
            table,
            pl.BlockSpec((tile, 1), lambda h, i: (i, 0)),
            pl.BlockSpec((1, rows), lambda h, i: (0, 0)),
        ],
        out_specs=[own, whole, whole],
        compiler_params=pltpu.CompilerParams(vmem_limit_bytes=48 << 20),
        cost_estimate=pl.CostEstimate(
            flops=10 * pairs * HD, bytes_accessed=20 * rows * width, transcendentals=pairs
        ),
    )(q, k, v, grad, cosine, sine, seg[:, None], seg[None, :])


def pick_rows(tok, low, windows, source_ref, acc_ref):
    last = source_ref.shape[0] - WIN
    span = lax.broadcasted_iota(jnp.int32, (TILE, WIN), 1)

    def window(j):
        base = low + j * WIN
        start = pl.multiple_of(jnp.minimum(base, last), 128)
        match = (tok - start == span) & (tok >= base)
        return dot(match.astype(F32).astype(BF), source_ref[pl.ds(start, WIN), :])

    acc_ref[...] = window(0)

    @pl.loop(1, windows)
    def _(j):
        acc_ref[...] += window(j)

    return acc_ref[...].astype(BF)


def copy_all(copies):
    for copy in copies:
        copy.start()
    for copy in copies:
        copy.wait()


def back_rows_kernel(tiles_ref, low_ref, windows_ref, me_ref, tok_ref, dy_ref, *refs):
    parts, (rows_ref, raw_ref, down_ref, acc_ref, sems) = refs[:-5], refs[-5:]
    i = pl.program_id(0)

    @pl.when(i == 0)
    def _():
        if len(parts) == 1:
            copy_all([pltpu.make_async_copy(parts[0], down_ref, sems.at[0])])
            return
        rows, width = down_ref.shape[0] // 4, down_ref.shape[1] // 2
        copies = []
        for away, part in enumerate(parts):
            owner = pl.multiple_of((me_ref[0] ^ away) * rows, rows)
            for k in range(2):
                copies.append(
                    pltpu.make_async_copy(
                        part.at[pl.ds((k + 1) * rows, rows)],
                        down_ref.at[pl.ds(owner, rows), pl.ds(k * width, width)],
                        sems.at[len(copies)],
                    )
                )
        copy_all(copies)

    @pl.when(i < tiles_ref[0])
    def _():
        rows = pick_rows(tok_ref[...], low_ref[i], windows_ref[i], dy_ref, acc_ref)
        rows_ref[...] = rows
        raw_ref[...] = dot(rows, down_ref[...], NT)

    @pl.when(i >= tiles_ref[0])
    def _():
        rows_ref[...] = jnp.zeros_like(rows_ref)
        raw_ref[...] = jnp.zeros_like(raw_ref)


def back_rows(tables, me, upstream, parts, ff):
    total, width = upstream.shape
    capacity = tables[3].shape[0]
    tile = lambda n: pl.BlockSpec((TILE, n), lambda i, *_: (i, 0))
    once = lambda shape: pl.BlockSpec(shape, lambda i, *_: (0, 0), pipeline_mode=pl.Buffered(1))
    return pl.pallas_call(
        back_rows_kernel,
        out_shape=[
            jax.ShapeDtypeStruct((capacity, width), BF),
            jax.ShapeDtypeStruct((capacity, ff), F32),
            jax.ShapeDtypeStruct((ff, width), BF),
        ],
        grid_spec=pltpu.PrefetchScalarGridSpec(
            num_scalar_prefetch=4,
            grid=(capacity // TILE,),
            in_specs=[tile(1), once((total, width))]
            + [pl.BlockSpec(memory_space=pl.ANY)] * len(parts),
            out_specs=[tile(width), tile(ff), pl.BlockSpec((ff, width), lambda i, *_: (0, 0))],
            scratch_shapes=[
                pltpu.VMEM((TILE, width), F32),
                pltpu.SemaphoreType.DMA((2 * len(parts),)),
            ],
        ),
        compiler_params=pltpu.CompilerParams(vmem_limit_bytes=48 << 20),
        cost_estimate=pl.CostEstimate(
            flops=total * (width * ff + WIN * width),
            bytes_accessed=2 * total * width + 4 * ff * width + capacity * (2 * width + 4 * ff),
            transcendentals=0,
        ),
    )(*tables[:3], me, tables[3], upstream, *parts)


def expert_kernel(
    own, tiles_ref, low_ref, windows_ref, ids_ref, tok_ref, h_ref, router_ref, raw_ref, *refs
):
    parts = refs[:-8]
    rows_ref, hid_ref, dab_ref, dh_ref, share_ref, both_ref, acc_ref, sems = refs[-8:]
    wg_ref, wu_ref = both_ref.at[0], both_ref.at[1]
    i = pl.program_id(0)
    ff = wg_ref.shape[1]

    @pl.when(i == 0)
    def _():
        if len(parts) == 1:
            copy_all([pltpu.make_async_copy(parts[0], both_ref, sems.at[0])])
            return
        rows = wg_ref.shape[0] // 4
        half = rows // 2
        copies = []
        for away in range(4):
            owner = pl.multiple_of((ids_ref[1] ^ away) * rows, rows)
            for part, first, count, which, shift in (
                (parts[away], 0, rows, 0, 0),
                (parts[away], rows, half, 1, 0),
                (parts[4 + away], 0, half, 1, half),
            ):
                copies.append(
                    pltpu.make_async_copy(
                        part.at[pl.ds(first, count)],
                        both_ref.at[which, pl.ds(owner + shift, count)],
                        sems.at[len(copies)],
                    )
                )
        copy_all(copies)

    @pl.when(i < tiles_ref[0])
    def _():
        rows = pick_rows(tok_ref[...], low_ref[i], windows_ref[i], h_ref, acc_ref)
        rows_ref[...] = rows
        logits = dot(rows, router_ref[...])
        probs = jnp.exp(logits - jnp.max(logits, axis=1, keepdims=True))
        column = lax.broadcasted_iota(jnp.int32, probs.shape, 1)
        mine = jnp.sum(jnp.where(column == ids_ref[0] + own, probs, 0.0), axis=1, keepdims=True)
        gate = mine / jnp.sum(probs, axis=1, keepdims=True)
        share = 0.0
        part = ff // 4
        for c in range(4):
            cols = slice(c * part, (c + 1) * part)
            a = dot(rows, wg_ref[:, cols])
            b = dot(rows, wu_ref[:, cols])
            raw = raw_ref[:, cols]
            sig = 1.0 / (1.0 + jnp.exp(-a))
            silu = a * sig
            hid = silu * b
            share += jnp.sum(hid * raw, axis=1, keepdims=True)
            raw = raw * gate
            hid_ref[:, cols] = (hid * gate).astype(BF)
            dab_ref[:, cols] = (raw * b * (sig * (1.0 + a * (1.0 - sig)))).astype(BF)
            dab_ref[:, ff + c * part : ff + (c + 1) * part] = (raw * silu).astype(BF)
        share_ref[...] = share
        dh = dot(dab_ref[:, :ff], wg_ref[...], NT) + dot(dab_ref[:, ff:], wu_ref[...], NT)
        dh_ref[...] = dh.astype(BF)

    @pl.when(i >= tiles_ref[0])
    def _():
        for ref in (rows_ref, hid_ref, dab_ref, dh_ref, share_ref):
            ref[...] = jnp.zeros_like(ref)


def expert_rows(tables, own, ids, hidden, router, parts, raw):
    total, width = hidden.shape
    capacity, ff = raw.shape
    tile = lambda n: pl.BlockSpec((TILE, n), lambda i, *_: (i, 0))
    once = lambda shape: pl.BlockSpec(shape, lambda i, *_: (0, 0), pipeline_mode=pl.Buffered(1))
    made = lambda n, dtype=BF: jax.ShapeDtypeStruct((capacity, n), dtype)
    return pl.pallas_call(
        functools.partial(expert_kernel, own),
        out_shape=[made(width), made(ff), made(2 * ff), made(width), made(1, F32)],
        grid_spec=pltpu.PrefetchScalarGridSpec(
            num_scalar_prefetch=4,
            grid=(capacity // TILE,),
            in_specs=[tile(1), once((total, width)), once(router.shape), tile(ff)]
            + [pl.BlockSpec(memory_space=pl.ANY)] * len(parts),
            out_specs=[tile(width), tile(ff), tile(2 * ff), tile(width), tile(1)],
            scratch_shapes=[
                pltpu.VMEM((2, width, ff), BF),
                pltpu.VMEM((TILE, width), F32),
                pltpu.SemaphoreType.DMA((12,)),
            ],
        ),
        compiler_params=pltpu.CompilerParams(vmem_limit_bytes=56 << 20),
        cost_estimate=pl.CostEstimate(
            flops=total * (4 * width * ff + WIN * width),
            bytes_accessed=2 * total * width + 4 * ff * width + capacity * (4 * width + 10 * ff),
            transcendentals=total * ff,
        ),
    )(*tables[:3], ids, tables[3], hidden, router, raw, *parts)


def combine_kernel(experts, shared, start_ref, more_ref, wide_ref, id_ref, pos_ref, *refs):
    rows_refs, share_refs = refs[:experts], refs[experts:-2]
    out_ref, acc_ref = refs[-2:]
    i = pl.program_id(0)
    span = lax.broadcasted_iota(jnp.int32, (TILE, TILE), 1)
    last, width = rows_refs[0].shape[0] - TILE, rows_refs[0].shape[1]

    def window(e, j):
        base = start_ref[e, i] + j * TILE
        start = pl.multiple_of(jnp.minimum(base, last), 16)
        pos = pos_ref[:, e : e + 1]
        match = (pos - start == span) & (pos >= base)
        return dot(match.astype(F32).astype(BF), rows_refs[e][pl.ds(start, TILE), :])

    acc_ref[...] = sum(window(e, 0) for e in range(experts))
    for e in range(experts):

        @pl.when(more_ref[e, i] > 0)
        def _():
            acc_ref[...] += window(e, 1)

    out_ref[:, :width] = acc_ref[...].astype(BF)
    if shared:
        wide_span = lax.broadcasted_iota(jnp.int32, (TILE, 384), 1)
        column = lax.broadcasted_iota(jnp.int32, (TILE, shared), 1)
        extra = jnp.zeros((TILE, shared), F32)
        for e in range(experts):
            wide = pl.multiple_of(wide_ref[e, i], 128)
            match = pos_ref[:, e : e + 1] - wide == wide_span
            share = share_refs[e][:, pl.ds(wide, 384)]
            own = jnp.sum(jnp.where(match, share, 0.0), axis=1, keepdims=True)
            head = own.astype(BF).astype(F32)
            first = 2 * (id_ref[0] + e)
            extra += jnp.where(column == first, head, 0.0)
            extra += jnp.where(column == first + 1, own - head, 0.0)
        out_ref[:, width:] = extra.astype(BF)


def combine_rows(tables, ids, rows, shares=()):
    experts, (capacity, width) = len(rows), rows[0].shape
    total = tables[3].shape[0]
    shared = 128 if shares else 0
    once = lambda shape: pl.BlockSpec(shape, lambda i, *_: (0, 0), pipeline_mode=pl.Buffered(1))
    tile = lambda n: pl.BlockSpec((TILE, n), lambda i, *_: (i, 0))
    return pl.pallas_call(
        functools.partial(combine_kernel, experts, shared),
        out_shape=jax.ShapeDtypeStruct((total, width + shared), BF),
        grid_spec=pltpu.PrefetchScalarGridSpec(
            num_scalar_prefetch=4,
            grid=(total // TILE,),
            in_specs=[tile(experts)]
            + [once((capacity, width))] * experts
            + [once((1, capacity))] * len(shares),
            out_specs=tile(width + shared),
            scratch_shapes=[pltpu.VMEM((TILE, width), F32)],
        ),
        compiler_params=pltpu.CompilerParams(vmem_limit_bytes=48 << 20),
        cost_estimate=pl.CostEstimate(
            flops=2 * experts * total * TILE * width,
            bytes_accessed=2 * (experts * capacity + total) * width,
            transcendentals=0,
        ),
    )(*tables[:3], ids, tables[3], *rows, *shares)


def local(
    tokens,
    cotangent,
    routes,
    block_of_slot,
    cont_seg,
    w_query,
    w_key,
    w_value,
    w_out,
    w_router,
    attn_gain,
    query_gain,
    key_gain,
    ffn_gain,
    w_gate,
    w_up,
    w_down,
):
    ctx_size = lax.axis_size("ctx")
    exp_size = lax.axis_size("exp")
    me = lax.axis_index("ctx")
    exp_index = lax.axis_index("exp")
    tok_rows = tokens.shape[0]
    part_rows = w_query.shape[0]
    own_width = D // ctx_size
    own_heads = HEADS // ctx_size
    experts = w_router.shape[1]
    own_experts = w_gate.shape[0]
    slot_table = block_of_slot[0]
    seg_row = cont_seg[0]
    group_rows = ctx_size * tok_rows
    factor = 1.0 / math.sqrt(HD)

    tokens_group, tokens_there = gather_group(tokens, slot_table, me)
    small = jnp.concatenate(
        [w_router] + [g[:, None] for g in (attn_gain, query_gain, key_gain, ffn_gain)], axis=1
    )
    small = jnp.pad(small, ((0, 0), (0, 128 - small.shape[1])))
    by_owner = jnp.stack(
        [w.reshape(part_rows, ctx_size, own_width) for w in (w_query, w_key, w_value)], axis=2
    )
    by_owner = jnp.swapaxes(by_owner, 0, 1).reshape(ctx_size, part_rows, 3 * own_width)
    by_owner = jnp.concatenate(
        [by_owner, jnp.broadcast_to(small, (ctx_size,) + small.shape)], axis=2
    )
    out_full = lax.all_gather(w_out, "exp", axis=0, tiled=True)
    own_columns, out_full = after_all((exchange(by_owner, me), out_full))
    packed = lax.all_gather(own_columns, "exp", axis=1, tiled=True).reshape(D, 3 * own_width + 128)
    small_full = packed[:, 3 * own_width :]
    router_full = small_full[:, :experts]
    gains = small_full[:, experts : experts + 4].astype(F32)
    gain_attn, gain_ffn = gains[:, 0], gains[:, 3]
    own_gains = lax.dynamic_slice(gains, (me * own_width, 0), (own_width, 4))
    gain_query, gain_key = own_gains[:, 1], own_gains[:, 2]
    routes_all = lax.all_to_all(
        jnp.broadcast_to(routes[None], (exp_size,) + routes.shape),
        "exp",
        split_axis=0,
        concat_axis=0,
        tiled=True,
    ).reshape(exp_size * tok_rows, TOP)
    upstream_all = lax.all_gather(cotangent, "exp", axis=0, tiled=True)
    packs = [pack_expert(w_gate[e], w_up[e], w_down[e]) for e in range(own_experts)]
    if ctx_size == 4:
        ahead = after_all(packs[0], *tokens_there)
        ahead = send_x(ahead[0]), send_y(ahead[1])

    seg_ids = jnp.concatenate([jnp.full((PROMPT,), -1, jnp.int32), seg_row])
    starts = jnp.sum(
        (seg_row[None, :] < jnp.arange(CONT, dtype=jnp.int32)[:, None]).astype(jnp.int32), axis=1
    )
    first_pos = jnp.sum(
        jnp.where(
            seg_row[:, None] == jnp.arange(CONT, dtype=jnp.int32)[None, :], starts[None, :], 0
        ),
        axis=1,
    )
    cont_pos = PROMPT + jnp.arange(CTOK, dtype=jnp.int32) - first_pos
    position = jnp.concatenate([jnp.arange(PROMPT, dtype=jnp.int32), cont_pos])
    cos_part, sin_part = angles(position)
    group_inputs = tokens_group.astype(F32)
    normed_group = group_inputs * inverse_root(group_inputs)
    hidden_one = (normed_group * gain_attn).astype(BF)
    projected = jnp.dot(hidden_one, packed, preferred_element_type=F32)
    query_pre = projected[:, :own_width]
    key_pre = projected[:, own_width : 2 * own_width]
    squares = jnp.stack([jnp.sum(query_pre * query_pre, axis=1), jnp.sum(key_pre * key_pre, axis=1)])
    if ctx_size == 4:
        squares = after(squares, *ahead)
    squares = sum_over_ctx(squares)
    if ctx_size == 4:
        direct = after_all(packs[0], squares)
        direct = send_x(direct[1]), send_y(direct[0])
    roots = lax.rsqrt(squares / D + epsilon)
    root_query, root_key = roots[0][:, None], roots[1][:, None]
    normed_query = query_pre * root_query
    normed_key = key_pre * root_key
    query_rot, key_rot, value_low, context_low = attend(
        projected,
        roots.T,
        jnp.stack([gain_query, gain_key]),
        cos_part,
        sin_part,
        seg_ids,
        own_width,
    )
    branch_part = jnp.dot(context_low, out_full, preferred_element_type=F32)
    if ctx_size == 4:
        branch_part = after(branch_part, *direct)
    branch, unused, unused, branch_there = scatter_group(branch_part, slot_table, me)
    me_table = jnp.reshape(me, (1,)).astype(jnp.int32)
    width = w_gate.shape[2]
    lows, highs, backs = [], [], []
    if ctx_size == 4:
        passed = after_all(ahead, *branch_there)
        passed = send_y(passed[0]), send_x(passed[1])
        lows.append((packs[0][0], ahead[0], direct[1], passed[0]))
        highs.append((packs[0][1], direct[0], ahead[1], passed[1]))
        upstream, first_passed = upstream_all, passed
        for e in range(1, own_experts):
            low, high = after_all(packs[e], *passed)
            ahead = send_x(low), send_y(high)
            low, high = after_all((low, high), *ahead)
            direct = send_x(high), send_y(low)
            passed = send_y(ahead[0]), send_x(ahead[1])
            lows.append((packs[e][0], ahead[0], direct[1], passed[0]))
            highs.append((packs[e][1], direct[0], ahead[1], passed[1]))
            upstream = after(upstream, *ahead)
    else:
        for e in range(own_experts):
            both, down = whole_expert(*after_all((w_gate[e], w_up[e], w_down[e]), *branch_there))
            lows.append((both,))
            highs.append((down,))
        upstream = upstream_all
        first_passed = branch_there

    own_ids = exp_index * own_experts + jnp.arange(own_experts, dtype=jnp.int32)
    member = jnp.any(after(routes_all, *first_passed)[:, :, None] == own_ids[None, None, :], axis=1)
    place_of = prefix_count(member)
    capacity = exp_size * 8 * ((5 * tok_rows * TOP // (4 * experts) + 7) // 8)
    row_tiles = (capacity + TILE - 1) // TILE
    capacity = row_tiles * TILE
    all_rows = exp_size * tok_rows
    row_ids = jnp.arange(capacity, dtype=jnp.int32)
    hit = (place_of.T[:, None, :] == row_ids[None, :, None]) & member.T[:, None, :]
    token_ids = jnp.arange(all_rows, dtype=jnp.int32)
    token_of_row = jnp.max(jnp.where(hit, token_ids[None, None, :], -1), axis=2)
    counts = jnp.sum(member.astype(jnp.int32), axis=0)
    used_tiles = (counts + TILE - 1) // TILE
    by_tile = token_of_row.reshape(own_experts * row_tiles, TILE)
    low_token = jnp.maximum(by_tile[:, 0], 0) // 128 * 128
    windows = jnp.maximum((jnp.max(by_tile, axis=1) - low_token) // WIN + 1, 1)
    low_token = low_token.reshape(own_experts, row_tiles)
    windows = windows.reshape(own_experts, row_tiles)
    row_tables = [
        (used_tiles[e : e + 1], low_token[e], windows[e], token_of_row[e][:, None])
        for e in range(own_experts)
    ]
    place_column = jnp.where(member, place_of, NOWHERE)
    first_place = place_of[::TILE].T
    in_tile = jnp.sum(member.reshape(-1, TILE, own_experts).astype(jnp.int32), axis=1).T
    first_row = first_place // 16 * 16
    more_rows = (first_place + in_tile - first_row > TILE).astype(jnp.int32)
    share_row_start = jnp.minimum(first_place // 128 * 128, capacity - 384)
    token_tables = (first_row, more_rows, share_row_start, place_column)

    ids = jnp.stack([own_ids[0], me.astype(jnp.int32)])
    backs.append(back_rows(row_tables[0], me_table, upstream, highs[0], width))

    inputs = tokens.astype(F32)
    middle = inputs + branch
    root_two = inverse_root(middle)
    normed_two = middle * root_two
    hidden_two = (normed_two * gain_ffn).astype(BF)
    hidden_all = lax.all_gather(hidden_two, "exp", axis=0, tiled=True)
    logits = jnp.dot(hidden_two, router_full, preferred_element_type=F32)
    router_prob = jax.nn.softmax(logits, axis=-1)

    every = range(own_experts)
    made = []
    for e in every:
        if e > 0:
            upstream = after(upstream_all, made[-1][3])
            highs[e] = after_all(highs[e], made[-1][3])
            backs.append(back_rows(row_tables[e], me_table, upstream, highs[e], width))
        parts = tuple(lows[e]) + tuple(highs[e]) if ctx_size == 4 else lows[e]
        made.append(
            expert_rows(row_tables[e], e, ids, hidden_all, router_full, parts, backs[e][1])
        )
    shares = [m[4].reshape(1, capacity) for m in made]
    grad_two_part = combine_rows(token_tables, ids, [m[3] for m in made], shares)
    grad_two = lax.psum_scatter(grad_two_part, "exp", scatter_dimension=0, tiled=True)
    def weight_grads(e, *others):
        rows, hidden, grad_hidden = after_all(made[e][:3], *others)
        return (
            lax.dot_general(rows, grad_hidden, TN, preferred_element_type=F32).astype(BF),
            lax.dot_general(hidden, backs[e][0], TN, preferred_element_type=F32).astype(BF),
        )

    expert_grads = [weight_grads(0, grad_two_part)]
    if ctx_size == 4:
        take = expert_take(expert_grads[0])
        payload = joined_payload(take, me)
    else:
        payload = expert_grads[0]
    results = [
        jnp.dot(
            after(made[e][1], *payload), backs[e][2], preferred_element_type=F32
        ).astype(BF)
        for e in every
    ]
    if ctx_size == 4:
        ahead, direct = split_sums((send_x(payload[0]), send_y(payload[1])))
        last = scatter_last_payload(take, me, ahead)
        results = after_all(results, *last)
        last = send_y(last[0]), send_x(last[1])
    else:
        direct, last = scatter_expert_first(expert_grads[0], me), ()
    mixture_part = combine_rows(token_tables, ids, results)
    directs, lasts = [direct], [last]

    mixture = lax.psum_scatter(mixture_part, "exp", scatter_dimension=0, tiled=True)
    output = (middle + mixture.astype(F32)).astype(BF)
    grad_two = after(grad_two, mixture_part)
    grad_prob = jnp.sum(
        grad_two[:, D : D + 2 * experts].astype(F32).reshape(tok_rows, experts, 2), axis=2
    )
    grad_two = grad_two[:, :D].astype(F32)
    grad_logits = (
        router_prob * (grad_prob - jnp.sum(router_prob * grad_prob, axis=-1, keepdims=True))
    ).astype(BF)
    grad_router = jnp.einsum("td,te->ed", hidden_two, grad_logits, preferred_element_type=F32)
    grad_two = grad_two + jnp.einsum(
        "te,de->td", grad_logits, router_full, preferred_element_type=F32
    )
    grad_ffn_gain = jnp.sum(grad_two * normed_two, axis=0)
    grad_middle = cotangent.astype(F32) + norm_back(grad_two * gain_ffn, normed_two, root_two)

    own_grad = after(grad_middle.astype(BF), *directs[0], *lasts[0])
    branch_grad, grad_there = gather_group(own_grad, slot_table, me)
    sums = []
    for e in range(1, own_experts):
        expert_grads.append(weight_grads(e, own_grad))
        sums.append(scatter_expert_first(after_all(expert_grads[e], *grad_there), me))
    grad_context = lax.dot_general(branch_grad, out_full, NT, preferred_element_type=F32).astype(BF)
    out_grad = lax.dot_general(
        context_low, branch_grad, TN, preferred_element_type=F32
    ).astype(BF)
    grad_query_norm, grad_key_norm, grad_value = attend_back(
        query_rot, key_rot, value_low, grad_context, cos_part, sin_part, seg_ids
    )
    grad_query_gain = jnp.sum(grad_query_norm * normed_query, axis=0)
    grad_key_gain = jnp.sum(grad_key_norm * normed_key, axis=0)
    scaled_query = grad_query_norm * gain_query
    scaled_key = grad_key_norm * gain_key
    products = jnp.stack(
        [jnp.sum(scaled_query * normed_query, axis=1), jnp.sum(scaled_key * normed_key, axis=1)]
    )
    direct, last = after_all(directs[0], grad_value), after_all(lasts[0], grad_value)
    weight_sums = [scatter_expert_end(expert_grads[0], direct, last, me)]
    *weight_sums[0], products = after_all(
        (*weight_sums[0], products), out_grad, *(piece for pieces in sums for piece in pieces)
    )
    means = sum_over_ctx(products) / D
    for e in range(1, own_experts):
        ahead, direct = split_sums(sums[e - 1])
        directs.append(direct)
        ahead = after_all(ahead, means)
        take = expert_take(expert_grads[e])
        if ctx_size == 4:
            last_sent = scatter_last_payload(take, me, ahead)
            lasts.append((send_y(last_sent[0]), send_x(last_sent[1])))
        else:
            last_sent = direct
            lasts.append(())
    grad_projected = jnp.concatenate(
        [
            root_query * (scaled_query - normed_query * means[0][:, None]),
            root_key * (scaled_key - normed_key * means[1][:, None]),
            grad_value,
        ],
        axis=1,
    ).astype(BF)
    grad_packed = jnp.pad(grad_projected, ((0, 0), (0, 128)))
    grad_one_part = lax.dot_general(grad_packed, packed, NT, preferred_element_type=F32)
    grad_attn_gain = jnp.sum(grad_one_part * normed_group, axis=0)
    left, right = after_all((hidden_one, grad_projected), *last_sent)
    qkv_grad = lax.dot_general(left, right, TN, preferred_element_type=F32).astype(BF)
    grad_one, one_first, one_sent, unused = scatter_group(
        after(grad_one_part, *(piece for pieces in lasts[1:] for piece in pieces)),
        slot_table,
        me,
        joined=True,
    )
    for e in range(1, own_experts):
        direct, last = after_all(directs[e], *one_sent), after_all(lasts[e], *one_sent)
        weight_sums.append(scatter_expert_end(expert_grads[e], direct, last, me))
    gate_grad, up_grad, down_grad = (jnp.stack(parts) for parts in zip(*weight_sums))
    out_sum = lax.psum_scatter(
        out_grad, "exp", scatter_dimension=0, tiled=True
    ).astype(F32)
    qkv_sum = lax.psum_scatter(
        after(qkv_grad, mixture).reshape(ctx_size, exp_size * part_rows, 3 * own_width),
        "exp",
        scatter_dimension=1,
        tiled=True,
    )
    qkv_own = exchange(qkv_sum, me).astype(F32)
    projection_grads = [
        jnp.swapaxes(qkv_own[:, :, i * own_width : (i + 1) * own_width], 0, 1).reshape(part_rows, D)
        for i in range(3)
    ]
    root_one = inverse_root(inputs)
    normed_one = inputs * root_one
    grad_input = grad_middle + norm_back(grad_one * gain_attn, normed_one, root_one)
    head_gains = lax.dynamic_update_slice(
        jnp.zeros((2, D), F32), jnp.stack([grad_query_gain, grad_key_gain]), (0, me * own_width)
    )
    small_sums = jnp.concatenate(
        [grad_router, jnp.stack([grad_ffn_gain, grad_attn_gain]), head_gains]
    )
    small_sums = sum_to_rows(after(small_sums, *one_first), me, one_sent, qkv_sum)
    return (
        output,
        grad_input,
        projection_grads[0],
        projection_grads[1],
        projection_grads[2],
        out_sum,
        small_sums[:experts].T,
        small_sums[experts + 1],
        small_sums[experts + 2],
        small_sums[experts + 3],
        small_sums[experts],
        gate_grad,
        up_grad,
        down_grad,
    )


def solution(mesh):
    rows = P(BOTH, None)
    weights = P("exp", "ctx", None)
    in_specs = (
        (rows, rows, rows, P("exp", None), P("exp", None))
        + (rows,) * 5
        + (P(BOTH),) * 4
        + (weights,) * 3
    )
    out_specs = (rows,) * 7 + (P(BOTH),) * 4 + (weights,) * 3
    return jax.shard_map(local, mesh=mesh, in_specs=in_specs, out_specs=out_specs, check_vma=False)
```
